32 devices in a mesh: dp: 8 (over z, y), expert: 4 (over x, core).
Axes of the slice: x: 2, y: 2, z: 4, core: 2. Of those that a mesh axis runs over, the one named last changes fastest.
Arguments:
- hidden_in: float32 [4, 2560, 1536], P('expert', 'dp'), may hold values from -6 to 6
- gain_attn: float32 [1536], replicated, may hold values from 0.5 to 1.5
- w_query: bfloat16 [1536, 1536], replicated, may hold values from -0.15625 to 0.15625
- w_key: bfloat16 [1536, 512], replicated, may hold values from -0.15625 to 0.15625
- w_value: bfloat16 [1536, 512], replicated, may hold values from -0.15625 to 0.15625
- w_output: bfloat16 [1536, 1536], replicated, may hold values from -1.25 to 1.25
- gain_mlp: float32 [1536], replicated, may hold values from 0.5 to 1.5
- w_router: bfloat16 [1536, 40], replicated, may hold values from -0.078125 to 0.078125
- w_gate: bfloat16 [40, 1536, 512], P('expert'), may hold values from -0.15625 to 0.15625
- w_up: bfloat16 [40, 1536, 512], P('expert'), may hold values from -0.15625 to 0.15625
- w_down: bfloat16 [40, 512, 1536], P('expert'), may hold values from -1 to 1
- expert_ids: int32 [4, 2560, 8], P('expert', 'dp'), may hold values from 0 to 39, all different within a row
- slot_order: int32 [4, 8, 2560], P('expert', 'dp'), may hold values from 0 to 2559, each once within a row
- grad_out: float32 [4, 2560, 1536], P('expert', 'dp'), may hold values from -6 to 6
Outputs:
- hidden_out: float32 [4, 2560, 1536], P('expert', 'dp')
- grad_in: float32 [4, 2560, 1536], P('expert', 'dp')
- grad_gain_attn: float32 [1536], P(('dp', 'expert'))
- grad_query: float32 [1536, 1536], P(('dp', 'expert'))
- grad_key: float32 [1536, 512], P(('dp', 'expert'))
- grad_value: float32 [1536, 512], P(('dp', 'expert'))
- grad_output: float32 [1536, 1536], P(('dp', 'expert'))
- grad_gain_mlp: float32 [1536], P(('dp', 'expert'))
- grad_router: float32 [1536, 40], P(('dp', 'expert'))
- grad_gate: float32 [40, 1536, 512], P('expert', 'dp')
- grad_up: float32 [40, 1536, 512], P('expert', 'dp')
- grad_down: float32 [40, 512, 1536], P('expert', 'dp')
The draws below stay inside these ranges and needn't reach their ends.
Inputs may be any that keep to these rules, and one draw needn't show every extreme that they name: `expert_ids`: each token names 8 different experts. `slot_order`: for every sequence and block, the 2560 ranks of the block's pairs are each of 0 to 2559 once.
All inputs are finite; a program needn't handle non-finite values.
Results may differ from the reference program's by a relative error of at most 0.019.
Values may be sent and summed in bfloat16 or wider, within the bound.
A program may use at most 320 MiB of HBM per device.

```python
import math
import jax
import jax.numpy as jnp
from jax import lax

D = 1536
HEADS = 24
KV_HEADS = 8
HEAD_DIM = 64
FFE = 512
EXPERTS = 40
TOP = 8
TOK_DEV = 320
SEQS = 4
SEQ_LEN = 2560
BLOCKS = 8
CAPACITY = 64
N_DP = 8


def steps_of(own_key, extent, shards, least, high):
    loudness, own = 1.0, jax.random.fold_in(own_key, 6)
    for dim, parts in shards:
        draws = jnp.exp(jax.random.uniform(jax.random.fold_in(own, dim), (parts,), jnp.float32, least / len(shards), high / len(shards)))
        loudness = loudness * jnp.repeat(draws, extent[dim] // parts).reshape([-1 if axis == dim else 1 for axis in range(len(extent))])
    return loudness


def picks_of(rng, rows, amount, top, lift):
    sequence = jax.random.permutation(jax.random.fold_in(rng, 1), amount)
    boost = sequence
    for power in range(3):
        boost = boost * boost // amount
    boost = boost * lift // amount
    chance = jax.random.randint(jax.random.fold_in(rng, 2), (rows, amount), 0, 4096) + boost
    sure = jax.random.permutation(jax.random.fold_in(rng, 3), rows)[jnp.arange(amount) % rows]
    chance = jnp.where(jnp.arange(rows)[:, None] == sure[None, :], 1 << 14, chance)
    score = chance * amount + jnp.arange(amount)
    return lax.top_k(score.astype(jnp.int32), top)[1].astype(jnp.int32)


def bell_draw(own_key, dims, spread, most, split=(), kind=jnp.bfloat16):
    level = steps_of(own_key, dims, split, -0.22, 0.18) if split else 1.0
    drawn = jax.random.normal(own_key, dims, jnp.float32) * spread * level
    return jnp.minimum(jnp.maximum(drawn, -most), most).astype(kind)


def setup_inputs(seed: int = 0) -> dict:
    key_of = jax.random.split(jax.random.key(seed), 15)
    hidden_in = bell_draw(key_of[0], (SEQS, SEQ_LEN, D), 1.0, 6.0, ((0, 4), (1, 8)), jnp.float32)
    gain_attn = jnp.clip(1.0 + 0.1 * jax.random.normal(key_of[1], (D,), jnp.float32), 0.5, 1.5)
    w_query = bell_draw(key_of[2], (D, HEADS * HEAD_DIM), D ** -0.5, 0.15625)
    w_key = bell_draw(key_of[3], (D, KV_HEADS * HEAD_DIM), D ** -0.5, 0.15625)
    w_value = bell_draw(key_of[4], (D, KV_HEADS * HEAD_DIM), D ** -0.5, 0.15625)
    w_output = bell_draw(key_of[5], (HEADS * HEAD_DIM, D), (HEADS * HEAD_DIM // 64) ** -0.5, 1.25)
    gain_mlp = jnp.clip(1.0 + 0.1 * jax.random.normal(key_of[6], (D,), jnp.float32), 0.5, 1.5)
    w_router = bell_draw(key_of[7], (D, EXPERTS), (4 * D) ** -0.5, 0.078125)
    w_gate = bell_draw(key_of[8], (EXPERTS, D, FFE), D ** -0.5, 0.15625, ((0, 4),))
    w_up = bell_draw(key_of[9], (EXPERTS, D, FFE), D ** -0.5, 0.15625, ((0, 4),))
    w_down = bell_draw(key_of[10], (EXPERTS, FFE, D), (FFE // 16) ** -0.5, 1.0, ((0, 4),))
    expert_ids = picks_of(key_of[11], SEQS * SEQ_LEN, EXPERTS, TOP, 1638).reshape((SEQS, SEQ_LEN, TOP))
    slot_order = jax.vmap(lambda own: jax.random.permutation(own, TOK_DEV * TOP))(jax.random.split(key_of[12], SEQS * BLOCKS)).reshape((SEQS, BLOCKS, TOK_DEV * TOP)).astype(jnp.int32)
    grad_out = bell_draw(key_of[13], (SEQS, SEQ_LEN, D), 1.0, 6.0, ((0, 4), (1, 8)), jnp.float32)
    return dict(hidden_in=hidden_in, gain_attn=gain_attn, w_query=w_query, w_key=w_key, w_value=w_value, w_output=w_output, gain_mlp=gain_mlp, w_router=w_router, w_gate=w_gate, w_up=w_up, w_down=w_down, expert_ids=expert_ids, slot_order=slot_order, grad_out=grad_out)


EPS = 1e-05
HIGH = lax.Precision.HIGHEST
MASKED = -1e+30

@jax.custom_vjp
def low(v):
    return lax.optimization_barrier(v.astype(jnp.bfloat16)).astype(jnp.float32)

@jax.custom_vjp
def low_back(v):
    return v

def low_keep(v):
    return (low(v), None)

def low_pass(kept, grad):
    return (grad,)

def back_keep(v):
    return (v, None)

def back_low(kept, grad):
    return (low(grad),)
low.defvjp(low_keep, low_pass)
low_back.defvjp(back_keep, back_low)

def rms_norm(values, gain):
    inverse = lax.rsqrt(lax.optimization_barrier(jnp.mean(values * values, axis=-1, keepdims=True)) + EPS)
    return values * inverse * gain

def rotary_tables(positions):
    half = HEAD_DIM // 2
    frequency = jnp.exp(-math.log(10000.0) * jnp.arange(half, dtype=jnp.float32) * 2.0 / HEAD_DIM)
    angles = positions.astype(jnp.float32)[:, None] * frequency[None, :]
    return (jnp.cos(angles)[:, None, :], jnp.sin(angles)[:, None, :])

def rotate(values, cosine, sine):
    half = values.shape[-1] // 2
    first = values[..., :half]
    second = values[..., half:]
    return jnp.concatenate([first * cosine - second * sine, second * cosine + first * sine], axis=-1)

def attend_sequence(queries, keys, values):
    length = queries.shape[0]
    block = min(512, length)
    groups = HEADS // KV_HEADS
    grouped = queries.reshape(length // block, block, KV_HEADS, groups, HEAD_DIM)
    starts = jnp.arange(length // block, dtype=jnp.int32) * block
    key_pos = jnp.arange(length, dtype=jnp.int32)

    @jax.checkpoint
    def one_block(operands):
        query_block, start = operands
        scores = jnp.einsum('qkgd,skd->kgqs', query_block, keys, precision=HIGH) * HEAD_DIM ** (-0.5)
        scores = low_back(scores)
        query_pos = start + jnp.arange(block, dtype=jnp.int32)
        allowed = key_pos[None, :] <= query_pos[:, None]
        scores = jnp.where(allowed, scores, MASKED)
        weights = low(jax.nn.softmax(scores, axis=-1))
        return jnp.einsum('kgqs,skd->qkgd', weights, values, precision=HIGH)
    result = lax.map(one_block, (grouped, starts))
    return result.reshape(length, HEADS * HEAD_DIM)

def assign_slots(chosen, ranks):
    pairs = TOK_DEV * TOP
    flat_chosen = chosen.reshape(N_DP, pairs)

    def per_block(row_chosen, row_ranks):
        by_rank = jnp.zeros((pairs,), jnp.int32).at[row_ranks].set(jnp.arange(pairs, dtype=jnp.int32))
        ordered = row_chosen[by_rank]
        table = (ordered[:, None] == jnp.arange(EXPERTS, dtype=jnp.int32)[None, :]).astype(jnp.int32)
        before = lax.optimization_barrier(jnp.sum(table * (jnp.cumsum(table, axis=0) - 1), axis=1))
        slot = before[row_ranks]
        target = jnp.where(slot < CAPACITY, row_chosen * CAPACITY + slot, EXPERTS * CAPACITY)
        owner = jnp.full((EXPERTS * CAPACITY,), pairs, jnp.int32).at[target].set(jnp.arange(pairs, dtype=jnp.int32), mode='drop')
        return owner
    return jax.vmap(per_block)(flat_chosen, ranks)

def pick_rows(table_rows, picks):
    return table_rows[picks]

def add_rows(block_rows, block_tokens):
    return jnp.zeros((TOK_DEV, D), jnp.float32).at[block_tokens].add(block_rows)

@jax.checkpoint
def one_expert(operands):
    inputs, gate_weight, up_weight, down_weight = operands
    gate_pre = low_back(jnp.dot(inputs, gate_weight, precision=HIGH))
    up_pre = low_back(jnp.dot(inputs, up_weight, precision=HIGH))
    hidden = low(jax.nn.silu(gate_pre) * up_pre)
    return low(low_back(jnp.dot(hidden, down_weight, precision=HIGH)))

def expert_layer(normed_two, gates, owner, w_gate, w_up, w_down):
    pairs = TOK_DEV * TOP
    valid = (owner < pairs).astype(jnp.float32)
    source = jnp.minimum(owner, pairs - 1)
    rows = jax.vmap(pick_rows)(normed_two.reshape(N_DP, TOK_DEV, D), source // TOP)
    rows = low_back(rows) * valid[:, :, None]
    slot_gate = jax.vmap(pick_rows)(gates.reshape(N_DP, pairs), source) * valid
    grouped = rows.reshape(N_DP, EXPERTS, CAPACITY, D).transpose(1, 0, 2, 3).reshape(EXPERTS, N_DP * CAPACITY, D)
    outputs = lax.map(one_expert, (grouped, w_gate, w_up, w_down))
    outputs = outputs.reshape(EXPERTS, N_DP, CAPACITY, D).transpose(1, 0, 2, 3).reshape(N_DP, EXPERTS * CAPACITY, D)
    weighted = outputs * slot_gate[:, :, None]
    mixed = jax.vmap(add_rows)(weighted, source // TOP)
    return mixed.reshape(N_DP * TOK_DEV, D)

def sequence_forward(weights, inputs, chosen, ranks):
    gain_attn, w_query, w_key, w_value, w_output, gain_mlp, w_router, w_gate, w_up, w_down = weights
    length = inputs.shape[0]
    normed = low(rms_norm(inputs, gain_attn))
    cosine, sine = rotary_tables(jnp.arange(length, dtype=jnp.int32))
    queries = low_back(jnp.dot(normed, w_query, precision=HIGH)).reshape(length, HEADS, HEAD_DIM)
    queries = low(rotate(queries, cosine, sine))
    keys = low_back(jnp.dot(normed, w_key, precision=HIGH)).reshape(length, KV_HEADS, HEAD_DIM)
    keys = low(rotate(keys, cosine, sine))
    values = low(low_back(jnp.dot(normed, w_value, precision=HIGH))).reshape(length, KV_HEADS, HEAD_DIM)
    attended = low(low_back(attend_sequence(queries, keys, values)))
    branch = low_back(jnp.dot(attended, w_output, precision=HIGH))
    middle = inputs + branch
    normed_two = low(rms_norm(middle, gain_mlp))
    logits = low_back(jnp.dot(normed_two, w_router, precision=HIGH))
    onehot = (chosen[:, :, None] == jnp.arange(EXPERTS, dtype=jnp.int32)[None, None, :]).astype(jnp.float32)
    picked = lax.optimization_barrier(jnp.sum(onehot * logits[:, None, :], axis=-1))
    gates = jax.nn.softmax(picked, axis=-1)
    owner = assign_slots(chosen, ranks)
    mixed = expert_layer(normed_two, gates, owner, w_gate, w_up, w_down)
    return middle + mixed

def reference(hidden_in, gain_attn, w_query, w_key, w_value, w_output, gain_mlp, w_router, w_gate, w_up, w_down, expert_ids, slot_order, grad_out):
    params = tuple((weight.astype(jnp.float32) for weight in (gain_attn, w_query, w_key, w_value, w_output, gain_mlp, w_router, w_gate, w_up, w_down)))

    def forward(inputs, weights):

        def one_sequence(operands):
            seq_inputs, seq_chosen, seq_ranks = operands
            return sequence_forward(weights, seq_inputs, seq_chosen, seq_ranks)
        return lax.map(jax.checkpoint(one_sequence), (inputs, expert_ids, slot_order))
    outputs, pullback = jax.vjp(forward, hidden_in.astype(jnp.float32), params)
    grad_inputs, grads = pullback(grad_out.astype(jnp.float32))
    return (outputs, grad_inputs, grads[0], grads[1], grads[2], grads[3], grads[4], grads[5], grads[6], grads[7], grads[8], grads[9])
```

```python
import math

import jax
import jax.numpy as jnp
from jax import lax
from jax.experimental import pallas as pl
from jax.experimental.pallas import tpu as pltpu
from jax.sharding import PartitionSpec as P

HEADS = 24
KV_HEADS = 8
HEAD_DIM = 64


EPS = 1e-05
MASKED = -1e30


def rotary_tables(positions):
    half = HEAD_DIM // 2
    frequency = jnp.exp(-math.log(10000.0) * jnp.arange(half, dtype=jnp.float32) * 2.0 / HEAD_DIM)
    angles = positions.astype(jnp.float32)[:, None] * frequency[None, :]
    return (jnp.cos(angles)[:, None, :], jnp.sin(angles)[:, None, :])


def rotate(values, cosine, sine):
    half = values.shape[-1] // 2
    first = values[..., :half]
    second = values[..., half:]
    return jnp.concatenate(
        [first * cosine - second * sine, second * cosine + first * sine], axis=-1
    )


def rotate_back(values, cosine, sine):
    half = values.shape[-1] // 2
    first = values[..., :half]
    second = values[..., half:]
    return jnp.concatenate(
        [first * cosine + second * sine, second * cosine - first * sine], axis=-1
    )


def assign_slots(row_chosen, row_ranks, all_experts, capacity):
    pairs = row_chosen.shape[0]
    by_rank = jnp.zeros((pairs,), jnp.int32).at[row_ranks].set(jnp.arange(pairs, dtype=jnp.int32))
    ordered = row_chosen[by_rank]
    table = (ordered[:, None] == jnp.arange(all_experts, dtype=jnp.int32)[None, :]).astype(
        jnp.int32
    )
    before = jnp.sum(table * (jnp.cumsum(table, axis=0) - 1), axis=1)
    slot = before[row_ranks]
    target = jnp.where(slot < capacity, row_chosen * capacity + slot, all_experts * capacity)
    owner = (
        jnp.full((all_experts * capacity,), pairs, jnp.int32)
        .at[target]
        .set(jnp.arange(pairs, dtype=jnp.int32), mode="drop")
    )
    return (target, owner)


def body(
    hidden_in,
    gain_attn,
    w_query,
    w_key,
    w_value,
    w_output,
    gain_mlp,
    w_router,
    w_gate,
    w_up,
    w_down,
    expert_ids,
    slot_order,
    grad_out,
):
    inputs = hidden_in[0]
    cotangent = grad_out[0]
    chosen = expert_ids[0]
    tokens, width = inputs.shape
    top = chosen.shape[1]
    local_experts = w_gate.shape[0]
    peers = lax.axis_size("expert")
    all_experts = local_experts * peers
    pairs = tokens * top
    capacity = pairs // all_experts
    shards = lax.axis_size("dp")
    index = lax.axis_index("dp")
    length = shards * tokens
    block = math.gcd(length, 512)
    groups = HEADS // KV_HEADS
    scale = HEAD_DIM ** (-0.5)
    query_pos = index * tokens + jnp.arange(tokens, dtype=jnp.int32)
    cosine, sine = rotary_tables(query_pos)
    count = ((index + 1) * tokens + block - 1) // block
    inv_one = lax.rsqrt(jnp.mean(inputs * inputs, axis=-1, keepdims=True) + EPS)
    normed = (inputs * inv_one * gain_attn).astype(jnp.bfloat16)
    query_pre = jnp.dot(normed, w_query, preferred_element_type=jnp.float32).reshape(
        tokens, HEADS, HEAD_DIM
    )
    queries = rotate(query_pre, cosine, sine).astype(jnp.bfloat16)
    key_pre = jnp.dot(normed, w_key, preferred_element_type=jnp.float32).reshape(
        tokens, KV_HEADS, HEAD_DIM
    )
    keys_low = rotate(key_pre, cosine, sine).astype(jnp.bfloat16)
    values_low = (
        jnp.dot(normed, w_value, preferred_element_type=jnp.float32)
        .astype(jnp.bfloat16)
        .reshape(tokens, KV_HEADS, HEAD_DIM)
    )
    keys_all, values_all = (
        lax.all_gather(keys_low, "dp", axis=0, tiled=True),
        lax.all_gather(values_low, "dp", axis=0, tiled=True),
    )
    query_groups = queries.reshape(tokens, KV_HEADS, groups, HEAD_DIM)

    def block_scores(key_block, start):
        raw = (
            jnp.einsum(
                "qkgd,skd->kgqs", query_groups, key_block, preferred_element_type=jnp.float32
            )
            * scale
        )
        key_pos = start + jnp.arange(block, dtype=jnp.int32)
        allowed = key_pos[None, :] <= query_pos[:, None]
        return jnp.where(allowed, raw, MASKED)

    def stats_step(step, carry):
        running, total = carry
        scores = block_scores(
            lax.dynamic_slice_in_dim(keys_all, step * block, block, 0), step * block
        )
        newest = jnp.maximum(running, jnp.max(scores, axis=-1))
        total = total * jnp.exp(running - newest) + jnp.sum(
            jnp.exp(scores - newest[..., None]), axis=-1
        )
        return (newest, total)

    stat_init = (
        jnp.full((KV_HEADS, groups, tokens), MASKED, jnp.float32),
        jnp.zeros((KV_HEADS, groups, tokens), jnp.float32),
    )
    running, total = lax.fori_loop(0, count, stats_step, stat_init)
    log_total = running + jnp.log(total)

    def output_step(step, accum):
        start = step * block
        scores = block_scores(lax.dynamic_slice_in_dim(keys_all, start, block, 0), start)
        probs = jnp.exp(scores - log_total[..., None]).astype(jnp.bfloat16)
        value_block = lax.dynamic_slice_in_dim(values_all, start, block, 0)
        return accum + jnp.einsum(
            "kgqs,skd->qkgd", probs, value_block, preferred_element_type=jnp.float32
        )

    attended_groups = lax.fori_loop(
        0, count, output_step, jnp.zeros((tokens, KV_HEADS, groups, HEAD_DIM), jnp.float32)
    )
    attended = attended_groups.reshape(tokens, HEADS * HEAD_DIM)
    attended_low = attended.astype(jnp.bfloat16)
    branch = jnp.dot(attended_low, w_output, preferred_element_type=jnp.float32)
    middle = inputs + branch
    inv_two = lax.rsqrt(jnp.mean(middle * middle, axis=-1, keepdims=True) + EPS)
    normed_two = (middle * inv_two * gain_mlp).astype(jnp.bfloat16)
    logits = jnp.dot(normed_two, w_router, preferred_element_type=jnp.float32)
    onehot = (chosen[:, :, None] == jnp.arange(all_experts, dtype=jnp.int32)[None, None, :]).astype(
        jnp.float32
    )
    picked = jnp.sum(onehot * logits[:, None, :], axis=-1)
    gates = jax.nn.softmax(picked, axis=-1)
    target, owner = assign_slots(chosen.reshape(pairs), slot_order[0, 0], all_experts, capacity)
    valid = owner < pairs
    source = jnp.minimum(owner, pairs - 1)
    rows_send = jnp.where(valid[:, None], normed_two[source // top], 0).reshape(
        peers, local_experts, capacity, width
    )
    received = lax.all_to_all(rows_send, "expert", split_axis=0, concat_axis=0, tiled=True)
    gate_pre = jnp.einsum("necd,edf->necf", received, w_gate, preferred_element_type=jnp.float32)
    up_pre = jnp.einsum("necd,edf->necf", received, w_up, preferred_element_type=jnp.float32)
    hidden = (jax.nn.silu(gate_pre) * up_pre).astype(jnp.bfloat16)
    result = jnp.einsum(
        "necf,efd->necd", hidden, w_down, preferred_element_type=jnp.float32
    ).astype(jnp.bfloat16)
    returned = lax.all_to_all(result, "expert", split_axis=0, concat_axis=0, tiled=True)
    returned, received, gate_pre, up_pre = (returned, received, gate_pre, up_pre)
    zero_row = jnp.zeros((1, width), jnp.bfloat16)
    pair_out = jnp.concatenate([returned.reshape(all_experts * capacity, width), zero_row], axis=0)[
        target
    ].reshape(tokens, top, width)
    mixed = jnp.einsum("tk,tkd->td", gates, pair_out, preferred_element_type=jnp.float32)
    hidden_out = middle + mixed
    dy_pairs = (
        (gates[:, :, None] * cotangent[:, None, :]).astype(jnp.bfloat16).reshape(pairs, width)
    )
    dy_send = jnp.where(valid[:, None], dy_pairs[source], 0).reshape(
        peers, local_experts, capacity, width
    )
    dy_received = lax.all_to_all(dy_send, "expert", split_axis=0, concat_axis=0, tiled=True)
    sigmoid_gate = jax.nn.sigmoid(gate_pre)
    silu_gate = gate_pre * sigmoid_gate
    hidden = (silu_gate * up_pre).astype(jnp.bfloat16)
    grad_down_part = jnp.einsum(
        "necf,necd->efd", hidden, dy_received, preferred_element_type=jnp.float32
    )
    d_hidden = jnp.einsum("necd,efd->necf", dy_received, w_down, preferred_element_type=jnp.float32)
    d_gate = (d_hidden * up_pre * sigmoid_gate * (1.0 + gate_pre * (1.0 - sigmoid_gate))).astype(
        jnp.bfloat16
    )
    d_up = (d_hidden * silu_gate).astype(jnp.bfloat16)
    grad_gate_part = jnp.einsum(
        "necd,necf->edf", received, d_gate, preferred_element_type=jnp.float32
    )
    grad_up_part = jnp.einsum("necd,necf->edf", received, d_up, preferred_element_type=jnp.float32)
    gate_total, up_total, down_total = (
        lax.psum_scatter(
            grad_gate_part.astype(jnp.bfloat16), "dp", scatter_dimension=1, tiled=True
        ).astype(jnp.float32),
        lax.psum_scatter(
            grad_up_part.astype(jnp.bfloat16), "dp", scatter_dimension=1, tiled=True
        ).astype(jnp.float32),
        lax.psum_scatter(
            grad_down_part.astype(jnp.bfloat16), "dp", scatter_dimension=1, tiled=True
        ).astype(jnp.float32),
    )
    d_rows = jnp.einsum("necf,edf->necd", d_gate, w_gate, preferred_element_type=jnp.float32)
    d_rows = (
        d_rows + jnp.einsum("necf,edf->necd", d_up, w_up, preferred_element_type=jnp.float32)
    ).astype(jnp.bfloat16)
    d_back = lax.all_to_all(d_rows, "expert", split_axis=0, concat_axis=0, tiled=True)
    d_pairs = jnp.concatenate([d_back.reshape(all_experts * capacity, width), zero_row], axis=0)[
        target
    ].reshape(tokens, top, width)
    d_normed_two = jnp.sum(d_pairs, axis=1, dtype=jnp.float32)
    d_gates = jnp.einsum("td,tkd->tk", cotangent, pair_out, preferred_element_type=jnp.float32)
    d_picked = gates * (d_gates - jnp.sum(gates * d_gates, axis=-1, keepdims=True))
    d_logits = jnp.sum(onehot * d_picked[:, :, None], axis=1).astype(jnp.bfloat16)
    grad_router_part = jnp.einsum(
        "td,te->de", normed_two, d_logits, preferred_element_type=jnp.float32
    )
    d_normed_two = d_normed_two + jnp.einsum(
        "te,de->td", d_logits, w_router, preferred_element_type=jnp.float32
    )
    scaled_two = d_normed_two * gain_mlp
    grad_gain_mlp_part = jnp.sum(d_normed_two * middle * inv_two, axis=0)
    d_middle = (
        cotangent
        + inv_two * scaled_two
        - middle * inv_two**3 * jnp.mean(middle * scaled_two, axis=-1, keepdims=True)
    )
    d_branch = d_middle.astype(jnp.bfloat16)
    grad_output_part = jnp.einsum(
        "tf,td->fd", attended_low, d_branch, preferred_element_type=jnp.float32
    )
    d_attended = jnp.einsum(
        "td,fd->tf", d_branch, w_output, preferred_element_type=jnp.float32
    ).astype(jnp.bfloat16)
    d_groups = d_attended.reshape(tokens, KV_HEADS, groups, HEAD_DIM)
    delta = jnp.einsum(
        "qkgd,qkgd->kgq", d_groups, attended_groups, preferred_element_type=jnp.float32
    )
    keys_back, values_back = (
        lax.all_gather(keys_low, "dp", axis=0, tiled=True),
        lax.all_gather(values_low, "dp", axis=0, tiled=True),
    )

    def grad_step(step, carry):
        d_query, d_keys, d_values = carry
        start = step * block
        key_block = lax.dynamic_slice_in_dim(keys_back, start, block, 0)
        value_block = lax.dynamic_slice_in_dim(values_back, start, block, 0)
        scores = block_scores(key_block, start)
        probs = jnp.exp(scores - log_total[..., None])
        probs_low = probs.astype(jnp.bfloat16)
        d_probs = jnp.einsum(
            "qkgd,skd->kgqs", d_groups, value_block, preferred_element_type=jnp.float32
        )
        d_scores = (probs * (d_probs - delta[..., None])).astype(jnp.bfloat16)
        d_query = d_query + jnp.einsum(
            "kgqs,skd->qkgd", d_scores, key_block, preferred_element_type=jnp.float32
        )
        key_part = jnp.einsum(
            "kgqs,qkgd->skd", d_scores, query_groups, preferred_element_type=jnp.float32
        )
        value_part = jnp.einsum(
            "kgqs,qkgd->skd", probs_low, d_groups, preferred_element_type=jnp.float32
        )
        d_keys = lax.dynamic_update_slice_in_dim(
            d_keys, lax.dynamic_slice_in_dim(d_keys, start, block, 0) + key_part, start, 0
        )
        d_values = lax.dynamic_update_slice_in_dim(
            d_values, lax.dynamic_slice_in_dim(d_values, start, block, 0) + value_part, start, 0
        )
        return (d_query, d_keys, d_values)

    grad_init = (
        jnp.zeros((tokens, KV_HEADS, groups, HEAD_DIM), jnp.float32),
        jnp.zeros((length, KV_HEADS, HEAD_DIM), jnp.float32),
        jnp.zeros((length, KV_HEADS, HEAD_DIM), jnp.float32),
    )
    d_query, d_keys, d_values = lax.fori_loop(0, count, grad_step, grad_init)
    key_sum, value_sum = (
        lax.psum_scatter(
            (d_keys * scale).reshape(length, KV_HEADS * HEAD_DIM).astype(jnp.bfloat16),
            "dp",
            scatter_dimension=0,
            tiled=True,
        ).astype(jnp.float32),
        lax.psum_scatter(
            d_values.reshape(length, KV_HEADS * HEAD_DIM).astype(jnp.bfloat16),
            "dp",
            scatter_dimension=0,
            tiled=True,
        ).astype(jnp.float32),
    )
    d_query_low = (
        rotate_back((d_query * scale).reshape(tokens, HEADS, HEAD_DIM), cosine, sine)
        .astype(jnp.bfloat16)
        .reshape(tokens, HEADS * HEAD_DIM)
    )
    d_key_low = (
        rotate_back(key_sum.reshape(tokens, KV_HEADS, HEAD_DIM), cosine, sine)
        .astype(jnp.bfloat16)
        .reshape(tokens, KV_HEADS * HEAD_DIM)
    )
    d_value_low = value_sum.astype(jnp.bfloat16)
    grad_query_part = jnp.einsum(
        "td,tf->df", normed, d_query_low, preferred_element_type=jnp.float32
    )
    grad_key_part = jnp.einsum("td,tf->df", normed, d_key_low, preferred_element_type=jnp.float32)
    grad_value_part = jnp.einsum(
        "td,tf->df", normed, d_value_low, preferred_element_type=jnp.float32
    )
    d_normed = jnp.einsum("tf,df->td", d_query_low, w_query, preferred_element_type=jnp.float32)
    d_normed = d_normed + jnp.einsum(
        "tf,df->td", d_key_low, w_key, preferred_element_type=jnp.float32
    )
    d_normed = d_normed + jnp.einsum(
        "tf,df->td", d_value_low, w_value, preferred_element_type=jnp.float32
    )
    scaled_one = d_normed * gain_attn
    grad_gain_attn_part = jnp.sum(d_normed * inputs * inv_one, axis=0)
    grad_in = (
        d_middle
        + inv_one * scaled_one
        - inputs * inv_one**3 * jnp.mean(inputs * scaled_one, axis=-1, keepdims=True)
    )
    dense = (
        lax.psum_scatter(grad_gain_attn_part, ("dp", "expert"), scatter_dimension=0, tiled=True),
        lax.psum_scatter(grad_query_part, ("dp", "expert"), scatter_dimension=0, tiled=True),
        lax.psum_scatter(grad_key_part, ("dp", "expert"), scatter_dimension=0, tiled=True),
        lax.psum_scatter(grad_value_part, ("dp", "expert"), scatter_dimension=0, tiled=True),
        lax.psum_scatter(grad_output_part, ("dp", "expert"), scatter_dimension=0, tiled=True),
        lax.psum_scatter(grad_gain_mlp_part, ("dp", "expert"), scatter_dimension=0, tiled=True),
        lax.psum_scatter(grad_router_part, ("dp", "expert"), scatter_dimension=0, tiled=True),
    )
    return (
        hidden_out[None],
        grad_in[None],
        dense[0],
        dense[1],
        dense[2],
        dense[3],
        dense[4],
        dense[5],
        dense[6],
        gate_total,
        up_total,
        down_total,
    )

BF = jnp.bfloat16
F32 = jnp.float32
WIDTH = 1536
LANES = 128
PER_KV = HEADS // KV_HEADS
ROWS_Q = PER_KV * HEAD_DIM
PACK = ROWS_Q + 2 * HEAD_DIM
BIT_Y, BIT_ZL, BIT_ZH = 1, 2, 4
BIT_C, BIT_X = 1, 2
BLOCK_Q = 256
BLOCK_K = 512
SLOTS = 64
CHUNK = 512
MIB = 1 << 20


def dot_nn(a, b):
    return lax.dot_general(a, b, (((1,), (0,)), ((), ())), preferred_element_type=F32)


def dot_nt(a, b):
    return lax.dot_general(a, b, (((1,), (1,)), ((), ())), preferred_element_type=F32)


def dot_tn(a, b):
    return lax.dot_general(a, b, (((0,), (0,)), ((), ())), preferred_element_type=F32)


def cost(flops, moved, transcendentals=0):
    return pl.CostEstimate(
        flops=int(flops), bytes_accessed=int(moved), transcendentals=int(transcendentals)
    )


def params(mib, dims=None):
    return pltpu.CompilerParams(vmem_limit_bytes=mib * MIB, dimension_semantics=dims)


def swap(values, axis, mask):
    size = lax.axis_size(axis)
    return lax.ppermute(values, axis, [(i, i ^ mask) for i in range(size)])


def swap_bit(values, bit):
    axis, mask = bit
    return swap(values, axis, mask)


C_BIT = ("expert", BIT_C)
X_BIT = ("expert", BIT_X)
Y_BIT = ("dp", BIT_Y)
ZL_BIT = ("dp", BIT_ZL)
ZH_BIT = ("dp", BIT_ZH)


def pre_kernel(hid_ref, gain_ref, wq_ref, wk_ref, wv_ref, cos_ref, sin_ref, norm_ref, pack_ref):
    tokens = hid_ref.shape[0]
    inputs = hid_ref[...]
    inv = lax.rsqrt(jnp.mean(inputs * inputs, axis=-1, keepdims=True) + EPS)
    normed = (inputs * inv * gain_ref[...]).astype(BF)
    norm_ref[...] = normed
    low = (lax.broadcasted_iota(jnp.int32, (tokens, LANES), 1) % HEAD_DIM) < HEAD_DIM // 2
    cosine, sine = cos_ref[...], sin_ref[...]

    def turn(tile):
        other = jnp.where(
            low,
            pltpu.roll(tile, LANES - HEAD_DIM // 2, 1),
            pltpu.roll(tile, HEAD_DIM // 2, 1),
        )
        return (tile * cosine + other * sine).astype(BF)

    def put_heads(tiles, width, start):
        flat = jnp.concatenate(tiles, axis=1)
        for g in range(KV_HEADS):
            pack_ref[g, :, start : start + width] = flat[:, g * width : (g + 1) * width]

    tiles = []
    for n in range(wq_ref.shape[1] // CHUNK):
        pre = dot_nn(normed, wq_ref[:, n * CHUNK : (n + 1) * CHUNK])
        tiles += [turn(pre[:, m * LANES : (m + 1) * LANES]) for m in range(CHUNK // LANES)]
    put_heads(tiles, ROWS_Q, 0)
    pre = dot_nn(normed, wk_ref[...])
    put_heads(
        [turn(pre[:, m * LANES : (m + 1) * LANES]) for m in range(pre.shape[1] // LANES)],
        HEAD_DIM,
        ROWS_Q,
    )
    put_heads([dot_nn(normed, wv_ref[...]).astype(BF)], HEAD_DIM, ROWS_Q + HEAD_DIM)


def run_pre(inputs, gain, w_query, w_key, w_value, cos_tab, sin_tab):
    tokens = inputs.shape[0]
    return pl.pallas_call(
        pre_kernel,
        out_shape=(
            jax.ShapeDtypeStruct((tokens, WIDTH), BF),
            jax.ShapeDtypeStruct((KV_HEADS, tokens, PACK), BF),
        ),
        compiler_params=params(48),
        cost_estimate=cost(2 * tokens * WIDTH * 2560, 14e6),
    )(inputs, gain[None], w_query, w_key, w_value, cos_tab, sin_tab)


def heads_t(block, width):
    return jnp.concatenate(
        [block[:, h * HEAD_DIM : (h + 1) * HEAD_DIM].astype(F32).T for h in range(width)], axis=1
    )


def heads_rows(block, width):
    return jnp.concatenate(
        [block[:, h * HEAD_DIM : (h + 1) * HEAD_DIM] for h in range(width)], axis=0
    )


def allowed_t(step, block):
    shape = (BLOCK_K, PER_KV * BLOCK_Q)
    key_pos = step * BLOCK_K + lax.broadcasted_iota(jnp.int32, shape, 0)
    query_pos = block * BLOCK_Q + lax.broadcasted_iota(jnp.int32, shape, 1) % BLOCK_Q
    return key_pos <= query_pos


def forward_kernel(pack_ref, out_ref, out_t_ref, lse_ref, k_s, vt_s):
    block = pl.program_id(0)

    @pl.when(block == 0)
    def _():
        k_s[...] = pack_ref[:, ROWS_Q : ROWS_Q + HEAD_DIM]
        vt_s[...] = pack_ref[:, ROWS_Q + HEAD_DIM : PACK].astype(F32).T.astype(BF)

    rows = pl.ds(pl.multiple_of(block * BLOCK_Q, BLOCK_Q), BLOCK_Q)
    scale = HEAD_DIM ** (-0.5)
    q_t = (heads_t(pack_ref[rows, 0:ROWS_Q], PER_KV) * scale).astype(BF)
    columns = PER_KV * BLOCK_Q

    def step(j, carry, masked):
        running, total, accum = carry
        keys = pl.ds(pl.multiple_of(j * BLOCK_K, BLOCK_K), BLOCK_K)
        scores = dot_nn(k_s[keys, :], q_t)
        if masked:
            scores = jnp.where(allowed_t(j, block), scores, MASKED)
        newest = jnp.maximum(running, jnp.max(scores, axis=0, keepdims=True))
        fade = jnp.exp(running - newest)
        probs = jnp.exp(scores - newest)
        total = total * fade + jnp.sum(probs, axis=0, keepdims=True)
        accum = accum * fade + dot_nn(vt_s[:, keys], probs.astype(BF))
        return newest, total, accum

    carry = (
        jnp.full((1, columns), MASKED, F32),
        jnp.zeros((1, columns), F32),
        jnp.zeros((HEAD_DIM, columns), F32),
    )
    last = (block * BLOCK_Q) // BLOCK_K
    carry = lax.fori_loop(0, last, lambda j, c: step(j, c, False), carry)
    running, total, accum = step(last, carry, True)
    out_t = accum / total
    out_t_ref[0] = out_t
    lse_ref[0] = running + jnp.log(total)
    out_ref[...] = jnp.concatenate(
        [out_t[:, h * BLOCK_Q : (h + 1) * BLOCK_Q].T for h in range(PER_KV)], axis=1
    ).astype(BF)


def run_forward(pack):
    length = pack.shape[0]
    blocks = length // BLOCK_Q
    columns = PER_KV * BLOCK_Q
    return pl.pallas_call(
        forward_kernel,
        grid=(blocks,),
        in_specs=[pl.BlockSpec((length, PACK), lambda i: (0, 0))],
        out_specs=(
            pl.BlockSpec((BLOCK_Q, ROWS_Q), lambda i: (i, 0)),
            pl.BlockSpec((1, HEAD_DIM, columns), lambda i: (i, 0, 0)),
            pl.BlockSpec((1, 1, columns), lambda i: (i, 0, 0)),
        ),
        out_shape=(
            jax.ShapeDtypeStruct((length, ROWS_Q), BF),
            jax.ShapeDtypeStruct((blocks, HEAD_DIM, columns), F32),
            jax.ShapeDtypeStruct((blocks, 1, columns), F32),
        ),
        scratch_shapes=[pltpu.VMEM((length, HEAD_DIM), BF), pltpu.VMEM((HEAD_DIM, length), BF)],
        compiler_params=params(40, ("arbitrary",)),
        cost_estimate=cost(8 * length * length * ROWS_Q, 6e6, length * length * PER_KV),
    )(pack)


def backward_kernel(
    pack_ref, grad_ref, out_t_ref, lse_ref, cos_ref, sin_ref, res_ref, k_s, v_s, kt_s, dk_s, dv_s
):
    block = pl.program_id(0)

    @pl.when(block == 0)
    def _():
        keys = pack_ref[:, ROWS_Q : ROWS_Q + HEAD_DIM]
        k_s[...] = keys
        kt_s[...] = keys.astype(F32).T.astype(BF)
        v_s[...] = pack_ref[:, ROWS_Q + HEAD_DIM : PACK]
        dk_s[...] = jnp.zeros_like(dk_s)
        dv_s[...] = jnp.zeros_like(dv_s)

    scale = HEAD_DIM ** (-0.5)
    half = HEAD_DIM // 2
    rows = pl.ds(pl.multiple_of(block * BLOCK_Q, BLOCK_Q), BLOCK_Q)
    q_block = pack_ref[rows, 0:ROWS_Q]
    q_t = (heads_t(q_block, PER_KV) * scale).astype(BF)
    q_rows = (heads_rows(q_block, PER_KV).astype(F32) * scale).astype(BF)
    do_block = grad_ref[...]
    do_f32 = heads_t(do_block, PER_KV)
    do_t = do_f32.astype(BF)
    do_rows = heads_rows(do_block, PER_KV)
    delta = jnp.sum(do_f32 * out_t_ref[0], axis=0, keepdims=True)
    lse = lse_ref[0]

    def step(j, dq_t, masked):
        keys = pl.ds(pl.multiple_of(j * BLOCK_K, BLOCK_K), BLOCK_K)
        scores = dot_nn(k_s[keys, :], q_t)
        if masked:
            scores = jnp.where(allowed_t(j, block), scores, MASKED)
        probs = jnp.exp(scores - lse)
        d_probs = dot_nn(v_s[keys, :], do_t)
        d_scores = (probs * (d_probs - delta)).astype(BF)
        dv_s[keys, :] += dot_nn(probs.astype(BF), do_rows)
        dk_s[keys, :] += dot_nn(d_scores, q_rows)
        return dq_t + dot_nn(kt_s[:, keys], d_scores)

    last = (block * BLOCK_Q) // BLOCK_K
    dq_t = jnp.zeros((HEAD_DIM, PER_KV * BLOCK_Q), F32)
    dq_t = lax.fori_loop(0, last, lambda j, c: step(j, c, False), dq_t)
    dq_t = step(last, dq_t, True) * scale

    def turn_back(values, cosine, sine):
        first, second = values[:half], values[half:]
        return jnp.concatenate(
            [first * cosine + second * sine, second * cosine - first * sine], axis=0
        )

    columns = pl.ds(pl.multiple_of(block * BLOCK_Q, BLOCK_Q), BLOCK_Q)
    cosine, sine = cos_ref[:, columns], sin_ref[:, columns]
    res_ref[rows, 0:ROWS_Q] = jnp.concatenate(
        [
            turn_back(dq_t[:, h * BLOCK_Q : (h + 1) * BLOCK_Q], cosine, sine).T
            for h in range(PER_KV)
        ],
        axis=1,
    ).astype(BF)

    @pl.when(block == pl.num_programs(0) - 1)
    def _():
        dk_t = turn_back(dk_s[...].T, cos_ref[...], sin_ref[...])
        res_ref[:, ROWS_Q : ROWS_Q + HEAD_DIM] = dk_t.T.astype(BF)
        res_ref[:, ROWS_Q + HEAD_DIM : PACK] = dv_s[...].astype(BF)


def run_backward(pack, grad, out_t, lse, cos_t, sin_t):
    length = pack.shape[0]
    blocks = length // BLOCK_Q
    columns = PER_KV * BLOCK_Q
    half = HEAD_DIM // 2
    return pl.pallas_call(
        backward_kernel,
        grid=(blocks,),
        in_specs=[
            pl.BlockSpec((length, PACK), lambda i: (0, 0)),
            pl.BlockSpec((BLOCK_Q, ROWS_Q), lambda i: (i, 0)),
            pl.BlockSpec((1, HEAD_DIM, columns), lambda i: (i, 0, 0)),
            pl.BlockSpec((1, 1, columns), lambda i: (i, 0, 0)),
            pl.BlockSpec((half, length), lambda i: (0, 0)),
            pl.BlockSpec((half, length), lambda i: (0, 0)),
        ],
        out_specs=pl.BlockSpec((length, PACK), lambda i: (0, 0)),
        out_shape=jax.ShapeDtypeStruct((length, PACK), BF),
        scratch_shapes=[
            pltpu.VMEM((length, HEAD_DIM), BF),
            pltpu.VMEM((length, HEAD_DIM), BF),
            pltpu.VMEM((HEAD_DIM, length), BF),
            pltpu.VMEM((length, HEAD_DIM), F32),
            pltpu.VMEM((length, HEAD_DIM), F32),
        ],
        compiler_params=params(48, ("arbitrary",)),
        cost_estimate=cost(20 * length * length * ROWS_Q, 8e6, length * length * PER_KV),
    )(pack, grad, out_t, lse, cos_t, sin_t)


def mid_kernel(att_ref, wo_ref, hid_ref, gain_ref, mid_ref, norm_ref, full_ref):
    for g in range(KV_HEADS):
        full_ref[:, g * ROWS_Q : (g + 1) * ROWS_Q] = att_ref[g]
    middle = hid_ref[...] + dot_nn(full_ref[...], wo_ref[...])
    mid_ref[...] = middle
    inv = lax.rsqrt(jnp.mean(middle * middle, axis=-1, keepdims=True) + EPS)
    norm_ref[...] = (middle * inv * gain_ref[...]).astype(BF)


def run_mid(att, w_output, inputs, gain):
    tokens = inputs.shape[0]
    return pl.pallas_call(
        mid_kernel,
        out_shape=(
            jax.ShapeDtypeStruct((tokens, WIDTH), F32),
            jax.ShapeDtypeStruct((tokens, WIDTH), BF),
            jax.ShapeDtypeStruct((tokens, WIDTH), BF),
        ),
        compiler_params=params(40),
        cost_estimate=cost(2 * tokens * WIDTH * WIDTH, 12e6),
    )(att, w_output, inputs, gain[None])


def expert_kernel(
    place_ref,
    x_ref,
    g_ref,
    map_ref,
    wr_ref,
    wg0_ref,
    wg1_ref,
    wu0_ref,
    wu1_ref,
    wd0_ref,
    wd1_ref,
    mix_keep,
    mix_send,
    dx_keep,
    dx_send,
    gate_keep,
    gate_send,
    up_keep,
    up_send,
    down_keep,
    down_send,
    xs,
    gs,
    gate_s,
    wide_s,
    tall_s,
):
    step = pl.program_id(0)
    sources = map_ref.shape[0]
    experts = xs.shape[0]
    tokens = x_ref.shape[1]
    rows = experts * SLOTS
    count = WIDTH // CHUNK

    def one_hot(source):
        slots = map_ref[source, 0:experts, :]
        wide = jnp.broadcast_to(slots[:, None, :], (experts, SLOTS, tokens))
        rank = lax.broadcasted_iota(jnp.int32, (experts, SLOTS, tokens), 1).astype(F32)
        return (wide == rank).astype(F32).reshape(rows, tokens)

    @pl.when(step < sources)
    def _():
        slot_map = map_ref[step]
        chosen = slot_map >= 0.0
        logits = dot_nt(wr_ref[...], x_ref[0])[0 : slot_map.shape[0]]
        logits = jnp.where(chosen, logits, MASKED)
        raised = jnp.exp(logits - jnp.max(logits, axis=0, keepdims=True))
        raised = jnp.where(chosen, raised, 0.0)
        gates = raised / jnp.sum(raised, axis=0, keepdims=True)
        pick = one_hot(step)
        wide = jnp.broadcast_to(gates[0:experts, None, :], (experts, SLOTS, tokens))
        gate_rows = jnp.sum(pick * wide.reshape(rows, tokens), axis=1, keepdims=True)
        pick = pick.astype(BF)
        here = pl.ds(pl.multiple_of(step * SLOTS, SLOTS), SLOTS)
        for e in range(experts):
            gate_s[e, here, :] = gate_rows[e * SLOTS : (e + 1) * SLOTS]
        for n in range(count):
            cols = slice(n * CHUNK, (n + 1) * CHUNK)
            got = dot_nn(pick, x_ref[0, :, cols]).astype(BF)
            xs[:, here, cols] = got.reshape(experts, SLOTS, CHUNK)
            got = dot_nn(pick, g_ref[0, :, cols]).astype(BF)
            gs[:, here, cols] = got.reshape(experts, SLOTS, CHUNK)

    @pl.when((step >= sources) & (step < sources + experts))
    def _():
        e = step - sources
        x = xs[e]
        w_gate = jnp.concatenate([wg0_ref[0], wg1_ref[0]], axis=1)
        w_up = jnp.concatenate([wu0_ref[0], wu1_ref[0]], axis=1)
        gate_pre = dot_nn(x, w_gate)
        up_pre = dot_nn(x, w_up)
        sig = jax.nn.sigmoid(gate_pre)
        silu = gate_pre * sig
        hidden = (silu * up_pre).astype(BF)
        gate = gate_s[e]
        d_hidden = jnp.zeros(hidden.shape, F32)
        d_gates = jnp.zeros(gate.shape, F32)
        for n in range(count):
            cols = slice(n * CHUNK, (n + 1) * CHUNK)
            w_down = jnp.concatenate([wd0_ref[0, :, cols], wd1_ref[0, :, cols]], axis=0)
            grad = gs[e, :, cols].astype(F32)
            d_y = (gate * grad).astype(BF)
            y = dot_nn(hidden, w_down)
            d_gates += jnp.sum(y * grad, axis=1, keepdims=True)
            gs[e, :, cols] = (gate * y).astype(BF)
            d_hidden += dot_nt(d_y, w_down)
            wide_s[:, cols] = dot_tn(hidden, d_y).astype(BF)
        gate_s[e] = d_gates
        d_gate = (d_hidden * up_pre * sig * (1.0 + gate_pre * (1.0 - sig))).astype(BF)
        d_up = (d_hidden * silu).astype(BF)

        y_at, zl_at, zh_at = place_ref[1], place_ref[2], place_ref[3]
        part = down_keep.shape[2]
        for z in range(2):
            base = (zh_at ^ z) * 2
            down_keep[z, 0] = wide_s[pl.ds(pl.multiple_of((base + y_at) * part, part), part), :]
            down_send[z, 0] = wide_s[
                pl.ds(pl.multiple_of((base + (1 - y_at)) * part, part), part), :
            ]

        def spread(keep, send):
            part = keep.shape[3]
            for z in range(2):
                for low in range(2):
                    base = ((zh_at ^ z) * 2 + (zl_at ^ low)) * 2
                    keep[z, 0, low] = tall_s[
                        pl.ds(pl.multiple_of((base + y_at) * part, part), part), :
                    ]
                    send[z, 0, low] = tall_s[
                        pl.ds(pl.multiple_of((base + (1 - y_at)) * part, part), part), :
                    ]

        for n in range(count):
            cols = slice(n * CHUNK, (n + 1) * CHUNK)
            tall_s[cols, :] = dot_tn(x[:, cols], d_gate).astype(BF)
        spread(gate_keep, gate_send)
        for n in range(count):
            cols = slice(n * CHUNK, (n + 1) * CHUNK)
            tall_s[cols, :] = dot_tn(x[:, cols], d_up).astype(BF)
        spread(up_keep, up_send)
        for n in range(count):
            cols = slice(n * CHUNK, (n + 1) * CHUNK)
            d_x = dot_nt(d_gate, w_gate[cols]) + dot_nt(d_up, w_up[cols])
            xs[e, :, cols] = d_x.astype(BF)

    def combine(source, mix_out, dx_out):
        here = pl.ds(pl.multiple_of(source * SLOTS, SLOTS), SLOTS)
        pick = one_hot(source).astype(BF)
        for n in range(count):
            cols = slice(n * CHUNK, (n + 1) * CHUNK)
            dx_out[0, :, cols] = dot_tn(pick, xs[:, here, cols].reshape(rows, CHUNK)).astype(BF)
            mix_out[0, :, cols] = dot_tn(pick, gs[:, here, cols].reshape(rows, CHUNK)).astype(BF)
        values = gate_s[:, here, :].reshape(rows, 1)
        column = lax.broadcasted_iota(jnp.int32, (rows, LANES), 1)
        owner = lax.broadcasted_iota(jnp.int32, (rows, LANES), 0) // SLOTS
        spread_out = jnp.where(column == owner + place_ref[4], values, 0.0).astype(BF)
        dx_out[0, :, WIDTH:] = dot_tn(pick, spread_out).astype(BF)

    @pl.when((step >= sources + experts) & (step < sources + experts + sources // 2))
    def _():
        combine(step - experts - sources // 2, mix_send, dx_send)

    @pl.when(step >= sources + experts + sources // 2)
    def _():
        combine(step - experts - sources - sources // 2, mix_keep, dx_keep)


def run_experts(place, x_all, g_all, maps, wr_t, w_gate, w_up, w_down):
    sources, tokens, width = x_all.shape
    experts = w_gate.shape[0]
    ffe = w_gate.shape[2]
    part = ffe // 8
    quarter = width // 8
    half = ffe // 2
    slots = sources * SLOTS
    extra = width + LANES
    first = sources
    second = sources + experts
    third = second + sources // 2

    def at(i, low, size):
        return jnp.clip(i - low, 0, size - 1)

    def expert_of(i):
        return at(i, first, experts)

    def w_cols(block):
        return pl.BlockSpec((1, width, LANES), lambda i, p: (expert_of(i), 0, p[0] + 2 * block))

    def w_rows(block):
        return pl.BlockSpec((1, LANES, width), lambda i, p: (expert_of(i), p[0] + 2 * block, 0))

    token_spec = pl.BlockSpec(
        (1, tokens, width),
        lambda i, p: (at(i, 0, sources), 0, 0),
        pipeline_mode=pl.Buffered(1),
    )

    def out_tokens(low, cols):
        return pl.BlockSpec((1, tokens, cols), lambda i, p: (at(i, low, sources // 2), 0, 0))

    tall_spec = pl.BlockSpec(
        (2, 1, 2, quarter, half), lambda i, p: (0, expert_of(i), 0, 0, 0)
    )
    wide_spec = pl.BlockSpec((2, 1, part, width), lambda i, p: (0, expert_of(i), 0, 0))
    tall = jax.ShapeDtypeStruct((2, experts, 2, quarter, half), BF)
    wide = jax.ShapeDtypeStruct((2, experts, part, width), BF)
    mixed = jax.ShapeDtypeStruct((sources // 2, tokens, width), BF)
    d_x = jax.ShapeDtypeStruct((sources // 2, tokens, extra), BF)
    return pl.pallas_call(
        expert_kernel,
        grid_spec=pltpu.PrefetchScalarGridSpec(
            num_scalar_prefetch=1,
            grid=(third + sources // 2,),
            in_specs=[
                token_spec,
                token_spec,
                pl.BlockSpec(maps.shape, lambda i, p: (0, 0, 0)),
                pl.BlockSpec(wr_t.shape, lambda i, p: (0, 0)),
                w_cols(0),
                w_cols(1),
                w_cols(0),
                w_cols(1),
                w_rows(0),
                w_rows(1),
            ],
            out_specs=(
                out_tokens(third, width),
                out_tokens(second, width),
                out_tokens(third, extra),
                out_tokens(second, extra),
                tall_spec,
                tall_spec,
                tall_spec,
                tall_spec,
                wide_spec,
                wide_spec,
            ),
            scratch_shapes=[
                pltpu.VMEM((experts, slots, width), BF),
                pltpu.VMEM((experts, slots, width), BF),
                pltpu.VMEM((experts, slots, 1), F32),
                pltpu.VMEM((half, width), BF),
                pltpu.VMEM((width, half), BF),
            ],
        ),
        out_shape=(mixed, mixed, d_x, d_x, tall, tall, tall, tall, wide, wide),
        compiler_params=params(63, ("arbitrary",)),
        cost_estimate=cost(60e9, 90e6),
    )(place, x_all, g_all, maps, wr_t, w_gate, w_gate, w_up, w_up, w_down, w_down)


def post_kernel(
    dx_ref,
    mid_ref,
    cot_ref,
    norm_ref,
    wr_ref,
    map_ref,
    gain_ref,
    wo_ref,
    datt_ref,
    dmid_ref,
    dlow_ref,
    dlog_ref,
    ggain_ref,
):
    middle = mid_ref[...]
    inv = lax.rsqrt(jnp.mean(middle * middle, axis=-1, keepdims=True) + EPS)
    chosen = map_ref[...] >= 0.0
    logits = jnp.where(chosen, dot_nn(norm_ref[...], wr_ref[...]), MASKED)
    raised = jnp.exp(logits - jnp.max(logits, axis=-1, keepdims=True))
    raised = jnp.where(chosen, raised, 0.0)
    gates = raised / jnp.sum(raised, axis=-1, keepdims=True)
    d_gates = dx_ref[:, WIDTH:]
    d_picked = gates * (d_gates - jnp.sum(gates * d_gates, axis=-1, keepdims=True))
    d_logits = d_picked.astype(BF)
    dlog_ref[...] = d_logits
    d_norm = dx_ref[:, :WIDTH] + dot_nt(d_logits, wr_ref[...])
    scaled = d_norm * gain_ref[...]
    ggain_ref[...] = jnp.sum(d_norm * middle * inv, axis=0, keepdims=True)
    d_mid = (
        cot_ref[...]
        + inv * scaled
        - middle * inv**3 * jnp.mean(middle * scaled, axis=-1, keepdims=True)
    )
    dmid_ref[...] = d_mid
    d_low = d_mid.astype(BF)
    dlow_ref[...] = d_low
    d_att = dot_nt(d_low, wo_ref[...]).astype(BF)
    for g in range(KV_HEADS):
        datt_ref[g] = d_att[:, g * ROWS_Q : (g + 1) * ROWS_Q]


def run_post(dx_sum, middle, cotangent, normed_two, wr_pad, map_rows, gain, w_output):
    tokens = middle.shape[0]
    return pl.pallas_call(
        post_kernel,
        out_shape=(
            jax.ShapeDtypeStruct((KV_HEADS, tokens, ROWS_Q), BF),
            jax.ShapeDtypeStruct((tokens, WIDTH), F32),
            jax.ShapeDtypeStruct((tokens, WIDTH), BF),
            jax.ShapeDtypeStruct((tokens, LANES), BF),
            jax.ShapeDtypeStruct((1, WIDTH), F32),
        ),
        compiler_params=params(48),
        cost_estimate=cost(2 * tokens * WIDTH * WIDTH, 14e6),
    )(dx_sum, middle, cotangent, normed_two, wr_pad, map_rows, gain[None], w_output)


def put_rows(place_ref, held, keep, send):
    part = keep.shape[1]
    for b in range(keep.shape[0]):
        own = (2 * b) ^ place_ref[5]
        keep[b] = held[pl.ds(pl.multiple_of(own * part, part), part), :]
        other = own ^ 1
        send[b] = held[pl.ds(pl.multiple_of(other * part, part), part), :]


def outgrad_kernel(place_ref, a_ref, b_ref, keep, send, held):
    held[...] = dot_tn(a_ref[...], b_ref[...]).astype(BF)
    put_rows(place_ref, held, keep, send)


def run_outgrad(place, left, right, blocks):
    tokens, rows = left.shape
    cols = right.shape[1]
    part = rows // blocks
    spec = pl.BlockSpec((blocks // 2, part, 256), lambda i, p: (0, 0, i))
    shape = jax.ShapeDtypeStruct((blocks // 2, part, cols), BF)
    return pl.pallas_call(
        outgrad_kernel,
        grid_spec=pltpu.PrefetchScalarGridSpec(
            num_scalar_prefetch=1,
            grid=(cols // 256,),
            in_specs=[
                pl.BlockSpec((tokens, rows), lambda i, p: (0, 0)),
                pl.BlockSpec((tokens, 256), lambda i, p: (0, i)),
            ],
            out_specs=(spec, spec),
            scratch_shapes=[pltpu.VMEM((rows, 256), BF)],
        ),
        out_shape=(shape, shape),
        compiler_params=params(32, ("arbitrary",)),
        cost_estimate=cost(2 * tokens * rows * cols, 8e6),
    )(place, left, right)


def qkvgrad_kernel(
    place_ref, a_ref, d_ref, full_ref, keep0, send0, keep1, send1, keep2, send2, held
):
    step = pl.program_id(0)

    @pl.when(step == 0)
    def _():
        key_at = KV_HEADS * ROWS_Q
        value_at = key_at + KV_HEADS * HEAD_DIM
        for g in range(KV_HEADS):
            full_ref[:, g * ROWS_Q : (g + 1) * ROWS_Q] = d_ref[g, :, 0:ROWS_Q]
            full_ref[:, key_at + g * HEAD_DIM : key_at + (g + 1) * HEAD_DIM] = d_ref[
                g, :, ROWS_Q : ROWS_Q + HEAD_DIM
            ]
            full_ref[:, value_at + g * HEAD_DIM : value_at + (g + 1) * HEAD_DIM] = d_ref[
                g, :, ROWS_Q + HEAD_DIM : PACK
            ]

    cols = pl.ds(pl.multiple_of(step * 256, 256), 256)
    held[...] = dot_tn(a_ref[...], full_ref[:, cols]).astype(BF)

    @pl.when(step < 3)
    def _():
        put_rows(place_ref, held, keep0, send0)

    @pl.when((step >= 3) & (step < 6))
    def _():
        put_rows(place_ref, held, keep1, send1)

    @pl.when(step >= 6)
    def _():
        put_rows(place_ref, held, keep2, send2)


def run_qkvgrad(place, normed, d_pack, blocks):
    tokens, rows = normed.shape
    cols = KV_HEADS * PACK
    part = rows // blocks

    def spec(low, size):
        return pl.BlockSpec(
            (blocks // 2, part, 256), lambda i, p: (0, 0, jnp.clip(i - low, 0, size - 1))
        )

    def shape(size):
        return jax.ShapeDtypeStruct((blocks // 2, part, size * 256), BF)

    return pl.pallas_call(
        qkvgrad_kernel,
        grid_spec=pltpu.PrefetchScalarGridSpec(
            num_scalar_prefetch=1,
            grid=(cols // 256,),
            in_specs=[
                pl.BlockSpec((tokens, rows), lambda i, p: (0, 0)),
                pl.BlockSpec(d_pack.shape, lambda i, p: (0, 0, 0)),
            ],
            out_specs=(
                pl.BlockSpec((tokens, cols), lambda i, p: (0, 0)),
                spec(0, 3),
                spec(0, 3),
                spec(3, 3),
                spec(3, 3),
                spec(6, 4),
                spec(6, 4),
            ),
            scratch_shapes=[pltpu.VMEM((rows, 256), BF)],
        ),
        out_shape=(
            jax.ShapeDtypeStruct((tokens, cols), BF),
            shape(3),
            shape(3),
            shape(3),
            shape(3),
            shape(4),
            shape(4),
        ),
        compiler_params=params(40, ("arbitrary",)),
        cost_estimate=cost(2 * tokens * rows * cols, 12e6),
    )(place, normed, d_pack)


def last_kernel(d_ref, wq_ref, wk_ref, wv_ref, dmid_ref, hid_ref, gain_ref, out_ref, ggain_ref):
    key_at = KV_HEADS * ROWS_Q
    value_at = key_at + KV_HEADS * HEAD_DIM
    d_norm = dot_nt(d_ref[:, 0:key_at], wq_ref[...])
    d_norm += dot_nt(d_ref[:, key_at:value_at], wk_ref[...])
    d_norm += dot_nt(d_ref[:, value_at:], wv_ref[...])
    inputs = hid_ref[...]
    inv = lax.rsqrt(jnp.mean(inputs * inputs, axis=-1, keepdims=True) + EPS)
    scaled = d_norm * gain_ref[...]
    ggain_ref[...] = jnp.sum(d_norm * inputs * inv, axis=0, keepdims=True)
    out_ref[...] = (
        dmid_ref[...]
        + inv * scaled
        - inputs * inv**3 * jnp.mean(inputs * scaled, axis=-1, keepdims=True)
    )


def run_last(d_full, w_query, w_key, w_value, d_middle, inputs, gain):
    tokens = inputs.shape[0]
    return pl.pallas_call(
        last_kernel,
        out_shape=(
            jax.ShapeDtypeStruct((tokens, WIDTH), F32),
            jax.ShapeDtypeStruct((1, WIDTH), F32),
        ),
        compiler_params=params(48),
        cost_estimate=cost(2 * tokens * WIDTH * 2560, 16e6),
    )(d_full, w_query, w_key, w_value, d_middle, inputs, gain[None])


def gather_relative(values):
    held = values[None]
    for bit in (X_BIT, ZL_BIT, C_BIT):
        held = jnp.concatenate([held, swap_bit(held, bit)], axis=0)
    return held


def sum_pair(kept, received):
    return kept.astype(F32) + received.astype(F32)


def scatter_tokens(keep, send):
    tokens, cols = keep.shape[1:]
    got = swap_bit(send, C_BIT)
    both = sum_pair(keep, got).reshape(2, 2, tokens, cols)
    half = tokens // 2
    results = []
    for part in range(2):
        rows = slice(part * half, (part + 1) * half)
        if part == 0:
            mine, other = both[:, 0, rows], both[:, 1, rows]
            bits = (X_BIT, ZL_BIT)
        else:
            mine, other = both[0, :, rows], both[1, :, rows]
            bits = (ZL_BIT, X_BIT)
        held = sum_pair(mine, swap_bit(other.astype(BF), bits[0]))
        results.append(sum_pair(held[0], swap_bit(held[1].astype(BF), bits[1])))
    return jnp.concatenate(results, axis=0)


BITS = {"zh": ZH_BIT, "zl": ZL_BIT, "y": Y_BIT, "x": X_BIT}


def scatter_dense(keep, send, order, low=BF):
    part, cols = keep.shape[1:]
    held = sum_pair(keep, swap_bit(send, C_BIT)).reshape(2, 2, 2, 2, part, cols)
    names = ["zh", "zl", "y", "x"]
    for name in order:
        axis = names.index(name)
        mine = lax.index_in_dim(held, 0, axis, keepdims=False)
        other = lax.index_in_dim(held, 1, axis, keepdims=False)
        held = sum_pair(mine, swap_bit(other.astype(low), BITS[name]))
        names.remove(name)
    return held


def scatter_expert(keep, send):
    held = sum_pair(keep, swap_bit(send, Y_BIT))
    return sum_pair(held[0], swap_bit(held[1].astype(BF), ZH_BIT))


def join_columns(total, zl_at):
    mine = total[:, 0]
    other = swap_bit(total[:, 1].astype(BF), ZL_BIT).astype(F32)
    experts, rows, cols = mine.shape
    mine = mine.reshape(experts, rows, 2, 1, LANES)
    other = other.reshape(experts, rows, 2, 1, LANES)
    low = jnp.where(zl_at == 0, mine, other)
    high = jnp.where(zl_at == 0, other, mine)
    return jnp.concatenate([low, high], axis=3).reshape(experts, rows, 2 * cols)


def fast_body(
    hidden_in,
    gain_attn,
    w_query,
    w_key,
    w_value,
    w_output,
    gain_mlp,
    w_router,
    w_gate,
    w_up,
    w_down,
    expert_ids,
    slot_order,
    grad_out,
):
    inputs = hidden_in[0]
    cotangent = grad_out[0]
    chosen = expert_ids[0]
    tokens = inputs.shape[0]
    top = chosen.shape[1]
    local_experts = w_gate.shape[0]
    peers = lax.axis_size("expert")
    all_experts = local_experts * peers
    shards = lax.axis_size("dp")
    length = shards * tokens
    devices = shards * peers
    index = lax.axis_index("dp")
    column = lax.axis_index("expert")
    y_at = index % 2
    zl_at = (index // 2) % 2
    zh_at = index // 4
    place = jnp.stack(
        [zl_at, y_at, zl_at, zh_at, column * local_experts, index * peers + column]
    ).astype(jnp.int32)

    ranks = slot_order[0, 0].reshape(tokens, top)
    far = tokens * top
    match = chosen.T[None] == jnp.arange(all_experts, dtype=jnp.int32)[:, None, None]
    rank_map = jnp.min(jnp.where(match, ranks.T[None], far), axis=1)
    before = jnp.sum((rank_map[:, None, :] < rank_map[:, :, None]).astype(jnp.int32), axis=-1)
    slot_map = jnp.where(rank_map < far, jnp.minimum(before, SLOTS), -1).astype(BF)
    map_rows = jnp.pad(slot_map.T.astype(F32), ((0, 0), (0, LANES - all_experts)), constant_values=-1.0)
    maps = gather_relative(slot_map).astype(F32)
    maps = jnp.roll(maps, -column * local_experts, axis=1)
    g_all = gather_relative(cotangent.astype(BF))
    wr_pad = jnp.pad(w_router, ((0, 0), (0, LANES - all_experts)))
    wr_t = jnp.roll(w_router.T, -column * local_experts, axis=0)
    wr_t = jnp.pad(wr_t, ((0, LANES - all_experts), (0, 0)))

    half = HEAD_DIM // 2
    frequency = jnp.exp(-math.log(10000.0) * jnp.arange(half, dtype=F32) * 2.0 / HEAD_DIM)
    own_angles = (index * tokens + jnp.arange(tokens, dtype=jnp.int32)).astype(F32)[:, None] * frequency
    cos_own, sin_own = jnp.cos(own_angles), jnp.sin(own_angles)
    cos_tab = jnp.concatenate([cos_own] * 4, axis=1)
    sin_tab = jnp.concatenate([-sin_own, sin_own] * 2, axis=1)
    angles = frequency[:, None] * jnp.arange(length, dtype=jnp.int32).astype(F32)[None]
    cos_t, sin_t = jnp.cos(angles), jnp.sin(angles)

    normed, pack = run_pre(inputs, gain_attn, w_query, w_key, w_value, cos_tab, sin_tab)
    pack = lax.all_to_all(pack, "dp", 0, 0, tiled=True).reshape(length, PACK)
    out, out_t, lse = run_forward(pack)
    att = lax.all_to_all(out.reshape(shards, tokens, ROWS_Q), "dp", 0, 0, tiled=True)
    middle, normed_two, att_full = run_mid(att, w_output, inputs, gain_mlp)
    x_all = gather_relative(normed_two)
    (
        mix_keep,
        mix_send,
        dx_keep,
        dx_send,
        gate_keep,
        gate_send,
        up_keep,
        up_send,
        down_keep,
        down_send,
    ) = run_experts(place, x_all, g_all, maps, wr_t, w_gate, w_up, w_down)
    dx_sum = scatter_tokens(dx_keep, dx_send)
    hidden_out = middle + scatter_tokens(mix_keep, mix_send)
    gate_total = join_columns(scatter_expert(gate_keep, gate_send), zl_at)
    up_total = join_columns(scatter_expert(up_keep, up_send), zl_at)
    down_total = scatter_expert(down_keep, down_send)

    d_att, d_middle, d_low, d_log, ggain_mlp = run_post(
        dx_sum, middle, cotangent, normed_two, wr_pad, map_rows, gain_mlp, w_output
    )
    d_out = lax.all_to_all(d_att, "dp", 0, 0, tiled=True).reshape(length, ROWS_Q)
    out_keep, out_send = run_outgrad(place, att_full, d_low, devices)
    output_total = scatter_dense(out_keep, out_send, ("x", "y", "zl", "zh"))
    router_part = dot_tn(normed_two, d_log)[:, :all_experts]

    d_pack = run_backward(pack, d_out, out_t, lse, cos_t, sin_t)
    d_pack = lax.all_to_all(
        d_pack.reshape(shards, tokens, PACK), "dp", 0, 0, tiled=True
    )
    d_full, keep0, send0, keep1, send1, keep2, send2 = run_qkvgrad(place, normed, d_pack, devices)
    total0 = scatter_dense(keep0, send0, ("x", "y", "zl", "zh"))
    total1 = scatter_dense(keep1, send1, ("y", "zl", "x", "zh"))
    total2 = scatter_dense(keep2, send2, ("zl", "x", "y", "zh"))
    grad_in, ggain_attn = run_last(
        d_full, w_query, w_key, w_value, d_middle, inputs, gain_attn
    )
    small = jnp.concatenate([router_part, ggain_mlp.T, ggain_attn.T], axis=1)
    small = lax.psum_scatter(small, ("dp", "expert"), scatter_dimension=0, tiled=True)
    key_width = KV_HEADS * HEAD_DIM
    return (
        hidden_out[None],
        grad_in[None],
        small[:, all_experts + 1],
        jnp.concatenate([total0, total1], axis=1),
        total2[:, :key_width],
        total2[:, key_width:],
        output_total,
        small[:, all_experts],
        small[:, :all_experts],
        gate_total,
        up_total,
        down_total,
    )


def fits(mesh):
    return mesh.shape["dp"] == KV_HEADS and mesh.shape["expert"] == 4


def solution(mesh):
    in_specs = (
        P("expert", "dp", None),
        P(),
        P(),
        P(),
        P(),
        P(),
        P(),
        P(),
        P("expert", None, None),
        P("expert", None, None),
        P("expert", None, None),
        P("expert", "dp", None),
        P("expert", "dp", None),
        P("expert", "dp", None),
    )
    out_specs = (
        P("expert", "dp", None),
        P("expert", "dp", None),
        P(("dp", "expert")),
        P(("dp", "expert"), None),
        P(("dp", "expert"), None),
        P(("dp", "expert"), None),
        P(("dp", "expert"), None),
        P(("dp", "expert")),
        P(("dp", "expert"), None),
        P("expert", "dp", None),
        P("expert", "dp", None),
        P("expert", "dp", None),
    )
    chosen = fast_body if fits(mesh) else body
    return jax.shard_map(chosen, mesh=mesh, in_specs=in_specs, out_specs=out_specs, check_vma=False)
```

```python
import functools
import math

import jax
import jax.numpy as jnp
from jax import lax
from jax.experimental import pallas as pl
from jax.experimental.pallas import tpu as pltpu
from jax.sharding import PartitionSpec as P

HEADS = 24
KV_HEADS = 8
HEAD_DIM = 64


EPS = 1e-05
MASKED = -1e30


def rotary_tables(positions):
    half = HEAD_DIM // 2
    frequency = jnp.exp(-math.log(10000.0) * jnp.arange(half, dtype=jnp.float32) * 2.0 / HEAD_DIM)
    angles = positions.astype(jnp.float32)[:, None] * frequency[None, :]
    return (jnp.cos(angles)[:, None, :], jnp.sin(angles)[:, None, :])


def rotate(values, cosine, sine):
    half = values.shape[-1] // 2
    first = values[..., :half]
    second = values[..., half:]
    return jnp.concatenate(
        [first * cosine - second * sine, second * cosine + first * sine], axis=-1
    )


def rotate_back(values, cosine, sine):
    half = values.shape[-1] // 2
    first = values[..., :half]
    second = values[..., half:]
    return jnp.concatenate(
        [first * cosine + second * sine, second * cosine - first * sine], axis=-1
    )


def assign_slots(row_chosen, row_ranks, all_experts, capacity):
    pairs = row_chosen.shape[0]
    by_rank = jnp.zeros((pairs,), jnp.int32).at[row_ranks].set(jnp.arange(pairs, dtype=jnp.int32))
    ordered = row_chosen[by_rank]
    table = (ordered[:, None] == jnp.arange(all_experts, dtype=jnp.int32)[None, :]).astype(
        jnp.int32
    )
    before = jnp.sum(table * (jnp.cumsum(table, axis=0) - 1), axis=1)
    slot = before[row_ranks]
    target = jnp.where(slot < capacity, row_chosen * capacity + slot, all_experts * capacity)
    owner = (
        jnp.full((all_experts * capacity,), pairs, jnp.int32)
        .at[target]
        .set(jnp.arange(pairs, dtype=jnp.int32), mode="drop")
    )
    return (target, owner)


def body(
    hidden_in,
    gain_attn,
    w_query,
    w_key,
    w_value,
    w_output,
    gain_mlp,
    w_router,
    w_gate,
    w_up,
    w_down,
    expert_ids,
    slot_order,
    grad_out,
):
    inputs = hidden_in[0]
    cotangent = grad_out[0]
    chosen = expert_ids[0]
    tokens, width = inputs.shape
    top = chosen.shape[1]
    local_experts = w_gate.shape[0]
    peers = lax.axis_size("expert")
    all_experts = local_experts * peers
    pairs = tokens * top
    capacity = pairs // all_experts
    shards = lax.axis_size("dp")
    index = lax.axis_index("dp")
    length = shards * tokens
    block = math.gcd(length, 512)
    groups = HEADS // KV_HEADS
    scale = HEAD_DIM ** (-0.5)
    query_pos = index * tokens + jnp.arange(tokens, dtype=jnp.int32)
    cosine, sine = rotary_tables(query_pos)
    count = ((index + 1) * tokens + block - 1) // block
    inv_one = lax.rsqrt(jnp.mean(inputs * inputs, axis=-1, keepdims=True) + EPS)
    normed = (inputs * inv_one * gain_attn).astype(jnp.bfloat16)
    query_pre = jnp.dot(normed, w_query, preferred_element_type=jnp.float32).reshape(
        tokens, HEADS, HEAD_DIM
    )
    queries = rotate(query_pre, cosine, sine).astype(jnp.bfloat16)
    key_pre = jnp.dot(normed, w_key, preferred_element_type=jnp.float32).reshape(
        tokens, KV_HEADS, HEAD_DIM
    )
    keys_low = rotate(key_pre, cosine, sine).astype(jnp.bfloat16)
    values_low = (
        jnp.dot(normed, w_value, preferred_element_type=jnp.float32)
        .astype(jnp.bfloat16)
        .reshape(tokens, KV_HEADS, HEAD_DIM)
    )
    keys_all, values_all = (
        lax.all_gather(keys_low, "dp", axis=0, tiled=True),
        lax.all_gather(values_low, "dp", axis=0, tiled=True),
    )
    query_groups = queries.reshape(tokens, KV_HEADS, groups, HEAD_DIM)

    def block_scores(key_block, start):
        raw = (
            jnp.einsum(
                "qkgd,skd->kgqs", query_groups, key_block, preferred_element_type=jnp.float32
            )
            * scale
        )
        key_pos = start + jnp.arange(block, dtype=jnp.int32)
        allowed = key_pos[None, :] <= query_pos[:, None]
        return jnp.where(allowed, raw, MASKED)

    def stats_step(step, carry):
        running, total = carry
        scores = block_scores(
            lax.dynamic_slice_in_dim(keys_all, step * block, block, 0), step * block
        )
        newest = jnp.maximum(running, jnp.max(scores, axis=-1))
        total = total * jnp.exp(running - newest) + jnp.sum(
            jnp.exp(scores - newest[..., None]), axis=-1
        )
        return (newest, total)

    stat_init = (
        jnp.full((KV_HEADS, groups, tokens), MASKED, jnp.float32),
        jnp.zeros((KV_HEADS, groups, tokens), jnp.float32),
    )
    running, total = lax.fori_loop(0, count, stats_step, stat_init)
    log_total = running + jnp.log(total)

    def output_step(step, accum):
        start = step * block
        scores = block_scores(lax.dynamic_slice_in_dim(keys_all, start, block, 0), start)
        probs = jnp.exp(scores - log_total[..., None]).astype(jnp.bfloat16)
        value_block = lax.dynamic_slice_in_dim(values_all, start, block, 0)
        return accum + jnp.einsum(
            "kgqs,skd->qkgd", probs, value_block, preferred_element_type=jnp.float32
        )

    attended_groups = lax.fori_loop(
        0, count, output_step, jnp.zeros((tokens, KV_HEADS, groups, HEAD_DIM), jnp.float32)
    )
    attended = attended_groups.reshape(tokens, HEADS * HEAD_DIM)
    attended_low = attended.astype(jnp.bfloat16)
    branch = jnp.dot(attended_low, w_output, preferred_element_type=jnp.float32)
    middle = inputs + branch
    inv_two = lax.rsqrt(jnp.mean(middle * middle, axis=-1, keepdims=True) + EPS)
    normed_two = (middle * inv_two * gain_mlp).astype(jnp.bfloat16)
    logits = jnp.dot(normed_two, w_router, preferred_element_type=jnp.float32)
    onehot = (chosen[:, :, None] == jnp.arange(all_experts, dtype=jnp.int32)[None, None, :]).astype(
        jnp.float32
    )
    picked = jnp.sum(onehot * logits[:, None, :], axis=-1)
    gates = jax.nn.softmax(picked, axis=-1)
    target, owner = assign_slots(chosen.reshape(pairs), slot_order[0, 0], all_experts, capacity)
    valid = owner < pairs
    source = jnp.minimum(owner, pairs - 1)
    rows_send = jnp.where(valid[:, None], normed_two[source // top], 0).reshape(
        peers, local_experts, capacity, width
    )
    received = lax.all_to_all(rows_send, "expert", split_axis=0, concat_axis=0, tiled=True)
    gate_pre = jnp.einsum("necd,edf->necf", received, w_gate, preferred_element_type=jnp.float32)
    up_pre = jnp.einsum("necd,edf->necf", received, w_up, preferred_element_type=jnp.float32)
    hidden = (jax.nn.silu(gate_pre) * up_pre).astype(jnp.bfloat16)
    result = jnp.einsum(
        "necf,efd->necd", hidden, w_down, preferred_element_type=jnp.float32
    ).astype(jnp.bfloat16)
    returned = lax.all_to_all(result, "expert", split_axis=0, concat_axis=0, tiled=True)
    returned, received, gate_pre, up_pre = (returned, received, gate_pre, up_pre)
    zero_row = jnp.zeros((1, width), jnp.bfloat16)
    pair_out = jnp.concatenate([returned.reshape(all_experts * capacity, width), zero_row], axis=0)[
        target
    ].reshape(tokens, top, width)
    mixed = jnp.einsum("tk,tkd->td", gates, pair_out, preferred_element_type=jnp.float32)
    hidden_out = middle + mixed
    dy_pairs = (
        (gates[:, :, None] * cotangent[:, None, :]).astype(jnp.bfloat16).reshape(pairs, width)
    )
    dy_send = jnp.where(valid[:, None], dy_pairs[source], 0).reshape(
        peers, local_experts, capacity, width
    )
    dy_received = lax.all_to_all(dy_send, "expert", split_axis=0, concat_axis=0, tiled=True)
    sigmoid_gate = jax.nn.sigmoid(gate_pre)
    silu_gate = gate_pre * sigmoid_gate
    hidden = (silu_gate * up_pre).astype(jnp.bfloat16)
    grad_down_part = jnp.einsum(
        "necf,necd->efd", hidden, dy_received, preferred_element_type=jnp.float32
    )
    d_hidden = jnp.einsum("necd,efd->necf", dy_received, w_down, preferred_element_type=jnp.float32)
    d_gate = (d_hidden * up_pre * sigmoid_gate * (1.0 + gate_pre * (1.0 - sigmoid_gate))).astype(
        jnp.bfloat16
    )
    d_up = (d_hidden * silu_gate).astype(jnp.bfloat16)
    grad_gate_part = jnp.einsum(
        "necd,necf->edf", received, d_gate, preferred_element_type=jnp.float32
    )
    grad_up_part = jnp.einsum("necd,necf->edf", received, d_up, preferred_element_type=jnp.float32)
    gate_total, up_total, down_total = (
        lax.psum_scatter(
            grad_gate_part.astype(jnp.bfloat16), "dp", scatter_dimension=1, tiled=True
        ).astype(jnp.float32),
        lax.psum_scatter(
            grad_up_part.astype(jnp.bfloat16), "dp", scatter_dimension=1, tiled=True
        ).astype(jnp.float32),
        lax.psum_scatter(
            grad_down_part.astype(jnp.bfloat16), "dp", scatter_dimension=1, tiled=True
        ).astype(jnp.float32),
    )
    d_rows = jnp.einsum("necf,edf->necd", d_gate, w_gate, preferred_element_type=jnp.float32)
    d_rows = (
        d_rows + jnp.einsum("necf,edf->necd", d_up, w_up, preferred_element_type=jnp.float32)
    ).astype(jnp.bfloat16)
    d_back = lax.all_to_all(d_rows, "expert", split_axis=0, concat_axis=0, tiled=True)
    d_pairs = jnp.concatenate([d_back.reshape(all_experts * capacity, width), zero_row], axis=0)[
        target
    ].reshape(tokens, top, width)
    d_normed_two = jnp.sum(d_pairs, axis=1, dtype=jnp.float32)
    d_gates = jnp.einsum("td,tkd->tk", cotangent, pair_out, preferred_element_type=jnp.float32)
    d_picked = gates * (d_gates - jnp.sum(gates * d_gates, axis=-1, keepdims=True))
    d_logits = jnp.sum(onehot * d_picked[:, :, None], axis=1).astype(jnp.bfloat16)
    grad_router_part = jnp.einsum(
        "td,te->de", normed_two, d_logits, preferred_element_type=jnp.float32
    )
    d_normed_two = d_normed_two + jnp.einsum(
        "te,de->td", d_logits, w_router, preferred_element_type=jnp.float32
    )
    scaled_two = d_normed_two * gain_mlp
    grad_gain_mlp_part = jnp.sum(d_normed_two * middle * inv_two, axis=0)
    d_middle = (
        cotangent
        + inv_two * scaled_two
        - middle * inv_two**3 * jnp.mean(middle * scaled_two, axis=-1, keepdims=True)
    )
    d_branch = d_middle.astype(jnp.bfloat16)
    grad_output_part = jnp.einsum(
        "tf,td->fd", attended_low, d_branch, preferred_element_type=jnp.float32
    )
    d_attended = jnp.einsum(
        "td,fd->tf", d_branch, w_output, preferred_element_type=jnp.float32
    ).astype(jnp.bfloat16)
    d_groups = d_attended.reshape(tokens, KV_HEADS, groups, HEAD_DIM)
    delta = jnp.einsum(
        "qkgd,qkgd->kgq", d_groups, attended_groups, preferred_element_type=jnp.float32
    )
    keys_back, values_back = (
        lax.all_gather(keys_low, "dp", axis=0, tiled=True),
        lax.all_gather(values_low, "dp", axis=0, tiled=True),
    )

    def grad_step(step, carry):
        d_query, d_keys, d_values = carry
        start = step * block
        key_block = lax.dynamic_slice_in_dim(keys_back, start, block, 0)
        value_block = lax.dynamic_slice_in_dim(values_back, start, block, 0)
        scores = block_scores(key_block, start)
        probs = jnp.exp(scores - log_total[..., None])
        probs_low = probs.astype(jnp.bfloat16)
        d_probs = jnp.einsum(
            "qkgd,skd->kgqs", d_groups, value_block, preferred_element_type=jnp.float32
        )
        d_scores = (probs * (d_probs - delta[..., None])).astype(jnp.bfloat16)
        d_query = d_query + jnp.einsum(
            "kgqs,skd->qkgd", d_scores, key_block, preferred_element_type=jnp.float32
        )
        key_part = jnp.einsum(
            "kgqs,qkgd->skd", d_scores, query_groups, preferred_element_type=jnp.float32
        )
        value_part = jnp.einsum(
            "kgqs,qkgd->skd", probs_low, d_groups, preferred_element_type=jnp.float32
        )
        d_keys = lax.dynamic_update_slice_in_dim(
            d_keys, lax.dynamic_slice_in_dim(d_keys, start, block, 0) + key_part, start, 0
        )
        d_values = lax.dynamic_update_slice_in_dim(
            d_values, lax.dynamic_slice_in_dim(d_values, start, block, 0) + value_part, start, 0
        )
        return (d_query, d_keys, d_values)

    grad_init = (
        jnp.zeros((tokens, KV_HEADS, groups, HEAD_DIM), jnp.float32),
        jnp.zeros((length, KV_HEADS, HEAD_DIM), jnp.float32),
        jnp.zeros((length, KV_HEADS, HEAD_DIM), jnp.float32),
    )
    d_query, d_keys, d_values = lax.fori_loop(0, count, grad_step, grad_init)
    key_sum, value_sum = (
        lax.psum_scatter(
            (d_keys * scale).reshape(length, KV_HEADS * HEAD_DIM).astype(jnp.bfloat16),
            "dp",
            scatter_dimension=0,
            tiled=True,
        ).astype(jnp.float32),
        lax.psum_scatter(
            d_values.reshape(length, KV_HEADS * HEAD_DIM).astype(jnp.bfloat16),
            "dp",
            scatter_dimension=0,
            tiled=True,
        ).astype(jnp.float32),
    )
    d_query_low = (
        rotate_back((d_query * scale).reshape(tokens, HEADS, HEAD_DIM), cosine, sine)
        .astype(jnp.bfloat16)
        .reshape(tokens, HEADS * HEAD_DIM)
    )
    d_key_low = (
        rotate_back(key_sum.reshape(tokens, KV_HEADS, HEAD_DIM), cosine, sine)
        .astype(jnp.bfloat16)
        .reshape(tokens, KV_HEADS * HEAD_DIM)
    )
    d_value_low = value_sum.astype(jnp.bfloat16)
    grad_query_part = jnp.einsum(
        "td,tf->df", normed, d_query_low, preferred_element_type=jnp.float32
    )
    grad_key_part = jnp.einsum("td,tf->df", normed, d_key_low, preferred_element_type=jnp.float32)
    grad_value_part = jnp.einsum(
        "td,tf->df", normed, d_value_low, preferred_element_type=jnp.float32
    )
    d_normed = jnp.einsum("tf,df->td", d_query_low, w_query, preferred_element_type=jnp.float32)
    d_normed = d_normed + jnp.einsum(
        "tf,df->td", d_key_low, w_key, preferred_element_type=jnp.float32
    )
    d_normed = d_normed + jnp.einsum(
        "tf,df->td", d_value_low, w_value, preferred_element_type=jnp.float32
    )
    scaled_one = d_normed * gain_attn
    grad_gain_attn_part = jnp.sum(d_normed * inputs * inv_one, axis=0)
    grad_in = (
        d_middle
        + inv_one * scaled_one
        - inputs * inv_one**3 * jnp.mean(inputs * scaled_one, axis=-1, keepdims=True)
    )
    dense = (
        lax.psum_scatter(grad_gain_attn_part, ("dp", "expert"), scatter_dimension=0, tiled=True),
        lax.psum_scatter(grad_query_part, ("dp", "expert"), scatter_dimension=0, tiled=True),
        lax.psum_scatter(grad_key_part, ("dp", "expert"), scatter_dimension=0, tiled=True),
        lax.psum_scatter(grad_value_part, ("dp", "expert"), scatter_dimension=0, tiled=True),
        lax.psum_scatter(grad_output_part, ("dp", "expert"), scatter_dimension=0, tiled=True),
        lax.psum_scatter(grad_gain_mlp_part, ("dp", "expert"), scatter_dimension=0, tiled=True),
        lax.psum_scatter(grad_router_part, ("dp", "expert"), scatter_dimension=0, tiled=True),
    )
    return (
        hidden_out[None],
        grad_in[None],
        dense[0],
        dense[1],
        dense[2],
        dense[3],
        dense[4],
        dense[5],
        dense[6],
        gate_total,
        up_total,
        down_total,
    )

BF = jnp.bfloat16
F32 = jnp.float32
WIDTH = 1536
LANES = 128
PER_KV = HEADS // KV_HEADS
ROWS_Q = PER_KV * HEAD_DIM
PACK = ROWS_Q + 2 * HEAD_DIM
BIT_Y, BIT_ZL, BIT_ZH = 1, 2, 4
BIT_C, BIT_X = 1, 2
BLOCK_Q = 256
BLOCK_K = 512
SLOTS = 64
CHUNK = 512
MIB = 1 << 20


def dot_nn(a, b):
    return lax.dot_general(a, b, (((1,), (0,)), ((), ())), preferred_element_type=F32)


def dot_nt(a, b):
    return lax.dot_general(a, b, (((1,), (1,)), ((), ())), preferred_element_type=F32)


def dot_tn(a, b):
    return lax.dot_general(a, b, (((0,), (0,)), ((), ())), preferred_element_type=F32)


def cost(flops, moved, transcendentals=0):
    return pl.CostEstimate(
        flops=int(flops), bytes_accessed=int(moved), transcendentals=int(transcendentals)
    )


def params(mib, dims=None):
    return pltpu.CompilerParams(vmem_limit_bytes=mib * MIB, dimension_semantics=dims)


def swap(values, axis, mask):
    size = lax.axis_size(axis)
    return lax.ppermute(values, axis, [(i, i ^ mask) for i in range(size)])


def swap_bit(values, bit):
    axis, mask = bit
    return swap(values, axis, mask)


def fence(*values):
    return lax.optimization_barrier(values)


C_BIT = ("expert", BIT_C)
X_BIT = ("expert", BIT_X)
Y_BIT = ("dp", BIT_Y)
ZL_BIT = ("dp", BIT_ZL)
ZH_BIT = ("dp", BIT_ZH)


def pre_kernel(hid_ref, gain_ref, wq_ref, wk_ref, wv_ref, cos_ref, sin_ref, norm_ref, pack_ref):
    tokens = hid_ref.shape[0]
    inputs = hid_ref[...]
    inv = lax.rsqrt(jnp.mean(inputs * inputs, axis=-1, keepdims=True) + EPS)
    normed = (inputs * inv * gain_ref[...]).astype(BF)
    norm_ref[...] = normed
    low = (lax.broadcasted_iota(jnp.int32, (tokens, LANES), 1) % HEAD_DIM) < HEAD_DIM // 2
    cosine, sine = cos_ref[...], sin_ref[...]

    def turn(tile):
        other = jnp.where(
            low,
            pltpu.roll(tile, LANES - HEAD_DIM // 2, 1),
            pltpu.roll(tile, HEAD_DIM // 2, 1),
        )
        return (tile * cosine + other * sine).astype(BF)

    def put_heads(tiles, width, start):
        flat = jnp.concatenate(tiles, axis=1)
        for g in range(KV_HEADS):
            pack_ref[g, :, start : start + width] = flat[:, g * width : (g + 1) * width]

    tiles = []
    for n in range(wq_ref.shape[1] // CHUNK):
        pre = dot_nn(normed, wq_ref[:, n * CHUNK : (n + 1) * CHUNK])
        tiles += [turn(pre[:, m * LANES : (m + 1) * LANES]) for m in range(CHUNK // LANES)]
    put_heads(tiles, ROWS_Q, 0)
    pre = dot_nn(normed, wk_ref[...])
    put_heads(
        [turn(pre[:, m * LANES : (m + 1) * LANES]) for m in range(pre.shape[1] // LANES)],
        HEAD_DIM,
        ROWS_Q,
    )
    put_heads([dot_nn(normed, wv_ref[...]).astype(BF)], HEAD_DIM, ROWS_Q + HEAD_DIM)


def run_pre(inputs, gain, w_query, w_key, w_value, cos_tab, sin_tab):
    tokens = inputs.shape[0]
    return pl.pallas_call(
        pre_kernel,
        out_shape=(
            jax.ShapeDtypeStruct((tokens, WIDTH), BF),
            jax.ShapeDtypeStruct((KV_HEADS, tokens, PACK), BF),
        ),
        compiler_params=params(48),
        cost_estimate=cost(2 * tokens * WIDTH * 2560, 14e6),
    )(inputs, gain[None], w_query, w_key, w_value, cos_tab, sin_tab)


def heads_t(block, width):
    return jnp.concatenate(
        [block[:, h * HEAD_DIM : (h + 1) * HEAD_DIM].astype(F32).T for h in range(width)], axis=1
    )


def heads_rows(block, width):
    return jnp.concatenate(
        [block[:, h * HEAD_DIM : (h + 1) * HEAD_DIM] for h in range(width)], axis=0
    )


def allowed_t(step, block):
    shape = (BLOCK_K, PER_KV * BLOCK_Q)
    key_pos = step * BLOCK_K + lax.broadcasted_iota(jnp.int32, shape, 0)
    query_pos = block * BLOCK_Q + lax.broadcasted_iota(jnp.int32, shape, 1) % BLOCK_Q
    return key_pos <= query_pos


def forward_kernel(pack_ref, out_ref, out_t_ref, lse_ref, k_s, vt_s):
    block = pl.program_id(0)

    @pl.when(block == 0)
    def _():
        k_s[...] = pack_ref[:, ROWS_Q : ROWS_Q + HEAD_DIM]
        vt_s[...] = pack_ref[:, ROWS_Q + HEAD_DIM : PACK].astype(F32).T.astype(BF)

    rows = pl.ds(pl.multiple_of(block * BLOCK_Q, BLOCK_Q), BLOCK_Q)
    scale = HEAD_DIM ** (-0.5)
    q_t = (heads_t(pack_ref[rows, 0:ROWS_Q], PER_KV) * scale).astype(BF)
    columns = PER_KV * BLOCK_Q

    def step(j, carry, masked):
        running, total, accum = carry
        keys = pl.ds(pl.multiple_of(j * BLOCK_K, BLOCK_K), BLOCK_K)
        scores = dot_nn(k_s[keys, :], q_t)
        if masked:
            scores = jnp.where(allowed_t(j, block), scores, MASKED)
        newest = jnp.maximum(running, jnp.max(scores, axis=0, keepdims=True))
        fade = jnp.exp(running - newest)
        probs = jnp.exp(scores - newest)
        total = total * fade + jnp.sum(probs, axis=0, keepdims=True)
        accum = accum * fade + dot_nn(vt_s[:, keys], probs.astype(BF))
        return newest, total, accum

    carry = (
        jnp.full((1, columns), MASKED, F32),
        jnp.zeros((1, columns), F32),
        jnp.zeros((HEAD_DIM, columns), F32),
    )
    last = (block * BLOCK_Q) // BLOCK_K
    carry = lax.fori_loop(0, last, lambda j, c: step(j, c, False), carry)
    running, total, accum = step(last, carry, True)
    out_t = accum / total
    out_t_ref[0] = out_t
    lse_ref[0] = running + jnp.log(total)
    out_ref[...] = jnp.concatenate(
        [out_t[:, h * BLOCK_Q : (h + 1) * BLOCK_Q].T for h in range(PER_KV)], axis=1
    ).astype(BF)


def run_forward(pack):
    length = pack.shape[0]
    blocks = length // BLOCK_Q
    columns = PER_KV * BLOCK_Q
    return pl.pallas_call(
        forward_kernel,
        grid=(blocks,),
        in_specs=[pl.BlockSpec((length, PACK), lambda i: (0, 0))],
        out_specs=(
            pl.BlockSpec((BLOCK_Q, ROWS_Q), lambda i: (i, 0)),
            pl.BlockSpec((1, HEAD_DIM, columns), lambda i: (i, 0, 0)),
            pl.BlockSpec((1, 1, columns), lambda i: (i, 0, 0)),
        ),
        out_shape=(
            jax.ShapeDtypeStruct((length, ROWS_Q), BF),
            jax.ShapeDtypeStruct((blocks, HEAD_DIM, columns), F32),
            jax.ShapeDtypeStruct((blocks, 1, columns), F32),
        ),
        scratch_shapes=[pltpu.VMEM((length, HEAD_DIM), BF), pltpu.VMEM((HEAD_DIM, length), BF)],
        compiler_params=params(40, ("arbitrary",)),
        cost_estimate=cost(8 * length * length * ROWS_Q, 6e6, length * length * PER_KV),
    )(pack)


def backward_kernel(
    pack_ref, grad_ref, out_t_ref, lse_ref, cos_ref, sin_ref, res_ref, k_s, v_s, kt_s, dk_s, dv_s
):
    block = pl.program_id(0)

    @pl.when(block == 0)
    def _():
        keys = pack_ref[:, ROWS_Q : ROWS_Q + HEAD_DIM]
        k_s[...] = keys
        kt_s[...] = keys.astype(F32).T.astype(BF)
        v_s[...] = pack_ref[:, ROWS_Q + HEAD_DIM : PACK]
        dk_s[...] = jnp.zeros_like(dk_s)
        dv_s[...] = jnp.zeros_like(dv_s)

    scale = HEAD_DIM ** (-0.5)
    half = HEAD_DIM // 2
    rows = pl.ds(pl.multiple_of(block * BLOCK_Q, BLOCK_Q), BLOCK_Q)
    q_block = pack_ref[rows, 0:ROWS_Q]
    q_t = (heads_t(q_block, PER_KV) * scale).astype(BF)
    q_rows = (heads_rows(q_block, PER_KV).astype(F32) * scale).astype(BF)
    do_block = grad_ref[...]
    do_f32 = heads_t(do_block, PER_KV)
    do_t = do_f32.astype(BF)
    do_rows = heads_rows(do_block, PER_KV)
    delta = jnp.sum(do_f32 * out_t_ref[0], axis=0, keepdims=True)
    lse = lse_ref[0]

    def step(j, dq_t, masked):
        keys = pl.ds(pl.multiple_of(j * BLOCK_K, BLOCK_K), BLOCK_K)
        scores = dot_nn(k_s[keys, :], q_t)
        if masked:
            scores = jnp.where(allowed_t(j, block), scores, MASKED)
        probs = jnp.exp(scores - lse)
        d_probs = dot_nn(v_s[keys, :], do_t)
        d_scores = (probs * (d_probs - delta)).astype(BF)
        dv_s[keys, :] += dot_nn(probs.astype(BF), do_rows)
        dk_s[keys, :] += dot_nn(d_scores, q_rows)
        return dq_t + dot_nn(kt_s[:, keys], d_scores)

    last = (block * BLOCK_Q) // BLOCK_K
    dq_t = jnp.zeros((HEAD_DIM, PER_KV * BLOCK_Q), F32)
    dq_t = lax.fori_loop(0, last, lambda j, c: step(j, c, False), dq_t)
    dq_t = step(last, dq_t, True) * scale

    def turn_back(values, cosine, sine):
        first, second = values[:half], values[half:]
        return jnp.concatenate(
            [first * cosine + second * sine, second * cosine - first * sine], axis=0
        )

    columns = pl.ds(pl.multiple_of(block * BLOCK_Q, BLOCK_Q), BLOCK_Q)
    cosine, sine = cos_ref[:, columns], sin_ref[:, columns]
    res_ref[rows, 0:ROWS_Q] = jnp.concatenate(
        [
            turn_back(dq_t[:, h * BLOCK_Q : (h + 1) * BLOCK_Q], cosine, sine).T
            for h in range(PER_KV)
        ],
        axis=1,
    ).astype(BF)

    @pl.when(block == pl.num_programs(0) - 1)
    def _():
        dk_t = turn_back(dk_s[...].T, cos_ref[...], sin_ref[...])
        res_ref[:, ROWS_Q : ROWS_Q + HEAD_DIM] = dk_t.T.astype(BF)
        res_ref[:, ROWS_Q + HEAD_DIM : PACK] = dv_s[...].astype(BF)


def run_backward(pack, grad, out_t, lse, cos_t, sin_t):
    length = pack.shape[0]
    blocks = length // BLOCK_Q
    columns = PER_KV * BLOCK_Q
    half = HEAD_DIM // 2
    return pl.pallas_call(
        backward_kernel,
        grid=(blocks,),
        in_specs=[
            pl.BlockSpec((length, PACK), lambda i: (0, 0)),
            pl.BlockSpec((BLOCK_Q, ROWS_Q), lambda i: (i, 0)),
            pl.BlockSpec((1, HEAD_DIM, columns), lambda i: (i, 0, 0)),
            pl.BlockSpec((1, 1, columns), lambda i: (i, 0, 0)),
            pl.BlockSpec((half, length), lambda i: (0, 0)),
            pl.BlockSpec((half, length), lambda i: (0, 0)),
        ],
        out_specs=pl.BlockSpec((length, PACK), lambda i: (0, 0)),
        out_shape=jax.ShapeDtypeStruct((length, PACK), BF),
        scratch_shapes=[
            pltpu.VMEM((length, HEAD_DIM), BF),
            pltpu.VMEM((length, HEAD_DIM), BF),
            pltpu.VMEM((HEAD_DIM, length), BF),
            pltpu.VMEM((length, HEAD_DIM), F32),
            pltpu.VMEM((length, HEAD_DIM), F32),
        ],
        compiler_params=params(48, ("arbitrary",)),
        cost_estimate=cost(20 * length * length * ROWS_Q, 8e6, length * length * PER_KV),
    )(pack, grad, out_t, lse, cos_t, sin_t)


def mid_kernel(att_ref, wo_ref, hid_ref, gain_ref, mid_ref, norm_ref, full_ref):
    for g in range(KV_HEADS):
        full_ref[:, g * ROWS_Q : (g + 1) * ROWS_Q] = att_ref[g]
    middle = hid_ref[...] + dot_nn(full_ref[...], wo_ref[...])
    mid_ref[...] = middle
    inv = lax.rsqrt(jnp.mean(middle * middle, axis=-1, keepdims=True) + EPS)
    norm_ref[...] = (middle * inv * gain_ref[...]).astype(BF)


def run_mid(att, w_output, inputs, gain):
    tokens = inputs.shape[0]
    return pl.pallas_call(
        mid_kernel,
        out_shape=(
            jax.ShapeDtypeStruct((tokens, WIDTH), F32),
            jax.ShapeDtypeStruct((tokens, WIDTH), BF),
            jax.ShapeDtypeStruct((tokens, WIDTH), BF),
        ),
        compiler_params=params(40),
        cost_estimate=cost(2 * tokens * WIDTH * WIDTH, 12e6),
    )(att, w_output, inputs, gain[None])


def expert_kernel(
    place_ref,
    x_ref,
    g_ref,
    map_ref,
    wr_ref,
    wg0_ref,
    wg1_ref,
    wu0_ref,
    wu1_ref,
    wd0_ref,
    wd1_ref,
    *refs,
    first,
):
    if first:
        mix_prior = dx_prior = None
    else:
        mix_prior, dx_prior = refs[0:2], refs[2:4]
        refs = refs[4:]
    (
    mix_keep,
    mix_send,
    dx_keep,
    dx_send,
    gate_keep,
    gate_send,
    up_keep,
    up_send,
    down_keep,
    down_send,
    xs,
    gs,
    gate_s,
    wide_s,
    tall_s,
    ) = refs
    step = pl.program_id(0)
    sources = map_ref.shape[0]
    experts = xs.shape[0]
    low = 0 if first else experts
    tokens = x_ref.shape[1]
    rows = experts * SLOTS
    count = WIDTH // CHUNK

    def one_hot(source):
        slots = map_ref[source, low : low + experts, :]
        wide = jnp.broadcast_to(slots[:, None, :], (experts, SLOTS, tokens))
        rank = lax.broadcasted_iota(jnp.int32, (experts, SLOTS, tokens), 1).astype(F32)
        return (wide == rank).astype(F32).reshape(rows, tokens)

    @pl.when(step < sources)
    def _():
        slot_map = map_ref[step]
        chosen = slot_map >= 0.0
        logits = dot_nt(wr_ref[...], x_ref[0])[0 : slot_map.shape[0]]
        logits = jnp.where(chosen, logits, MASKED)
        raised = jnp.exp(logits - jnp.max(logits, axis=0, keepdims=True))
        raised = jnp.where(chosen, raised, 0.0)
        gates = raised / jnp.sum(raised, axis=0, keepdims=True)
        pick = one_hot(step)
        wide = jnp.broadcast_to(gates[low : low + experts, None, :], (experts, SLOTS, tokens))
        gate_rows = jnp.sum(pick * wide.reshape(rows, tokens), axis=1, keepdims=True)
        pick = pick.astype(BF)
        here = pl.ds(pl.multiple_of(step * SLOTS, SLOTS), SLOTS)
        for e in range(experts):
            gate_s[e, here, :] = gate_rows[e * SLOTS : (e + 1) * SLOTS]
        for n in range(count):
            cols = slice(n * CHUNK, (n + 1) * CHUNK)
            got = dot_nn(pick, x_ref[0, :, cols]).astype(BF)
            xs[:, here, cols] = got.reshape(experts, SLOTS, CHUNK)
            got = dot_nn(pick, g_ref[0, :, cols]).astype(BF)
            gs[:, here, cols] = got.reshape(experts, SLOTS, CHUNK)

    @pl.when((step >= sources) & (step < sources + experts))
    def _():
        e = step - sources
        x = xs[e]
        w_gate = jnp.concatenate([wg0_ref[0], wg1_ref[0]], axis=1)
        w_up = jnp.concatenate([wu0_ref[0], wu1_ref[0]], axis=1)
        gate_pre = dot_nn(x, w_gate)
        up_pre = dot_nn(x, w_up)
        sig = jax.nn.sigmoid(gate_pre)
        silu = gate_pre * sig
        hidden = (silu * up_pre).astype(BF)
        gate = gate_s[e]
        d_hidden = jnp.zeros(hidden.shape, F32)
        d_gates = jnp.zeros(gate.shape, F32)
        for n in range(count):
            cols = slice(n * CHUNK, (n + 1) * CHUNK)
            w_down = jnp.concatenate([wd0_ref[0, :, cols], wd1_ref[0, :, cols]], axis=0)
            grad = gs[e, :, cols].astype(F32)
            d_y = (gate * grad).astype(BF)
            y = dot_nn(hidden, w_down)
            d_gates += jnp.sum(y * grad, axis=1, keepdims=True)
            gs[e, :, cols] = (gate * y).astype(BF)
            d_hidden += dot_nt(d_y, w_down)
            wide_s[:, cols] = dot_tn(hidden, d_y).astype(BF)
        gate_s[e] = d_gates
        d_gate = (d_hidden * up_pre * sig * (1.0 + gate_pre * (1.0 - sig))).astype(BF)
        d_up = (d_hidden * silu).astype(BF)

        y_at, zl_at, zh_at = place_ref[1], place_ref[2], place_ref[3]
        part = down_keep.shape[2]
        for z in range(2):
            base = (zh_at ^ z) * 2
            down_keep[z, 0] = wide_s[pl.ds(pl.multiple_of((base + y_at) * part, part), part), :]
            down_send[z, 0] = wide_s[
                pl.ds(pl.multiple_of((base + (1 - y_at)) * part, part), part), :
            ]

        def spread(keep, send):
            part = keep.shape[3]
            for z in range(2):
                for low in range(2):
                    base = ((zh_at ^ z) * 2 + (zl_at ^ low)) * 2
                    keep[z, low, 0] = tall_s[
                        pl.ds(pl.multiple_of((base + y_at) * part, part), part), :
                    ]
                    send[z, low, 0] = tall_s[
                        pl.ds(pl.multiple_of((base + (1 - y_at)) * part, part), part), :
                    ]

        for n in range(count):
            cols = slice(n * CHUNK, (n + 1) * CHUNK)
            tall_s[cols, :] = dot_tn(x[:, cols], d_gate).astype(BF)
        spread(gate_keep, gate_send)
        for n in range(count):
            cols = slice(n * CHUNK, (n + 1) * CHUNK)
            tall_s[cols, :] = dot_tn(x[:, cols], d_up).astype(BF)
        spread(up_keep, up_send)
        for n in range(count):
            cols = slice(n * CHUNK, (n + 1) * CHUNK)
            d_x = dot_nt(d_gate, w_gate[cols]) + dot_nt(d_up, w_up[cols])
            xs[e, :, cols] = d_x.astype(BF)

    def combine(source, mix_out, dx_out, mix_in, dx_in):
        def put(out, prior, cols, values):
            if prior is not None:
                values += prior[0, :, cols].astype(F32)
            out[0, :, cols] = values.astype(BF)

        here = pl.ds(pl.multiple_of(source * SLOTS, SLOTS), SLOTS)
        pick = one_hot(source).astype(BF)
        for n in range(count):
            cols = slice(n * CHUNK, (n + 1) * CHUNK)
            put(dx_out, dx_in, cols, dot_tn(pick, xs[:, here, cols].reshape(rows, CHUNK)))
            put(mix_out, mix_in, cols, dot_tn(pick, gs[:, here, cols].reshape(rows, CHUNK)))
        values = gate_s[:, here, :].reshape(rows, 1)
        column = lax.broadcasted_iota(jnp.int32, (rows, LANES), 1)
        owner = lax.broadcasted_iota(jnp.int32, (rows, LANES), 0) // SLOTS
        spread_out = jnp.where(column == owner + (place_ref[4] + low), values, 0.0).astype(BF)
        put(dx_out, dx_in, slice(WIDTH, WIDTH + LANES), dot_tn(pick, spread_out))

    @pl.when((step >= sources + experts) & (step < sources + experts + sources // 2))
    def _():
        source = step - experts - sources // 2
        prior = (None, None) if first else (mix_prior[1], dx_prior[1])
        combine(source, mix_send, dx_send, *prior)

    @pl.when(step >= sources + experts + sources // 2)
    def _():
        source = step - experts - sources - sources // 2
        prior = (None, None) if first else (mix_prior[0], dx_prior[0])
        combine(source, mix_keep, dx_keep, *prior)


def run_experts(place, x_all, g_all, maps, wr_t, w_gate, w_up, w_down, prior=()):
    sources, tokens, width = x_all.shape
    experts = w_gate.shape[0] // 2
    low = experts if prior else 0
    ffe = w_gate.shape[2]
    part = ffe // 8
    quarter = width // 8
    half = ffe // 2
    slots = sources * SLOTS
    extra = width + LANES
    second = sources + experts
    third = second + sources // 2

    def at(i, low, size):
        return jnp.clip(i - low, 0, size - 1)

    def expert_of(i):
        return at(i, sources, experts)

    def w_cols(block):
        return pl.BlockSpec(
            (1, width, LANES), lambda i, p: (expert_of(i) + low, 0, p[0] + 2 * block)
        )

    def w_rows(block):
        return pl.BlockSpec(
            (1, LANES, width), lambda i, p: (expert_of(i) + low, p[0] + 2 * block, 0)
        )

    token_spec = pl.BlockSpec(
        (1, tokens, width),
        lambda i, p: (at(i, 0, sources), 0, 0),
    )

    def out_tokens(low, cols):
        return pl.BlockSpec((1, tokens, cols), lambda i, p: (at(i, low, sources // 2), 0, 0))

    tall_spec = pl.BlockSpec(
        (2, 2, 1, quarter, half), lambda i, p: (0, 0, expert_of(i), 0, 0)
    )
    wide_spec = pl.BlockSpec((2, 1, part, width), lambda i, p: (0, expert_of(i), 0, 0))
    tall = jax.ShapeDtypeStruct((2, 2, experts, quarter, half), BF)
    wide = jax.ShapeDtypeStruct((2, experts, part, width), BF)
    mixed = jax.ShapeDtypeStruct((sources // 2, tokens, width), BF)
    d_x = jax.ShapeDtypeStruct((sources // 2, tokens, extra), BF)
    sums = (
        out_tokens(third, width),
        out_tokens(second, width),
        out_tokens(third, extra),
        out_tokens(second, extra),
    )
    return pl.pallas_call(
        functools.partial(expert_kernel, first=not prior),
        grid_spec=pltpu.PrefetchScalarGridSpec(
            num_scalar_prefetch=1,
            grid=(third + sources // 2,),
            in_specs=[
                token_spec,
                token_spec,
                pl.BlockSpec(maps.shape, lambda i, p: (0, 0, 0)),
                pl.BlockSpec(wr_t.shape, lambda i, p: (0, 0)),
                w_cols(0),
                w_cols(1),
                w_cols(0),
                w_cols(1),
                w_rows(0),
                w_rows(1),
                *(sums if prior else ()),
            ],
            out_specs=(
                *sums,
                tall_spec,
                tall_spec,
                tall_spec,
                tall_spec,
                wide_spec,
                wide_spec,
            ),
            scratch_shapes=[
                pltpu.VMEM((experts, slots, width), BF),
                pltpu.VMEM((experts, slots, width), BF),
                pltpu.VMEM((experts, slots, 1), F32),
                pltpu.VMEM((half, width), BF),
                pltpu.VMEM((width, half), BF),
            ],
        ),
        out_shape=(mixed, mixed, d_x, d_x, tall, tall, tall, tall, wide, wide),
        compiler_params=params(56, ("arbitrary",)),
        cost_estimate=cost(30e9, 60e6),
    )(place, x_all, g_all, maps, wr_t, w_gate, w_gate, w_up, w_up, w_down, w_down, *prior)


def post_kernel(
    dx_ref,
    mid_ref,
    cot_ref,
    norm_ref,
    wr_ref,
    map_ref,
    gain_ref,
    wo_ref,
    datt_ref,
    dmid_ref,
    dlow_ref,
    dlog_ref,
    ggain_ref,
):
    middle = mid_ref[...]
    inv = lax.rsqrt(jnp.mean(middle * middle, axis=-1, keepdims=True) + EPS)
    chosen = map_ref[...] >= 0.0
    logits = jnp.where(chosen, dot_nn(norm_ref[...], wr_ref[...]), MASKED)
    raised = jnp.exp(logits - jnp.max(logits, axis=-1, keepdims=True))
    raised = jnp.where(chosen, raised, 0.0)
    gates = raised / jnp.sum(raised, axis=-1, keepdims=True)
    d_gates = dx_ref[:, WIDTH:]
    d_picked = gates * (d_gates - jnp.sum(gates * d_gates, axis=-1, keepdims=True))
    d_logits = d_picked.astype(BF)
    dlog_ref[...] = d_logits
    d_norm = dx_ref[:, :WIDTH] + dot_nt(d_logits, wr_ref[...])
    scaled = d_norm * gain_ref[...]
    ggain_ref[...] = jnp.sum(d_norm * middle * inv, axis=0, keepdims=True)
    d_mid = (
        cot_ref[...]
        + inv * scaled
        - middle * inv**3 * jnp.mean(middle * scaled, axis=-1, keepdims=True)
    )
    dmid_ref[...] = d_mid
    d_low = d_mid.astype(BF)
    dlow_ref[...] = d_low
    d_att = dot_nt(d_low, wo_ref[...]).astype(BF)
    for g in range(KV_HEADS):
        datt_ref[g] = d_att[:, g * ROWS_Q : (g + 1) * ROWS_Q]


def run_post(dx_sum, middle, cotangent, normed_two, wr_pad, map_rows, gain, w_output):
    tokens = middle.shape[0]
    return pl.pallas_call(
        post_kernel,
        out_shape=(
            jax.ShapeDtypeStruct((KV_HEADS, tokens, ROWS_Q), BF),
            jax.ShapeDtypeStruct((tokens, WIDTH), F32),
            jax.ShapeDtypeStruct((tokens, WIDTH), BF),
            jax.ShapeDtypeStruct((tokens, LANES), BF),
            jax.ShapeDtypeStruct((1, WIDTH), F32),
        ),
        compiler_params=params(48),
        cost_estimate=cost(2 * tokens * WIDTH * WIDTH, 14e6),
    )(dx_sum, middle, cotangent, normed_two, wr_pad, map_rows, gain[None], w_output)


def put_rows(place_ref, held, keep, send):
    part = keep.shape[1]
    for b in range(keep.shape[0]):
        own = (2 * b) ^ place_ref[5]
        keep[b] = held[pl.ds(pl.multiple_of(own * part, part), part), :]
        other = own ^ 1
        send[b] = held[pl.ds(pl.multiple_of(other * part, part), part), :]


def outgrad_kernel(place_ref, a_ref, b_ref, keep, send, held):
    held[...] = dot_tn(a_ref[...], b_ref[...]).astype(BF)
    put_rows(place_ref, held, keep, send)


def run_outgrad(place, left, right, blocks):
    tokens, rows = left.shape
    cols = right.shape[1]
    part = rows // blocks
    spec = pl.BlockSpec((blocks // 2, part, 256), lambda i, p: (0, 0, i))
    shape = jax.ShapeDtypeStruct((blocks // 2, part, cols), BF)
    return pl.pallas_call(
        outgrad_kernel,
        grid_spec=pltpu.PrefetchScalarGridSpec(
            num_scalar_prefetch=1,
            grid=(cols // 256,),
            in_specs=[
                pl.BlockSpec((tokens, rows), lambda i, p: (0, 0)),
                pl.BlockSpec((tokens, 256), lambda i, p: (0, i)),
            ],
            out_specs=(spec, spec),
            scratch_shapes=[pltpu.VMEM((rows, 256), BF)],
        ),
        out_shape=(shape, shape),
        compiler_params=params(32, ("arbitrary",)),
        cost_estimate=cost(2 * tokens * rows * cols, 8e6),
    )(place, left, right)


def qkvgrad_kernel(place_ref, a_ref, d_ref, full_ref, keep, send, held):
    step = pl.program_id(0)

    @pl.when(step == 0)
    def _():
        key_at = KV_HEADS * ROWS_Q
        value_at = key_at + KV_HEADS * HEAD_DIM
        for g in range(KV_HEADS):
            full_ref[:, g * ROWS_Q : (g + 1) * ROWS_Q] = d_ref[g, :, 0:ROWS_Q]
            full_ref[:, key_at + g * HEAD_DIM : key_at + (g + 1) * HEAD_DIM] = d_ref[
                g, :, ROWS_Q : ROWS_Q + HEAD_DIM
            ]
            full_ref[:, value_at + g * HEAD_DIM : value_at + (g + 1) * HEAD_DIM] = d_ref[
                g, :, ROWS_Q + HEAD_DIM : PACK
            ]

    cols = pl.ds(pl.multiple_of(step * 256, 256), 256)
    held[...] = dot_tn(a_ref[...], full_ref[:, cols]).astype(BF)
    put_rows(place_ref, held, keep, send)


def run_qkvgrad(place, normed, d_pack, blocks):
    tokens, rows = normed.shape
    cols = KV_HEADS * PACK
    part = rows // blocks
    spec = pl.BlockSpec((blocks // 2, part, 256), lambda i, p: (0, 0, i))
    shape = jax.ShapeDtypeStruct((blocks // 2, part, cols), BF)
    return pl.pallas_call(
        qkvgrad_kernel,
        grid_spec=pltpu.PrefetchScalarGridSpec(
            num_scalar_prefetch=1,
            grid=(cols // 256,),
            in_specs=[
                pl.BlockSpec((tokens, rows), lambda i, p: (0, 0)),
                pl.BlockSpec(d_pack.shape, lambda i, p: (0, 0, 0)),
            ],
            out_specs=(pl.BlockSpec((tokens, cols), lambda i, p: (0, 0)), spec, spec),
            scratch_shapes=[pltpu.VMEM((rows, 256), BF)],
        ),
        out_shape=(jax.ShapeDtypeStruct((tokens, cols), BF), shape, shape),
        compiler_params=params(40, ("arbitrary",)),
        cost_estimate=cost(2 * tokens * rows * cols, 12e6),
    )(place, normed, d_pack)


def last_kernel(d_ref, wq_ref, wk_ref, wv_ref, dmid_ref, hid_ref, gain_ref, out_ref, ggain_ref):
    key_at = KV_HEADS * ROWS_Q
    value_at = key_at + KV_HEADS * HEAD_DIM
    d_norm = dot_nt(d_ref[:, 0:key_at], wq_ref[...])
    d_norm += dot_nt(d_ref[:, key_at:value_at], wk_ref[...])
    d_norm += dot_nt(d_ref[:, value_at:], wv_ref[...])
    inputs = hid_ref[...]
    inv = lax.rsqrt(jnp.mean(inputs * inputs, axis=-1, keepdims=True) + EPS)
    scaled = d_norm * gain_ref[...]
    ggain_ref[...] = jnp.sum(d_norm * inputs * inv, axis=0, keepdims=True)
    out_ref[...] = (
        dmid_ref[...]
        + inv * scaled
        - inputs * inv**3 * jnp.mean(inputs * scaled, axis=-1, keepdims=True)
    )


def run_last(d_full, w_query, w_key, w_value, d_middle, inputs, gain):
    tokens = inputs.shape[0]
    return pl.pallas_call(
        last_kernel,
        out_shape=(
            jax.ShapeDtypeStruct((tokens, WIDTH), F32),
            jax.ShapeDtypeStruct((1, WIDTH), F32),
        ),
        compiler_params=params(48),
        cost_estimate=cost(2 * tokens * WIDTH * 2560, 16e6),
    )(d_full, w_query, w_key, w_value, d_middle, inputs, gain[None])


def small_kernel(place_ref, norm_ref, dlog_ref, gmlp_ref, gattn_ref, keep, send, held):
    columns = dot_tn(norm_ref[...], dlog_ref[...])
    lane = lax.broadcasted_iota(jnp.int32, columns.shape, 1)
    for n, ref in enumerate((gmlp_ref, gattn_ref)):
        turned = jnp.broadcast_to(ref[...], (8, ref.shape[1])).T[:, 0:1]
        columns = jnp.where(lane == LANES - 2 + n, turned, columns)
    held[...] = columns
    put_rows(place_ref, held, keep, send)


def run_small(place, normed_two, d_log, ggain_mlp, ggain_attn, blocks):
    part = WIDTH // blocks
    shape = jax.ShapeDtypeStruct((blocks // 2, part, LANES), F32)
    smem = pl.BlockSpec(memory_space=pltpu.SMEM)
    vmem = pl.BlockSpec(memory_space=pltpu.VMEM)
    return pl.pallas_call(
        small_kernel,
        in_specs=[smem] + [vmem] * 4,
        out_shape=(shape, shape),
        scratch_shapes=[pltpu.VMEM((WIDTH, LANES), F32)],
        compiler_params=params(24),
        cost_estimate=cost(1e8, 3e6),
    )(place, normed_two, d_log, ggain_mlp, ggain_attn)


def stack_swap(values, bit):
    return jnp.concatenate([values, swap_bit(values, bit)], axis=0)


MESH = pl.DeviceIdType.MESH


def peer_of(bit):
    axis, mask = bit
    return {axis: lax.axis_index(axis) ^ mask}


def greet(ids):
    barrier = pltpu.get_barrier_semaphore()
    for device in ids:
        pl.semaphore_signal(barrier, inc=1, device_id=device, device_id_type=MESH)
    pl.semaphore_wait(barrier, len(ids))


GATHER_BITS = (X_BIT, ZL_BIT, C_BIT)


def gather_steps(x_ref, all_ref, send_sem, recv_sem, local_sem):
    half = x_ref.shape[0] // 2
    own = pltpu.make_async_copy(x_ref, all_ref.at[0], local_sem)
    own.start()
    copies = []

    def send(source, slot, rows, bit):
        n = len(copies)
        copy = pltpu.make_async_remote_copy(
            src_ref=source if rows is None else source.at[rows],
            dst_ref=all_ref.at[slot] if rows is None else all_ref.at[slot, rows],
            send_sem=send_sem.at[n],
            recv_sem=recv_sem.at[n],
            device_id=peer_of(bit),
            device_id_type=MESH,
        )
        copy.start()
        copies.append(copy)
        return copy

    top, low = pl.ds(0, half), pl.ds(half, half)
    x_top = send(x_ref, 1, top, X_BIT)
    z_low = send(x_ref, 2, low, ZL_BIT)
    x_low = send(x_ref, 1, low, X_BIT)
    z_top = send(x_ref, 2, top, ZL_BIT)
    last = [send(x_ref, 4, None, C_BIT)]
    x_top.wait_recv()
    far_top = send(all_ref.at[1], 3, top, ZL_BIT)
    z_low.wait_recv()
    far_low = send(all_ref.at[2], 3, low, X_BIT)
    x_low.wait_recv()
    last.append(send(all_ref.at[1], 5, None, C_BIT))
    z_top.wait_recv()
    last.append(send(all_ref.at[2], 6, None, C_BIT))
    far_top.wait_recv()
    far_low.wait_recv()
    last.append(send(all_ref.at[3], 7, None, C_BIT))
    for copy in last:
        copy.wait_recv()
    for copy in copies:
        copy.wait_send()
    own.wait()


def gather_kernel(*refs):
    x_ref, blocks = refs[0], refs[1:5]
    all_ref, other_ref = refs[5:7]
    send_sem, recv_sem, more_send, more_recv, local_sem = refs[7:]
    greet([peer_of(bit) for bit in GATHER_BITS])
    local = []
    remote = []
    for n, block in enumerate(blocks):
        copy = pltpu.make_async_remote_copy(
            src_ref=block,
            dst_ref=other_ref.at[4 + n],
            send_sem=more_send.at[n],
            recv_sem=more_recv.at[n],
            device_id=peer_of(C_BIT),
            device_id_type=MESH,
        )
        copy.start()
        remote.append(copy)
        copy = pltpu.make_async_copy(block, other_ref.at[n], local_sem.at[1 + n])
        copy.start()
        local.append(copy)
    gather_steps(x_ref, all_ref, send_sem, recv_sem, local_sem.at[0])
    for copy in local:
        copy.wait()
    for copy in remote:
        copy.wait()


def run_gather(values, blocks):
    tokens, width = values.shape
    hbm = pl.BlockSpec(memory_space=pl.ANY)
    shape = jax.ShapeDtypeStruct((8, tokens, width), values.dtype)
    return pl.pallas_call(
        gather_kernel,
        in_specs=[hbm] * 5,
        out_specs=(hbm, hbm),
        out_shape=(shape, shape),
        scratch_shapes=[pltpu.SemaphoreType.DMA((n,)) for n in (10, 10, 4, 4, 5)],
        compiler_params=pltpu.CompilerParams(
            collective_id=1, has_side_effects=True, vmem_limit_bytes=16 * MIB
        ),
        cost_estimate=cost(0, 150e6),
    )(values, *blocks)


def trade_peers(size):
    me = lax.axis_index("dp")
    return [{"dp": me ^ k} for k in range(size - 1, 0, -1)]


def trade_start(a_ref, out_ref, send_sem, recv_sem, local_sem):
    me = lax.axis_index("dp")
    copies = []
    for n, device in enumerate(trade_peers(a_ref.shape[0])):
        copy = pltpu.make_async_remote_copy(
            src_ref=a_ref.at[device["dp"]],
            dst_ref=out_ref.at[me],
            send_sem=send_sem.at[n],
            recv_sem=recv_sem.at[n],
            device_id=device,
            device_id_type=MESH,
        )
        copy.start()
        copies.append(copy)
    own = pltpu.make_async_copy(a_ref.at[me], out_ref.at[me], local_sem)
    own.start()
    return copies, own


def trade_end(copies, own):
    own.wait()
    for copy in copies:
        copy.wait_recv()
    for copy in copies:
        copy.wait_send()


def trade_kernel(a_ref, out_ref, send_sem, recv_sem, local_sem):
    greet(trade_peers(a_ref.shape[0]))
    trade_end(*trade_start(a_ref, out_ref, send_sem, recv_sem, local_sem.at[0]))


def run_trade(values, number):
    size = values.shape[0]
    return pl.pallas_call(
        trade_kernel,
        in_specs=[pl.BlockSpec(memory_space=pl.ANY)],
        out_specs=pl.BlockSpec(memory_space=pl.ANY),
        out_shape=jax.ShapeDtypeStruct(values.shape, values.dtype),
        scratch_shapes=[
            pltpu.SemaphoreType.DMA((size - 1,)),
            pltpu.SemaphoreType.DMA((size - 1,)),
            pltpu.SemaphoreType.DMA((1,)),
        ],
        compiler_params=pltpu.CompilerParams(
            collective_id=number, has_side_effects=True, vmem_limit_bytes=8 * MIB
        ),
        cost_estimate=cost(0, 170e6),
    )(values)


def reduce_chain(job, part, keep_ref, send_ref, out_ref, acc, got, staged, send_sem, recv_sem):
    bits, row, rows, column, columns, order = part
    blocks = keep_ref.shape[0]
    stages = len(bits) + 1
    low = send_ref.dtype
    at = (pl.ds(row, rows), pl.ds(column, columns))
    copies = []

    def exchange(source, target, bit):
        n = job * stages + len(copies)
        copy = pltpu.make_async_remote_copy(
            src_ref=source,
            dst_ref=target,
            send_sem=send_sem.at[n],
            recv_sem=recv_sem.at[n],
            device_id=peer_of(bit),
            device_id_type=MESH,
        )
        copy.start()
        copies.append(copy)

    live = list(range(blocks))
    base_got, base_sent = 0, 0
    exchange(send_ref.at[(slice(None),) + at], got.at[(pl.ds(0, blocks),) + at], C_BIT)
    yield
    for stage in range(stages):
        copies[-1].wait_recv()

        def total(position):
            index = live[position]
            kept = keep_ref[(index,) + at].astype(F32) if stage == 0 else acc[(index,) + at]
            return kept + got[(base_got + position,) + at].astype(F32)

        if stage == stages - 1:
            out_ref[at] = total(0)
            break
        mask = 1 << order[stage]
        rest = [i for i in live if not i & mask]
        for m, i in enumerate(rest):
            staged[(base_sent + m,) + at] = total(live.index(i ^ mask)).astype(low)
        exchange(
            staged.at[(pl.ds(base_sent, len(rest)),) + at],
            got.at[(pl.ds(base_got + len(live), len(rest)),) + at],
            bits[order[stage]],
        )
        for i in rest:
            acc[(i,) + at] = total(live.index(i))
        base_got += len(live)
        base_sent += len(rest)
        live = rest
        yield
    for copy in copies:
        copy.wait_send()


def reduce_kernel(*refs, parts, bits):
    jobs = len(parts)
    keeps, sends, outs = refs[:jobs], refs[jobs : 2 * jobs], refs[2 * jobs : 3 * jobs]
    scratch = refs[3 * jobs :]
    greet([peer_of(bit) for bit in (C_BIT,) + bits])
    send_sem, recv_sem = scratch[-2:]
    chains, number = [], 0
    for n in range(jobs):
        buffers = scratch[3 * n : 3 * n + 3]
        for part in parts[n]:
            chains.append(
                reduce_chain(
                    number, (bits,) + part, keeps[n], sends[n], outs[n], *buffers, send_sem, recv_sem
                )
            )
            number += 1
    while chains:
        rest = []
        for chain in chains:
            try:
                next(chain)
                rest.append(chain)
            except StopIteration:
                pass
        chains = rest


def run_reduce(pairs, parts, bits, number):
    slots = sum(len(part) for part in parts) * (len(bits) + 1)
    vmem = pl.BlockSpec(memory_space=pltpu.VMEM)
    scratch, shapes = [], []
    for keep, send in pairs:
        blocks, rows, cols = keep.shape
        scratch += [
            pltpu.VMEM((blocks, rows, cols), F32),
            pltpu.VMEM((2 * blocks - 1, rows, cols), send.dtype),
            pltpu.VMEM((max(blocks - 1, 1), rows, cols), send.dtype),
        ]
        shapes.append(jax.ShapeDtypeStruct((rows, cols), F32))
    return pl.pallas_call(
        functools.partial(reduce_kernel, parts=parts, bits=bits),
        in_specs=[vmem] * len(pairs) + [pl.BlockSpec(memory_space=pl.ANY)] * len(pairs),
        out_specs=tuple(vmem for _ in pairs),
        out_shape=tuple(shapes),
        scratch_shapes=scratch
        + [pltpu.SemaphoreType.DMA((slots,)), pltpu.SemaphoreType.DMA((slots,))],
        compiler_params=pltpu.CompilerParams(
            collective_id=number, has_side_effects=True, vmem_limit_bytes=56 * MIB
        ),
        cost_estimate=cost(0, 170e6),
    )(*(keep for keep, _ in pairs), *(send for _, send in pairs))


def sum_pair(kept, received):
    return kept.astype(F32) + received.astype(F32)


def first_sum(keep, got):
    return sum_pair(keep[1], got[1]).astype(BF)


def low_sum(keep, got, more):
    return (sum_pair(keep[0, 1], got[0, 1]) + more[1].astype(F32)).astype(BF)


def join_down_kernel(*refs):
    out = refs[-1]
    step = pl.program_id(0)
    for part in range(2):
        keep, got, more = refs[3 * part : 3 * part + 3]

        @pl.when((step >= 5 * part) & (step < 5 * part + 5))
        def _():
            total = keep[0, 0].astype(F32) + got[0, 0].astype(F32)
            out[0] = total + more[0].astype(F32)


def join_tall_kernel(place_ref, *refs):
    out = refs[-1]
    step = pl.program_id(0)
    zl_at = place_ref[0]
    for part in range(2):
        keep, got, more, other = refs[4 * part : 4 * part + 4]

        @pl.when((step >= 5 * part) & (step < 5 * part + 5))
        def _():
            total = keep[0, 0, 0].astype(F32) + got[0, 0, 0].astype(F32)
            total += more[0, 0].astype(F32)
            across = other[0].astype(F32)
            for n in range(2):
                cols = slice(n * LANES, (n + 1) * LANES)
                mine = pl.multiple_of((2 * n + zl_at) * LANES, LANES)
                theirs = pl.multiple_of((2 * n + 1 - zl_at) * LANES, LANES)
                out[0, :, pl.ds(mine, LANES)] = total[:, cols]
                out[0, :, pl.ds(theirs, LANES)] = across[:, cols]


def run_join_down(parts):
    experts, rows, cols = parts[0][2].shape
    specs = []
    for part in range(2):
        def of(i, part=part):
            return jnp.clip(i - part * experts, 0, experts - 1)

        specs += [
            pl.BlockSpec((1, 1, rows, cols), lambda i, of=of: (0, of(i), 0, 0)),
            pl.BlockSpec((1, 1, rows, cols), lambda i, of=of: (0, of(i), 0, 0)),
            pl.BlockSpec((1, rows, cols), lambda i, of=of: (of(i), 0, 0)),
        ]
    return pl.pallas_call(
        join_down_kernel,
        grid=(2 * experts,),
        in_specs=specs,
        out_specs=pl.BlockSpec((1, rows, cols), lambda i: (i, 0, 0)),
        out_shape=jax.ShapeDtypeStruct((2 * experts, rows, cols), F32),
        compiler_params=params(24, ("arbitrary",)),
        cost_estimate=cost(1e6, 10e6),
    )(*parts[0], *parts[1])


def run_join_tall(place, parts):
    experts, rows, cols = parts[0][3].shape
    specs = []
    for part in range(2):
        def of(i, part=part):
            return jnp.clip(i - part * experts, 0, experts - 1)

        wide = pl.BlockSpec((1, 1, 1, rows, cols), lambda i, p, of=of: (0, 0, of(i), 0, 0))
        specs += [
            wide,
            wide,
            pl.BlockSpec((1, 1, rows, cols), lambda i, p, of=of: (0, of(i), 0, 0)),
            pl.BlockSpec((1, rows, cols), lambda i, p, of=of: (of(i), 0, 0)),
        ]
    return pl.pallas_call(
        join_tall_kernel,
        grid_spec=pltpu.PrefetchScalarGridSpec(
            num_scalar_prefetch=1,
            grid=(2 * experts,),
            in_specs=specs,
            out_specs=pl.BlockSpec((1, rows, 2 * cols), lambda i, p: (i, 0, 0)),
        ),
        out_shape=jax.ShapeDtypeStruct((2 * experts, rows, 2 * cols), F32),
        compiler_params=params(24, ("arbitrary",)),
        cost_estimate=cost(1e6, 12e6),
    )(place, *parts[0], *parts[1])


def fast_body(
    hidden_in,
    gain_attn,
    w_query,
    w_key,
    w_value,
    w_output,
    gain_mlp,
    w_router,
    w_gate,
    w_up,
    w_down,
    expert_ids,
    slot_order,
    grad_out,
):
    inputs = hidden_in[0]
    cotangent = grad_out[0]
    chosen = expert_ids[0]
    tokens = inputs.shape[0]
    top = chosen.shape[1]
    local_experts = w_gate.shape[0]
    peers = lax.axis_size("expert")
    all_experts = local_experts * peers
    shards = lax.axis_size("dp")
    length = shards * tokens
    devices = shards * peers
    index = lax.axis_index("dp")
    column = lax.axis_index("expert")
    y_at = index % 2
    zl_at = (index // 2) % 2
    zh_at = index // 4
    place = jnp.stack(
        [zl_at, y_at, zl_at, zh_at, column * local_experts, index * peers + column]
    ).astype(jnp.int32)

    ranks = slot_order[0, 0].reshape(tokens, top)
    far = tokens * top
    match = chosen.T[None] == jnp.arange(all_experts, dtype=jnp.int32)[:, None, None]
    rank_map = jnp.min(jnp.where(match, ranks.T[None], far), axis=1)
    before = jnp.sum((rank_map[:, None, :] < rank_map[:, :, None]).astype(jnp.int32), axis=-1)
    slot_map = jnp.where(rank_map < far, jnp.minimum(before, SLOTS), -1).astype(BF)
    map_rows = jnp.pad(slot_map.T.astype(F32), ((0, 0), (0, LANES - all_experts)), constant_values=-1.0)
    wr_pad = jnp.pad(w_router, ((0, 0), (0, LANES - all_experts)))
    wr_t = jnp.roll(w_router.T, -column * local_experts, axis=0)
    wr_t = jnp.pad(wr_t, ((0, LANES - all_experts), (0, 0)))

    half = HEAD_DIM // 2
    frequency = jnp.exp(-math.log(10000.0) * jnp.arange(half, dtype=F32) * 2.0 / HEAD_DIM)
    own_angles = (index * tokens + jnp.arange(tokens, dtype=jnp.int32)).astype(F32)[:, None] * frequency
    cos_own, sin_own = jnp.cos(own_angles), jnp.sin(own_angles)
    cos_tab = jnp.concatenate([cos_own] * 4, axis=1)
    sin_tab = jnp.concatenate([-sin_own, sin_own] * 2, axis=1)
    angles = frequency[:, None] * jnp.arange(length, dtype=jnp.int32).astype(F32)[None]
    cos_t, sin_t = jnp.cos(angles), jnp.sin(angles)

    normed, pack = run_pre(inputs, gain_attn, w_query, w_key, w_value, cos_tab, sin_tab)
    g_own = cotangent.astype(BF)
    pack, g_own, slot_map = fence(pack, g_own, slot_map)
    g_x = swap_bit(g_own, X_BIT)
    maps = stack_swap(slot_map[None], X_BIT)
    pack = run_trade(pack, 2).reshape(length, PACK)
    pack, g_x, maps, g_own = fence(pack, g_x, maps, g_own)
    g_z = swap_bit(g_own, ZL_BIT)
    maps = stack_swap(maps, ZL_BIT)
    out, out_t, lse = run_forward(pack)
    out, g_z, maps = fence(out, g_z, maps)
    g_zx = swap_bit(g_z, X_BIT)
    maps = stack_swap(maps, C_BIT)
    att = run_trade(out.reshape(shards, tokens, ROWS_Q), 3)
    att, g_zx, maps = fence(att, g_zx, maps)
    maps = jnp.roll(maps.astype(F32), -column * local_experts, axis=1)
    middle, normed_two, att_full = run_mid(att, w_output, inputs, gain_mlp)
    x_all, g_all = run_gather(normed_two, (g_own, g_x, g_z, g_zx))
    expert_args = (place, x_all, g_all, maps, wr_t, w_gate, w_up, w_down)
    *sums, gate_ka, gate_sa, up_ka, up_sa, down_ka, down_sa = run_experts(*expert_args)
    down_ga = swap_bit(down_sa, Y_BIT)
    (
        mix_keep,
        mix_send,
        dx_keep,
        dx_send,
        gate_kb,
        gate_sb,
        up_kb,
        up_sb,
        down_kb,
        down_sb,
    ) = run_experts(*expert_args, prior=tuple(sums))
    dx_send, gate_sa, down_ga, mix_send = fence(dx_send, gate_sa, down_ga, mix_send)
    down_ma = swap_bit(first_sum(down_ka, down_ga), ZH_BIT)
    gate_ga = swap_bit(gate_sa, Y_BIT)
    quarter = tokens // 4
    extra = dx_keep.shape[2]
    token_parts = tuple((n * quarter, quarter, 0, extra, (0, 1)) for n in range(4))
    (dx_sum,) = run_reduce(((dx_keep, dx_send),), (token_parts,), (X_BIT, ZL_BIT), 6)
    dx_sum, gate_ga, down_ma = fence(dx_sum, gate_ga, down_ma)
    d_att, d_middle, d_low, d_log, ggain_mlp = run_post(
        dx_sum, middle, cotangent, normed_two, wr_pad, map_rows, gain_mlp, w_output
    )
    mix_got = swap_bit(mix_send, C_BIT)
    out_keep, out_send = run_outgrad(place, att_full, d_low, devices)
    d_att, up_sa, out_send, mix_got = fence(d_att, up_sa, out_send, mix_got)
    gate_ma = swap_bit(first_sum(gate_ka, gate_ga), ZH_BIT)
    up_ga = swap_bit(up_sa, Y_BIT)
    out_got = swap_bit(out_send, C_BIT)
    mix_keep = mix_keep.reshape(2, 2, tokens, WIDTH)
    mix_got = mix_got.reshape(2, 2, tokens, WIDTH)
    mix_x = swap_bit(sum_pair(mix_keep[:, 1], mix_got[:, 1]).astype(BF), X_BIT)
    d_out = run_trade(d_att, 4).reshape(length, ROWS_Q)
    d_out, up_ga, gate_ma, gate_sb, mix_x, out_got = fence(
        d_out, up_ga, gate_ma, gate_sb, mix_x, out_got
    )
    up_ma = swap_bit(first_sum(up_ka, up_ga), ZH_BIT)
    gate_gb = swap_bit(gate_sb, Y_BIT)
    gate_oa = swap_bit(low_sum(gate_ka, gate_ga, gate_ma), ZL_BIT)
    mix_z = swap_bit(
        (sum_pair(mix_keep[1, 0], mix_got[1, 0]) + mix_x[1].astype(F32)).astype(BF), ZL_BIT
    )
    split = (2, 2, 2, 2, WIDTH // devices, WIDTH)
    out_keep, out_got = out_keep.reshape(split), out_got.reshape(split)
    out_x = swap_bit(sum_pair(out_keep[:, :, :, 1], out_got[:, :, :, 1]).astype(BF), X_BIT)
    d_pack = run_backward(pack, d_out, out_t, lse, cos_t, sin_t)
    d_pack, gate_gb, up_ma, up_sb, gate_oa, mix_z, out_x = fence(
        d_pack, gate_gb, up_ma, up_sb, gate_oa, mix_z, out_x
    )
    gate_mb, up_oa = first_sum(gate_kb, gate_gb), low_sum(up_ka, up_ga, up_ma)
    out_held = sum_pair(out_keep[:, :, :, 0], out_got[:, :, :, 0]) + out_x.astype(F32)
    out_z = out_held[:, 1].astype(BF)
    d_pack, gate_mb, up_oa, out_z = fence(d_pack, gate_mb, up_oa, out_z)
    gate_mb = swap_bit(gate_mb, ZH_BIT)
    up_gb = swap_bit(up_sb, Y_BIT)
    up_oa = swap_bit(up_oa, ZL_BIT)
    out_z = swap_bit(out_z, ZL_BIT)
    d_pack = run_trade(d_pack.reshape(shards, tokens, PACK), 5)
    d_pack, up_gb, gate_mb, down_sb, up_oa, out_z = fence(
        d_pack, up_gb, gate_mb, down_sb, up_oa, out_z
    )
    up_mb = swap_bit(first_sum(up_kb, up_gb), ZH_BIT)
    down_gb = swap_bit(down_sb, Y_BIT)
    gate_ob = swap_bit(low_sum(gate_kb, gate_gb, gate_mb), ZL_BIT)
    out_held = out_held[:, 0] + out_z.astype(F32)
    out_y = swap_bit(out_held[:, 1].astype(BF), Y_BIT)
    d_full, qkv_keep, qkv_send = run_qkvgrad(place, normed, d_pack, devices)
    grad_in, ggain_attn = run_last(
        d_full, w_query, w_key, w_value, d_middle, inputs, gain_attn
    )
    small_keep, small_send = run_small(place, normed_two, d_log, ggain_mlp, ggain_attn, devices)
    mixed = sum_pair(mix_keep[0, 0], mix_got[0, 0]) + sum_pair(mix_x[0], mix_z)
    hidden_out = middle + mixed
    qkv_send, small_send, up_mb, down_gb, gate_ob, out_y, hidden_out = fence(
        qkv_send, small_send, up_mb, down_gb, gate_ob, out_y, hidden_out
    )
    down_mb = swap_bit(first_sum(down_kb, down_gb), ZH_BIT)
    up_ob = swap_bit(low_sum(up_kb, up_gb, up_mb), ZL_BIT)
    out_held = out_held[:, 0] + out_y.astype(F32)
    out_h = swap_bit(out_held[1].astype(BF), ZH_BIT)
    rows = WIDTH // devices
    dense_parts = (
        (0, rows, 0, 768, (0, 1, 2, 3)),
        (0, rows, 768, 768, (1, 2, 0, 3)),
        (0, rows, 1536, 1024, (2, 0, 1, 3)),
    )
    qkv_total, small = run_reduce(
        ((qkv_keep, qkv_send), (small_keep, small_send)),
        (dense_parts, ((0, rows, 0, LANES, (0, 1, 2, 3)),)),
        (X_BIT, Y_BIT, ZL_BIT, ZH_BIT),
        7,
    )
    qkv_total, small, down_mb, up_ob, out_h = fence(qkv_total, small, down_mb, up_ob, out_h)
    output_total = sum_pair(out_held[0], out_h)
    down_total = run_join_down(((down_ka, down_ga, down_ma), (down_kb, down_gb, down_mb)))
    gate_total = run_join_tall(
        place, ((gate_ka, gate_ga, gate_ma, gate_oa), (gate_kb, gate_gb, gate_mb, gate_ob))
    )
    up_total = run_join_tall(
        place, ((up_ka, up_ga, up_ma, up_oa), (up_kb, up_gb, up_mb, up_ob))
    )
    key_width = KV_HEADS * HEAD_DIM
    return (
        hidden_out[None],
        grad_in[None],
        small[:, LANES - 1],
        qkv_total[:, :WIDTH],
        qkv_total[:, WIDTH : WIDTH + key_width],
        qkv_total[:, WIDTH + key_width :],
        output_total,
        small[:, LANES - 2],
        small[:, :all_experts],
        gate_total,
        up_total,
        down_total,
    )


def fits(mesh):
    return mesh.shape["dp"] == KV_HEADS and mesh.shape["expert"] == 4


def solution(mesh):
    in_specs = (
        P("expert", "dp", None),
        P(),
        P(),
        P(),
        P(),
        P(),
        P(),
        P(),
        P("expert", None, None),
        P("expert", None, None),
        P("expert", None, None),
        P("expert", "dp", None),
        P("expert", "dp", None),
        P("expert", "dp", None),
    )
    out_specs = (
        P("expert", "dp", None),
        P("expert", "dp", None),
        P(("dp", "expert")),
        P(("dp", "expert"), None),
        P(("dp", "expert"), None),
        P(("dp", "expert"), None),
        P(("dp", "expert"), None),
        P(("dp", "expert")),
        P(("dp", "expert"), None),
        P("expert", "dp", None),
        P("expert", "dp", None),
        P("expert", "dp", None),
    )
    chosen = fast_body if fits(mesh) else body
    return jax.shard_map(chosen, mesh=mesh, in_specs=in_specs, out_specs=out_specs, check_vma=False)
```

```python
import functools
import math

import jax
import jax.numpy as jnp
from jax import lax
from jax.experimental import pallas as pl
from jax.experimental.pallas import tpu as pltpu
from jax.sharding import PartitionSpec as P

HEADS = 24
KV_HEADS = 8
HEAD_DIM = 64


EPS = 1e-05
MASKED = -1e30


def rotary_tables(positions):
    half = HEAD_DIM // 2
    frequency = jnp.exp(-math.log(10000.0) * jnp.arange(half, dtype=jnp.float32) * 2.0 / HEAD_DIM)
    angles = positions.astype(jnp.float32)[:, None] * frequency[None, :]
    return (jnp.cos(angles)[:, None, :], jnp.sin(angles)[:, None, :])


def rotate(values, cosine, sine):
    half = values.shape[-1] // 2
    first = values[..., :half]
    second = values[..., half:]
    return jnp.concatenate(
        [first * cosine - second * sine, second * cosine + first * sine], axis=-1
    )


def rotate_back(values, cosine, sine):
    half = values.shape[-1] // 2
    first = values[..., :half]
    second = values[..., half:]
    return jnp.concatenate(
        [first * cosine + second * sine, second * cosine - first * sine], axis=-1
    )


def assign_slots(row_chosen, row_ranks, all_experts, capacity):
    pairs = row_chosen.shape[0]
    by_rank = jnp.zeros((pairs,), jnp.int32).at[row_ranks].set(jnp.arange(pairs, dtype=jnp.int32))
    ordered = row_chosen[by_rank]
    table = (ordered[:, None] == jnp.arange(all_experts, dtype=jnp.int32)[None, :]).astype(
        jnp.int32
    )
    before = jnp.sum(table * (jnp.cumsum(table, axis=0) - 1), axis=1)
    slot = before[row_ranks]
    target = jnp.where(slot < capacity, row_chosen * capacity + slot, all_experts * capacity)
    owner = (
        jnp.full((all_experts * capacity,), pairs, jnp.int32)
        .at[target]
        .set(jnp.arange(pairs, dtype=jnp.int32), mode="drop")
    )
    return (target, owner)


def body(
    hidden_in,
    gain_attn,
    w_query,
    w_key,
    w_value,
    w_output,
    gain_mlp,
    w_router,
    w_gate,
    w_up,
    w_down,
    expert_ids,
    slot_order,
    grad_out,
):
    inputs = hidden_in[0]
    cotangent = grad_out[0]
    chosen = expert_ids[0]
    tokens, width = inputs.shape
    top = chosen.shape[1]
    local_experts = w_gate.shape[0]
    peers = lax.axis_size("expert")
    all_experts = local_experts * peers
    pairs = tokens * top
    capacity = pairs // all_experts
    shards = lax.axis_size("dp")
    index = lax.axis_index("dp")
    length = shards * tokens
    block = math.gcd(length, 512)
    groups = HEADS // KV_HEADS
    scale = HEAD_DIM ** (-0.5)
    query_pos = index * tokens + jnp.arange(tokens, dtype=jnp.int32)
    cosine, sine = rotary_tables(query_pos)
    count = ((index + 1) * tokens + block - 1) // block
    inv_one = lax.rsqrt(jnp.mean(inputs * inputs, axis=-1, keepdims=True) + EPS)
    normed = (inputs * inv_one * gain_attn).astype(jnp.bfloat16)
    query_pre = jnp.dot(normed, w_query, preferred_element_type=jnp.float32).reshape(
        tokens, HEADS, HEAD_DIM
    )
    queries = rotate(query_pre, cosine, sine).astype(jnp.bfloat16)
    key_pre = jnp.dot(normed, w_key, preferred_element_type=jnp.float32).reshape(
        tokens, KV_HEADS, HEAD_DIM
    )
    keys_low = rotate(key_pre, cosine, sine).astype(jnp.bfloat16)
    values_low = (
        jnp.dot(normed, w_value, preferred_element_type=jnp.float32)
        .astype(jnp.bfloat16)
        .reshape(tokens, KV_HEADS, HEAD_DIM)
    )
    keys_all, values_all = (
        lax.all_gather(keys_low, "dp", axis=0, tiled=True),
        lax.all_gather(values_low, "dp", axis=0, tiled=True),
    )
    query_groups = queries.reshape(tokens, KV_HEADS, groups, HEAD_DIM)

    def block_scores(key_block, start):
        raw = (
            jnp.einsum(
                "qkgd,skd->kgqs", query_groups, key_block, preferred_element_type=jnp.float32
            )
            * scale
        )
        key_pos = start + jnp.arange(block, dtype=jnp.int32)
        allowed = key_pos[None, :] <= query_pos[:, None]
        return jnp.where(allowed, raw, MASKED)

    def stats_step(step, carry):
        running, total = carry
        scores = block_scores(
            lax.dynamic_slice_in_dim(keys_all, step * block, block, 0), step * block
        )
        newest = jnp.maximum(running, jnp.max(scores, axis=-1))
        total = total * jnp.exp(running - newest) + jnp.sum(
            jnp.exp(scores - newest[..., None]), axis=-1
        )
        return (newest, total)

    stat_init = (
        jnp.full((KV_HEADS, groups, tokens), MASKED, jnp.float32),
        jnp.zeros((KV_HEADS, groups, tokens), jnp.float32),
    )
    running, total = lax.fori_loop(0, count, stats_step, stat_init)
    log_total = running + jnp.log(total)

    def output_step(step, accum):
        start = step * block
        scores = block_scores(lax.dynamic_slice_in_dim(keys_all, start, block, 0), start)
        probs = jnp.exp(scores - log_total[..., None]).astype(jnp.bfloat16)
        value_block = lax.dynamic_slice_in_dim(values_all, start, block, 0)
        return accum + jnp.einsum(
            "kgqs,skd->qkgd", probs, value_block, preferred_element_type=jnp.float32
        )

    attended_groups = lax.fori_loop(
        0, count, output_step, jnp.zeros((tokens, KV_HEADS, groups, HEAD_DIM), jnp.float32)
    )
    attended = attended_groups.reshape(tokens, HEADS * HEAD_DIM)
    attended_low = attended.astype(jnp.bfloat16)
    branch = jnp.dot(attended_low, w_output, preferred_element_type=jnp.float32)
    middle = inputs + branch
    inv_two = lax.rsqrt(jnp.mean(middle * middle, axis=-1, keepdims=True) + EPS)
    normed_two = (middle * inv_two * gain_mlp).astype(jnp.bfloat16)
    logits = jnp.dot(normed_two, w_router, preferred_element_type=jnp.float32)
    onehot = (chosen[:, :, None] == jnp.arange(all_experts, dtype=jnp.int32)[None, None, :]).astype(
        jnp.float32
    )
    picked = jnp.sum(onehot * logits[:, None, :], axis=-1)
    gates = jax.nn.softmax(picked, axis=-1)
    target, owner = assign_slots(chosen.reshape(pairs), slot_order[0, 0], all_experts, capacity)
    valid = owner < pairs
    source = jnp.minimum(owner, pairs - 1)
    rows_send = jnp.where(valid[:, None], normed_two[source // top], 0).reshape(
        peers, local_experts, capacity, width
    )
    received = lax.all_to_all(rows_send, "expert", split_axis=0, concat_axis=0, tiled=True)
    gate_pre = jnp.einsum("necd,edf->necf", received, w_gate, preferred_element_type=jnp.float32)
    up_pre = jnp.einsum("necd,edf->necf", received, w_up, preferred_element_type=jnp.float32)
    hidden = (jax.nn.silu(gate_pre) * up_pre).astype(jnp.bfloat16)
    result = jnp.einsum(
        "necf,efd->necd", hidden, w_down, preferred_element_type=jnp.float32
    ).astype(jnp.bfloat16)
    returned = lax.all_to_all(result, "expert", split_axis=0, concat_axis=0, tiled=True)
    returned, received, gate_pre, up_pre = (returned, received, gate_pre, up_pre)
    zero_row = jnp.zeros((1, width), jnp.bfloat16)
    pair_out = jnp.concatenate([returned.reshape(all_experts * capacity, width), zero_row], axis=0)[
        target
    ].reshape(tokens, top, width)
    mixed = jnp.einsum("tk,tkd->td", gates, pair_out, preferred_element_type=jnp.float32)
    hidden_out = middle + mixed
    dy_pairs = (
        (gates[:, :, None] * cotangent[:, None, :]).astype(jnp.bfloat16).reshape(pairs, width)
    )
    dy_send = jnp.where(valid[:, None], dy_pairs[source], 0).reshape(
        peers, local_experts, capacity, width
    )
    dy_received = lax.all_to_all(dy_send, "expert", split_axis=0, concat_axis=0, tiled=True)
    sigmoid_gate = jax.nn.sigmoid(gate_pre)
    silu_gate = gate_pre * sigmoid_gate
    hidden = (silu_gate * up_pre).astype(jnp.bfloat16)
    grad_down_part = jnp.einsum(
        "necf,necd->efd", hidden, dy_received, preferred_element_type=jnp.float32
    )
    d_hidden = jnp.einsum("necd,efd->necf", dy_received, w_down, preferred_element_type=jnp.float32)
    d_gate = (d_hidden * up_pre * sigmoid_gate * (1.0 + gate_pre * (1.0 - sigmoid_gate))).astype(
        jnp.bfloat16
    )
    d_up = (d_hidden * silu_gate).astype(jnp.bfloat16)
    grad_gate_part = jnp.einsum(
        "necd,necf->edf", received, d_gate, preferred_element_type=jnp.float32
    )
    grad_up_part = jnp.einsum("necd,necf->edf", received, d_up, preferred_element_type=jnp.float32)
    gate_total, up_total, down_total = (
        lax.psum_scatter(
            grad_gate_part.astype(jnp.bfloat16), "dp", scatter_dimension=1, tiled=True
        ).astype(jnp.float32),
        lax.psum_scatter(
            grad_up_part.astype(jnp.bfloat16), "dp", scatter_dimension=1, tiled=True
        ).astype(jnp.float32),
        lax.psum_scatter(
            grad_down_part.astype(jnp.bfloat16), "dp", scatter_dimension=1, tiled=True
        ).astype(jnp.float32),
    )
    d_rows = jnp.einsum("necf,edf->necd", d_gate, w_gate, preferred_element_type=jnp.float32)
    d_rows = (
        d_rows + jnp.einsum("necf,edf->necd", d_up, w_up, preferred_element_type=jnp.float32)
    ).astype(jnp.bfloat16)
    d_back = lax.all_to_all(d_rows, "expert", split_axis=0, concat_axis=0, tiled=True)
    d_pairs = jnp.concatenate([d_back.reshape(all_experts * capacity, width), zero_row], axis=0)[
        target
    ].reshape(tokens, top, width)
    d_normed_two = jnp.sum(d_pairs, axis=1, dtype=jnp.float32)
    d_gates = jnp.einsum("td,tkd->tk", cotangent, pair_out, preferred_element_type=jnp.float32)
    d_picked = gates * (d_gates - jnp.sum(gates * d_gates, axis=-1, keepdims=True))
    d_logits = jnp.sum(onehot * d_picked[:, :, None], axis=1).astype(jnp.bfloat16)
    grad_router_part = jnp.einsum(
        "td,te->de", normed_two, d_logits, preferred_element_type=jnp.float32
    )
    d_normed_two = d_normed_two + jnp.einsum(
        "te,de->td", d_logits, w_router, preferred_element_type=jnp.float32
    )
    scaled_two = d_normed_two * gain_mlp
    grad_gain_mlp_part = jnp.sum(d_normed_two * middle * inv_two, axis=0)
    d_middle = (
        cotangent
        + inv_two * scaled_two
        - middle * inv_two**3 * jnp.mean(middle * scaled_two, axis=-1, keepdims=True)
    )
    d_branch = d_middle.astype(jnp.bfloat16)
    grad_output_part = jnp.einsum(
        "tf,td->fd", attended_low, d_branch, preferred_element_type=jnp.float32
    )
    d_attended = jnp.einsum(
        "td,fd->tf", d_branch, w_output, preferred_element_type=jnp.float32
    ).astype(jnp.bfloat16)
    d_groups = d_attended.reshape(tokens, KV_HEADS, groups, HEAD_DIM)
    delta = jnp.einsum(
        "qkgd,qkgd->kgq", d_groups, attended_groups, preferred_element_type=jnp.float32
    )
    keys_back, values_back = (
        lax.all_gather(keys_low, "dp", axis=0, tiled=True),
        lax.all_gather(values_low, "dp", axis=0, tiled=True),
    )

    def grad_step(step, carry):
        d_query, d_keys, d_values = carry
        start = step * block
        key_block = lax.dynamic_slice_in_dim(keys_back, start, block, 0)
        value_block = lax.dynamic_slice_in_dim(values_back, start, block, 0)
        scores = block_scores(key_block, start)
        probs = jnp.exp(scores - log_total[..., None])
        probs_low = probs.astype(jnp.bfloat16)
        d_probs = jnp.einsum(
            "qkgd,skd->kgqs", d_groups, value_block, preferred_element_type=jnp.float32
        )
        d_scores = (probs * (d_probs - delta[..., None])).astype(jnp.bfloat16)
        d_query = d_query + jnp.einsum(
            "kgqs,skd->qkgd", d_scores, key_block, preferred_element_type=jnp.float32
        )
        key_part = jnp.einsum(
            "kgqs,qkgd->skd", d_scores, query_groups, preferred_element_type=jnp.float32
        )
        value_part = jnp.einsum(
            "kgqs,qkgd->skd", probs_low, d_groups, preferred_element_type=jnp.float32
        )
        d_keys = lax.dynamic_update_slice_in_dim(
            d_keys, lax.dynamic_slice_in_dim(d_keys, start, block, 0) + key_part, start, 0
        )
        d_values = lax.dynamic_update_slice_in_dim(
            d_values, lax.dynamic_slice_in_dim(d_values, start, block, 0) + value_part, start, 0
        )
        return (d_query, d_keys, d_values)

    grad_init = (
        jnp.zeros((tokens, KV_HEADS, groups, HEAD_DIM), jnp.float32),
        jnp.zeros((length, KV_HEADS, HEAD_DIM), jnp.float32),
        jnp.zeros((length, KV_HEADS, HEAD_DIM), jnp.float32),
    )
    d_query, d_keys, d_values = lax.fori_loop(0, count, grad_step, grad_init)
    key_sum, value_sum = (
        lax.psum_scatter(
            (d_keys * scale).reshape(length, KV_HEADS * HEAD_DIM).astype(jnp.bfloat16),
            "dp",
            scatter_dimension=0,
            tiled=True,
        ).astype(jnp.float32),
        lax.psum_scatter(
            d_values.reshape(length, KV_HEADS * HEAD_DIM).astype(jnp.bfloat16),
            "dp",
            scatter_dimension=0,
            tiled=True,
        ).astype(jnp.float32),
    )
    d_query_low = (
        rotate_back((d_query * scale).reshape(tokens, HEADS, HEAD_DIM), cosine, sine)
        .astype(jnp.bfloat16)
        .reshape(tokens, HEADS * HEAD_DIM)
    )
    d_key_low = (
        rotate_back(key_sum.reshape(tokens, KV_HEADS, HEAD_DIM), cosine, sine)
        .astype(jnp.bfloat16)
        .reshape(tokens, KV_HEADS * HEAD_DIM)
    )
    d_value_low = value_sum.astype(jnp.bfloat16)
    grad_query_part = jnp.einsum(
        "td,tf->df", normed, d_query_low, preferred_element_type=jnp.float32
    )
    grad_key_part = jnp.einsum("td,tf->df", normed, d_key_low, preferred_element_type=jnp.float32)
    grad_value_part = jnp.einsum(
        "td,tf->df", normed, d_value_low, preferred_element_type=jnp.float32
    )
    d_normed = jnp.einsum("tf,df->td", d_query_low, w_query, preferred_element_type=jnp.float32)
    d_normed = d_normed + jnp.einsum(
        "tf,df->td", d_key_low, w_key, preferred_element_type=jnp.float32
    )
    d_normed = d_normed + jnp.einsum(
        "tf,df->td", d_value_low, w_value, preferred_element_type=jnp.float32
    )
    scaled_one = d_normed * gain_attn
    grad_gain_attn_part = jnp.sum(d_normed * inputs * inv_one, axis=0)
    grad_in = (
        d_middle
        + inv_one * scaled_one
        - inputs * inv_one**3 * jnp.mean(inputs * scaled_one, axis=-1, keepdims=True)
    )
    dense = (
        lax.psum_scatter(grad_gain_attn_part, ("dp", "expert"), scatter_dimension=0, tiled=True),
        lax.psum_scatter(grad_query_part, ("dp", "expert"), scatter_dimension=0, tiled=True),
        lax.psum_scatter(grad_key_part, ("dp", "expert"), scatter_dimension=0, tiled=True),
        lax.psum_scatter(grad_value_part, ("dp", "expert"), scatter_dimension=0, tiled=True),
        lax.psum_scatter(grad_output_part, ("dp", "expert"), scatter_dimension=0, tiled=True),
        lax.psum_scatter(grad_gain_mlp_part, ("dp", "expert"), scatter_dimension=0, tiled=True),
        lax.psum_scatter(grad_router_part, ("dp", "expert"), scatter_dimension=0, tiled=True),
    )
    return (
        hidden_out[None],
        grad_in[None],
        dense[0],
        dense[1],
        dense[2],
        dense[3],
        dense[4],
        dense[5],
        dense[6],
        gate_total,
        up_total,
        down_total,
    )

BF = jnp.bfloat16
F32 = jnp.float32
WIDTH = 1536
LANES = 128
PER_KV = HEADS // KV_HEADS
ROWS_Q = PER_KV * HEAD_DIM
PACK = ROWS_Q + 2 * HEAD_DIM
BIT_Y, BIT_ZL, BIT_ZH = 1, 2, 4
BIT_C, BIT_X = 1, 2
BLOCK_Q = 256
BLOCK_K = 512
SLOTS = 64
CHUNK = 512
MIB = 1 << 20


def dot_nn(a, b):
    return lax.dot_general(a, b, (((1,), (0,)), ((), ())), preferred_element_type=F32)


def dot_nt(a, b):
    return lax.dot_general(a, b, (((1,), (1,)), ((), ())), preferred_element_type=F32)


def dot_tn(a, b):
    return lax.dot_general(a, b, (((0,), (0,)), ((), ())), preferred_element_type=F32)


def cost(flops, moved, transcendentals=0):
    return pl.CostEstimate(
        flops=int(flops), bytes_accessed=int(moved), transcendentals=int(transcendentals)
    )


def params(mib, dims=None):
    return pltpu.CompilerParams(vmem_limit_bytes=mib * MIB, dimension_semantics=dims)


def swap(values, axis, mask):
    size = lax.axis_size(axis)
    return lax.ppermute(values, axis, [(i, i ^ mask) for i in range(size)])


def swap_bit(values, bit):
    axis, mask = bit
    return swap(values, axis, mask)


def fence(*values):
    return lax.optimization_barrier(values)


C_BIT = ("expert", BIT_C)
X_BIT = ("expert", BIT_X)
Y_BIT = ("dp", BIT_Y)
ZL_BIT = ("dp", BIT_ZL)
ZH_BIT = ("dp", BIT_ZH)


def pre_kernel(
    hid_ref,
    gain_ref,
    wq_ref,
    wk_ref,
    wv_ref,
    cos_ref,
    sin_ref,
    cot_ref,
    norm_ref,
    pack_ref,
    low_ref,
):
    tokens = hid_ref.shape[0]
    half = tokens // 2
    low_ref[...] = cot_ref[...].astype(BF)
    inputs = hid_ref[...]
    inv = lax.rsqrt(jnp.mean(inputs * inputs, axis=-1, keepdims=True) + EPS)
    normed = (inputs * inv * gain_ref[...]).astype(BF)
    norm_ref[...] = normed
    low = (lax.broadcasted_iota(jnp.int32, (tokens, LANES), 1) % HEAD_DIM) < HEAD_DIM // 2
    cosine, sine = cos_ref[...], sin_ref[...]

    def turn(tile):
        other = jnp.where(
            low,
            pltpu.roll(tile, LANES - HEAD_DIM // 2, 1),
            pltpu.roll(tile, HEAD_DIM // 2, 1),
        )
        return (tile * cosine + other * sine).astype(BF)

    tiles = []
    for n in range(wq_ref.shape[1] // CHUNK):
        pre = dot_nn(normed, wq_ref[:, n * CHUNK : (n + 1) * CHUNK])
        tiles += [turn(pre[:, m * LANES : (m + 1) * LANES]) for m in range(CHUNK // LANES)]
    queries = jnp.concatenate(tiles, axis=1)
    pre = dot_nn(normed, wk_ref[...])
    keys = jnp.concatenate(
        [turn(pre[:, m * LANES : (m + 1) * LANES]) for m in range(pre.shape[1] // LANES)], axis=1
    )
    values = dot_nn(normed, wv_ref[...]).astype(BF)
    for g in range(KV_HEADS):
        at = g * ROWS_Q
        head = slice(g * HEAD_DIM, (g + 1) * HEAD_DIM)
        pack_ref[g, 0:tokens] = queries[:, at : at + LANES]
        pack_ref[g, tokens : 2 * tokens] = jnp.concatenate(
            [queries[:, at + LANES : at + ROWS_Q], keys[:, head]], axis=1
        )
        pack_ref[g, 2 * tokens :] = jnp.concatenate(
            [values[:half, head], values[half:, head]], axis=1
        )


def run_pre(inputs, gain, w_query, w_key, w_value, cos_tab, sin_tab, cotangent):
    tokens = inputs.shape[0]
    return pl.pallas_call(
        pre_kernel,
        out_shape=(
            jax.ShapeDtypeStruct((tokens, WIDTH), BF),
            jax.ShapeDtypeStruct((KV_HEADS, tokens * PACK // LANES, LANES), BF),
            jax.ShapeDtypeStruct((tokens, WIDTH), BF),
        ),
        compiler_params=params(60),
        cost_estimate=cost(2 * tokens * WIDTH * 2560, 14e6),
    )(inputs, gain[None], w_query, w_key, w_value, cos_tab, sin_tab, cotangent)


def unpack_heads(block_ref, out_ref, row, tokens, column):
    half = tokens // 2
    out_ref[row : row + tokens, column : column + LANES] = block_ref[0:tokens]
    rest = block_ref[tokens : tokens + half]
    out_ref[row : row + half, column + LANES : column + ROWS_Q] = rest[:, :HEAD_DIM]
    out_ref[row + half : row + tokens, column + LANES : column + ROWS_Q] = rest[:, HEAD_DIM:]


def pack_heads(block_ref, rows, tokens):
    half = tokens // 2
    block_ref[0:tokens] = rows[:, 0:LANES]
    block_ref[tokens : tokens + half] = jnp.concatenate(
        [rows[:half, LANES:ROWS_Q], rows[half:, LANES:ROWS_Q]], axis=1
    )


def unpack_all(block_ref, q_ref, k_ref, v_ref, row, tokens, q_at=0, k_at=0, v_at=0):
    half = tokens // 2
    rows = slice(row, row + tokens)
    q_ref[rows, q_at : q_at + LANES] = block_ref[0:tokens]
    two = block_ref[tokens : 2 * tokens]
    q_ref[rows, q_at + LANES : q_at + ROWS_Q] = two[:, :HEAD_DIM]
    k_ref[rows, k_at : k_at + HEAD_DIM] = two[:, HEAD_DIM:]
    rest = block_ref[2 * tokens : 2 * tokens + half]
    v_ref[row : row + half, v_at : v_at + HEAD_DIM] = rest[:, :HEAD_DIM]
    v_ref[row + half : row + tokens, v_at : v_at + HEAD_DIM] = rest[:, HEAD_DIM:]


def heads_t(block, width):
    return jnp.concatenate(
        [block[:, h * HEAD_DIM : (h + 1) * HEAD_DIM].astype(F32).T for h in range(width)], axis=1
    )


def heads_rows(block, width):
    return jnp.concatenate(
        [block[:, h * HEAD_DIM : (h + 1) * HEAD_DIM] for h in range(width)], axis=0
    )


def allowed_t(step, block):
    shape = (BLOCK_K, PER_KV * BLOCK_Q)
    key_pos = step * BLOCK_K + lax.broadcasted_iota(jnp.int32, shape, 0)
    query_pos = block * BLOCK_Q + lax.broadcasted_iota(jnp.int32, shape, 1) % BLOCK_Q
    return key_pos <= query_pos


def forward_kernel(pack_ref, out_ref, out_t_ref, lse_ref, q_s, k_s, v_s, vt_s, out_s):
    block = pl.program_id(0)
    sources = pack_ref.shape[0]
    tokens = q_s.shape[0] // sources

    @pl.when(block == 0)
    def _():
        for n in range(sources):
            unpack_all(pack_ref.at[n], q_s, k_s, v_s, n * tokens, tokens)
        vt_s[...] = v_s[...].astype(F32).T.astype(BF)

    rows = pl.ds(pl.multiple_of(block * BLOCK_Q, BLOCK_Q), BLOCK_Q)
    scale = HEAD_DIM ** (-0.5)
    q_t = (heads_t(q_s[rows, :], PER_KV) * scale).astype(BF)
    columns = PER_KV * BLOCK_Q

    def step(j, carry, masked):
        running, total, accum = carry
        keys = pl.ds(pl.multiple_of(j * BLOCK_K, BLOCK_K), BLOCK_K)
        scores = dot_nn(k_s[keys, :], q_t)
        if masked:
            scores = jnp.where(allowed_t(j, block), scores, MASKED)
        newest = jnp.maximum(running, jnp.max(scores, axis=0, keepdims=True))
        fade = jnp.exp(running - newest)
        probs = jnp.exp(scores - newest)
        total = total * fade + jnp.sum(probs, axis=0, keepdims=True)
        accum = accum * fade + dot_nn(vt_s[:, keys], probs.astype(BF))
        return newest, total, accum

    carry = (
        jnp.full((1, columns), MASKED, F32),
        jnp.zeros((1, columns), F32),
        jnp.zeros((HEAD_DIM, columns), F32),
    )
    last = (block * BLOCK_Q) // BLOCK_K
    carry = lax.fori_loop(0, last, lambda j, c: step(j, c, False), carry)
    running, total, accum = step(last, carry, True)
    out_t = accum / total
    out_t_ref[0] = out_t
    lse_ref[0] = running + jnp.log(total)
    out_s[rows, :] = jnp.concatenate(
        [out_t[:, h * BLOCK_Q : (h + 1) * BLOCK_Q].T for h in range(PER_KV)], axis=1
    ).astype(BF)

    @pl.when(block == pl.num_programs(0) - 1)
    def _():
        for n in range(sources):
            pack_heads(out_ref.at[n], out_s[n * tokens : (n + 1) * tokens, :], tokens)


def run_forward(pack):
    sources = pack.shape[0]
    length = sources * (pack.shape[1] * LANES // PACK)
    packed = (sources, length // sources * ROWS_Q // LANES, LANES)
    blocks = length // BLOCK_Q
    columns = PER_KV * BLOCK_Q
    return pl.pallas_call(
        forward_kernel,
        grid=(blocks,),
        in_specs=[pl.BlockSpec(pack.shape, lambda i: (0, 0, 0))],
        out_specs=(
            pl.BlockSpec(packed, lambda i: (0, 0, 0)),
            pl.BlockSpec((1, HEAD_DIM, columns), lambda i: (i, 0, 0)),
            pl.BlockSpec((1, 1, columns), lambda i: (i, 0, 0)),
        ),
        out_shape=(
            jax.ShapeDtypeStruct(packed, BF),
            jax.ShapeDtypeStruct((blocks, HEAD_DIM, columns), F32),
            jax.ShapeDtypeStruct((blocks, 1, columns), F32),
        ),
        scratch_shapes=[
            pltpu.VMEM((length, ROWS_Q), BF),
            pltpu.VMEM((length, HEAD_DIM), BF),
            pltpu.VMEM((length, HEAD_DIM), BF),
            pltpu.VMEM((HEAD_DIM, length), BF),
            pltpu.VMEM((length, ROWS_Q), BF),
        ],
        compiler_params=params(60, ("arbitrary",)),
        cost_estimate=cost(8 * length * length * ROWS_Q, 6e6, length * length * PER_KV),
    )(pack)


def backward_kernel(
    pack_ref,
    grad_ref,
    out_t_ref,
    lse_ref,
    cos_ref,
    sin_ref,
    res_ref,
    q_s,
    do_s,
    k_s,
    v_s,
    kt_s,
    dk_s,
    dv_s,
):
    block = pl.program_id(0)
    sources = pack_ref.shape[0]
    tokens = q_s.shape[0] // sources

    @pl.when(block == 0)
    def _():
        for n in range(sources):
            unpack_all(pack_ref.at[n], q_s, k_s, v_s, n * tokens, tokens)
            unpack_heads(grad_ref.at[n], do_s, n * tokens, tokens, 0)
        kt_s[...] = k_s[...].astype(F32).T.astype(BF)
        dk_s[...] = jnp.zeros_like(dk_s)
        dv_s[...] = jnp.zeros_like(dv_s)

    scale = HEAD_DIM ** (-0.5)
    half = HEAD_DIM // 2
    rows = pl.ds(pl.multiple_of(block * BLOCK_Q, BLOCK_Q), BLOCK_Q)
    q_block = q_s[rows, :]
    q_t = (heads_t(q_block, PER_KV) * scale).astype(BF)
    q_rows = (heads_rows(q_block, PER_KV).astype(F32) * scale).astype(BF)
    do_block = do_s[rows, :]
    do_f32 = heads_t(do_block, PER_KV)
    do_t = do_f32.astype(BF)
    do_rows = heads_rows(do_block, PER_KV)
    delta = jnp.sum(do_f32 * out_t_ref[0], axis=0, keepdims=True)
    lse = lse_ref[0]

    def step(j, dq_t, masked):
        keys = pl.ds(pl.multiple_of(j * BLOCK_K, BLOCK_K), BLOCK_K)
        scores = dot_nn(k_s[keys, :], q_t)
        if masked:
            scores = jnp.where(allowed_t(j, block), scores, MASKED)
        probs = jnp.exp(scores - lse)
        d_probs = dot_nn(v_s[keys, :], do_t)
        d_scores = (probs * (d_probs - delta)).astype(BF)
        dv_s[keys, :] += dot_nn(probs.astype(BF), do_rows)
        dk_s[keys, :] += dot_nn(d_scores, q_rows)
        return dq_t + dot_nn(kt_s[:, keys], d_scores)

    last = (block * BLOCK_Q) // BLOCK_K
    dq_t = jnp.zeros((HEAD_DIM, PER_KV * BLOCK_Q), F32)
    dq_t = lax.fori_loop(0, last, lambda j, c: step(j, c, False), dq_t)
    dq_t = step(last, dq_t, True) * scale

    def turn_back(values, cosine, sine):
        first, second = values[:half], values[half:]
        return jnp.concatenate(
            [first * cosine + second * sine, second * cosine - first * sine], axis=0
        )

    columns = pl.ds(pl.multiple_of(block * BLOCK_Q, BLOCK_Q), BLOCK_Q)
    cosine, sine = cos_ref[:, columns], sin_ref[:, columns]
    q_s[rows, :] = jnp.concatenate(
        [
            turn_back(dq_t[:, h * BLOCK_Q : (h + 1) * BLOCK_Q], cosine, sine).T
            for h in range(PER_KV)
        ],
        axis=1,
    ).astype(BF)

    @pl.when(block == pl.num_programs(0) - 1)
    def _():
        dk = turn_back(dk_s[...].T, cos_ref[...], sin_ref[...]).T.astype(BF)
        half = tokens // 2
        for n in range(sources):
            row = n * tokens
            res_ref[n, 0:tokens] = q_s[row : row + tokens, 0:LANES]
            res_ref[n, tokens : 2 * tokens] = jnp.concatenate(
                [q_s[row : row + tokens, LANES:ROWS_Q], dk[row : row + tokens]], axis=1
            )
            res_ref[n, 2 * tokens :] = jnp.concatenate(
                [dv_s[row : row + half, :], dv_s[row + half : row + tokens, :]], axis=1
            ).astype(BF)


def run_backward(pack, grad, out_t, lse, cos_t, sin_t):
    length = cos_t.shape[1]
    blocks = length // BLOCK_Q
    columns = PER_KV * BLOCK_Q
    half = HEAD_DIM // 2
    return pl.pallas_call(
        backward_kernel,
        grid=(blocks,),
        in_specs=[
            pl.BlockSpec(pack.shape, lambda i: (0, 0, 0)),
            pl.BlockSpec(grad.shape, lambda i: (0, 0, 0)),
            pl.BlockSpec((1, HEAD_DIM, columns), lambda i: (i, 0, 0)),
            pl.BlockSpec((1, 1, columns), lambda i: (i, 0, 0)),
            pl.BlockSpec((half, length), lambda i: (0, 0)),
            pl.BlockSpec((half, length), lambda i: (0, 0)),
        ],
        out_specs=pl.BlockSpec(pack.shape, lambda i: (0, 0, 0)),
        out_shape=jax.ShapeDtypeStruct(pack.shape, BF),
        scratch_shapes=[
            pltpu.VMEM((length, ROWS_Q), BF),
            pltpu.VMEM((length, ROWS_Q), BF),
            pltpu.VMEM((length, HEAD_DIM), BF),
            pltpu.VMEM((length, HEAD_DIM), BF),
            pltpu.VMEM((HEAD_DIM, length), BF),
            pltpu.VMEM((length, HEAD_DIM), F32),
            pltpu.VMEM((length, HEAD_DIM), F32),
        ],
        compiler_params=params(60, ("arbitrary",)),
        cost_estimate=cost(20 * length * length * ROWS_Q, 8e6, length * length * PER_KV),
    )(pack, grad, out_t, lse, cos_t, sin_t)


def mid_kernel(att_ref, wo_ref, hid_ref, gain_ref, mid_ref, norm_ref, full_ref):
    for g in range(KV_HEADS):
        unpack_heads(att_ref.at[g], full_ref, 0, full_ref.shape[0], g * ROWS_Q)
    middle = hid_ref[...] + dot_nn(full_ref[...], wo_ref[...])
    mid_ref[...] = middle
    inv = lax.rsqrt(jnp.mean(middle * middle, axis=-1, keepdims=True) + EPS)
    norm_ref[...] = (middle * inv * gain_ref[...]).astype(BF)


def run_mid(att, w_output, inputs, gain):
    tokens = inputs.shape[0]
    return pl.pallas_call(
        mid_kernel,
        out_shape=(
            jax.ShapeDtypeStruct((tokens, WIDTH), F32),
            jax.ShapeDtypeStruct((tokens, WIDTH), BF),
            jax.ShapeDtypeStruct((tokens, WIDTH), BF),
        ),
        compiler_params=params(60),
        cost_estimate=cost(2 * tokens * WIDTH * WIDTH, 12e6),
    )(att, w_output, inputs, gain[None])


def expert_kernel(
    place_ref,
    x_ref,
    g_ref,
    map_ref,
    wr_ref,
    wg0_ref,
    wg1_ref,
    wu0_ref,
    wu1_ref,
    wd0_ref,
    wd1_ref,
    *refs,
    first,
):
    if first:
        mix_prior = dx_prior = None
    else:
        mix_prior, dx_prior = refs[0:2], refs[2:4]
        refs = refs[4:]
    (
    mix_keep,
    mix_send,
    dx_keep,
    dx_send,
    gate_keep,
    gate_send0,
    gate_send1,
    up_keep,
    up_send0,
    up_send1,
    down_keep,
    down_send0,
    down_send1,
    xs,
    gs,
    gate_s,
    wide_s,
    tall_s,
    ) = refs
    step = pl.program_id(0)
    sources = map_ref.shape[0]
    experts = xs.shape[0]
    low = 0 if first else experts
    tokens = x_ref.shape[1]
    rows = experts * SLOTS
    count = WIDTH // CHUNK

    def one_hot(source):
        slots = map_ref[source, low : low + experts, :]
        wide = jnp.broadcast_to(slots[:, None, :], (experts, SLOTS, tokens))
        rank = lax.broadcasted_iota(jnp.int32, (experts, SLOTS, tokens), 1).astype(F32)
        return (wide == rank).astype(F32).reshape(rows, tokens)

    @pl.when(step < sources)
    def _():
        slot_map = map_ref[step]
        chosen = slot_map >= 0.0
        logits = dot_nt(wr_ref[...], x_ref[0])[0 : slot_map.shape[0]]
        logits = jnp.where(chosen, logits, MASKED)
        raised = jnp.exp(logits - jnp.max(logits, axis=0, keepdims=True))
        raised = jnp.where(chosen, raised, 0.0)
        gates = raised / jnp.sum(raised, axis=0, keepdims=True)
        pick = one_hot(step)
        wide = jnp.broadcast_to(gates[low : low + experts, None, :], (experts, SLOTS, tokens))
        gate_rows = jnp.sum(pick * wide.reshape(rows, tokens), axis=1, keepdims=True)
        pick = pick.astype(BF)
        here = pl.ds(pl.multiple_of(step * SLOTS, SLOTS), SLOTS)
        for e in range(experts):
            gate_s[e, here, :] = gate_rows[e * SLOTS : (e + 1) * SLOTS]
        for n in range(count):
            cols = slice(n * CHUNK, (n + 1) * CHUNK)
            got = dot_nn(pick, x_ref[0, :, cols]).astype(BF)
            xs[:, here, cols] = got.reshape(experts, SLOTS, CHUNK)
            got = dot_nn(pick, g_ref[0, :, cols]).astype(BF)
            gs[:, here, cols] = got.reshape(experts, SLOTS, CHUNK)

    @pl.when((step >= sources) & (step < sources + experts))
    def _():
        e = step - sources
        x = xs[e]
        w_gate = jnp.concatenate([wg0_ref[0], wg1_ref[0]], axis=1)
        w_up = jnp.concatenate([wu0_ref[0], wu1_ref[0]], axis=1)
        gate_pre = dot_nn(x, w_gate)
        up_pre = dot_nn(x, w_up)
        sig = jax.nn.sigmoid(gate_pre)
        silu = gate_pre * sig
        hidden = (silu * up_pre).astype(BF)
        gate = gate_s[e]
        d_hidden = jnp.zeros(hidden.shape, F32)
        d_gates = jnp.zeros(gate.shape, F32)
        for n in range(count):
            cols = slice(n * CHUNK, (n + 1) * CHUNK)
            w_down = jnp.concatenate([wd0_ref[0, :, cols], wd1_ref[0, :, cols]], axis=0)
            grad = gs[e, :, cols].astype(F32)
            d_y = (gate * grad).astype(BF)
            y = dot_nn(hidden, w_down)
            d_gates += jnp.sum(y * grad, axis=1, keepdims=True)
            gs[e, :, cols] = (gate * y).astype(BF)
            d_hidden += dot_nt(d_y, w_down)
            wide_s[:, cols] = dot_tn(hidden, d_y).astype(BF)
        gate_s[e] = d_gates
        d_gate = (d_hidden * up_pre * sig * (1.0 + gate_pre * (1.0 - sig))).astype(BF)
        d_up = (d_hidden * silu).astype(BF)

        y_at, zl_at, zh_at = place_ref[1], place_ref[2], place_ref[3]
        part = down_keep.shape[2]
        for z in range(2):
            base = (zh_at ^ z) * 2
            down_keep[z, 0] = wide_s[pl.ds(pl.multiple_of((base + y_at) * part, part), part), :]
            (down_send0, down_send1)[z][0] = wide_s[
                pl.ds(pl.multiple_of((base + (1 - y_at)) * part, part), part), :
            ]

        def spread(keep, send):
            part = keep.shape[3]
            for z in range(2):
                for low in range(2):
                    base = ((zh_at ^ z) * 2 + (zl_at ^ low)) * 2
                    keep[z, low, 0] = tall_s[
                        pl.ds(pl.multiple_of((base + y_at) * part, part), part), :
                    ]
                    send[z][low, 0] = tall_s[
                        pl.ds(pl.multiple_of((base + (1 - y_at)) * part, part), part), :
                    ]

        for n in range(count):
            cols = slice(n * CHUNK, (n + 1) * CHUNK)
            tall_s[cols, :] = dot_tn(x[:, cols], d_gate).astype(BF)
        spread(gate_keep, (gate_send0, gate_send1))
        for n in range(count):
            cols = slice(n * CHUNK, (n + 1) * CHUNK)
            tall_s[cols, :] = dot_tn(x[:, cols], d_up).astype(BF)
        spread(up_keep, (up_send0, up_send1))
        for n in range(count):
            cols = slice(n * CHUNK, (n + 1) * CHUNK)
            d_x = dot_nt(d_gate, w_gate[cols]) + dot_nt(d_up, w_up[cols])
            xs[e, :, cols] = d_x.astype(BF)

    def combine(source, mix_out, dx_out, mix_in, dx_in):
        def put(out, prior, cols, values):
            if prior is not None:
                values += prior[0, :, cols].astype(F32)
            out[0, :, cols] = values.astype(BF)

        here = pl.ds(pl.multiple_of(source * SLOTS, SLOTS), SLOTS)
        pick = one_hot(source).astype(BF)
        for n in range(count):
            cols = slice(n * CHUNK, (n + 1) * CHUNK)
            put(dx_out, dx_in, cols, dot_tn(pick, xs[:, here, cols].reshape(rows, CHUNK)))
            put(mix_out, mix_in, cols, dot_tn(pick, gs[:, here, cols].reshape(rows, CHUNK)))
        values = gate_s[:, here, :].reshape(rows, 1)
        column = lax.broadcasted_iota(jnp.int32, (rows, LANES), 1)
        owner = lax.broadcasted_iota(jnp.int32, (rows, LANES), 0) // SLOTS
        spread_out = jnp.where(column == owner + (place_ref[4] + low), values, 0.0).astype(BF)
        put(dx_out, dx_in, slice(WIDTH, WIDTH + LANES), dot_tn(pick, spread_out))

    @pl.when((step >= sources + experts) & (step < sources + experts + sources // 2))
    def _():
        source = step - experts - sources // 2
        prior = (None, None) if first else (mix_prior[1], dx_prior[1])
        combine(source, mix_send, dx_send, *prior)

    @pl.when(step >= sources + experts + sources // 2)
    def _():
        source = step - experts - sources - sources // 2
        prior = (None, None) if first else (mix_prior[0], dx_prior[0])
        combine(source, mix_keep, dx_keep, *prior)


def less(shape):
    return jax.ShapeDtypeStruct(shape.shape[1:], shape.dtype)


def run_experts(place, x_all, g_all, maps, wr_t, w_gate, w_up, w_down, prior=()):
    sources, tokens, width = x_all.shape
    experts = w_gate.shape[0] // 2
    low = experts if prior else 0
    ffe = w_gate.shape[2]
    part = ffe // 8
    quarter = width // 8
    half = ffe // 2
    slots = sources * SLOTS
    extra = width + LANES
    second = sources + experts
    third = second + sources // 2

    def at(i, low, size):
        return jnp.clip(i - low, 0, size - 1)

    def expert_of(i):
        return at(i, sources, experts)

    def w_cols(block):
        return pl.BlockSpec(
            (1, width, LANES), lambda i, p: (expert_of(i) + low, 0, p[0] + 2 * block)
        )

    def w_rows(block):
        return pl.BlockSpec(
            (1, LANES, width), lambda i, p: (expert_of(i) + low, p[0] + 2 * block, 0)
        )

    token_spec = pl.BlockSpec(
        (1, tokens, width),
        lambda i, p: (at(i, 0, sources), 0, 0),
    )

    def out_tokens(low, cols):
        return pl.BlockSpec((1, tokens, cols), lambda i, p: (at(i, low, sources // 2), 0, 0))

    tall_spec = pl.BlockSpec(
        (2, 2, 1, quarter, half), lambda i, p: (0, 0, expert_of(i), 0, 0)
    )
    wide_spec = pl.BlockSpec((2, 1, part, width), lambda i, p: (0, expert_of(i), 0, 0))
    tall_half = pl.BlockSpec((2, 1, quarter, half), lambda i, p: (0, expert_of(i), 0, 0))
    wide_half = pl.BlockSpec((1, part, width), lambda i, p: (expert_of(i), 0, 0))
    tall = jax.ShapeDtypeStruct((2, 2, experts, quarter, half), BF)
    wide = jax.ShapeDtypeStruct((2, experts, part, width), BF)
    mixed = jax.ShapeDtypeStruct((sources // 2, tokens, width), BF)
    d_x = jax.ShapeDtypeStruct((sources // 2, tokens, extra), BF)
    sums = (
        out_tokens(third, width),
        out_tokens(second, width),
        out_tokens(third, extra),
        out_tokens(second, extra),
    )
    return pl.pallas_call(
        functools.partial(expert_kernel, first=not prior),
        grid_spec=pltpu.PrefetchScalarGridSpec(
            num_scalar_prefetch=1,
            grid=(third + sources // 2,),
            in_specs=[
                token_spec,
                token_spec,
                pl.BlockSpec(maps.shape, lambda i, p: (0, 0, 0)),
                pl.BlockSpec(wr_t.shape, lambda i, p: (0, 0)),
                w_cols(0),
                w_cols(1),
                w_cols(0),
                w_cols(1),
                w_rows(0),
                w_rows(1),
                *(sums if prior else ()),
            ],
            out_specs=(
                *sums,
                tall_spec,
                tall_half,
                tall_half,
                tall_spec,
                tall_half,
                tall_half,
                wide_spec,
                wide_half,
                wide_half,
            ),
            scratch_shapes=[
                pltpu.VMEM((experts, slots, width), BF),
                pltpu.VMEM((experts, slots, width), BF),
                pltpu.VMEM((experts, slots, 1), F32),
                pltpu.VMEM((half, width), BF),
                pltpu.VMEM((width, half), BF),
            ],
        ),
        out_shape=(mixed, mixed, d_x, d_x)
        + (tall, less(tall), less(tall)) * 2
        + (wide, less(wide), less(wide)),
        compiler_params=params(60, ("arbitrary",)),
        cost_estimate=cost(30e9, 60e6),
    )(place, x_all, g_all, maps, wr_t, w_gate, w_gate, w_up, w_up, w_down, w_down, *prior)


def post_kernel(
    dx_ref,
    mid_ref,
    cot_ref,
    norm_ref,
    wr_ref,
    map_ref,
    gain_ref,
    wo_ref,
    datt_ref,
    dmid_ref,
    dlow_ref,
    dlog_ref,
    ggain_ref,
):
    middle = mid_ref[...]
    inv = lax.rsqrt(jnp.mean(middle * middle, axis=-1, keepdims=True) + EPS)
    chosen = map_ref[...] >= 0.0
    logits = jnp.where(chosen, dot_nn(norm_ref[...], wr_ref[...]), MASKED)
    raised = jnp.exp(logits - jnp.max(logits, axis=-1, keepdims=True))
    raised = jnp.where(chosen, raised, 0.0)
    gates = raised / jnp.sum(raised, axis=-1, keepdims=True)
    d_gates = dx_ref[:, WIDTH:]
    d_picked = gates * (d_gates - jnp.sum(gates * d_gates, axis=-1, keepdims=True))
    d_logits = d_picked.astype(BF)
    dlog_ref[...] = d_logits
    d_norm = dx_ref[:, :WIDTH] + dot_nt(d_logits, wr_ref[...])
    scaled = d_norm * gain_ref[...]
    ggain_ref[...] = jnp.sum(d_norm * middle * inv, axis=0, keepdims=True)
    d_mid = (
        cot_ref[...]
        + inv * scaled
        - middle * inv**3 * jnp.mean(middle * scaled, axis=-1, keepdims=True)
    )
    dmid_ref[...] = d_mid
    d_low = d_mid.astype(BF)
    dlow_ref[...] = d_low
    d_att = dot_nt(d_low, wo_ref[...]).astype(BF)
    for g in range(KV_HEADS):
        pack_heads(datt_ref.at[g], d_att[:, g * ROWS_Q : (g + 1) * ROWS_Q], d_att.shape[0])


def run_post(dx_sum, middle, cotangent, normed_two, wr_pad, map_rows, gain, w_output):
    tokens = middle.shape[0]
    return pl.pallas_call(
        post_kernel,
        out_shape=(
            jax.ShapeDtypeStruct((KV_HEADS, tokens * ROWS_Q // LANES, LANES), BF),
            jax.ShapeDtypeStruct((tokens, WIDTH), F32),
            jax.ShapeDtypeStruct((tokens, WIDTH), BF),
            jax.ShapeDtypeStruct((tokens, LANES), BF),
            jax.ShapeDtypeStruct((1, WIDTH), F32),
        ),
        compiler_params=params(60),
        cost_estimate=cost(2 * tokens * WIDTH * WIDTH, 14e6),
    )(dx_sum, middle, cotangent, normed_two, wr_pad, map_rows, gain[None], w_output)


def put_rows(place_ref, held, keep, send):
    part = keep.shape[1]
    for b in range(keep.shape[0]):
        own = (2 * b) ^ place_ref[5]
        keep[b] = held[pl.ds(pl.multiple_of(own * part, part), part), :]
        other = own ^ 1
        send[b] = held[pl.ds(pl.multiple_of(other * part, part), part), :]


def outgrad_kernel(place_ref, a_ref, b_ref, keep, send, held):
    held[...] = dot_tn(a_ref[...], b_ref[...]).astype(BF)
    put_rows(place_ref, held, keep, send)


def run_outgrad(place, left, right, blocks):
    tokens, rows = left.shape
    cols = right.shape[1]
    part = rows // blocks
    spec = pl.BlockSpec((blocks // 2, part, 256), lambda i, p: (0, 0, i))
    shape = jax.ShapeDtypeStruct((blocks // 2, part, cols), BF)
    return pl.pallas_call(
        outgrad_kernel,
        grid_spec=pltpu.PrefetchScalarGridSpec(
            num_scalar_prefetch=1,
            grid=(cols // 256,),
            in_specs=[
                pl.BlockSpec((tokens, rows), lambda i, p: (0, 0)),
                pl.BlockSpec((tokens, 256), lambda i, p: (0, i)),
            ],
            out_specs=(spec, spec),
            scratch_shapes=[pltpu.VMEM((rows, 256), BF)],
        ),
        out_shape=(shape, shape),
        compiler_params=params(60, ("arbitrary",)),
        cost_estimate=cost(2 * tokens * rows * cols, 8e6),
    )(place, left, right)


def qkvgrad_kernel(place_ref, a_ref, d_ref, full_ref, keep, send, held):
    step = pl.program_id(0)

    @pl.when(step == 0)
    def _():
        key_at = KV_HEADS * ROWS_Q
        value_at = key_at + KV_HEADS * HEAD_DIM
        for g in range(KV_HEADS):
            unpack_all(
                d_ref.at[g],
                full_ref,
                full_ref,
                full_ref,
                0,
                full_ref.shape[0],
                g * ROWS_Q,
                key_at + g * HEAD_DIM,
                value_at + g * HEAD_DIM,
            )

    cols = pl.ds(pl.multiple_of(step * 256, 256), 256)
    held[...] = dot_tn(a_ref[...], full_ref[:, cols]).astype(BF)
    put_rows(place_ref, held, keep, send)


def run_qkvgrad(place, normed, d_pack, blocks):
    tokens, rows = normed.shape
    cols = KV_HEADS * PACK
    part = rows // blocks
    spec = pl.BlockSpec((blocks // 2, part, 256), lambda i, p: (0, 0, i))
    shape = jax.ShapeDtypeStruct((blocks // 2, part, cols), BF)
    return pl.pallas_call(
        qkvgrad_kernel,
        grid_spec=pltpu.PrefetchScalarGridSpec(
            num_scalar_prefetch=1,
            grid=(cols // 256,),
            in_specs=[
                pl.BlockSpec((tokens, rows), lambda i, p: (0, 0)),
                pl.BlockSpec(d_pack.shape, lambda i, p: (0, 0, 0)),
            ],
            out_specs=(pl.BlockSpec((tokens, cols), lambda i, p: (0, 0)), spec, spec),
            scratch_shapes=[pltpu.VMEM((rows, 256), BF)],
        ),
        out_shape=(jax.ShapeDtypeStruct((tokens, cols), BF), shape, shape),
        compiler_params=params(60, ("arbitrary",)),
        cost_estimate=cost(2 * tokens * rows * cols, 12e6),
    )(place, normed, d_pack)


def last_kernel(d_ref, wq_ref, wk_ref, wv_ref, dmid_ref, hid_ref, gain_ref, out_ref, ggain_ref):
    key_at = KV_HEADS * ROWS_Q
    value_at = key_at + KV_HEADS * HEAD_DIM
    d_norm = dot_nt(d_ref[:, 0:key_at], wq_ref[...])
    d_norm += dot_nt(d_ref[:, key_at:value_at], wk_ref[...])
    d_norm += dot_nt(d_ref[:, value_at:], wv_ref[...])
    inputs = hid_ref[...]
    inv = lax.rsqrt(jnp.mean(inputs * inputs, axis=-1, keepdims=True) + EPS)
    scaled = d_norm * gain_ref[...]
    ggain_ref[...] = jnp.sum(d_norm * inputs * inv, axis=0, keepdims=True)
    out_ref[...] = (
        dmid_ref[...]
        + inv * scaled
        - inputs * inv**3 * jnp.mean(inputs * scaled, axis=-1, keepdims=True)
    )


def run_last(d_full, w_query, w_key, w_value, d_middle, inputs, gain):
    tokens = inputs.shape[0]
    return pl.pallas_call(
        last_kernel,
        out_shape=(
            jax.ShapeDtypeStruct((tokens, WIDTH), F32),
            jax.ShapeDtypeStruct((1, WIDTH), F32),
        ),
        compiler_params=params(60),
        cost_estimate=cost(2 * tokens * WIDTH * 2560, 16e6),
    )(d_full, w_query, w_key, w_value, d_middle, inputs, gain[None])


def small_kernel(place_ref, norm_ref, dlog_ref, gmlp_ref, gattn_ref, keep, send, held):
    columns = dot_tn(norm_ref[...], dlog_ref[...])
    lane = lax.broadcasted_iota(jnp.int32, columns.shape, 1)
    for n, ref in enumerate((gmlp_ref, gattn_ref)):
        turned = jnp.broadcast_to(ref[...], (8, ref.shape[1])).T[:, 0:1]
        columns = jnp.where(lane == LANES - 2 + n, turned, columns)
    held[...] = columns
    put_rows(place_ref, held, keep, send)


def run_small(place, normed_two, d_log, ggain_mlp, ggain_attn, blocks):
    part = WIDTH // blocks
    shape = jax.ShapeDtypeStruct((blocks // 2, part, LANES), F32)
    smem = pl.BlockSpec(memory_space=pltpu.SMEM)
    vmem = pl.BlockSpec(memory_space=pltpu.VMEM)
    return pl.pallas_call(
        small_kernel,
        in_specs=[smem] + [vmem] * 4,
        out_shape=(shape, shape),
        scratch_shapes=[pltpu.VMEM((WIDTH, LANES), F32)],
        compiler_params=params(60),
        cost_estimate=cost(1e8, 3e6),
    )(place, normed_two, d_log, ggain_mlp, ggain_attn)


def stack_swap(values, bit):
    return jnp.concatenate([values, swap_bit(values, bit)], axis=0)


MESH = pl.DeviceIdType.MESH
hbm = pl.BlockSpec(memory_space=pltpu.HBM)


def peer_of(bit):
    axis, mask = bit
    return {axis: lax.axis_index(axis) ^ mask}


def greet(ids):
    barrier = pltpu.get_barrier_semaphore()
    for device in ids:
        pl.semaphore_signal(barrier, inc=1, device_id=device, device_id_type=MESH)
    pl.semaphore_wait(barrier, len(ids))


GATHER_BITS = (X_BIT, ZL_BIT, C_BIT)


def gather_steps(x_ref, all_ref, send_sem, recv_sem, local_sem):
    half = x_ref.shape[0] // 2
    own = pltpu.make_async_copy(x_ref, all_ref.at[0], local_sem)
    own.start()
    copies = []

    def send(source, slot, rows, bit):
        n = len(copies)
        copy = pltpu.make_async_remote_copy(
            src_ref=source if rows is None else source.at[rows],
            dst_ref=all_ref.at[slot] if rows is None else all_ref.at[slot, rows],
            send_sem=send_sem.at[n],
            recv_sem=recv_sem.at[n],
            device_id=peer_of(bit),
            device_id_type=MESH,
        )
        copy.start()
        copies.append(copy)
        return copy

    top, low = pl.ds(0, half), pl.ds(half, half)
    x_top = send(x_ref, 1, top, X_BIT)
    z_low = send(x_ref, 2, low, ZL_BIT)
    x_low = send(x_ref, 1, low, X_BIT)
    z_top = send(x_ref, 2, top, ZL_BIT)
    last = [send(x_ref, 4, None, C_BIT)]
    x_top.wait_recv()
    far_top = send(all_ref.at[1], 3, top, ZL_BIT)
    z_low.wait_recv()
    far_low = send(all_ref.at[2], 3, low, X_BIT)
    x_low.wait_recv()
    last.append(send(all_ref.at[1], 5, None, C_BIT))
    z_top.wait_recv()
    last.append(send(all_ref.at[2], 6, None, C_BIT))
    far_top.wait_recv()
    far_low.wait_recv()
    last.append(send(all_ref.at[3], 7, None, C_BIT))
    for copy in last:
        copy.wait_recv()
    for copy in copies:
        copy.wait_send()
    own.wait()


def gather_kernel(x_ref, *refs):
    blocks, maps_ref = refs[0:4], refs[4]
    all_ref, other_ref, all_maps_ref = refs[5:8]
    send_sem, recv_sem, more_send, more_recv, local_sem = refs[8:]
    greet([peer_of(bit) for bit in GATHER_BITS])
    pairs = [(block, other_ref.at[n], other_ref.at[4 + n]) for n, block in enumerate(blocks)]
    pairs.append((maps_ref, all_maps_ref.at[pl.ds(0, 4)], all_maps_ref.at[pl.ds(4, 4)]))
    copies = []
    for n, (block, here, there) in enumerate(pairs):
        copy = pltpu.make_async_remote_copy(
            src_ref=block,
            dst_ref=there,
            send_sem=more_send.at[n],
            recv_sem=more_recv.at[n],
            device_id=peer_of(C_BIT),
            device_id_type=MESH,
        )
        copy.start()
        copies.append(copy)
        copy = pltpu.make_async_copy(block, here, local_sem.at[1 + n])
        copy.start()
        copies.append(copy)
    gather_steps(x_ref, all_ref, send_sem, recv_sem, local_sem.at[0])
    for copy in copies:
        copy.wait()


def run_gather(values, blocks, maps):
    shape = jax.ShapeDtypeStruct((8,) + values.shape, values.dtype)
    return pl.pallas_call(
        gather_kernel,
        in_specs=[pl.BlockSpec(memory_space=pltpu.VMEM)] * 6,
        out_specs=(hbm,) * 3,
        out_shape=(shape, shape, jax.ShapeDtypeStruct((8,) + maps.shape[1:], maps.dtype)),
        scratch_shapes=[pltpu.SemaphoreType.DMA((n,)) for n in (10, 10, 5, 5, 6)],
        compiler_params=pltpu.CompilerParams(
            collective_id=1, has_side_effects=True, vmem_limit_bytes=60 * MIB
        ),
        cost_estimate=cost(0, 150e6),
    )(values, *blocks, maps)


def trade_peers(size):
    me = lax.axis_index("dp")
    return [{"dp": me ^ k} for k in range(size - 1, 0, -1)]


def trade_start(a_ref, out_ref, send_sem, recv_sem, local_sem):
    me = lax.axis_index("dp")
    copies = []
    for n, device in enumerate(trade_peers(a_ref.shape[0])):
        copy = pltpu.make_async_remote_copy(
            src_ref=a_ref.at[device["dp"]],
            dst_ref=out_ref.at[me],
            send_sem=send_sem.at[n],
            recv_sem=recv_sem.at[n],
            device_id=device,
            device_id_type=MESH,
        )
        copy.start()
        copies.append(copy)
    own = pltpu.make_async_copy(a_ref.at[me], out_ref.at[me], local_sem)
    own.start()
    return copies, own


def trade_end(copies, own):
    own.wait()
    for copy in copies:
        copy.wait_recv()
    for copy in copies:
        copy.wait_send()


def ride_pieces(sources, targets, riders, send_sem, recv_sem):
    starts, copies = [], []
    for n, (bit, pieces) in enumerate(riders):
        size = sources[n].shape[0] // pieces
        for m in range(pieces):
            at = pl.ds(m * size, size)
            slot = len(starts)

            def start(n=n, at=at, slot=slot, bit=bit):
                copy = pltpu.make_async_remote_copy(
                    src_ref=sources[n].at[at],
                    dst_ref=targets[n].at[at],
                    send_sem=send_sem.at[slot],
                    recv_sem=recv_sem.at[slot],
                    device_id=peer_of(bit),
                    device_id_type=MESH,
                )
                copy.start()
                copies.append(copy)

            starts.append(start)
    return starts, copies


def rider_shapes(riders):
    return tuple(jax.ShapeDtypeStruct(array.shape, array.dtype) for array, _, _ in riders)


def all_peers(bits):
    size = lax.axis_size("dp")
    return trade_peers(size) + [peer_of(bit) for bit in bits if bit[0] == "expert"]


def trade_kernel(*refs, riders):
    count = len(riders)
    a_ref, sources = refs[0], refs[1 : 1 + count]
    out_ref, targets = refs[1 + count], refs[2 + count : 2 + 2 * count]
    send_sem, recv_sem, local_sem, *more = refs[2 + 2 * count :]
    greet(all_peers(sorted({bit for bit, _ in riders})))
    trade = trade_start(a_ref, out_ref, send_sem, recv_sem, local_sem.at[0])
    copies = []
    if riders:
        starts, copies = ride_pieces(sources, targets, riders, *more)
        for start in starts:
            start()
    trade_end(*trade)
    for copy in copies:
        copy.wait()


def run_trade(values, number, riders=()):
    size = values.shape[0]
    count = len(riders)
    total = sum(rider[2] for rider in riders)
    sems = [size - 1, size - 1, 1] + [total] * (2 if count else 0)
    out = pl.pallas_call(
        functools.partial(trade_kernel, riders=tuple(rider[1:] for rider in riders)),
        in_specs=[hbm] * (1 + count),
        out_specs=(hbm,) * (1 + count),
        out_shape=(jax.ShapeDtypeStruct(values.shape, values.dtype),) + rider_shapes(riders),
        scratch_shapes=[pltpu.SemaphoreType.DMA((n,)) for n in sems],
        compiler_params=pltpu.CompilerParams(
            collective_id=number, has_side_effects=True, vmem_limit_bytes=60 * MIB
        ),
        cost_estimate=cost(0, 170e6),
    )(values, *(rider[0] for rider in riders))
    return out if count else out[0]


def first_kernel(a_ref, rank_ref, turned_ref, out_ref, slot_ref, send_sem, recv_sem, local_sem, *, far):
    greet(trade_peers(a_ref.shape[0]))
    trade = trade_start(a_ref, out_ref, send_sem, recv_sem, local_sem.at[0])
    for e in range(rank_ref.shape[0]):
        own = rank_ref[e : e + 1, :]
        smaller = (turned_ref[:, e : e + 1] < own).astype(F32)
        before = jnp.sum(smaller, axis=0, keepdims=True)
        slot_ref[e : e + 1, :] = jnp.where(own < far, jnp.minimum(before, SLOTS), -1.0)
    trade_end(*trade)


def run_first(values, rank_map, turned, far):
    size = values.shape[0]
    vmem = pl.BlockSpec(memory_space=pltpu.VMEM)
    return pl.pallas_call(
        functools.partial(first_kernel, far=far),
        in_specs=[hbm, vmem, vmem],
        out_specs=(hbm, vmem),
        out_shape=(
            jax.ShapeDtypeStruct(values.shape, values.dtype),
            jax.ShapeDtypeStruct(rank_map.shape, F32),
        ),
        scratch_shapes=[pltpu.SemaphoreType.DMA((n,)) for n in (size - 1, size - 1, 1)],
        compiler_params=pltpu.CompilerParams(
            collective_id=2, has_side_effects=True, vmem_limit_bytes=60 * MIB
        ),
        cost_estimate=cost(0, 170e6),
    )(values, rank_map, turned)


def reduce_chain(slot, part, keep_ref, send_ref, outs, acc, got, staged, send_sem, recv_sem):
    first, bits, row, rows, column, columns, order = part
    blocks = keep_ref.shape[0]
    stages = len(bits) + 1
    low = send_ref.dtype
    at = (pl.ds(row, rows), pl.ds(column, columns))
    copies = []

    def exchange(source, target, bit):
        n = slot + len(copies)
        copy = pltpu.make_async_remote_copy(
            src_ref=source,
            dst_ref=target,
            send_sem=send_sem.at[n],
            recv_sem=recv_sem.at[n],
            device_id=peer_of(bit),
            device_id_type=MESH,
        )
        copy.start()
        copies.append(copy)

    live = list(range(blocks))
    base_got, base_sent = 0, 0
    exchange(send_ref.at[(slice(None),) + at], got.at[(pl.ds(0, blocks),) + at], first)
    yield
    for stage in range(stages):
        copies[-1].wait_recv()

        def total(position):
            index = live[position]
            kept = keep_ref[(index,) + at].astype(F32) if stage == 0 else acc[(index,) + at]
            return kept + got[(base_got + position,) + at].astype(F32)

        if stage == stages - 1:
            low_column = 0
            for out_ref in outs:
                if low_column <= column < low_column + out_ref.shape[1]:
                    out_ref[at[0], pl.ds(column - low_column, columns)] = total(0)
                low_column += out_ref.shape[1]
            break
        mask = 1 << order[stage]
        rest = [i for i in live if not i & mask]
        for m, i in enumerate(rest):
            staged[(base_sent + m,) + at] = total(live.index(i ^ mask)).astype(low)
        exchange(
            staged.at[(pl.ds(base_sent, len(rest)),) + at],
            got.at[(pl.ds(base_got + len(live), len(rest)),) + at],
            bits[order[stage]],
        )
        for i in rest:
            acc[(i,) + at] = total(live.index(i))
        base_got += len(live)
        base_sent += len(rest)
        live = rest
        yield
    for copy in copies:
        copy.wait_send()


def reduce_kernel(*refs, jobs, riders):
    size, count = len(jobs), len(riders)
    keeps, sends, sources = refs[:size], refs[size : 2 * size], refs[2 * size : 2 * size + count]
    refs = refs[2 * size + count :]
    outs = []
    for _, _, _, widths in jobs:
        outs.append(refs[: len(widths)])
        refs = refs[len(widths) :]
    targets, scratch = refs[:count], refs[count:]
    send_sem, recv_sem, ride_send, ride_recv = scratch[3 * size :]
    used = {bit for first, bits, *_ in jobs for bit in (first,) + bits}
    used |= {bit for bit, _ in riders}
    greet([peer_of(bit) for bit in sorted(used)])
    chains, slot = [], 0
    for n, (first, bits, parts, _) in enumerate(jobs):
        for part in parts:
            chains.append(
                reduce_chain(
                    slot,
                    (first, bits) + part,
                    keeps[n],
                    sends[n],
                    outs[n],
                    *scratch[3 * n : 3 * n + 3],
                    send_sem,
                    recv_sem,
                )
            )
            slot += len(bits) + 1
    starts, copies = ride_pieces(sources, targets, riders, ride_send, ride_recv)
    turn, plain = 0, sum(pieces == 1 for _, pieces in riders)
    while chains:
        rest = []
        for chain in chains:
            try:
                next(chain)
                rest.append(chain)
            except StopIteration:
                pass
            if turn >= 2 and starts:
                starts.pop(0)()
        chains = rest
        for _ in range(plain if turn == 0 else 0):
            starts.pop(0)()
        if turn <= 1 and starts:
            starts.pop(0)()
        turn += 1
    for start in starts:
        start()
    for copy in copies:
        copy.wait()


def run_reduce(pairs, jobs, number, riders=()):
    slots = sum(len(parts) * (len(bits) + 1) for _, bits, parts, _ in jobs)
    vmem = pl.BlockSpec(memory_space=pltpu.VMEM)
    scratch, shapes = [], []
    for (keep, send), (_, _, _, widths) in zip(pairs, jobs):
        blocks, rows, cols = keep.shape
        scratch += [
            pltpu.VMEM((blocks, rows, cols), F32),
            pltpu.VMEM((2 * blocks - 1, rows, cols), send.dtype),
            pltpu.VMEM((max(blocks - 1, 1), rows, cols), send.dtype),
        ]
        shapes += [jax.ShapeDtypeStruct((rows, width), F32) for width in widths]
    pieces = max(sum(rider[2] for rider in riders), 1)
    sems = (slots, slots, pieces, pieces)
    return pl.pallas_call(
        functools.partial(
            reduce_kernel, jobs=jobs, riders=tuple(rider[1:] for rider in riders)
        ),
        in_specs=[vmem] * len(pairs) + [hbm] * (len(pairs) + len(riders)),
        out_specs=(vmem,) * len(shapes) + (hbm,) * len(riders),
        out_shape=tuple(shapes) + rider_shapes(riders),
        scratch_shapes=scratch + [pltpu.SemaphoreType.DMA((n,)) for n in sems],
        compiler_params=pltpu.CompilerParams(
            collective_id=number, has_side_effects=True, vmem_limit_bytes=60 * MIB
        ),
        cost_estimate=cost(0, 170e6),
    )(*(keep for keep, _ in pairs), *(send for _, send in pairs), *(rider[0] for rider in riders))


def sum_pair(kept, received):
    return kept.astype(F32) + received.astype(F32)


def add_low(*terms):
    return sum(term.astype(F32) for term in terms).astype(BF)


def join_kernel(place_ref, *refs):
    outs = refs[-3:]
    zl_at = place_ref[0]

    def total(*terms):
        return sum(term.astype(F32) for term in terms)

    def work(parts, part):
        for n in range(2):
            keep, got, more, other = parts[4 * n : 4 * n + 4]
            mine = total(keep[0, 0, 0], got[0, 0], more[0])
            across = other[0].astype(F32)
            for m in range(2):
                cols = slice(m * LANES, (m + 1) * LANES)
                at = pl.multiple_of((2 * m + zl_at) * LANES, LANES)
                outs[n][part, 0, :, pl.ds(at, LANES)] = mine[:, cols]
                at = pl.multiple_of((2 * m + 1 - zl_at) * LANES, LANES)
                outs[n][part, 0, :, pl.ds(at, LANES)] = across[:, cols]
        keep, got, more = parts[8:]
        outs[2][part, 0] = total(keep[0, 0], got[0], more[0])

    work(refs[0:11], 0)
    work(refs[11:22], 1)


def run_join(place, halves):
    experts, rows, cols = halves[0][2].shape
    wide_rows, width = halves[0][8].shape[2:]
    specs = []
    for part in range(2):
        tall = [
            pl.BlockSpec((1, 1, 1, rows, cols), lambda i, p: (0, 0, i, 0, 0)),
            pl.BlockSpec((1, 1, rows, cols), lambda i, p: (0, i, 0, 0)),
            pl.BlockSpec((1, rows, cols), lambda i, p: (i, 0, 0)),
            pl.BlockSpec((1, rows, cols), lambda i, p: (i, 0, 0)),
        ]
        specs += tall + tall
        specs += [
            pl.BlockSpec((1, 1, wide_rows, width), lambda i, p: (0, i, 0, 0)),
            pl.BlockSpec((1, wide_rows, width), lambda i, p: (i, 0, 0)),
            pl.BlockSpec((1, wide_rows, width), lambda i, p: (i, 0, 0)),
        ]
    shapes = [(rows, 2 * cols), (rows, 2 * cols), (wide_rows, width)]
    return pl.pallas_call(
        join_kernel,
        grid_spec=pltpu.PrefetchScalarGridSpec(
            num_scalar_prefetch=1,
            grid=(experts,),
            in_specs=specs,
            out_specs=tuple(
                pl.BlockSpec((2, 1) + shape, lambda i, p: (0, i, 0, 0)) for shape in shapes
            ),
        ),
        out_shape=tuple(
            jax.ShapeDtypeStruct((2, experts) + shape, F32) for shape in shapes
        ),
        compiler_params=params(60, ("arbitrary",)),
        cost_estimate=cost(1e6, 26e6),
    )(place, *halves[0], *halves[1])


def fast_body(
    hidden_in,
    gain_attn,
    w_query,
    w_key,
    w_value,
    w_output,
    gain_mlp,
    w_router,
    w_gate,
    w_up,
    w_down,
    expert_ids,
    slot_order,
    grad_out,
):
    inputs = hidden_in[0]
    cotangent = grad_out[0]
    chosen = expert_ids[0]
    tokens = inputs.shape[0]
    top = chosen.shape[1]
    local_experts = w_gate.shape[0]
    peers = lax.axis_size("expert")
    all_experts = local_experts * peers
    shards = lax.axis_size("dp")
    length = shards * tokens
    devices = shards * peers
    index = lax.axis_index("dp")
    column = lax.axis_index("expert")
    y_at = index % 2
    zl_at = (index // 2) % 2
    zh_at = index // 4
    place = jnp.stack(
        [zl_at, y_at, zl_at, zh_at, column * local_experts, index * peers + column]
    ).astype(jnp.int32)

    ranks = slot_order[0, 0].reshape(tokens, top)
    far = tokens * top
    names = jnp.arange(all_experts, dtype=jnp.int32)
    match = chosen.T[None] == names[:, None, None]
    rank_map = jnp.min(jnp.where(match, ranks.T[None], far), axis=1).astype(F32)
    turned = rank_map.T
    map_rows = jnp.pad(
        jnp.where(turned < far, 0.0, -1.0),
        ((0, 0), (0, LANES - all_experts)),
        constant_values=-1.0,
    )
    wr_pad = jnp.pad(w_router, ((0, 0), (0, LANES - all_experts)))
    wr_t = jnp.roll(w_router.T, -column * local_experts, axis=0)
    wr_t = jnp.pad(wr_t, ((0, LANES - all_experts), (0, 0)))

    half = HEAD_DIM // 2
    frequency = jnp.exp(-math.log(10000.0) * jnp.arange(half, dtype=F32) * 2.0 / HEAD_DIM)
    own_angles = (index * tokens + jnp.arange(tokens, dtype=jnp.int32)).astype(F32)[:, None] * frequency
    cos_own, sin_own = jnp.cos(own_angles), jnp.sin(own_angles)
    cos_tab = jnp.concatenate([cos_own] * 4, axis=1)
    sin_tab = jnp.concatenate([-sin_own, sin_own] * 2, axis=1)
    angles = frequency[:, None] * jnp.arange(length, dtype=jnp.int32).astype(F32)[None]
    cos_t, sin_t = jnp.cos(angles), jnp.sin(angles)

    normed, pack, g_own = run_pre(
        inputs, gain_attn, w_query, w_key, w_value, cos_tab, sin_tab, cotangent
    )
    pack, slot_map = run_first(pack, rank_map, turned, float(far))
    pack, slot_map, g_late = fence(pack, slot_map, g_own)
    g_x = swap_bit(g_own, X_BIT)
    g_z = swap_bit(g_late, ZL_BIT)
    maps = stack_swap(slot_map[None], X_BIT)
    out, out_t, lse = run_forward(pack)
    out, g_x, g_z, maps = fence(out, g_x, g_z, maps)
    g_zx = swap_bit(g_z, X_BIT)
    maps = stack_swap(maps, ZL_BIT)
    att = run_trade(out, 3)
    att, g_zx, maps = fence(att, g_zx, maps)
    middle, normed_two, att_full = run_mid(att, w_output, inputs, gain_mlp)
    x_all, g_all, maps = run_gather(normed_two, (g_own, g_x, g_z, g_zx), maps)
    maps = jnp.roll(maps, -column * local_experts, axis=1)
    expert_args = (place, x_all, g_all, maps, wr_t, w_gate, w_up, w_down)
    first = run_experts(*expert_args)
    gate_ka, gate_s0, gate_s1, up_ka, up_s0, up_s1, down_ka, down_s0, down_s1 = first[4:]
    down_ya = swap_bit(down_s1, Y_BIT)
    gate_ya = swap_bit(gate_s1, Y_BIT)
    mix_keep, mix_send, dx_keep, dx_send, *second = run_experts(*expert_args, prior=first[:4])
    gate_kb, gate_t0, gate_t1, up_kb, up_t0, up_t1, down_kb, down_t0, down_t1 = second
    dx_send, down_ya, gate_ya = fence(dx_send, down_ya, gate_ya)
    quarter = tokens // 4
    extra = dx_keep.shape[2]
    token_parts = tuple(
        (n * quarter, quarter, 0, extra, (1, 0) if n < 2 else (0, 1)) for n in (2, 0, 3, 1)
    )
    dx_sum, up_ya, gate_ga, mix_got, down_ma = run_reduce(
        ((dx_keep, dx_send),),
        ((C_BIT, (X_BIT, ZL_BIT), token_parts, (extra,)),),
        6,
        riders=(
            (up_s1, Y_BIT, 1),
            (gate_s0, Y_BIT, 1),
            (mix_send, C_BIT, 1),
            (add_low(down_ka[1], down_ya), ZH_BIT, 5),
        ),
    )
    dx_sum, gate_ya, down_s0 = fence(dx_sum, gate_ya, down_s0)
    down_ga = swap_bit(down_s0, Y_BIT)
    gate_za = swap_bit(add_low(gate_ka[1, 1], gate_ya[1]), ZH_BIT)
    d_att, d_middle, d_low, d_log, ggain_mlp = run_post(
        dx_sum, middle, cotangent, normed_two, wr_pad, map_rows, gain_mlp, w_output
    )
    out_keep, out_send = run_outgrad(place, att_full, d_low, devices)
    d_att, out_send, gate_za, down_ga = fence(d_att, out_send, gate_za, down_ga)
    mix_keep = mix_keep.reshape(2, 2, tokens, WIDTH)
    mix_got = mix_got.reshape(2, 2, tokens, WIDTH)
    d_out, gate_ma, up_za, gate_yb, up_yb, gate_oa, mix_x, out_got = run_trade(
        d_att,
        4,
        riders=(
            (add_low(gate_ka[1, 0], gate_ya[0]), ZH_BIT, 1),
            (add_low(up_ka[1, 1], up_ya[1]), ZH_BIT, 1),
            (gate_t1, Y_BIT, 1),
            (up_t1, Y_BIT, 1),
            (add_low(gate_ka[0, 1], gate_ga[1], gate_za), ZL_BIT, 1),
            (add_low(mix_keep[:, 1], mix_got[:, 1]), X_BIT, 1),
            (out_send, C_BIT, 1),
        ),
    )
    split = (2, 2, 2, 2, WIDTH // devices, WIDTH)
    out_keep, out_got = out_keep.reshape(split), out_got.reshape(split)
    both = jnp.stack([add_low(up_ka[1, 0], up_ya[0]), add_low(gate_kb[1, 1], gate_yb[1])])
    both = swap_bit(both, ZH_BIT)
    up_ga, down_yb = fence(up_s0, down_t1, d_out)[:2]
    up_ga = swap_bit(up_ga, Y_BIT)
    down_yb = swap_bit(down_yb, Y_BIT)
    d_pack = run_backward(pack, d_out, out_t, lse, cos_t, sin_t)
    d_pack, both, up_ga, down_yb = fence(d_pack, both, up_ga, down_yb)
    up_ma, gate_zb = both[0], both[1]
    d_pack, gate_mb, up_zb, mix_z, out_x, gate_gb, up_gb, up_oa = run_trade(
        d_pack,
        5,
        riders=(
            (add_low(gate_kb[1, 0], gate_yb[0]), ZH_BIT, 1),
            (add_low(up_kb[1, 1], up_yb[1]), ZH_BIT, 1),
            (add_low(mix_keep[1, 0], mix_got[1, 0], mix_x[1]), ZL_BIT, 1),
            (add_low(out_keep[:, :, :, 1], out_got[:, :, :, 1]), X_BIT, 1),
            (gate_t0, Y_BIT, 1),
            (up_t0, Y_BIT, 1),
            (add_low(up_ka[0, 1], up_ga[1], up_za), ZL_BIT, 1),
        ),
    )
    d_pack, up_yb, down_yb, gate_gb, down_t0, mix_z, out_x = fence(
        d_pack, up_yb, down_yb, gate_gb, down_t0, mix_z, out_x
    )
    up_mb = swap_bit(add_low(up_kb[1, 0], up_yb[0]), ZH_BIT)
    down_mb = swap_bit(add_low(down_kb[1], down_yb), ZH_BIT)
    down_gb = swap_bit(down_t0, Y_BIT)
    d_full, qkv_keep, qkv_send = run_qkvgrad(place, normed, d_pack, devices)
    grad_in, ggain_attn = run_last(
        d_full, w_query, w_key, w_value, d_middle, inputs, gain_attn
    )
    small_keep, small_send = run_small(place, normed_two, d_log, ggain_mlp, ggain_attn, devices)
    mixed = sum_pair(mix_keep[0, 0], mix_got[0, 0]) + sum_pair(mix_x[0], mix_z)
    hidden_out = middle + mixed
    out_held = add_low(out_keep[:, :, :, 0], out_got[:, :, :, 0], out_x)
    rows = WIDTH // devices
    out_first = out_held[:, :, 0].reshape(4, rows, WIDTH)
    out_second = out_held[:, :, 1].reshape(4, rows, WIDTH)
    qkv_send, small_send, out_second, hidden_out = fence(
        qkv_send, small_send, out_second, hidden_out
    )
    qkv_parts = (
        (0, rows, 0, 768, (0, 1, 2, 3)),
        (0, rows, 768, 768, (1, 0, 2, 3)),
        (0, rows, 1536, 512, (0, 1, 2, 3)),
        (0, rows, 2048, 512, (1, 0, 2, 3)),
    )
    dense_bits = (X_BIT, Y_BIT, ZL_BIT, ZH_BIT)
    query_total, key_total, value_total, small, output_total, gate_ob, up_ob = run_reduce(
        ((qkv_keep, qkv_send), (small_keep, small_send), (out_first, out_second)),
        (
            (C_BIT, dense_bits, qkv_parts, (WIDTH, KV_HEADS * HEAD_DIM, KV_HEADS * HEAD_DIM)),
            (C_BIT, dense_bits, ((0, rows, 0, LANES, (0, 1, 2, 3)),), (LANES,)),
            (Y_BIT, (ZL_BIT, ZH_BIT), ((0, rows, 0, WIDTH, (0, 1)),), (WIDTH,)),
        ),
        7,
        riders=(
            (add_low(gate_kb[0, 1], gate_gb[1], gate_zb), ZL_BIT, 1),
            (add_low(up_kb[0, 1], up_gb[1], up_zb), ZL_BIT, 1),
        ),
    )
    query_total, small, up_mb, down_mb, down_gb, up_ob = fence(
        query_total, small, up_mb, down_mb, down_gb, up_ob
    )
    joined = run_join(
        place,
        (
            (gate_ka, gate_ga, gate_ma, gate_oa, up_ka, up_ga, up_ma, up_oa)
            + (down_ka, down_ga, down_ma),
            (gate_kb, gate_gb, gate_mb, gate_ob, up_kb, up_gb, up_mb, up_ob)
            + (down_kb, down_gb, down_mb),
        ),
    )
    gate_total, up_total, down_total = [
        total.reshape((local_experts,) + total.shape[2:]) for total in joined
    ]
    return (
        hidden_out[None],
        grad_in[None],
        small[:, LANES - 1],
        query_total,
        key_total,
        value_total,
        output_total,
        small[:, LANES - 2],
        small[:, :all_experts],
        gate_total,
        up_total,
        down_total,
    )


def fits(mesh):
    return mesh.shape["dp"] == KV_HEADS and mesh.shape["expert"] == 4


def solution(mesh):
    in_specs = (
        P("expert", "dp", None),
        P(),
        P(),
        P(),
        P(),
        P(),
        P(),
        P(),
        P("expert", None, None),
        P("expert", None, None),
        P("expert", None, None),
        P("expert", "dp", None),
        P("expert", "dp", None),
        P("expert", "dp", None),
    )
    out_specs = (
        P("expert", "dp", None),
        P("expert", "dp", None),
        P(("dp", "expert")),
        P(("dp", "expert"), None),
        P(("dp", "expert"), None),
        P(("dp", "expert"), None),
        P(("dp", "expert"), None),
        P(("dp", "expert")),
        P(("dp", "expert"), None),
        P("expert", "dp", None),
        P("expert", "dp", None),
        P("expert", "dp", None),
    )
    chosen = fast_body if fits(mesh) else body
    return jax.shard_map(chosen, mesh=mesh, in_specs=in_specs, out_specs=out_specs, check_vma=False)
```

```python
import functools
import math

import jax
import jax.numpy as jnp
from jax import lax
from jax.experimental import pallas as pl
from jax.experimental.pallas import tpu as pltpu
from jax.sharding import PartitionSpec as P

HEADS = 24
KV_HEADS = 8
HEAD_DIM = 64


EPS = 1e-05
MASKED = -1e30


def rotary_tables(positions):
    half = HEAD_DIM // 2
    frequency = jnp.exp(-math.log(10000.0) * jnp.arange(half, dtype=jnp.float32) * 2.0 / HEAD_DIM)
    angles = positions.astype(jnp.float32)[:, None] * frequency[None, :]
    return (jnp.cos(angles)[:, None, :], jnp.sin(angles)[:, None, :])


def rotate(values, cosine, sine):
    half = values.shape[-1] // 2
    first = values[..., :half]
    second = values[..., half:]
    return jnp.concatenate(
        [first * cosine - second * sine, second * cosine + first * sine], axis=-1
    )


def rotate_back(values, cosine, sine):
    half = values.shape[-1] // 2
    first = values[..., :half]
    second = values[..., half:]
    return jnp.concatenate(
        [first * cosine + second * sine, second * cosine - first * sine], axis=-1
    )


def assign_slots(row_chosen, row_ranks, all_experts, capacity):
    pairs = row_chosen.shape[0]
    by_rank = jnp.zeros((pairs,), jnp.int32).at[row_ranks].set(jnp.arange(pairs, dtype=jnp.int32))
    ordered = row_chosen[by_rank]
    table = (ordered[:, None] == jnp.arange(all_experts, dtype=jnp.int32)[None, :]).astype(
        jnp.int32
    )
    before = jnp.sum(table * (jnp.cumsum(table, axis=0) - 1), axis=1)
    slot = before[row_ranks]
    target = jnp.where(slot < capacity, row_chosen * capacity + slot, all_experts * capacity)
    owner = (
        jnp.full((all_experts * capacity,), pairs, jnp.int32)
        .at[target]
        .set(jnp.arange(pairs, dtype=jnp.int32), mode="drop")
    )
    return (target, owner)


def body(
    hidden_in,
    gain_attn,
    w_query,
    w_key,
    w_value,
    w_output,
    gain_mlp,
    w_router,
    w_gate,
    w_up,
    w_down,
    expert_ids,
    slot_order,
    grad_out,
):
    inputs = hidden_in[0]
    cotangent = grad_out[0]
    chosen = expert_ids[0]
    tokens, width = inputs.shape
    top = chosen.shape[1]
    local_experts = w_gate.shape[0]
    peers = lax.axis_size("expert")
    all_experts = local_experts * peers
    pairs = tokens * top
    capacity = pairs // all_experts
    shards = lax.axis_size("dp")
    index = lax.axis_index("dp")
    length = shards * tokens
    block = math.gcd(length, 512)
    groups = HEADS // KV_HEADS
    scale = HEAD_DIM ** (-0.5)
    query_pos = index * tokens + jnp.arange(tokens, dtype=jnp.int32)
    cosine, sine = rotary_tables(query_pos)
    count = ((index + 1) * tokens + block - 1) // block
    inv_one = lax.rsqrt(jnp.mean(inputs * inputs, axis=-1, keepdims=True) + EPS)
    normed = (inputs * inv_one * gain_attn).astype(jnp.bfloat16)
    query_pre = jnp.dot(normed, w_query, preferred_element_type=jnp.float32).reshape(
        tokens, HEADS, HEAD_DIM
    )
    queries = rotate(query_pre, cosine, sine).astype(jnp.bfloat16)
    key_pre = jnp.dot(normed, w_key, preferred_element_type=jnp.float32).reshape(
        tokens, KV_HEADS, HEAD_DIM
    )
    keys_low = rotate(key_pre, cosine, sine).astype(jnp.bfloat16)
    values_low = (
        jnp.dot(normed, w_value, preferred_element_type=jnp.float32)
        .astype(jnp.bfloat16)
        .reshape(tokens, KV_HEADS, HEAD_DIM)
    )
    keys_all, values_all = (
        lax.all_gather(keys_low, "dp", axis=0, tiled=True),
        lax.all_gather(values_low, "dp", axis=0, tiled=True),
    )
    query_groups = queries.reshape(tokens, KV_HEADS, groups, HEAD_DIM)

    def block_scores(key_block, start):
        raw = (
            jnp.einsum(
                "qkgd,skd->kgqs", query_groups, key_block, preferred_element_type=jnp.float32
            )
            * scale
        )
        key_pos = start + jnp.arange(block, dtype=jnp.int32)
        allowed = key_pos[None, :] <= query_pos[:, None]
        return jnp.where(allowed, raw, MASKED)

    def stats_step(step, carry):
        running, total = carry
        scores = block_scores(
            lax.dynamic_slice_in_dim(keys_all, step * block, block, 0), step * block
        )
        newest = jnp.maximum(running, jnp.max(scores, axis=-1))
        total = total * jnp.exp(running - newest) + jnp.sum(
            jnp.exp(scores - newest[..., None]), axis=-1
        )
        return (newest, total)

    stat_init = (
        jnp.full((KV_HEADS, groups, tokens), MASKED, jnp.float32),
        jnp.zeros((KV_HEADS, groups, tokens), jnp.float32),
    )
    running, total = lax.fori_loop(0, count, stats_step, stat_init)
    log_total = running + jnp.log(total)

    def output_step(step, accum):
        start = step * block
        scores = block_scores(lax.dynamic_slice_in_dim(keys_all, start, block, 0), start)
        probs = jnp.exp(scores - log_total[..., None]).astype(jnp.bfloat16)
        value_block = lax.dynamic_slice_in_dim(values_all, start, block, 0)
        return accum + jnp.einsum(
            "kgqs,skd->qkgd", probs, value_block, preferred_element_type=jnp.float32
        )

    attended_groups = lax.fori_loop(
        0, count, output_step, jnp.zeros((tokens, KV_HEADS, groups, HEAD_DIM), jnp.float32)
    )
    attended = attended_groups.reshape(tokens, HEADS * HEAD_DIM)
    attended_low = attended.astype(jnp.bfloat16)
    branch = jnp.dot(attended_low, w_output, preferred_element_type=jnp.float32)
    middle = inputs + branch
    inv_two = lax.rsqrt(jnp.mean(middle * middle, axis=-1, keepdims=True) + EPS)
    normed_two = (middle * inv_two * gain_mlp).astype(jnp.bfloat16)
    logits = jnp.dot(normed_two, w_router, preferred_element_type=jnp.float32)
    onehot = (chosen[:, :, None] == jnp.arange(all_experts, dtype=jnp.int32)[None, None, :]).astype(
        jnp.float32
    )
    picked = jnp.sum(onehot * logits[:, None, :], axis=-1)
    gates = jax.nn.softmax(picked, axis=-1)
    target, owner = assign_slots(chosen.reshape(pairs), slot_order[0, 0], all_experts, capacity)
    valid = owner < pairs
    source = jnp.minimum(owner, pairs - 1)
    rows_send = jnp.where(valid[:, None], normed_two[source // top], 0).reshape(
        peers, local_experts, capacity, width
    )
    received = lax.all_to_all(rows_send, "expert", split_axis=0, concat_axis=0, tiled=True)
    gate_pre = jnp.einsum("necd,edf->necf", received, w_gate, preferred_element_type=jnp.float32)
    up_pre = jnp.einsum("necd,edf->necf", received, w_up, preferred_element_type=jnp.float32)
    hidden = (jax.nn.silu(gate_pre) * up_pre).astype(jnp.bfloat16)
    result = jnp.einsum(
        "necf,efd->necd", hidden, w_down, preferred_element_type=jnp.float32
    ).astype(jnp.bfloat16)
    returned = lax.all_to_all(result, "expert", split_axis=0, concat_axis=0, tiled=True)
    returned, received, gate_pre, up_pre = (returned, received, gate_pre, up_pre)
    zero_row = jnp.zeros((1, width), jnp.bfloat16)
    pair_out = jnp.concatenate([returned.reshape(all_experts * capacity, width), zero_row], axis=0)[
        target
    ].reshape(tokens, top, width)
    mixed = jnp.einsum("tk,tkd->td", gates, pair_out, preferred_element_type=jnp.float32)
    hidden_out = middle + mixed
    dy_pairs = (
        (gates[:, :, None] * cotangent[:, None, :]).astype(jnp.bfloat16).reshape(pairs, width)
    )
    dy_send = jnp.where(valid[:, None], dy_pairs[source], 0).reshape(
        peers, local_experts, capacity, width
    )
    dy_received = lax.all_to_all(dy_send, "expert", split_axis=0, concat_axis=0, tiled=True)
    sigmoid_gate = jax.nn.sigmoid(gate_pre)
    silu_gate = gate_pre * sigmoid_gate
    hidden = (silu_gate * up_pre).astype(jnp.bfloat16)
    grad_down_part = jnp.einsum(
        "necf,necd->efd", hidden, dy_received, preferred_element_type=jnp.float32
    )
    d_hidden = jnp.einsum("necd,efd->necf", dy_received, w_down, preferred_element_type=jnp.float32)
    d_gate = (d_hidden * up_pre * sigmoid_gate * (1.0 + gate_pre * (1.0 - sigmoid_gate))).astype(
        jnp.bfloat16
    )
    d_up = (d_hidden * silu_gate).astype(jnp.bfloat16)
    grad_gate_part = jnp.einsum(
        "necd,necf->edf", received, d_gate, preferred_element_type=jnp.float32
    )
    grad_up_part = jnp.einsum("necd,necf->edf", received, d_up, preferred_element_type=jnp.float32)
    gate_total, up_total, down_total = (
        lax.psum_scatter(
            grad_gate_part.astype(jnp.bfloat16), "dp", scatter_dimension=1, tiled=True
        ).astype(jnp.float32),
        lax.psum_scatter(
            grad_up_part.astype(jnp.bfloat16), "dp", scatter_dimension=1, tiled=True
        ).astype(jnp.float32),
        lax.psum_scatter(
            grad_down_part.astype(jnp.bfloat16), "dp", scatter_dimension=1, tiled=True
        ).astype(jnp.float32),
    )
    d_rows = jnp.einsum("necf,edf->necd", d_gate, w_gate, preferred_element_type=jnp.float32)
    d_rows = (
        d_rows + jnp.einsum("necf,edf->necd", d_up, w_up, preferred_element_type=jnp.float32)
    ).astype(jnp.bfloat16)
    d_back = lax.all_to_all(d_rows, "expert", split_axis=0, concat_axis=0, tiled=True)
    d_pairs = jnp.concatenate([d_back.reshape(all_experts * capacity, width), zero_row], axis=0)[
        target
    ].reshape(tokens, top, width)
    d_normed_two = jnp.sum(d_pairs, axis=1, dtype=jnp.float32)
    d_gates = jnp.einsum("td,tkd->tk", cotangent, pair_out, preferred_element_type=jnp.float32)
    d_picked = gates * (d_gates - jnp.sum(gates * d_gates, axis=-1, keepdims=True))
    d_logits = jnp.sum(onehot * d_picked[:, :, None], axis=1).astype(jnp.bfloat16)
    grad_router_part = jnp.einsum(
        "td,te->de", normed_two, d_logits, preferred_element_type=jnp.float32
    )
    d_normed_two = d_normed_two + jnp.einsum(
        "te,de->td", d_logits, w_router, preferred_element_type=jnp.float32
    )
    scaled_two = d_normed_two * gain_mlp
    grad_gain_mlp_part = jnp.sum(d_normed_two * middle * inv_two, axis=0)
    d_middle = (
        cotangent
        + inv_two * scaled_two
        - middle * inv_two**3 * jnp.mean(middle * scaled_two, axis=-1, keepdims=True)
    )
    d_branch = d_middle.astype(jnp.bfloat16)
    grad_output_part = jnp.einsum(
        "tf,td->fd", attended_low, d_branch, preferred_element_type=jnp.float32
    )
    d_attended = jnp.einsum(
        "td,fd->tf", d_branch, w_output, preferred_element_type=jnp.float32
    ).astype(jnp.bfloat16)
    d_groups = d_attended.reshape(tokens, KV_HEADS, groups, HEAD_DIM)
    delta = jnp.einsum(
        "qkgd,qkgd->kgq", d_groups, attended_groups, preferred_element_type=jnp.float32
    )
    keys_back, values_back = (
        lax.all_gather(keys_low, "dp", axis=0, tiled=True),
        lax.all_gather(values_low, "dp", axis=0, tiled=True),
    )

    def grad_step(step, carry):
        d_query, d_keys, d_values = carry
        start = step * block
        key_block = lax.dynamic_slice_in_dim(keys_back, start, block, 0)
        value_block = lax.dynamic_slice_in_dim(values_back, start, block, 0)
        scores = block_scores(key_block, start)
        probs = jnp.exp(scores - log_total[..., None])
        probs_low = probs.astype(jnp.bfloat16)
        d_probs = jnp.einsum(
            "qkgd,skd->kgqs", d_groups, value_block, preferred_element_type=jnp.float32
        )
        d_scores = (probs * (d_probs - delta[..., None])).astype(jnp.bfloat16)
        d_query = d_query + jnp.einsum(
            "kgqs,skd->qkgd", d_scores, key_block, preferred_element_type=jnp.float32
        )
        key_part = jnp.einsum(
            "kgqs,qkgd->skd", d_scores, query_groups, preferred_element_type=jnp.float32
        )
        value_part = jnp.einsum(
            "kgqs,qkgd->skd", probs_low, d_groups, preferred_element_type=jnp.float32
        )
        d_keys = lax.dynamic_update_slice_in_dim(
            d_keys, lax.dynamic_slice_in_dim(d_keys, start, block, 0) + key_part, start, 0
        )
        d_values = lax.dynamic_update_slice_in_dim(
            d_values, lax.dynamic_slice_in_dim(d_values, start, block, 0) + value_part, start, 0
        )
        return (d_query, d_keys, d_values)

    grad_init = (
        jnp.zeros((tokens, KV_HEADS, groups, HEAD_DIM), jnp.float32),
        jnp.zeros((length, KV_HEADS, HEAD_DIM), jnp.float32),
        jnp.zeros((length, KV_HEADS, HEAD_DIM), jnp.float32),
    )
    d_query, d_keys, d_values = lax.fori_loop(0, count, grad_step, grad_init)
    key_sum, value_sum = (
        lax.psum_scatter(
            (d_keys * scale).reshape(length, KV_HEADS * HEAD_DIM).astype(jnp.bfloat16),
            "dp",
            scatter_dimension=0,
            tiled=True,
        ).astype(jnp.float32),
        lax.psum_scatter(
            d_values.reshape(length, KV_HEADS * HEAD_DIM).astype(jnp.bfloat16),
            "dp",
            scatter_dimension=0,
            tiled=True,
        ).astype(jnp.float32),
    )
    d_query_low = (
        rotate_back((d_query * scale).reshape(tokens, HEADS, HEAD_DIM), cosine, sine)
        .astype(jnp.bfloat16)
        .reshape(tokens, HEADS * HEAD_DIM)
    )
    d_key_low = (
        rotate_back(key_sum.reshape(tokens, KV_HEADS, HEAD_DIM), cosine, sine)
        .astype(jnp.bfloat16)
        .reshape(tokens, KV_HEADS * HEAD_DIM)
    )
    d_value_low = value_sum.astype(jnp.bfloat16)
    grad_query_part = jnp.einsum(
        "td,tf->df", normed, d_query_low, preferred_element_type=jnp.float32
    )
    grad_key_part = jnp.einsum("td,tf->df", normed, d_key_low, preferred_element_type=jnp.float32)
    grad_value_part = jnp.einsum(
        "td,tf->df", normed, d_value_low, preferred_element_type=jnp.float32
    )
    d_normed = jnp.einsum("tf,df->td", d_query_low, w_query, preferred_element_type=jnp.float32)
    d_normed = d_normed + jnp.einsum(
        "tf,df->td", d_key_low, w_key, preferred_element_type=jnp.float32
    )
    d_normed = d_normed + jnp.einsum(
        "tf,df->td", d_value_low, w_value, preferred_element_type=jnp.float32
    )
    scaled_one = d_normed * gain_attn
    grad_gain_attn_part = jnp.sum(d_normed * inputs * inv_one, axis=0)
    grad_in = (
        d_middle
        + inv_one * scaled_one
        - inputs * inv_one**3 * jnp.mean(inputs * scaled_one, axis=-1, keepdims=True)
    )
    dense = (
        lax.psum_scatter(grad_gain_attn_part, ("dp", "expert"), scatter_dimension=0, tiled=True),
        lax.psum_scatter(grad_query_part, ("dp", "expert"), scatter_dimension=0, tiled=True),
        lax.psum_scatter(grad_key_part, ("dp", "expert"), scatter_dimension=0, tiled=True),
        lax.psum_scatter(grad_value_part, ("dp", "expert"), scatter_dimension=0, tiled=True),
        lax.psum_scatter(grad_output_part, ("dp", "expert"), scatter_dimension=0, tiled=True),
        lax.psum_scatter(grad_gain_mlp_part, ("dp", "expert"), scatter_dimension=0, tiled=True),
        lax.psum_scatter(grad_router_part, ("dp", "expert"), scatter_dimension=0, tiled=True),
    )
    return (
        hidden_out[None],
        grad_in[None],
        dense[0],
        dense[1],
        dense[2],
        dense[3],
        dense[4],
        dense[5],
        dense[6],
        gate_total,
        up_total,
        down_total,
    )

BF = jnp.bfloat16
F32 = jnp.float32
WIDTH = 1536
LANES = 128
PER_KV = HEADS // KV_HEADS
ROWS_Q = PER_KV * HEAD_DIM
PACK = ROWS_Q + 2 * HEAD_DIM
BIT_Y, BIT_ZL, BIT_ZH = 1, 2, 4
BIT_C, BIT_X = 1, 2
BLOCK_Q = 256
BLOCK_K = 512
SLOTS = 64
CHUNK = 512
MIB = 1 << 20


def dot_nn(a, b):
    return lax.dot_general(a, b, (((1,), (0,)), ((), ())), preferred_element_type=F32)


def dot_nt(a, b):
    return lax.dot_general(a, b, (((1,), (1,)), ((), ())), preferred_element_type=F32)


def dot_tn(a, b):
    return lax.dot_general(a, b, (((0,), (0,)), ((), ())), preferred_element_type=F32)


def cost(flops, moved, transcendentals=0):
    return pl.CostEstimate(
        flops=int(flops), bytes_accessed=int(moved), transcendentals=int(transcendentals)
    )


def params(mib, dims=None):
    return pltpu.CompilerParams(vmem_limit_bytes=mib * MIB, dimension_semantics=dims)


def swap(values, axis, mask):
    size = lax.axis_size(axis)
    return lax.ppermute(values, axis, [(i, i ^ mask) for i in range(size)])


def swap_bit(values, bit):
    axis, mask = bit
    return swap(values, axis, mask)


def fence(*values):
    return lax.optimization_barrier(values)


C_BIT = ("expert", BIT_C)
X_BIT = ("expert", BIT_X)
Y_BIT = ("dp", BIT_Y)
ZL_BIT = ("dp", BIT_ZL)
ZH_BIT = ("dp", BIT_ZH)


def pre_kernel(
    hid_ref,
    gain_ref,
    wq_ref,
    wk_ref,
    wv_ref,
    cos_ref,
    sin_ref,
    cot_ref,
    norm_ref,
    pack_ref,
    low_ref,
):
    tokens = hid_ref.shape[0]
    half = tokens // 2
    low_ref[...] = cot_ref[...].astype(BF)
    inputs = hid_ref[...]
    inv = lax.rsqrt(jnp.mean(inputs * inputs, axis=-1, keepdims=True) + EPS)
    normed = (inputs * inv * gain_ref[...]).astype(BF)
    norm_ref[...] = normed
    low = (lax.broadcasted_iota(jnp.int32, (tokens, LANES), 1) % HEAD_DIM) < HEAD_DIM // 2
    cosine, sine = cos_ref[...], sin_ref[...]

    def turn(tile):
        other = jnp.where(
            low,
            pltpu.roll(tile, LANES - HEAD_DIM // 2, 1),
            pltpu.roll(tile, HEAD_DIM // 2, 1),
        )
        return (tile * cosine + other * sine).astype(BF)

    tiles = []
    for n in range(wq_ref.shape[1] // CHUNK):
        pre = dot_nn(normed, wq_ref[:, n * CHUNK : (n + 1) * CHUNK])
        tiles += [turn(pre[:, m * LANES : (m + 1) * LANES]) for m in range(CHUNK // LANES)]
    queries = jnp.concatenate(tiles, axis=1)
    pre = dot_nn(normed, wk_ref[...])
    keys = jnp.concatenate(
        [turn(pre[:, m * LANES : (m + 1) * LANES]) for m in range(pre.shape[1] // LANES)], axis=1
    )
    values = dot_nn(normed, wv_ref[...]).astype(BF)
    for g in range(KV_HEADS):
        at = g * ROWS_Q
        head = slice(g * HEAD_DIM, (g + 1) * HEAD_DIM)
        pack_ref[g, 0:tokens] = queries[:, at : at + LANES]
        pack_ref[g, tokens : 2 * tokens] = jnp.concatenate(
            [queries[:, at + LANES : at + ROWS_Q], keys[:, head]], axis=1
        )
        pack_ref[g, 2 * tokens :] = jnp.concatenate(
            [values[:half, head], values[half:, head]], axis=1
        )


def run_pre(inputs, gain, w_query, w_key, w_value, cos_tab, sin_tab, cotangent):
    tokens = inputs.shape[0]
    return pl.pallas_call(
        pre_kernel,
        out_shape=(
            jax.ShapeDtypeStruct((tokens, WIDTH), BF),
            jax.ShapeDtypeStruct((KV_HEADS, tokens * PACK // LANES, LANES), BF),
            jax.ShapeDtypeStruct((tokens, WIDTH), BF),
        ),
        compiler_params=params(60),
        cost_estimate=cost(2 * tokens * WIDTH * 2560, 14e6),
    )(inputs, gain[None], w_query, w_key, w_value, cos_tab, sin_tab, cotangent)


def unpack_heads(block_ref, out_ref, row, tokens, column):
    half = tokens // 2
    out_ref[row : row + tokens, column : column + LANES] = block_ref[0:tokens]
    rest = block_ref[tokens : tokens + half]
    out_ref[row : row + half, column + LANES : column + ROWS_Q] = rest[:, :HEAD_DIM]
    out_ref[row + half : row + tokens, column + LANES : column + ROWS_Q] = rest[:, HEAD_DIM:]


def pack_heads(block_ref, rows, tokens):
    half = tokens // 2
    block_ref[0:tokens] = rows[:, 0:LANES]
    block_ref[tokens : tokens + half] = jnp.concatenate(
        [rows[:half, LANES:ROWS_Q], rows[half:, LANES:ROWS_Q]], axis=1
    )


def unpack_all(block_ref, q_ref, k_ref, v_ref, row, tokens, q_at=0, k_at=0, v_at=0):
    half = tokens // 2
    rows = slice(row, row + tokens)
    q_ref[rows, q_at : q_at + LANES] = block_ref[0:tokens]
    two = block_ref[tokens : 2 * tokens]
    q_ref[rows, q_at + LANES : q_at + ROWS_Q] = two[:, :HEAD_DIM]
    k_ref[rows, k_at : k_at + HEAD_DIM] = two[:, HEAD_DIM:]
    rest = block_ref[2 * tokens : 2 * tokens + half]
    v_ref[row : row + half, v_at : v_at + HEAD_DIM] = rest[:, :HEAD_DIM]
    v_ref[row + half : row + tokens, v_at : v_at + HEAD_DIM] = rest[:, HEAD_DIM:]


def heads_t(block, width):
    return jnp.concatenate(
        [block[:, h * HEAD_DIM : (h + 1) * HEAD_DIM].astype(F32).T for h in range(width)], axis=1
    )


def heads_rows(block, width):
    return jnp.concatenate(
        [block[:, h * HEAD_DIM : (h + 1) * HEAD_DIM] for h in range(width)], axis=0
    )


def allowed_t(step, block):
    shape = (BLOCK_K, PER_KV * BLOCK_Q)
    key_pos = step * BLOCK_K + lax.broadcasted_iota(jnp.int32, shape, 0)
    query_pos = block * BLOCK_Q + lax.broadcasted_iota(jnp.int32, shape, 1) % BLOCK_Q
    return key_pos <= query_pos


def forward_kernel(pack_ref, out_ref, out_t_ref, lse_ref, q_s, k_s, v_s, vt_s, out_s):
    block = pl.program_id(0)
    sources = pack_ref.shape[0]
    tokens = q_s.shape[0] // sources

    @pl.when(block == 0)
    def _():
        for n in range(sources):
            unpack_all(pack_ref.at[n], q_s, k_s, v_s, n * tokens, tokens)
        vt_s[...] = v_s[...].astype(F32).T.astype(BF)

    rows = pl.ds(pl.multiple_of(block * BLOCK_Q, BLOCK_Q), BLOCK_Q)
    scale = HEAD_DIM ** (-0.5)
    q_t = (heads_t(q_s[rows, :], PER_KV) * scale).astype(BF)
    columns = PER_KV * BLOCK_Q

    def step(j, carry, masked):
        running, total, accum = carry
        keys = pl.ds(pl.multiple_of(j * BLOCK_K, BLOCK_K), BLOCK_K)
        scores = dot_nn(k_s[keys, :], q_t)
        if masked:
            scores = jnp.where(allowed_t(j, block), scores, MASKED)
        newest = jnp.maximum(running, jnp.max(scores, axis=0, keepdims=True))
        fade = jnp.exp(running - newest)
        probs = jnp.exp(scores - newest)
        total = total * fade + jnp.sum(probs, axis=0, keepdims=True)
        accum = accum * fade + dot_nn(vt_s[:, keys], probs.astype(BF))
        return newest, total, accum

    carry = (
        jnp.full((1, columns), MASKED, F32),
        jnp.zeros((1, columns), F32),
        jnp.zeros((HEAD_DIM, columns), F32),
    )
    last = (block * BLOCK_Q) // BLOCK_K
    carry = lax.fori_loop(0, last, lambda j, c: step(j, c, False), carry)
    running, total, accum = step(last, carry, True)
    out_t = accum / total
    out_t_ref[0] = out_t
    lse_ref[0] = running + jnp.log(total)
    out_s[rows, :] = jnp.concatenate(
        [out_t[:, h * BLOCK_Q : (h + 1) * BLOCK_Q].T for h in range(PER_KV)], axis=1
    ).astype(BF)

    @pl.when(block == pl.num_programs(0) - 1)
    def _():
        for n in range(sources):
            pack_heads(out_ref.at[n], out_s[n * tokens : (n + 1) * tokens, :], tokens)


def run_forward(pack):
    sources = pack.shape[0]
    length = sources * (pack.shape[1] * LANES // PACK)
    packed = (sources, length // sources * ROWS_Q // LANES, LANES)
    blocks = length // BLOCK_Q
    columns = PER_KV * BLOCK_Q
    return pl.pallas_call(
        forward_kernel,
        grid=(blocks,),
        in_specs=[pl.BlockSpec(pack.shape, lambda i: (0, 0, 0))],
        out_specs=(
            pl.BlockSpec(packed, lambda i: (0, 0, 0)),
            pl.BlockSpec((1, HEAD_DIM, columns), lambda i: (i, 0, 0)),
            pl.BlockSpec((1, 1, columns), lambda i: (i, 0, 0)),
        ),
        out_shape=(
            jax.ShapeDtypeStruct(packed, BF),
            jax.ShapeDtypeStruct((blocks, HEAD_DIM, columns), F32),
            jax.ShapeDtypeStruct((blocks, 1, columns), F32),
        ),
        scratch_shapes=[
            pltpu.VMEM((length, ROWS_Q), BF),
            pltpu.VMEM((length, HEAD_DIM), BF),
            pltpu.VMEM((length, HEAD_DIM), BF),
            pltpu.VMEM((HEAD_DIM, length), BF),
            pltpu.VMEM((length, ROWS_Q), BF),
        ],
        compiler_params=params(60, ("arbitrary",)),
        cost_estimate=cost(8 * length * length * ROWS_Q, 6e6, length * length * PER_KV),
    )(pack)


def backward_kernel(
    pack_ref,
    grad_ref,
    out_t_ref,
    lse_ref,
    cos_ref,
    sin_ref,
    res_ref,
    q_s,
    do_s,
    k_s,
    v_s,
    kt_s,
    dk_s,
    dv_s,
):
    block = pl.program_id(0)
    sources = pack_ref.shape[0]
    tokens = q_s.shape[0] // sources

    @pl.when(block == 0)
    def _():
        for n in range(sources):
            unpack_all(pack_ref.at[n], q_s, k_s, v_s, n * tokens, tokens)
            unpack_heads(grad_ref.at[n], do_s, n * tokens, tokens, 0)
        kt_s[...] = k_s[...].astype(F32).T.astype(BF)
        dk_s[...] = jnp.zeros_like(dk_s)
        dv_s[...] = jnp.zeros_like(dv_s)

    scale = HEAD_DIM ** (-0.5)
    half = HEAD_DIM // 2
    rows = pl.ds(pl.multiple_of(block * BLOCK_Q, BLOCK_Q), BLOCK_Q)
    q_block = q_s[rows, :]
    q_t = (heads_t(q_block, PER_KV) * scale).astype(BF)
    q_rows = (heads_rows(q_block, PER_KV).astype(F32) * scale).astype(BF)
    do_block = do_s[rows, :]
    do_f32 = heads_t(do_block, PER_KV)
    do_t = do_f32.astype(BF)
    do_rows = heads_rows(do_block, PER_KV)
    delta = jnp.sum(do_f32 * out_t_ref[0], axis=0, keepdims=True)
    lse = lse_ref[0]

    def step(j, dq_t, masked):
        keys = pl.ds(pl.multiple_of(j * BLOCK_K, BLOCK_K), BLOCK_K)
        scores = dot_nn(k_s[keys, :], q_t)
        if masked:
            scores = jnp.where(allowed_t(j, block), scores, MASKED)
        probs = jnp.exp(scores - lse)
        d_probs = dot_nn(v_s[keys, :], do_t)
        d_scores = (probs * (d_probs - delta)).astype(BF)
        dv_s[keys, :] += dot_nn(probs.astype(BF), do_rows)
        dk_s[keys, :] += dot_nn(d_scores, q_rows)
        return dq_t + dot_nn(kt_s[:, keys], d_scores)

    last = (block * BLOCK_Q) // BLOCK_K
    dq_t = jnp.zeros((HEAD_DIM, PER_KV * BLOCK_Q), F32)
    dq_t = lax.fori_loop(0, last, lambda j, c: step(j, c, False), dq_t)
    dq_t = step(last, dq_t, True) * scale

    def turn_back(values, cosine, sine):
        first, second = values[:half], values[half:]
        return jnp.concatenate(
            [first * cosine + second * sine, second * cosine - first * sine], axis=0
        )

    columns = pl.ds(pl.multiple_of(block * BLOCK_Q, BLOCK_Q), BLOCK_Q)
    cosine, sine = cos_ref[:, columns], sin_ref[:, columns]
    q_s[rows, :] = jnp.concatenate(
        [
            turn_back(dq_t[:, h * BLOCK_Q : (h + 1) * BLOCK_Q], cosine, sine).T
            for h in range(PER_KV)
        ],
        axis=1,
    ).astype(BF)

    @pl.when(block == pl.num_programs(0) - 1)
    def _():
        dk = turn_back(dk_s[...].T, cos_ref[...], sin_ref[...]).T.astype(BF)
        half = tokens // 2
        for n in range(sources):
            row = n * tokens
            res_ref[n, 0:tokens] = q_s[row : row + tokens, 0:LANES]
            res_ref[n, tokens : 2 * tokens] = jnp.concatenate(
                [q_s[row : row + tokens, LANES:ROWS_Q], dk[row : row + tokens]], axis=1
            )
            res_ref[n, 2 * tokens :] = jnp.concatenate(
                [dv_s[row : row + half, :], dv_s[row + half : row + tokens, :]], axis=1
            ).astype(BF)


def run_backward(pack, grad, out_t, lse, cos_t, sin_t):
    length = cos_t.shape[1]
    blocks = length // BLOCK_Q
    columns = PER_KV * BLOCK_Q
    half = HEAD_DIM // 2
    return pl.pallas_call(
        backward_kernel,
        grid=(blocks,),
        in_specs=[
            pl.BlockSpec(pack.shape, lambda i: (0, 0, 0)),
            pl.BlockSpec(grad.shape, lambda i: (0, 0, 0)),
            pl.BlockSpec((1, HEAD_DIM, columns), lambda i: (i, 0, 0)),
            pl.BlockSpec((1, 1, columns), lambda i: (i, 0, 0)),
            pl.BlockSpec((half, length), lambda i: (0, 0)),
            pl.BlockSpec((half, length), lambda i: (0, 0)),
        ],
        out_specs=pl.BlockSpec(pack.shape, lambda i: (0, 0, 0)),
        out_shape=jax.ShapeDtypeStruct(pack.shape, BF),
        scratch_shapes=[
            pltpu.VMEM((length, ROWS_Q), BF),
            pltpu.VMEM((length, ROWS_Q), BF),
            pltpu.VMEM((length, HEAD_DIM), BF),
            pltpu.VMEM((length, HEAD_DIM), BF),
            pltpu.VMEM((HEAD_DIM, length), BF),
            pltpu.VMEM((length, HEAD_DIM), F32),
            pltpu.VMEM((length, HEAD_DIM), F32),
        ],
        compiler_params=params(60, ("arbitrary",)),
        cost_estimate=cost(20 * length * length * ROWS_Q, 8e6, length * length * PER_KV),
    )(pack, grad, out_t, lse, cos_t, sin_t)


def mid_kernel(att_ref, wo_ref, hid_ref, gain_ref, mid_ref, norm_ref, full_ref):
    for g in range(KV_HEADS):
        unpack_heads(att_ref.at[g], full_ref, 0, full_ref.shape[0], g * ROWS_Q)
    middle = hid_ref[...] + dot_nn(full_ref[...], wo_ref[...])
    mid_ref[...] = middle
    inv = lax.rsqrt(jnp.mean(middle * middle, axis=-1, keepdims=True) + EPS)
    norm_ref[...] = (middle * inv * gain_ref[...]).astype(BF)


def run_mid(att, w_output, inputs, gain):
    tokens = inputs.shape[0]
    return pl.pallas_call(
        mid_kernel,
        out_shape=(
            jax.ShapeDtypeStruct((tokens, WIDTH), F32),
            jax.ShapeDtypeStruct((tokens, WIDTH), BF),
            jax.ShapeDtypeStruct((tokens, WIDTH), BF),
        ),
        compiler_params=params(60),
        cost_estimate=cost(2 * tokens * WIDTH * WIDTH, 12e6),
    )(att, w_output, inputs, gain[None])


def expert_kernel(
    place_ref,
    x_ref,
    g_ref,
    map_ref,
    wr_ref,
    wg0_ref,
    wg1_ref,
    wu0_ref,
    wu1_ref,
    wd0_ref,
    wd1_ref,
    *refs,
    first,
):
    if first:
        mix_prior = dx_prior = None
    else:
        mix_prior, dx_prior = refs[0:2], refs[2:4]
        refs = refs[4:]
    (
    mix_keep,
    mix_send,
    dx_keep,
    dx_send,
    gate_keep,
    gate_send0,
    gate_send1,
    up_keep,
    up_send0,
    up_send1,
    down_keep,
    down_send0,
    down_send1,
    xs,
    gs,
    gate_s,
    wide_s,
    tall_s,
    ) = refs
    step = pl.program_id(0)
    sources = map_ref.shape[0]
    experts = xs.shape[0]
    low = 0 if first else experts
    tokens = x_ref.shape[1]
    rows = experts * SLOTS
    count = WIDTH // CHUNK

    def one_hot(source):
        slots = map_ref[source, low : low + experts, :]
        wide = jnp.broadcast_to(slots[:, None, :], (experts, SLOTS, tokens))
        rank = lax.broadcasted_iota(jnp.int32, (experts, SLOTS, tokens), 1).astype(F32)
        return (wide == rank).astype(F32).reshape(rows, tokens)

    @pl.when(step < sources)
    def _():
        slot_map = map_ref[step]
        chosen = slot_map >= 0.0
        logits = dot_nt(wr_ref[...], x_ref[0])[0 : slot_map.shape[0]]
        logits = jnp.where(chosen, logits, MASKED)
        raised = jnp.exp(logits - jnp.max(logits, axis=0, keepdims=True))
        raised = jnp.where(chosen, raised, 0.0)
        gates = raised / jnp.sum(raised, axis=0, keepdims=True)
        pick = one_hot(step)
        wide = jnp.broadcast_to(gates[low : low + experts, None, :], (experts, SLOTS, tokens))
        gate_rows = jnp.sum(pick * wide.reshape(rows, tokens), axis=1, keepdims=True)
        pick = pick.astype(BF)
        here = pl.ds(pl.multiple_of(step * SLOTS, SLOTS), SLOTS)
        for e in range(experts):
            gate_s[e, here, :] = gate_rows[e * SLOTS : (e + 1) * SLOTS]
        for n in range(count):
            cols = slice(n * CHUNK, (n + 1) * CHUNK)
            got = dot_nn(pick, x_ref[0, :, cols]).astype(BF)
            xs[:, here, cols] = got.reshape(experts, SLOTS, CHUNK)
            got = dot_nn(pick, g_ref[0, :, cols]).astype(BF)
            gs[:, here, cols] = got.reshape(experts, SLOTS, CHUNK)

    @pl.when((step >= sources) & (step < sources + experts))
    def _():
        e = step - sources
        x = xs[e]
        w_gate = jnp.concatenate([wg0_ref[0], wg1_ref[0]], axis=1)
        w_up = jnp.concatenate([wu0_ref[0], wu1_ref[0]], axis=1)
        gate_pre = dot_nn(x, w_gate)
        up_pre = dot_nn(x, w_up)
        sig = jax.nn.sigmoid(gate_pre)
        silu = gate_pre * sig
        hidden = (silu * up_pre).astype(BF)
        gate = gate_s[e]
        d_hidden = jnp.zeros(hidden.shape, F32)
        d_gates = jnp.zeros(gate.shape, F32)
        for n in range(count):
            cols = slice(n * CHUNK, (n + 1) * CHUNK)
            w_down = jnp.concatenate([wd0_ref[0, :, cols], wd1_ref[0, :, cols]], axis=0)
            grad = gs[e, :, cols].astype(F32)
            d_y = (gate * grad).astype(BF)
            y = dot_nn(hidden, w_down)
            d_gates += jnp.sum(y * grad, axis=1, keepdims=True)
            gs[e, :, cols] = (gate * y).astype(BF)
            d_hidden += dot_nt(d_y, w_down)
            wide_s[:, cols] = dot_tn(hidden, d_y).astype(BF)
        gate_s[e] = d_gates
        d_gate = (d_hidden * up_pre * sig * (1.0 + gate_pre * (1.0 - sig))).astype(BF)
        d_up = (d_hidden * silu).astype(BF)

        y_at, zl_at, zh_at = place_ref[1], place_ref[2], place_ref[3]
        part = down_keep.shape[2]
        for z in range(2):
            base = (zh_at ^ z) * 2
            down_keep[z, 0] = wide_s[pl.ds(pl.multiple_of((base + y_at) * part, part), part), :]
            (down_send0, down_send1)[z][0] = wide_s[
                pl.ds(pl.multiple_of((base + (1 - y_at)) * part, part), part), :
            ]

        def spread(keep, send):
            part = keep.shape[3]
            for z in range(2):
                for low in range(2):
                    base = ((zh_at ^ z) * 2 + (zl_at ^ low)) * 2
                    keep[z, low, 0] = tall_s[
                        pl.ds(pl.multiple_of((base + y_at) * part, part), part), :
                    ]
                    send[z][low, 0] = tall_s[
                        pl.ds(pl.multiple_of((base + (1 - y_at)) * part, part), part), :
                    ]

        for n in range(count):
            cols = slice(n * CHUNK, (n + 1) * CHUNK)
            tall_s[cols, :] = dot_tn(x[:, cols], d_gate).astype(BF)
        spread(gate_keep, (gate_send0, gate_send1))
        for n in range(count):
            cols = slice(n * CHUNK, (n + 1) * CHUNK)
            tall_s[cols, :] = dot_tn(x[:, cols], d_up).astype(BF)
        spread(up_keep, (up_send0, up_send1))
        for n in range(count):
            cols = slice(n * CHUNK, (n + 1) * CHUNK)
            d_x = dot_nt(d_gate, w_gate[cols]) + dot_nt(d_up, w_up[cols])
            xs[e, :, cols] = d_x.astype(BF)

    def combine(source, mix_out, dx_out, mix_in, dx_in):
        def put(out, prior, cols, values):
            if prior is not None:
                values += prior[0, :, cols].astype(F32)
            out[0, :, cols] = values.astype(BF)

        here = pl.ds(pl.multiple_of(source * SLOTS, SLOTS), SLOTS)
        pick = one_hot(source).astype(BF)
        for n in range(count):
            cols = slice(n * CHUNK, (n + 1) * CHUNK)
            put(dx_out, dx_in, cols, dot_tn(pick, xs[:, here, cols].reshape(rows, CHUNK)))
            put(mix_out, mix_in, cols, dot_tn(pick, gs[:, here, cols].reshape(rows, CHUNK)))
        values = gate_s[:, here, :].reshape(rows, 1)
        column = lax.broadcasted_iota(jnp.int32, (rows, LANES), 1)
        owner = lax.broadcasted_iota(jnp.int32, (rows, LANES), 0) // SLOTS
        spread_out = jnp.where(column == owner + (place_ref[4] + low), values, 0.0).astype(BF)
        put(dx_out, dx_in, slice(WIDTH, WIDTH + LANES), dot_tn(pick, spread_out))

    @pl.when((step >= sources + experts) & (step < sources + experts + sources // 2))
    def _():
        source = step - experts - sources // 2
        prior = (None, None) if first else (mix_prior[1], dx_prior[1])
        combine(source, mix_send, dx_send, *prior)

    @pl.when(step >= sources + experts + sources // 2)
    def _():
        source = step - experts - sources - sources // 2
        prior = (None, None) if first else (mix_prior[0], dx_prior[0])
        combine(source, mix_keep, dx_keep, *prior)


def less(shape):
    return jax.ShapeDtypeStruct(shape.shape[1:], shape.dtype)


def run_experts(place, x_all, g_all, maps, wr_t, w_gate, w_up, w_down, prior=()):
    sources, tokens, width = x_all.shape
    experts = w_gate.shape[0] // 2
    low = experts if prior else 0
    ffe = w_gate.shape[2]
    part = ffe // 8
    quarter = width // 8
    half = ffe // 2
    slots = sources * SLOTS
    extra = width + LANES
    second = sources + experts
    third = second + sources // 2

    def at(i, low, size):
        return jnp.clip(i - low, 0, size - 1)

    def expert_of(i):
        return at(i, sources, experts)

    def w_cols(block):
        return pl.BlockSpec(
            (1, width, LANES), lambda i, p: (expert_of(i) + low, 0, p[0] + 2 * block)
        )

    def w_rows(block):
        return pl.BlockSpec(
            (1, LANES, width), lambda i, p: (expert_of(i) + low, p[0] + 2 * block, 0)
        )

    token_spec = pl.BlockSpec(
        (1, tokens, width),
        lambda i, p: (at(i, 0, sources), 0, 0),
    )

    def out_tokens(low, cols):
        return pl.BlockSpec((1, tokens, cols), lambda i, p: (at(i, low, sources // 2), 0, 0))

    tall_spec = pl.BlockSpec(
        (2, 2, 1, quarter, half), lambda i, p: (0, 0, expert_of(i), 0, 0)
    )
    wide_spec = pl.BlockSpec((2, 1, part, width), lambda i, p: (0, expert_of(i), 0, 0))
    tall_half = pl.BlockSpec((2, 1, quarter, half), lambda i, p: (0, expert_of(i), 0, 0))
    wide_half = pl.BlockSpec((1, part, width), lambda i, p: (expert_of(i), 0, 0))
    tall = jax.ShapeDtypeStruct((2, 2, experts, quarter, half), BF)
    wide = jax.ShapeDtypeStruct((2, experts, part, width), BF)
    mixed = jax.ShapeDtypeStruct((sources // 2, tokens, width), BF)
    d_x = jax.ShapeDtypeStruct((sources // 2, tokens, extra), BF)
    sums = (
        out_tokens(third, width),
        out_tokens(second, width),
        out_tokens(third, extra),
        out_tokens(second, extra),
    )
    return pl.pallas_call(
        functools.partial(expert_kernel, first=not prior),
        grid_spec=pltpu.PrefetchScalarGridSpec(
            num_scalar_prefetch=1,
            grid=(third + sources // 2,),
            in_specs=[
                token_spec,
                token_spec,
                pl.BlockSpec(maps.shape, lambda i, p: (0, 0, 0)),
                pl.BlockSpec(wr_t.shape, lambda i, p: (0, 0)),
                w_cols(0),
                w_cols(1),
                w_cols(0),
                w_cols(1),
                w_rows(0),
                w_rows(1),
                *(sums if prior else ()),
            ],
            out_specs=(
                *sums,
                tall_spec,
                tall_half,
                tall_half,
                tall_spec,
                tall_half,
                tall_half,
                wide_spec,
                wide_half,
                wide_half,
            ),
            scratch_shapes=[
                pltpu.VMEM((experts, slots, width), BF),
                pltpu.VMEM((experts, slots, width), BF),
                pltpu.VMEM((experts, slots, 1), F32),
                pltpu.VMEM((half, width), BF),
                pltpu.VMEM((width, half), BF),
            ],
        ),
        out_shape=(mixed, mixed, d_x, d_x)
        + (tall, less(tall), less(tall)) * 2
        + (wide, less(wide), less(wide)),
        compiler_params=params(60, ("arbitrary",)),
        cost_estimate=cost(30e9, 60e6),
    )(place, x_all, g_all, maps, wr_t, w_gate, w_gate, w_up, w_up, w_down, w_down, *prior)


def post_kernel(
    dx_ref,
    mid_ref,
    cot_ref,
    norm_ref,
    wr_ref,
    map_ref,
    gain_ref,
    wo_ref,
    datt_ref,
    dmid_ref,
    dlow_ref,
    dlog_ref,
    ggain_ref,
):
    middle = mid_ref[...]
    inv = lax.rsqrt(jnp.mean(middle * middle, axis=-1, keepdims=True) + EPS)
    chosen = map_ref[...] >= 0.0
    logits = jnp.where(chosen, dot_nn(norm_ref[...], wr_ref[...]), MASKED)
    raised = jnp.exp(logits - jnp.max(logits, axis=-1, keepdims=True))
    raised = jnp.where(chosen, raised, 0.0)
    gates = raised / jnp.sum(raised, axis=-1, keepdims=True)
    d_gates = dx_ref[:, WIDTH:]
    d_picked = gates * (d_gates - jnp.sum(gates * d_gates, axis=-1, keepdims=True))
    d_logits = d_picked.astype(BF)
    dlog_ref[...] = d_logits
    d_norm = dx_ref[:, :WIDTH] + dot_nt(d_logits, wr_ref[...])
    scaled = d_norm * gain_ref[...]
    ggain_ref[...] = jnp.sum(d_norm * middle * inv, axis=0, keepdims=True)
    d_mid = (
        cot_ref[...]
        + inv * scaled
        - middle * inv**3 * jnp.mean(middle * scaled, axis=-1, keepdims=True)
    )
    dmid_ref[...] = d_mid
    d_low = d_mid.astype(BF)
    dlow_ref[...] = d_low
    d_att = dot_nt(d_low, wo_ref[...]).astype(BF)
    for g in range(KV_HEADS):
        pack_heads(datt_ref.at[g], d_att[:, g * ROWS_Q : (g + 1) * ROWS_Q], d_att.shape[0])


def run_post(dx_sum, middle, cotangent, normed_two, wr_pad, map_rows, gain, w_output):
    tokens = middle.shape[0]
    return pl.pallas_call(
        post_kernel,
        out_shape=(
            jax.ShapeDtypeStruct((KV_HEADS, tokens * ROWS_Q // LANES, LANES), BF),
            jax.ShapeDtypeStruct((tokens, WIDTH), F32),
            jax.ShapeDtypeStruct((tokens, WIDTH), BF),
            jax.ShapeDtypeStruct((tokens, LANES), BF),
            jax.ShapeDtypeStruct((1, WIDTH), F32),
        ),
        compiler_params=params(60),
        cost_estimate=cost(2 * tokens * WIDTH * WIDTH, 14e6),
    )(dx_sum, middle, cotangent, normed_two, wr_pad, map_rows, gain[None], w_output)


def put_rows(place_ref, held, keep, send):
    part = keep.shape[1]
    for b in range(keep.shape[0]):
        own = (2 * b) ^ place_ref[5]
        keep[b] = held[pl.ds(pl.multiple_of(own * part, part), part), :]
        other = own ^ 1
        send[b] = held[pl.ds(pl.multiple_of(other * part, part), part), :]


def outgrad_kernel(place_ref, a_ref, b_ref, keep, send, held):
    held[...] = dot_tn(a_ref[...], b_ref[...]).astype(BF)
    put_rows(place_ref, held, keep, send)


def run_outgrad(place, left, right, blocks):
    tokens, rows = left.shape
    cols = right.shape[1]
    part = rows // blocks
    spec = pl.BlockSpec((blocks // 2, part, 256), lambda i, p: (0, 0, i))
    shape = jax.ShapeDtypeStruct((blocks // 2, part, cols), BF)
    return pl.pallas_call(
        outgrad_kernel,
        grid_spec=pltpu.PrefetchScalarGridSpec(
            num_scalar_prefetch=1,
            grid=(cols // 256,),
            in_specs=[
                pl.BlockSpec((tokens, rows), lambda i, p: (0, 0)),
                pl.BlockSpec((tokens, 256), lambda i, p: (0, i)),
            ],
            out_specs=(spec, spec),
            scratch_shapes=[pltpu.VMEM((rows, 256), BF)],
        ),
        out_shape=(shape, shape),
        compiler_params=params(60, ("arbitrary",)),
        cost_estimate=cost(2 * tokens * rows * cols, 8e6),
    )(place, left, right)


def qkvgrad_kernel(place_ref, a_ref, d_ref, full_ref, keep, send, held):
    step = pl.program_id(0)

    @pl.when(step == 0)
    def _():
        key_at = KV_HEADS * ROWS_Q
        value_at = key_at + KV_HEADS * HEAD_DIM
        for g in range(KV_HEADS):
            unpack_all(
                d_ref.at[g],
                full_ref,
                full_ref,
                full_ref,
                0,
                full_ref.shape[0],
                g * ROWS_Q,
                key_at + g * HEAD_DIM,
                value_at + g * HEAD_DIM,
            )

    cols = pl.ds(pl.multiple_of(step * 256, 256), 256)
    held[...] = dot_tn(a_ref[...], full_ref[:, cols]).astype(BF)
    put_rows(place_ref, held, keep, send)


def run_qkvgrad(place, normed, d_pack, blocks):
    tokens, rows = normed.shape
    cols = KV_HEADS * PACK
    part = rows // blocks
    spec = pl.BlockSpec((blocks // 2, part, 256), lambda i, p: (0, 0, i))
    shape = jax.ShapeDtypeStruct((blocks // 2, part, cols), BF)
    return pl.pallas_call(
        qkvgrad_kernel,
        grid_spec=pltpu.PrefetchScalarGridSpec(
            num_scalar_prefetch=1,
            grid=(cols // 256,),
            in_specs=[
                pl.BlockSpec((tokens, rows), lambda i, p: (0, 0)),
                pl.BlockSpec(d_pack.shape, lambda i, p: (0, 0, 0)),
            ],
            out_specs=(pl.BlockSpec((tokens, cols), lambda i, p: (0, 0)), spec, spec),
            scratch_shapes=[pltpu.VMEM((rows, 256), BF)],
        ),
        out_shape=(jax.ShapeDtypeStruct((tokens, cols), BF), shape, shape),
        compiler_params=params(60, ("arbitrary",)),
        cost_estimate=cost(2 * tokens * rows * cols, 12e6),
    )(place, normed, d_pack)


def last_kernel(d_ref, wq_ref, wk_ref, wv_ref, dmid_ref, hid_ref, gain_ref, out_ref, ggain_ref):
    key_at = KV_HEADS * ROWS_Q
    value_at = key_at + KV_HEADS * HEAD_DIM
    d_norm = dot_nt(d_ref[:, 0:key_at], wq_ref[...])
    d_norm += dot_nt(d_ref[:, key_at:value_at], wk_ref[...])
    d_norm += dot_nt(d_ref[:, value_at:], wv_ref[...])
    inputs = hid_ref[...]
    inv = lax.rsqrt(jnp.mean(inputs * inputs, axis=-1, keepdims=True) + EPS)
    scaled = d_norm * gain_ref[...]
    ggain_ref[...] = jnp.sum(d_norm * inputs * inv, axis=0, keepdims=True)
    out_ref[...] = (
        dmid_ref[...]
        + inv * scaled
        - inputs * inv**3 * jnp.mean(inputs * scaled, axis=-1, keepdims=True)
    )


def run_last(d_full, w_query, w_key, w_value, d_middle, inputs, gain):
    tokens = inputs.shape[0]
    return pl.pallas_call(
        last_kernel,
        out_shape=(
            jax.ShapeDtypeStruct((tokens, WIDTH), F32),
            jax.ShapeDtypeStruct((1, WIDTH), F32),
        ),
        compiler_params=params(60),
        cost_estimate=cost(2 * tokens * WIDTH * 2560, 16e6),
    )(d_full, w_query, w_key, w_value, d_middle, inputs, gain[None])


def small_kernel(place_ref, norm_ref, dlog_ref, gmlp_ref, gattn_ref, keep, send, held):
    columns = dot_tn(norm_ref[...], dlog_ref[...])
    lane = lax.broadcasted_iota(jnp.int32, columns.shape, 1)
    for n, ref in enumerate((gmlp_ref, gattn_ref)):
        turned = jnp.broadcast_to(ref[...], (8, ref.shape[1])).T[:, 0:1]
        columns = jnp.where(lane == LANES - 2 + n, turned, columns)
    held[...] = columns
    put_rows(place_ref, held, keep, send)


def run_small(place, normed_two, d_log, ggain_mlp, ggain_attn, blocks):
    part = WIDTH // blocks
    shape = jax.ShapeDtypeStruct((blocks // 2, part, LANES), F32)
    smem = pl.BlockSpec(memory_space=pltpu.SMEM)
    vmem = pl.BlockSpec(memory_space=pltpu.VMEM)
    return pl.pallas_call(
        small_kernel,
        in_specs=[smem] + [vmem] * 4,
        out_shape=(shape, shape),
        scratch_shapes=[pltpu.VMEM((WIDTH, LANES), F32)],
        compiler_params=params(60),
        cost_estimate=cost(1e8, 3e6),
    )(place, normed_two, d_log, ggain_mlp, ggain_attn)


def stack_swap(values, bit):
    return jnp.concatenate([values, swap_bit(values, bit)], axis=0)


MESH = pl.DeviceIdType.MESH
hbm = pl.BlockSpec(memory_space=pltpu.HBM)


def peer_of(bit):
    axis, mask = bit
    return {axis: lax.axis_index(axis) ^ mask}


def greet(ids):
    barrier = pltpu.get_barrier_semaphore()
    for device in ids:
        pl.semaphore_signal(barrier, inc=1, device_id=device, device_id_type=MESH)
    pl.semaphore_wait(barrier, len(ids))


GATHER_BITS = (X_BIT, ZL_BIT, C_BIT)


def gather_steps(x_ref, all_ref, send_sem, recv_sem, local_sem):
    half = x_ref.shape[0] // 2
    own = pltpu.make_async_copy(x_ref, all_ref.at[0], local_sem)
    own.start()
    copies = []

    def send(source, slot, rows, bit):
        n = len(copies)
        copy = pltpu.make_async_remote_copy(
            src_ref=source if rows is None else source.at[rows],
            dst_ref=all_ref.at[slot] if rows is None else all_ref.at[slot, rows],
            send_sem=send_sem.at[n],
            recv_sem=recv_sem.at[n],
            device_id=peer_of(bit),
            device_id_type=MESH,
        )
        copy.start()
        copies.append(copy)
        return copy

    top, low = pl.ds(0, half), pl.ds(half, half)
    x_top = send(x_ref, 1, top, X_BIT)
    z_low = send(x_ref, 2, low, ZL_BIT)
    x_low = send(x_ref, 1, low, X_BIT)
    z_top = send(x_ref, 2, top, ZL_BIT)
    last = [send(x_ref, 4, None, C_BIT)]
    x_top.wait_recv()
    far_top = send(all_ref.at[1], 3, top, ZL_BIT)
    z_low.wait_recv()
    far_low = send(all_ref.at[2], 3, low, X_BIT)
    x_low.wait_recv()
    last.append(send(all_ref.at[1], 5, None, C_BIT))
    z_top.wait_recv()
    last.append(send(all_ref.at[2], 6, None, C_BIT))
    far_top.wait_recv()
    far_low.wait_recv()
    last.append(send(all_ref.at[3], 7, None, C_BIT))
    for copy in last:
        copy.wait_recv()
    for copy in copies:
        copy.wait_send()
    own.wait()


def gather_kernel(x_ref, *refs):
    blocks, maps_ref = refs[0:4], refs[4]
    all_ref, other_ref, all_maps_ref = refs[5:8]
    send_sem, recv_sem, more_send, more_recv, local_sem = refs[8:]
    greet([peer_of(bit) for bit in GATHER_BITS])
    pairs = [(block, other_ref.at[n], other_ref.at[4 + n]) for n, block in enumerate(blocks)]
    pairs.append((maps_ref, all_maps_ref.at[pl.ds(0, 4)], all_maps_ref.at[pl.ds(4, 4)]))
    copies = []
    for n, (block, here, there) in enumerate(pairs):
        copy = pltpu.make_async_remote_copy(
            src_ref=block,
            dst_ref=there,
            send_sem=more_send.at[n],
            recv_sem=more_recv.at[n],
            device_id=peer_of(C_BIT),
            device_id_type=MESH,
        )
        copy.start()
        copies.append(copy)
        copy = pltpu.make_async_copy(block, here, local_sem.at[1 + n])
        copy.start()
        copies.append(copy)
    gather_steps(x_ref, all_ref, send_sem, recv_sem, local_sem.at[0])
    for copy in copies:
        copy.wait()


def run_gather(values, blocks, maps):
    shape = jax.ShapeDtypeStruct((8,) + values.shape, values.dtype)
    return pl.pallas_call(
        gather_kernel,
        in_specs=[pl.BlockSpec(memory_space=pltpu.VMEM)] * 6,
        out_specs=(hbm,) * 3,
        out_shape=(shape, shape, jax.ShapeDtypeStruct((8,) + maps.shape[1:], maps.dtype)),
        scratch_shapes=[pltpu.SemaphoreType.DMA((n,)) for n in (10, 10, 5, 5, 6)],
        compiler_params=pltpu.CompilerParams(
            collective_id=1, has_side_effects=True, vmem_limit_bytes=60 * MIB
        ),
        cost_estimate=cost(0, 150e6),
    )(values, *blocks, maps)


def trade_peers(size):
    me = lax.axis_index("dp")
    return [{"dp": me ^ k} for k in range(size - 1, 0, -1)]


def trade_start(a_ref, out_ref, send_sem, recv_sem, local_sem):
    me = lax.axis_index("dp")
    copies = []
    for n, device in enumerate(trade_peers(a_ref.shape[0])):
        copy = pltpu.make_async_remote_copy(
            src_ref=a_ref.at[device["dp"]],
            dst_ref=out_ref.at[me],
            send_sem=send_sem.at[n],
            recv_sem=recv_sem.at[n],
            device_id=device,
            device_id_type=MESH,
        )
        copy.start()
        copies.append(copy)
    own = pltpu.make_async_copy(a_ref.at[me], out_ref.at[me], local_sem)
    own.start()
    return copies, own


def trade_end(copies, own):
    own.wait()
    for copy in copies:
        copy.wait_recv()
    for copy in copies:
        copy.wait_send()


class Rider:
    def __init__(self, bit, *terms, pieces=1, turns=(0,)):
        self.bit, self.pieces, self.turns = bit, pieces, turns
        self.arrays = [term[0] if isinstance(term, tuple) else term for term in terms]
        self.parts = [term[1] if isinstance(term, tuple) else None for term in terms]
        array, part = self.arrays[0], self.parts[0]
        shape = array.shape
        if part is not None:
            kept = [len(range(n)[k]) for k, n in zip(part, shape) if not isinstance(k, int)]
            shape = tuple(kept) + shape[len(part) :]
        self.shape = jax.ShapeDtypeStruct(shape, array.dtype)
        self.direct = len(terms) == 1 and part is None

    def scratch(self):
        if self.direct:
            return []
        buffer = pltpu.VMEM(self.shape.shape, self.shape.dtype)
        return [buffer] * (len(self.arrays) + 1)

    def plan(self):
        return (self.bit, self.pieces, self.turns, tuple(self.parts), self.direct)


def rider_inputs(riders):
    return [array for rider in riders for array in rider.arrays]


def rider_shapes(riders):
    return tuple(rider.shape for rider in riders)


def rider_scratch(riders):
    remote = max(sum(rider.pieces for rider in riders), 1)
    local = max(sum(len(rider.arrays) for rider in riders), 1)
    buffers = [buffer for rider in riders for buffer in rider.scratch()]
    return buffers + [pltpu.SemaphoreType.DMA((n,)) for n in (remote, remote, local)]


def add_rows(result, buffers):
    step = 16

    @pl.loop(0, result.shape[1] // step)
    def _(r):
        rows = pl.ds(pl.multiple_of(r * step, step), step)
        for i in range(result.shape[0]):
            total = buffers[0][i, rows, :].astype(F32)
            for buffer in buffers[1:]:
                total += buffer[i, rows, :].astype(F32)
            result[i, rows, :] = total.astype(result.dtype)


def ride_pieces(sources, targets, plans, scratch):
    send_sem, recv_sem, local_sem = scratch[-3:]
    starts, finishes, loads, used, source, local = [], [], [], 0, 0, 0
    for n, (bit, pieces, turns, parts, direct) in enumerate(plans):
        arrays = sources[source : source + len(parts)]
        source += len(parts)
        if direct:
            held = arrays[0]
            prepare = None
        else:
            buffers = scratch[used : used + len(parts)]
            held = scratch[used + len(parts)]
            used += len(parts) + 1
            copies = []
            for array, part, buffer in zip(arrays, parts, buffers):
                view = array if part is None else array.at[part]
                copy = pltpu.make_async_copy(view, buffer, local_sem.at[local])
                local += 1
                loads.append(copy)
                copies.append(copy)

            def prepare(copies=copies, held=held, buffers=buffers):
                for copy in copies:
                    copy.wait()
                add_rows(held, buffers)

        size = targets[n].shape[0] // pieces
        for m in range(pieces):
            at = pl.ds(m * size, size)

            def remote(n=n, at=at, slot=len(starts), bit=bit, held=held):
                return pltpu.make_async_remote_copy(
                    src_ref=held.at[at],
                    dst_ref=targets[n].at[at],
                    send_sem=send_sem.at[slot],
                    recv_sem=recv_sem.at[slot],
                    device_id=peer_of(bit),
                    device_id_type=MESH,
                )

            def start(remote=remote):
                remote().start()

            def finish(remote=remote):
                remote().wait()

            starts.append((prepare if m == 0 else None, start, turns))
            finishes.append(finish)
    return starts, finishes, loads


def all_peers(bits):
    size = lax.axis_size("dp")
    return trade_peers(size) + [peer_of(bit) for bit in bits if bit[0] == "expert"]


def trade_kernel(*refs, plans):
    inputs = sum(len(plan[3]) for plan in plans)
    a_ref, sources = refs[0], refs[1 : 1 + inputs]
    out_ref, targets = refs[1 + inputs], refs[2 + inputs : 2 + inputs + len(plans)]
    send_sem, recv_sem, local_sem, *scratch = refs[2 + inputs + len(plans) :]
    greet(all_peers(sorted({plan[0] for plan in plans})))
    trade = trade_start(a_ref, out_ref, send_sem, recv_sem, local_sem.at[0])
    starts, finishes, loads = ride_pieces(sources, targets, plans, scratch)
    for load in loads:
        load.start()
    for prepare, start, _ in starts:
        if prepare is not None:
            prepare()
        start()
    trade_end(*trade)
    for finish in finishes:
        finish()


def run_trade(values, number, riders=()):
    size = values.shape[0]
    inputs = rider_inputs(riders)
    out = pl.pallas_call(
        functools.partial(trade_kernel, plans=tuple(rider.plan() for rider in riders)),
        in_specs=[hbm] * (1 + len(inputs)),
        out_specs=(hbm,) * (1 + len(riders)),
        out_shape=(jax.ShapeDtypeStruct(values.shape, values.dtype),) + rider_shapes(riders),
        scratch_shapes=[pltpu.SemaphoreType.DMA((n,)) for n in (size - 1, size - 1, 1)]
        + rider_scratch(riders),
        compiler_params=pltpu.CompilerParams(
            collective_id=number, has_side_effects=True, vmem_limit_bytes=60 * MIB
        ),
        cost_estimate=cost(0, 170e6),
    )(values, *inputs)
    return out if riders else out[0]


def first_kernel(a_ref, rank_ref, turned_ref, out_ref, slot_ref, send_sem, recv_sem, local_sem, *, far):
    greet(trade_peers(a_ref.shape[0]))
    trade = trade_start(a_ref, out_ref, send_sem, recv_sem, local_sem.at[0])
    for e in range(rank_ref.shape[0]):
        own = rank_ref[e : e + 1, :]
        smaller = (turned_ref[:, e : e + 1] < own).astype(F32)
        before = jnp.sum(smaller, axis=0, keepdims=True)
        slot_ref[e : e + 1, :] = jnp.where(own < far, jnp.minimum(before, SLOTS), -1.0)
    trade_end(*trade)


def run_first(values, rank_map, turned, far):
    size = values.shape[0]
    vmem = pl.BlockSpec(memory_space=pltpu.VMEM)
    return pl.pallas_call(
        functools.partial(first_kernel, far=far),
        in_specs=[hbm, vmem, vmem],
        out_specs=(hbm, vmem),
        out_shape=(
            jax.ShapeDtypeStruct(values.shape, values.dtype),
            jax.ShapeDtypeStruct(rank_map.shape, F32),
        ),
        scratch_shapes=[pltpu.SemaphoreType.DMA((n,)) for n in (size - 1, size - 1, 1)],
        compiler_params=pltpu.CompilerParams(
            collective_id=2, has_side_effects=True, vmem_limit_bytes=60 * MIB
        ),
        cost_estimate=cost(0, 170e6),
    )(values, rank_map, turned)


def reduce_chain(slot, part, keep_ref, send_ref, outs, acc, got, staged, send_sem, recv_sem):
    first, bits, row, rows, column, columns, order = part
    blocks = keep_ref.shape[0]
    stages = len(bits) + 1
    low = send_ref.dtype
    at = (pl.ds(row, rows), pl.ds(column, columns))
    copies = []

    def exchange(source, target, bit):
        n = slot + len(copies)
        copy = pltpu.make_async_remote_copy(
            src_ref=source,
            dst_ref=target,
            send_sem=send_sem.at[n],
            recv_sem=recv_sem.at[n],
            device_id=peer_of(bit),
            device_id_type=MESH,
        )
        copy.start()
        copies.append(copy)

    live = list(range(blocks))
    base_got, base_sent = 0, 0
    exchange(send_ref.at[(slice(None),) + at], got.at[(pl.ds(0, blocks),) + at], first)
    yield
    for stage in range(stages):
        copies[-1].wait_recv()

        def total(position):
            index = live[position]
            kept = keep_ref[(index,) + at].astype(F32) if stage == 0 else acc[(index,) + at]
            return kept + got[(base_got + position,) + at].astype(F32)

        if stage == stages - 1:
            low_column = 0
            for out_ref in outs:
                if low_column <= column < low_column + out_ref.shape[1]:
                    out_ref[at[0], pl.ds(column - low_column, columns)] = total(0)
                low_column += out_ref.shape[1]
            break
        mask = 1 << order[stage]
        rest = [i for i in live if not i & mask]
        for m, i in enumerate(rest):
            staged[(base_sent + m,) + at] = total(live.index(i ^ mask)).astype(low)
        exchange(
            staged.at[(pl.ds(base_sent, len(rest)),) + at],
            got.at[(pl.ds(base_got + len(live), len(rest)),) + at],
            bits[order[stage]],
        )
        for i in rest:
            acc[(i,) + at] = total(live.index(i))
        base_got += len(live)
        base_sent += len(rest)
        live = rest
        yield
    for copy in copies:
        copy.wait_send()


def reduce_kernel(*refs, jobs, plans):
    size = len(jobs)
    inputs = sum(len(plan[3]) for plan in plans)
    keeps, sends, sources = refs[:size], refs[size : 2 * size], refs[2 * size : 2 * size + inputs]
    refs = refs[2 * size + inputs :]
    outs = []
    for _, _, _, widths in jobs:
        outs.append(refs[: len(widths)])
        refs = refs[len(widths) :]
    targets, scratch = refs[: len(plans)], refs[len(plans) :]
    send_sem, recv_sem = scratch[3 * size : 3 * size + 2]
    used = {bit for first, bits, *_ in jobs for bit in (first,) + bits}
    used |= {plan[0] for plan in plans}
    starts, finishes, loads = ride_pieces(sources, targets, plans, scratch[3 * size + 2 :])
    for load in loads:
        load.start()
    greet([peer_of(bit) for bit in sorted(used)])
    chains, slot = [], 0
    for n, (first, bits, parts, _) in enumerate(jobs):
        for part in parts:
            chains.append(
                reduce_chain(
                    slot,
                    (first, bits) + part,
                    keeps[n],
                    sends[n],
                    outs[n],
                    *scratch[3 * n : 3 * n + 3],
                    send_sem,
                    recv_sem,
                )
            )
            slot += len(bits) + 1
    index = lax.axis_index("dp")
    outer = (index // BIT_ZH) % 2 == (index // BIT_ZL) % 2
    turn, last = 0, max([0] + [n for _, _, turns in starts for n in turns])
    while chains or turn <= last:
        rest = []
        for chain in chains:
            try:
                next(chain)
                rest.append(chain)
            except StopIteration:
                pass
        chains = rest
        for prepare, start, turns in starts:
            if prepare is not None and min(turns) == turn:
                prepare()
            if len(set(turns)) == 1:
                if turns[0] == turn:
                    start()
            else:
                for n, side in enumerate((outer, jnp.logical_not(outer))):
                    if turns[n] == turn:
                        pl.when(side)(start)
        turn += 1
    for finish in finishes:
        finish()


def run_reduce(pairs, jobs, number, riders=()):
    slots = sum(len(parts) * (len(bits) + 1) for _, bits, parts, _ in jobs)
    vmem = pl.BlockSpec(memory_space=pltpu.VMEM)
    scratch, shapes = [], []
    for (keep, send), (_, _, _, widths) in zip(pairs, jobs):
        blocks, rows, cols = keep.shape
        scratch += [
            pltpu.VMEM((blocks, rows, cols), F32),
            pltpu.VMEM((2 * blocks - 1, rows, cols), send.dtype),
            pltpu.VMEM((max(blocks - 1, 1), rows, cols), send.dtype),
        ]
        shapes += [jax.ShapeDtypeStruct((rows, width), F32) for width in widths]
    inputs = rider_inputs(riders)
    return pl.pallas_call(
        functools.partial(reduce_kernel, jobs=jobs, plans=tuple(rider.plan() for rider in riders)),
        in_specs=[vmem] * len(pairs) + [hbm] * (len(pairs) + len(inputs)),
        out_specs=(vmem,) * len(shapes) + (hbm,) * len(riders),
        out_shape=tuple(shapes) + rider_shapes(riders),
        scratch_shapes=scratch
        + [pltpu.SemaphoreType.DMA((n,)) for n in (slots, slots)]
        + rider_scratch(riders),
        compiler_params=pltpu.CompilerParams(
            collective_id=number, has_side_effects=True, vmem_limit_bytes=60 * MIB
        ),
        cost_estimate=cost(0, 170e6),
    )(*(keep for keep, _ in pairs), *(send for _, send in pairs), *inputs)


def sum_pair(kept, received):
    return kept.astype(F32) + received.astype(F32)


def add_low(*terms):
    return sum(term.astype(F32) for term in terms).astype(BF)


def join_kernel(place_ref, *refs):
    outs = refs[-3:]
    zl_at = place_ref[0]

    def total(*terms):
        return sum(term.astype(F32) for term in terms)

    def flat(ref):
        return ref[(0,) * (ref.ndim - 2)]

    def work(parts, part):
        for n in range(2):
            keep, got, more, other = parts[4 * n : 4 * n + 4]
            mine = total(*(flat(term) for term in (keep, got, more)))
            across = flat(other).astype(F32)
            for m in range(2):
                cols = slice(m * LANES, (m + 1) * LANES)
                at = pl.multiple_of((2 * m + zl_at) * LANES, LANES)
                outs[n][part, 0, :, pl.ds(at, LANES)] = mine[:, cols]
                at = pl.multiple_of((2 * m + 1 - zl_at) * LANES, LANES)
                outs[n][part, 0, :, pl.ds(at, LANES)] = across[:, cols]
        keep, got, more = parts[8:]
        outs[2][part, 0] = total(*(flat(term) for term in (keep, got, more)))

    work(refs[0:11], 0)
    work(refs[11:22], 1)


def run_join(place, halves):
    _, _, experts, rows, cols = halves[0][0].shape
    wide_rows, width = halves[0][8].shape[2:]
    arrays, specs = [], []
    for half in halves:
        for operand in half:
            array, lead = operand if isinstance(operand, tuple) else (operand, 0)
            extra = array.ndim - 3
            at = (lead,) + (0,) * (extra - 1) if extra else ()
            arrays.append(array)
            specs.append(
                pl.BlockSpec(
                    (1,) * (extra + 1) + array.shape[-2:],
                    lambda i, p, at=at: at + (i, 0, 0),
                )
            )
    shapes = [(rows, 2 * cols), (rows, 2 * cols), (wide_rows, width)]
    return pl.pallas_call(
        join_kernel,
        grid_spec=pltpu.PrefetchScalarGridSpec(
            num_scalar_prefetch=1,
            grid=(experts,),
            in_specs=specs,
            out_specs=tuple(
                pl.BlockSpec((2, 1) + shape, lambda i, p: (0, i, 0, 0)) for shape in shapes
            ),
        ),
        out_shape=tuple(jax.ShapeDtypeStruct((2, experts) + shape, F32) for shape in shapes),
        compiler_params=params(60, ("arbitrary",)),
        cost_estimate=cost(1e6, 26e6),
    )(place, *arrays)


def fast_body(
    hidden_in,
    gain_attn,
    w_query,
    w_key,
    w_value,
    w_output,
    gain_mlp,
    w_router,
    w_gate,
    w_up,
    w_down,
    expert_ids,
    slot_order,
    grad_out,
):
    inputs = hidden_in[0]
    cotangent = grad_out[0]
    chosen = expert_ids[0]
    tokens = inputs.shape[0]
    top = chosen.shape[1]
    local_experts = w_gate.shape[0]
    peers = lax.axis_size("expert")
    all_experts = local_experts * peers
    shards = lax.axis_size("dp")
    length = shards * tokens
    devices = shards * peers
    index = lax.axis_index("dp")
    column = lax.axis_index("expert")
    y_at = index % 2
    zl_at = (index // 2) % 2
    zh_at = index // 4
    place = jnp.stack(
        [zl_at, y_at, zl_at, zh_at, column * local_experts, index * peers + column]
    ).astype(jnp.int32)

    ranks = slot_order[0, 0].reshape(tokens, top)
    far = tokens * top
    names = jnp.arange(all_experts, dtype=jnp.int32)
    match = chosen.T[None] == names[:, None, None]
    rank_map = jnp.min(jnp.where(match, ranks.T[None], far), axis=1).astype(F32)
    turned = rank_map.T
    map_rows = jnp.pad(
        jnp.where(turned < far, 0.0, -1.0),
        ((0, 0), (0, LANES - all_experts)),
        constant_values=-1.0,
    )
    wr_pad = jnp.pad(w_router, ((0, 0), (0, LANES - all_experts)))
    wr_t = jnp.roll(w_router.T, -column * local_experts, axis=0)
    wr_t = jnp.pad(wr_t, ((0, LANES - all_experts), (0, 0)))

    half = HEAD_DIM // 2
    frequency = jnp.exp(-math.log(10000.0) * jnp.arange(half, dtype=F32) * 2.0 / HEAD_DIM)
    own_angles = (index * tokens + jnp.arange(tokens, dtype=jnp.int32)).astype(F32)[:, None] * frequency
    cos_own, sin_own = jnp.cos(own_angles), jnp.sin(own_angles)
    cos_tab = jnp.concatenate([cos_own] * 4, axis=1)
    sin_tab = jnp.concatenate([-sin_own, sin_own] * 2, axis=1)
    angles = frequency[:, None] * jnp.arange(length, dtype=jnp.int32).astype(F32)[None]
    cos_t, sin_t = jnp.cos(angles), jnp.sin(angles)

    normed, pack, g_own = run_pre(
        inputs, gain_attn, w_query, w_key, w_value, cos_tab, sin_tab, cotangent
    )
    pack, slot_map = run_first(pack, rank_map, turned, float(far))
    pack, slot_map, g_late = fence(pack, slot_map, g_own)
    g_x = swap_bit(g_own, X_BIT)
    g_z = swap_bit(g_late, ZL_BIT)
    maps = stack_swap(slot_map[None], X_BIT)
    out, out_t, lse = run_forward(pack)
    out, g_x, g_z, maps = fence(out, g_x, g_z, maps)
    g_zx = swap_bit(g_z, X_BIT)
    maps = stack_swap(maps, ZL_BIT)
    att = run_trade(out, 3)
    att, g_zx, maps = fence(att, g_zx, maps)
    middle, normed_two, att_full = run_mid(att, w_output, inputs, gain_mlp)
    x_all, g_all, maps = run_gather(normed_two, (g_own, g_x, g_z, g_zx), maps)
    maps = jnp.roll(maps, -column * local_experts, axis=1)
    expert_args = (place, x_all, g_all, maps, wr_t, w_gate, w_up, w_down)
    first = run_experts(*expert_args)
    gate_ka, gate_s0, gate_s1, up_ka, up_s0, up_s1, down_ka, down_s0, down_s1 = first[4:]
    down_ya = swap_bit(down_s1, Y_BIT)
    gate_ya = swap_bit(gate_s1, Y_BIT)
    early = swap_bit(jnp.stack([gate_ka[1, 1], gate_s1[1]]), ZH_BIT)
    mix_keep, mix_send, dx_keep, dx_send, *second = run_experts(*expert_args, prior=first[:4])
    gate_kb, gate_t0, gate_t1, up_kb, up_t0, up_t1, down_kb, down_t0, down_t1 = second
    dx_send, down_ya, gate_ya, early = fence(dx_send, down_ya, gate_ya, early)
    gate_s0 = jnp.stack([gate_s0[0], add_low(gate_s0[1], early[1])])
    quarter = tokens // 4
    extra = dx_keep.shape[2]
    token_parts = tuple(
        (n * quarter, quarter, 0, extra, (1, 0) if n < 2 else (0, 1)) for n in (2, 0, 3, 1)
    )
    dx_sum, up_ya, gate_ga, mix_got, down_ma = run_reduce(
        ((dx_keep, dx_send),),
        ((C_BIT, (X_BIT, ZL_BIT), token_parts, (extra,)),),
        6,
        riders=(
            Rider(Y_BIT, up_s1),
            Rider(Y_BIT, gate_s0),
            Rider(C_BIT, mix_send, turns=(1,)),
            Rider(ZH_BIT, (down_ka, (1,)), down_ya, turns=(1, 0)),
        ),
    )
    dx_sum, gate_ya, down_s0, gate_t1 = fence(dx_sum, gate_ya, down_s0, gate_t1)
    gate_ma = swap_bit(add_low(gate_ka[1, 0], gate_ya[0]), ZH_BIT)
    gate_yb = swap_bit(gate_t1, Y_BIT)
    d_att, d_middle, d_low, d_log, ggain_mlp = run_post(
        dx_sum, middle, cotangent, normed_two, wr_pad, map_rows, gain_mlp, w_output
    )
    out_keep, out_send = run_outgrad(place, att_full, d_low, devices)
    d_att, out_send, gate_ma, gate_yb = fence(d_att, out_send, gate_ma, gate_yb)
    mix_keep = mix_keep.reshape(2, 2, tokens, WIDTH)
    mix_got = mix_got.reshape(2, 2, tokens, WIDTH)
    every = slice(None)
    d_out, up_yb, down_ga, out_got, up_za, gate_oa, mix_x = run_trade(
        d_att,
        4,
        riders=(
            Rider(Y_BIT, up_t1),
            Rider(Y_BIT, down_s0),
            Rider(C_BIT, out_send),
            Rider(ZH_BIT, (up_ka, (1, 1)), (up_ya, (1,))),
            Rider(ZL_BIT, (gate_ka, (0, 1)), (early, (0,)), (gate_ga, (1,))),
            Rider(X_BIT, (mix_keep, (every, 1)), (mix_got, (every, 1))),
        ),
    )
    split = (8, 2, WIDTH // devices, WIDTH)
    out_keep, out_got = out_keep.reshape(split), out_got.reshape(split)
    up_ga, down_yb, up_late, gate_late, _ = fence(up_s0, down_t1, up_ya, gate_yb, d_out)
    both = jnp.stack([add_low(up_ka[1, 0], up_late[0]), add_low(gate_kb[1, 1], gate_late[1])])
    both = swap_bit(both, ZH_BIT)
    up_ga = swap_bit(up_ga, Y_BIT)
    down_yb = swap_bit(down_yb, Y_BIT)
    d_pack = run_backward(pack, d_out, out_t, lse, cos_t, sin_t)
    d_pack, both, up_ga, down_yb = fence(d_pack, both, up_ga, down_yb)
    d_pack, gate_gb, up_gb, gate_mb, up_zb, mix_z, out_x, up_oa = run_trade(
        d_pack,
        5,
        riders=(
            Rider(Y_BIT, gate_t0),
            Rider(Y_BIT, up_t0),
            Rider(ZH_BIT, (gate_kb, (1, 0)), (gate_yb, (0,))),
            Rider(ZH_BIT, (up_kb, (1, 1)), (up_yb, (1,))),
            Rider(
                ZL_BIT,
                (mix_keep, (slice(1, 2), 0)),
                (mix_got, (slice(1, 2), 0)),
                (mix_x, (slice(1, 2),)),
            ),
            Rider(X_BIT, (out_keep, (every, 1)), (out_got, (every, 1))),
            Rider(ZL_BIT, (up_ka, (0, 1)), (up_ga, (1,)), (up_za, (every,))),
        ),
    )
    d_pack, up_yb, down_yb, gate_gb, down_t0, mix_z, out_x = fence(
        d_pack, up_yb, down_yb, gate_gb, down_t0, mix_z, out_x
    )
    other = jnp.stack(
        [add_low(gate_kb[0, 1], gate_gb[1], both[1]), add_low(up_kb[0, 1], up_gb[1], up_zb)]
    )
    other = swap_bit(other, ZL_BIT)
    down_mb = swap_bit(add_low(down_kb[1], down_yb), ZH_BIT)
    down_gb = swap_bit(down_t0, Y_BIT)
    d_full, qkv_keep, qkv_send = run_qkvgrad(place, normed, d_pack, devices)
    grad_in, ggain_attn = run_last(
        d_full, w_query, w_key, w_value, d_middle, inputs, gain_attn
    )
    small_keep, small_send = run_small(place, normed_two, d_log, ggain_mlp, ggain_attn, devices)
    mixed = sum_pair(mix_keep[0, 0], mix_got[0, 0]) + sum_pair(mix_x[0], mix_z[0])
    hidden_out = middle + mixed
    rows = WIDTH // devices
    out_held = add_low(out_keep[:, 0], out_got[:, 0], out_x).reshape(4, 2, rows, WIDTH)
    out_first, out_second = out_held[:, 0], out_held[:, 1]
    qkv_send, small_send, out_second, hidden_out = fence(
        qkv_send, small_send, out_second, hidden_out
    )
    qkv_parts = (
        (0, rows, 0, 768, (0, 1, 2, 3)),
        (0, rows, 768, 768, (1, 0, 2, 3)),
        (0, rows, 1536, 512, (0, 1, 2, 3)),
        (0, rows, 2048, 512, (1, 0, 2, 3)),
    )
    dense_bits = (X_BIT, Y_BIT, ZL_BIT, ZH_BIT)
    query_total, key_total, value_total, small, output_total, up_mb = run_reduce(
        ((qkv_keep, qkv_send), (small_keep, small_send), (out_first, out_second)),
        (
            (C_BIT, dense_bits, qkv_parts, (WIDTH, KV_HEADS * HEAD_DIM, KV_HEADS * HEAD_DIM)),
            (C_BIT, dense_bits, ((0, rows, 0, LANES, (0, 1, 2, 3)),), (LANES,)),
            (Y_BIT, (ZL_BIT, ZH_BIT), ((0, rows, 0, WIDTH, (0, 1)),), (WIDTH,)),
        ),
        7,
        riders=(Rider(ZH_BIT, (up_kb, (1, 0)), (up_yb, (0,))),),
    )
    query_total, small, down_mb, down_gb, other = fence(
        query_total, small, down_mb, down_gb, other
    )
    joined = run_join(
        place,
        (
            (gate_ka, gate_ga, gate_ma, gate_oa, up_ka, up_ga, (both, 0), up_oa)
            + (down_ka, down_ga, down_ma),
            (gate_kb, gate_gb, gate_mb, (other, 0), up_kb, up_gb, up_mb, (other, 1))
            + (down_kb, down_gb, down_mb),
        ),
    )
    gate_total, up_total, down_total = [
        total.reshape((local_experts,) + total.shape[2:]) for total in joined
    ]
    return (
        hidden_out[None],
        grad_in[None],
        small[:, LANES - 1],
        query_total,
        key_total,
        value_total,
        output_total,
        small[:, LANES - 2],
        small[:, :all_experts],
        gate_total,
        up_total,
        down_total,
    )


def fits(mesh):
    return mesh.shape["dp"] == KV_HEADS and mesh.shape["expert"] == 4


def solution(mesh):
    in_specs = (
        P("expert", "dp", None),
        P(),
        P(),
        P(),
        P(),
        P(),
        P(),
        P(),
        P("expert", None, None),
        P("expert", None, None),
        P("expert", None, None),
        P("expert", "dp", None),
        P("expert", "dp", None),
        P("expert", "dp", None),
    )
    out_specs = (
        P("expert", "dp", None),
        P("expert", "dp", None),
        P(("dp", "expert")),
        P(("dp", "expert"), None),
        P(("dp", "expert"), None),
        P(("dp", "expert"), None),
        P(("dp", "expert"), None),
        P(("dp", "expert")),
        P(("dp", "expert"), None),
        P("expert", "dp", None),
        P("expert", "dp", None),
        P("expert", "dp", None),
    )
    chosen = fast_body if fits(mesh) else body
    return jax.shard_map(chosen, mesh=mesh, in_specs=in_specs, out_specs=out_specs, check_vma=False)
```

```python
import functools
import math

import jax
import jax.numpy as jnp
from jax import lax
from jax.experimental import pallas as pl
from jax.experimental.pallas import tpu as pltpu
from jax.sharding import PartitionSpec as P

HEADS = 24
KV_HEADS = 8
HEAD_DIM = 64


EPS = 1e-05
MASKED = -1e30


def rotary_tables(positions):
    half = HEAD_DIM // 2
    frequency = jnp.exp(-math.log(10000.0) * jnp.arange(half, dtype=jnp.float32) * 2.0 / HEAD_DIM)
    angles = positions.astype(jnp.float32)[:, None] * frequency[None, :]
    return (jnp.cos(angles)[:, None, :], jnp.sin(angles)[:, None, :])


def rotate(values, cosine, sine):
    half = values.shape[-1] // 2
    first = values[..., :half]
    second = values[..., half:]
    return jnp.concatenate(
        [first * cosine - second * sine, second * cosine + first * sine], axis=-1
    )


def rotate_back(values, cosine, sine):
    half = values.shape[-1] // 2
    first = values[..., :half]
    second = values[..., half:]
    return jnp.concatenate(
        [first * cosine + second * sine, second * cosine - first * sine], axis=-1
    )


def assign_slots(row_chosen, row_ranks, all_experts, capacity):
    pairs = row_chosen.shape[0]
    by_rank = jnp.zeros((pairs,), jnp.int32).at[row_ranks].set(jnp.arange(pairs, dtype=jnp.int32))
    ordered = row_chosen[by_rank]
    table = (ordered[:, None] == jnp.arange(all_experts, dtype=jnp.int32)[None, :]).astype(
        jnp.int32
    )
    before = jnp.sum(table * (jnp.cumsum(table, axis=0) - 1), axis=1)
    slot = before[row_ranks]
    target = jnp.where(slot < capacity, row_chosen * capacity + slot, all_experts * capacity)
    owner = (
        jnp.full((all_experts * capacity,), pairs, jnp.int32)
        .at[target]
        .set(jnp.arange(pairs, dtype=jnp.int32), mode="drop")
    )
    return (target, owner)


def body(
    hidden_in,
    gain_attn,
    w_query,
    w_key,
    w_value,
    w_output,
    gain_mlp,
    w_router,
    w_gate,
    w_up,
    w_down,
    expert_ids,
    slot_order,
    grad_out,
):
    inputs = hidden_in[0]
    cotangent = grad_out[0]
    chosen = expert_ids[0]
    tokens, width = inputs.shape
    top = chosen.shape[1]
    local_experts = w_gate.shape[0]
    peers = lax.axis_size("expert")
    all_experts = local_experts * peers
    pairs = tokens * top
    capacity = pairs // all_experts
    shards = lax.axis_size("dp")
    index = lax.axis_index("dp")
    length = shards * tokens
    block = math.gcd(length, 512)
    groups = HEADS // KV_HEADS
    scale = HEAD_DIM ** (-0.5)
    query_pos = index * tokens + jnp.arange(tokens, dtype=jnp.int32)
    cosine, sine = rotary_tables(query_pos)
    count = ((index + 1) * tokens + block - 1) // block
    inv_one = lax.rsqrt(jnp.mean(inputs * inputs, axis=-1, keepdims=True) + EPS)
    normed = (inputs * inv_one * gain_attn).astype(jnp.bfloat16)
    query_pre = jnp.dot(normed, w_query, preferred_element_type=jnp.float32).reshape(
        tokens, HEADS, HEAD_DIM
    )
    queries = rotate(query_pre, cosine, sine).astype(jnp.bfloat16)
    key_pre = jnp.dot(normed, w_key, preferred_element_type=jnp.float32).reshape(
        tokens, KV_HEADS, HEAD_DIM
    )
    keys_low = rotate(key_pre, cosine, sine).astype(jnp.bfloat16)
    values_low = (
        jnp.dot(normed, w_value, preferred_element_type=jnp.float32)
        .astype(jnp.bfloat16)
        .reshape(tokens, KV_HEADS, HEAD_DIM)
    )
    keys_all, values_all = (
        lax.all_gather(keys_low, "dp", axis=0, tiled=True),
        lax.all_gather(values_low, "dp", axis=0, tiled=True),
    )
    query_groups = queries.reshape(tokens, KV_HEADS, groups, HEAD_DIM)

    def block_scores(key_block, start):
        raw = (
            jnp.einsum(
                "qkgd,skd->kgqs", query_groups, key_block, preferred_element_type=jnp.float32
            )
            * scale
        )
        key_pos = start + jnp.arange(block, dtype=jnp.int32)
        allowed = key_pos[None, :] <= query_pos[:, None]
        return jnp.where(allowed, raw, MASKED)

    def stats_step(step, carry):
        running, total = carry
        scores = block_scores(
            lax.dynamic_slice_in_dim(keys_all, step * block, block, 0), step * block
        )
        newest = jnp.maximum(running, jnp.max(scores, axis=-1))
        total = total * jnp.exp(running - newest) + jnp.sum(
            jnp.exp(scores - newest[..., None]), axis=-1
        )
        return (newest, total)

    stat_init = (
        jnp.full((KV_HEADS, groups, tokens), MASKED, jnp.float32),
        jnp.zeros((KV_HEADS, groups, tokens), jnp.float32),
    )
    running, total = lax.fori_loop(0, count, stats_step, stat_init)
    log_total = running + jnp.log(total)

    def output_step(step, accum):
        start = step * block
        scores = block_scores(lax.dynamic_slice_in_dim(keys_all, start, block, 0), start)
        probs = jnp.exp(scores - log_total[..., None]).astype(jnp.bfloat16)
        value_block = lax.dynamic_slice_in_dim(values_all, start, block, 0)
        return accum + jnp.einsum(
            "kgqs,skd->qkgd", probs, value_block, preferred_element_type=jnp.float32
        )

    attended_groups = lax.fori_loop(
        0, count, output_step, jnp.zeros((tokens, KV_HEADS, groups, HEAD_DIM), jnp.float32)
    )
    attended = attended_groups.reshape(tokens, HEADS * HEAD_DIM)
    attended_low = attended.astype(jnp.bfloat16)
    branch = jnp.dot(attended_low, w_output, preferred_element_type=jnp.float32)
    middle = inputs + branch
    inv_two = lax.rsqrt(jnp.mean(middle * middle, axis=-1, keepdims=True) + EPS)
    normed_two = (middle * inv_two * gain_mlp).astype(jnp.bfloat16)
    logits = jnp.dot(normed_two, w_router, preferred_element_type=jnp.float32)
    onehot = (chosen[:, :, None] == jnp.arange(all_experts, dtype=jnp.int32)[None, None, :]).astype(
        jnp.float32
    )
    picked = jnp.sum(onehot * logits[:, None, :], axis=-1)
    gates = jax.nn.softmax(picked, axis=-1)
    target, owner = assign_slots(chosen.reshape(pairs), slot_order[0, 0], all_experts, capacity)
    valid = owner < pairs
    source = jnp.minimum(owner, pairs - 1)
    rows_send = jnp.where(valid[:, None], normed_two[source // top], 0).reshape(
        peers, local_experts, capacity, width
    )
    received = lax.all_to_all(rows_send, "expert", split_axis=0, concat_axis=0, tiled=True)
    gate_pre = jnp.einsum("necd,edf->necf", received, w_gate, preferred_element_type=jnp.float32)
    up_pre = jnp.einsum("necd,edf->necf", received, w_up, preferred_element_type=jnp.float32)
    hidden = (jax.nn.silu(gate_pre) * up_pre).astype(jnp.bfloat16)
    result = jnp.einsum(
        "necf,efd->necd", hidden, w_down, preferred_element_type=jnp.float32
    ).astype(jnp.bfloat16)
    returned = lax.all_to_all(result, "expert", split_axis=0, concat_axis=0, tiled=True)
    returned, received, gate_pre, up_pre = (returned, received, gate_pre, up_pre)
    zero_row = jnp.zeros((1, width), jnp.bfloat16)
    pair_out = jnp.concatenate([returned.reshape(all_experts * capacity, width), zero_row], axis=0)[
        target
    ].reshape(tokens, top, width)
    mixed = jnp.einsum("tk,tkd->td", gates, pair_out, preferred_element_type=jnp.float32)
    hidden_out = middle + mixed
    dy_pairs = (
        (gates[:, :, None] * cotangent[:, None, :]).astype(jnp.bfloat16).reshape(pairs, width)
    )
    dy_send = jnp.where(valid[:, None], dy_pairs[source], 0).reshape(
        peers, local_experts, capacity, width
    )
    dy_received = lax.all_to_all(dy_send, "expert", split_axis=0, concat_axis=0, tiled=True)
    sigmoid_gate = jax.nn.sigmoid(gate_pre)
    silu_gate = gate_pre * sigmoid_gate
    hidden = (silu_gate * up_pre).astype(jnp.bfloat16)
    grad_down_part = jnp.einsum(
        "necf,necd->efd", hidden, dy_received, preferred_element_type=jnp.float32
    )
    d_hidden = jnp.einsum("necd,efd->necf", dy_received, w_down, preferred_element_type=jnp.float32)
    d_gate = (d_hidden * up_pre * sigmoid_gate * (1.0 + gate_pre * (1.0 - sigmoid_gate))).astype(
        jnp.bfloat16
    )
    d_up = (d_hidden * silu_gate).astype(jnp.bfloat16)
    grad_gate_part = jnp.einsum(
        "necd,necf->edf", received, d_gate, preferred_element_type=jnp.float32
    )
    grad_up_part = jnp.einsum("necd,necf->edf", received, d_up, preferred_element_type=jnp.float32)
    gate_total, up_total, down_total = (
        lax.psum_scatter(
            grad_gate_part.astype(jnp.bfloat16), "dp", scatter_dimension=1, tiled=True
        ).astype(jnp.float32),
        lax.psum_scatter(
            grad_up_part.astype(jnp.bfloat16), "dp", scatter_dimension=1, tiled=True
        ).astype(jnp.float32),
        lax.psum_scatter(
            grad_down_part.astype(jnp.bfloat16), "dp", scatter_dimension=1, tiled=True
        ).astype(jnp.float32),
    )
    d_rows = jnp.einsum("necf,edf->necd", d_gate, w_gate, preferred_element_type=jnp.float32)
    d_rows = (
        d_rows + jnp.einsum("necf,edf->necd", d_up, w_up, preferred_element_type=jnp.float32)
    ).astype(jnp.bfloat16)
    d_back = lax.all_to_all(d_rows, "expert", split_axis=0, concat_axis=0, tiled=True)
    d_pairs = jnp.concatenate([d_back.reshape(all_experts * capacity, width), zero_row], axis=0)[
        target
    ].reshape(tokens, top, width)
    d_normed_two = jnp.sum(d_pairs, axis=1, dtype=jnp.float32)
    d_gates = jnp.einsum("td,tkd->tk", cotangent, pair_out, preferred_element_type=jnp.float32)
    d_picked = gates * (d_gates - jnp.sum(gates * d_gates, axis=-1, keepdims=True))
    d_logits = jnp.sum(onehot * d_picked[:, :, None], axis=1).astype(jnp.bfloat16)
    grad_router_part = jnp.einsum(
        "td,te->de", normed_two, d_logits, preferred_element_type=jnp.float32
    )
    d_normed_two = d_normed_two + jnp.einsum(
        "te,de->td", d_logits, w_router, preferred_element_type=jnp.float32
    )
    scaled_two = d_normed_two * gain_mlp
    grad_gain_mlp_part = jnp.sum(d_normed_two * middle * inv_two, axis=0)
    d_middle = (
        cotangent
        + inv_two * scaled_two
        - middle * inv_two**3 * jnp.mean(middle * scaled_two, axis=-1, keepdims=True)
    )
    d_branch = d_middle.astype(jnp.bfloat16)
    grad_output_part = jnp.einsum(
        "tf,td->fd", attended_low, d_branch, preferred_element_type=jnp.float32
    )
    d_attended = jnp.einsum(
        "td,fd->tf", d_branch, w_output, preferred_element_type=jnp.float32
    ).astype(jnp.bfloat16)
    d_groups = d_attended.reshape(tokens, KV_HEADS, groups, HEAD_DIM)
    delta = jnp.einsum(
        "qkgd,qkgd->kgq", d_groups, attended_groups, preferred_element_type=jnp.float32
    )
    keys_back, values_back = (
        lax.all_gather(keys_low, "dp", axis=0, tiled=True),
        lax.all_gather(values_low, "dp", axis=0, tiled=True),
    )

    def grad_step(step, carry):
        d_query, d_keys, d_values = carry
        start = step * block
        key_block = lax.dynamic_slice_in_dim(keys_back, start, block, 0)
        value_block = lax.dynamic_slice_in_dim(values_back, start, block, 0)
        scores = block_scores(key_block, start)
        probs = jnp.exp(scores - log_total[..., None])
        probs_low = probs.astype(jnp.bfloat16)
        d_probs = jnp.einsum(
            "qkgd,skd->kgqs", d_groups, value_block, preferred_element_type=jnp.float32
        )
        d_scores = (probs * (d_probs - delta[..., None])).astype(jnp.bfloat16)
        d_query = d_query + jnp.einsum(
            "kgqs,skd->qkgd", d_scores, key_block, preferred_element_type=jnp.float32
        )
        key_part = jnp.einsum(
            "kgqs,qkgd->skd", d_scores, query_groups, preferred_element_type=jnp.float32
        )
        value_part = jnp.einsum(
            "kgqs,qkgd->skd", probs_low, d_groups, preferred_element_type=jnp.float32
        )
        d_keys = lax.dynamic_update_slice_in_dim(
            d_keys, lax.dynamic_slice_in_dim(d_keys, start, block, 0) + key_part, start, 0
        )
        d_values = lax.dynamic_update_slice_in_dim(
            d_values, lax.dynamic_slice_in_dim(d_values, start, block, 0) + value_part, start, 0
        )
        return (d_query, d_keys, d_values)

    grad_init = (
        jnp.zeros((tokens, KV_HEADS, groups, HEAD_DIM), jnp.float32),
        jnp.zeros((length, KV_HEADS, HEAD_DIM), jnp.float32),
        jnp.zeros((length, KV_HEADS, HEAD_DIM), jnp.float32),
    )
    d_query, d_keys, d_values = lax.fori_loop(0, count, grad_step, grad_init)
    key_sum, value_sum = (
        lax.psum_scatter(
            (d_keys * scale).reshape(length, KV_HEADS * HEAD_DIM).astype(jnp.bfloat16),
            "dp",
            scatter_dimension=0,
            tiled=True,
        ).astype(jnp.float32),
        lax.psum_scatter(
            d_values.reshape(length, KV_HEADS * HEAD_DIM).astype(jnp.bfloat16),
            "dp",
            scatter_dimension=0,
            tiled=True,
        ).astype(jnp.float32),
    )
    d_query_low = (
        rotate_back((d_query * scale).reshape(tokens, HEADS, HEAD_DIM), cosine, sine)
        .astype(jnp.bfloat16)
        .reshape(tokens, HEADS * HEAD_DIM)
    )
    d_key_low = (
        rotate_back(key_sum.reshape(tokens, KV_HEADS, HEAD_DIM), cosine, sine)
        .astype(jnp.bfloat16)
        .reshape(tokens, KV_HEADS * HEAD_DIM)
    )
    d_value_low = value_sum.astype(jnp.bfloat16)
    grad_query_part = jnp.einsum(
        "td,tf->df", normed, d_query_low, preferred_element_type=jnp.float32
    )
    grad_key_part = jnp.einsum("td,tf->df", normed, d_key_low, preferred_element_type=jnp.float32)
    grad_value_part = jnp.einsum(
        "td,tf->df", normed, d_value_low, preferred_element_type=jnp.float32
    )
    d_normed = jnp.einsum("tf,df->td", d_query_low, w_query, preferred_element_type=jnp.float32)
    d_normed = d_normed + jnp.einsum(
        "tf,df->td", d_key_low, w_key, preferred_element_type=jnp.float32
    )
    d_normed = d_normed + jnp.einsum(
        "tf,df->td", d_value_low, w_value, preferred_element_type=jnp.float32
    )
    scaled_one = d_normed * gain_attn
    grad_gain_attn_part = jnp.sum(d_normed * inputs * inv_one, axis=0)
    grad_in = (
        d_middle
        + inv_one * scaled_one
        - inputs * inv_one**3 * jnp.mean(inputs * scaled_one, axis=-1, keepdims=True)
    )
    dense = (
        lax.psum_scatter(grad_gain_attn_part, ("dp", "expert"), scatter_dimension=0, tiled=True),
        lax.psum_scatter(grad_query_part, ("dp", "expert"), scatter_dimension=0, tiled=True),
        lax.psum_scatter(grad_key_part, ("dp", "expert"), scatter_dimension=0, tiled=True),
        lax.psum_scatter(grad_value_part, ("dp", "expert"), scatter_dimension=0, tiled=True),
        lax.psum_scatter(grad_output_part, ("dp", "expert"), scatter_dimension=0, tiled=True),
        lax.psum_scatter(grad_gain_mlp_part, ("dp", "expert"), scatter_dimension=0, tiled=True),
        lax.psum_scatter(grad_router_part, ("dp", "expert"), scatter_dimension=0, tiled=True),
    )
    return (
        hidden_out[None],
        grad_in[None],
        dense[0],
        dense[1],
        dense[2],
        dense[3],
        dense[4],
        dense[5],
        dense[6],
        gate_total,
        up_total,
        down_total,
    )

BF = jnp.bfloat16
F32 = jnp.float32
WIDTH = 1536
LANES = 128
PER_KV = HEADS // KV_HEADS
ROWS_Q = PER_KV * HEAD_DIM
PACK = ROWS_Q + 2 * HEAD_DIM
BIT_Y, BIT_ZL, BIT_ZH = 1, 2, 4
BIT_C, BIT_X = 1, 2
BLOCK_Q = 256
BLOCK_K = 512
SLOTS = 64
CHUNK = 512
MIB = 1 << 20


def dot_nn(a, b):
    return lax.dot_general(a, b, (((1,), (0,)), ((), ())), preferred_element_type=F32)


def dot_nt(a, b):
    return lax.dot_general(a, b, (((1,), (1,)), ((), ())), preferred_element_type=F32)


def dot_tn(a, b):
    return lax.dot_general(a, b, (((0,), (0,)), ((), ())), preferred_element_type=F32)


def cost(flops, moved, transcendentals=0):
    return pl.CostEstimate(
        flops=int(flops), bytes_accessed=int(moved), transcendentals=int(transcendentals)
    )


def params(mib, dims=None):
    return pltpu.CompilerParams(vmem_limit_bytes=mib * MIB, dimension_semantics=dims)


def swap(values, axis, mask):
    size = lax.axis_size(axis)
    return lax.ppermute(values, axis, [(i, i ^ mask) for i in range(size)])


def swap_bit(values, bit):
    axis, mask = bit
    return swap(values, axis, mask)


def fence(*values):
    return lax.optimization_barrier(values)


C_BIT = ("expert", BIT_C)
X_BIT = ("expert", BIT_X)
Y_BIT = ("dp", BIT_Y)
ZL_BIT = ("dp", BIT_ZL)
ZH_BIT = ("dp", BIT_ZH)


def pre_kernel(
    hid_ref,
    gain_ref,
    wq_ref,
    wk_ref,
    wv_ref,
    cos_ref,
    sin_ref,
    cot_ref,
    norm_ref,
    pack_ref,
    low_ref,
):
    tokens = hid_ref.shape[0]
    half = tokens // 2
    low_ref[...] = cot_ref[...].astype(BF)
    inputs = hid_ref[...]
    inv = lax.rsqrt(jnp.mean(inputs * inputs, axis=-1, keepdims=True) + EPS)
    normed = (inputs * inv * gain_ref[...]).astype(BF)
    norm_ref[...] = normed
    low = (lax.broadcasted_iota(jnp.int32, (tokens, LANES), 1) % HEAD_DIM) < HEAD_DIM // 2
    cosine, sine = cos_ref[...], sin_ref[...]

    def turn(tile):
        other = jnp.where(
            low,
            pltpu.roll(tile, LANES - HEAD_DIM // 2, 1),
            pltpu.roll(tile, HEAD_DIM // 2, 1),
        )
        return (tile * cosine + other * sine).astype(BF)

    tiles = []
    for n in range(wq_ref.shape[1] // CHUNK):
        pre = dot_nn(normed, wq_ref[:, n * CHUNK : (n + 1) * CHUNK])
        tiles += [turn(pre[:, m * LANES : (m + 1) * LANES]) for m in range(CHUNK // LANES)]
    queries = jnp.concatenate(tiles, axis=1)
    pre = dot_nn(normed, wk_ref[...])
    keys = jnp.concatenate(
        [turn(pre[:, m * LANES : (m + 1) * LANES]) for m in range(pre.shape[1] // LANES)], axis=1
    )
    values = dot_nn(normed, wv_ref[...]).astype(BF)
    for g in range(KV_HEADS):
        at = g * ROWS_Q
        head = slice(g * HEAD_DIM, (g + 1) * HEAD_DIM)
        pack_ref[g, 0:tokens] = queries[:, at : at + LANES]
        pack_ref[g, tokens : 2 * tokens] = jnp.concatenate(
            [queries[:, at + LANES : at + ROWS_Q], keys[:, head]], axis=1
        )
        pack_ref[g, 2 * tokens :] = jnp.concatenate(
            [values[:half, head], values[half:, head]], axis=1
        )


def run_pre(inputs, gain, w_query, w_key, w_value, cos_tab, sin_tab, cotangent):
    tokens = inputs.shape[0]
    return pl.pallas_call(
        pre_kernel,
        out_shape=(
            jax.ShapeDtypeStruct((tokens, WIDTH), BF),
            jax.ShapeDtypeStruct((KV_HEADS, tokens * PACK // LANES, LANES), BF),
            jax.ShapeDtypeStruct((tokens, WIDTH), BF),
        ),
        compiler_params=params(60),
        cost_estimate=cost(2 * tokens * WIDTH * 2560, 14e6),
    )(inputs, gain[None], w_query, w_key, w_value, cos_tab, sin_tab, cotangent)


def unpack_heads(block_ref, out_ref, row, tokens, column):
    half = tokens // 2
    out_ref[row : row + tokens, column : column + LANES] = block_ref[0:tokens]
    rest = block_ref[tokens : tokens + half]
    out_ref[row : row + half, column + LANES : column + ROWS_Q] = rest[:, :HEAD_DIM]
    out_ref[row + half : row + tokens, column + LANES : column + ROWS_Q] = rest[:, HEAD_DIM:]


def pack_heads(block_ref, rows, tokens):
    half = tokens // 2
    block_ref[0:tokens] = rows[:, 0:LANES]
    block_ref[tokens : tokens + half] = jnp.concatenate(
        [rows[:half, LANES:ROWS_Q], rows[half:, LANES:ROWS_Q]], axis=1
    )


def unpack_all(block_ref, q_ref, k_ref, v_ref, row, tokens, q_at=0, k_at=0, v_at=0):
    half = tokens // 2
    rows = slice(row, row + tokens)
    q_ref[rows, q_at : q_at + LANES] = block_ref[0:tokens]
    two = block_ref[tokens : 2 * tokens]
    q_ref[rows, q_at + LANES : q_at + ROWS_Q] = two[:, :HEAD_DIM]
    k_ref[rows, k_at : k_at + HEAD_DIM] = two[:, HEAD_DIM:]
    rest = block_ref[2 * tokens : 2 * tokens + half]
    v_ref[row : row + half, v_at : v_at + HEAD_DIM] = rest[:, :HEAD_DIM]
    v_ref[row + half : row + tokens, v_at : v_at + HEAD_DIM] = rest[:, HEAD_DIM:]


def heads_t(block, width):
    return jnp.concatenate(
        [block[:, h * HEAD_DIM : (h + 1) * HEAD_DIM].astype(F32).T for h in range(width)], axis=1
    )


def heads_rows(block, width):
    return jnp.concatenate(
        [block[:, h * HEAD_DIM : (h + 1) * HEAD_DIM] for h in range(width)], axis=0
    )


def allowed_t(step, block):
    shape = (BLOCK_K, PER_KV * BLOCK_Q)
    key_pos = step * BLOCK_K + lax.broadcasted_iota(jnp.int32, shape, 0)
    query_pos = block * BLOCK_Q + lax.broadcasted_iota(jnp.int32, shape, 1) % BLOCK_Q
    return key_pos <= query_pos


def forward_kernel(pack_ref, out_ref, out_t_ref, lse_ref, q_s, k_s, v_s, vt_s, out_s):
    block = pl.program_id(0)
    sources = pack_ref.shape[0]
    tokens = q_s.shape[0] // sources

    @pl.when(block == 0)
    def _():
        for n in range(sources):
            unpack_all(pack_ref.at[n], q_s, k_s, v_s, n * tokens, tokens)
        vt_s[...] = v_s[...].astype(F32).T.astype(BF)

    rows = pl.ds(pl.multiple_of(block * BLOCK_Q, BLOCK_Q), BLOCK_Q)
    scale = HEAD_DIM ** (-0.5)
    q_t = (heads_t(q_s[rows, :], PER_KV) * scale).astype(BF)
    columns = PER_KV * BLOCK_Q

    def step(j, carry, masked):
        running, total, accum = carry
        keys = pl.ds(pl.multiple_of(j * BLOCK_K, BLOCK_K), BLOCK_K)
        scores = dot_nn(k_s[keys, :], q_t)
        if masked:
            scores = jnp.where(allowed_t(j, block), scores, MASKED)
        newest = jnp.maximum(running, jnp.max(scores, axis=0, keepdims=True))
        fade = jnp.exp(running - newest)
        probs = jnp.exp(scores - newest)
        total = total * fade + jnp.sum(probs, axis=0, keepdims=True)
        accum = accum * fade + dot_nn(vt_s[:, keys], probs.astype(BF))
        return newest, total, accum

    carry = (
        jnp.full((1, columns), MASKED, F32),
        jnp.zeros((1, columns), F32),
        jnp.zeros((HEAD_DIM, columns), F32),
    )
    last = (block * BLOCK_Q) // BLOCK_K
    carry = lax.fori_loop(0, last, lambda j, c: step(j, c, False), carry)
    running, total, accum = step(last, carry, True)
    out_t = accum / total
    out_t_ref[0] = out_t
    lse_ref[0] = running + jnp.log(total)
    out_s[rows, :] = jnp.concatenate(
        [out_t[:, h * BLOCK_Q : (h + 1) * BLOCK_Q].T for h in range(PER_KV)], axis=1
    ).astype(BF)

    @pl.when(block == pl.num_programs(0) - 1)
    def _():
        for n in range(sources):
            pack_heads(out_ref.at[n], out_s[n * tokens : (n + 1) * tokens, :], tokens)


def run_forward(pack):
    sources = pack.shape[0]
    length = sources * (pack.shape[1] * LANES // PACK)
    packed = (sources, length // sources * ROWS_Q // LANES, LANES)
    blocks = length // BLOCK_Q
    columns = PER_KV * BLOCK_Q
    return pl.pallas_call(
        forward_kernel,
        grid=(blocks,),
        in_specs=[pl.BlockSpec(pack.shape, lambda i: (0, 0, 0))],
        out_specs=(
            pl.BlockSpec(packed, lambda i: (0, 0, 0)),
            pl.BlockSpec((1, HEAD_DIM, columns), lambda i: (i, 0, 0)),
            pl.BlockSpec((1, 1, columns), lambda i: (i, 0, 0)),
        ),
        out_shape=(
            jax.ShapeDtypeStruct(packed, BF),
            jax.ShapeDtypeStruct((blocks, HEAD_DIM, columns), F32),
            jax.ShapeDtypeStruct((blocks, 1, columns), F32),
        ),
        scratch_shapes=[
            pltpu.VMEM((length, ROWS_Q), BF),
            pltpu.VMEM((length, HEAD_DIM), BF),
            pltpu.VMEM((length, HEAD_DIM), BF),
            pltpu.VMEM((HEAD_DIM, length), BF),
            pltpu.VMEM((length, ROWS_Q), BF),
        ],
        compiler_params=params(60, ("arbitrary",)),
        cost_estimate=cost(8 * length * length * ROWS_Q, 6e6, length * length * PER_KV),
    )(pack)


def backward_kernel(
    pack_ref,
    grad_ref,
    out_t_ref,
    lse_ref,
    cos_ref,
    sin_ref,
    res_ref,
    q_s,
    do_s,
    k_s,
    v_s,
    kt_s,
    dk_s,
    dv_s,
):
    block = pl.program_id(0)
    sources = pack_ref.shape[0]
    tokens = q_s.shape[0] // sources

    @pl.when(block == 0)
    def _():
        for n in range(sources):
            unpack_all(pack_ref.at[n], q_s, k_s, v_s, n * tokens, tokens)
            unpack_heads(grad_ref.at[n], do_s, n * tokens, tokens, 0)
        kt_s[...] = k_s[...].astype(F32).T.astype(BF)
        dk_s[...] = jnp.zeros_like(dk_s)
        dv_s[...] = jnp.zeros_like(dv_s)

    scale = HEAD_DIM ** (-0.5)
    half = HEAD_DIM // 2
    rows = pl.ds(pl.multiple_of(block * BLOCK_Q, BLOCK_Q), BLOCK_Q)
    q_block = q_s[rows, :]
    q_t = (heads_t(q_block, PER_KV) * scale).astype(BF)
    q_rows = (heads_rows(q_block, PER_KV).astype(F32) * scale).astype(BF)
    do_block = do_s[rows, :]
    do_f32 = heads_t(do_block, PER_KV)
    do_t = do_f32.astype(BF)
    do_rows = heads_rows(do_block, PER_KV)
    delta = jnp.sum(do_f32 * out_t_ref[0], axis=0, keepdims=True)
    lse = lse_ref[0]

    def step(j, dq_t, masked):
        keys = pl.ds(pl.multiple_of(j * BLOCK_K, BLOCK_K), BLOCK_K)
        scores = dot_nn(k_s[keys, :], q_t)
        if masked:
            scores = jnp.where(allowed_t(j, block), scores, MASKED)
        probs = jnp.exp(scores - lse)
        d_probs = dot_nn(v_s[keys, :], do_t)
        d_scores = (probs * (d_probs - delta)).astype(BF)
        dv_s[keys, :] += dot_nn(probs.astype(BF), do_rows)
        dk_s[keys, :] += dot_nn(d_scores, q_rows)
        return dq_t + dot_nn(kt_s[:, keys], d_scores)

    last = (block * BLOCK_Q) // BLOCK_K
    dq_t = jnp.zeros((HEAD_DIM, PER_KV * BLOCK_Q), F32)
    dq_t = lax.fori_loop(0, last, lambda j, c: step(j, c, False), dq_t)
    dq_t = step(last, dq_t, True) * scale

    def turn_back(values, cosine, sine):
        first, second = values[:half], values[half:]
        return jnp.concatenate(
            [first * cosine + second * sine, second * cosine - first * sine], axis=0
        )

    columns = pl.ds(pl.multiple_of(block * BLOCK_Q, BLOCK_Q), BLOCK_Q)
    cosine, sine = cos_ref[:, columns], sin_ref[:, columns]
    q_s[rows, :] = jnp.concatenate(
        [
            turn_back(dq_t[:, h * BLOCK_Q : (h + 1) * BLOCK_Q], cosine, sine).T
            for h in range(PER_KV)
        ],
        axis=1,
    ).astype(BF)

    @pl.when(block == pl.num_programs(0) - 1)
    def _():
        dk = turn_back(dk_s[...].T, cos_ref[...], sin_ref[...]).T.astype(BF)
        half = tokens // 2
        for n in range(sources):
            row = n * tokens
            res_ref[n, 0:tokens] = q_s[row : row + tokens, 0:LANES]
            res_ref[n, tokens : 2 * tokens] = jnp.concatenate(
                [q_s[row : row + tokens, LANES:ROWS_Q], dk[row : row + tokens]], axis=1
            )
            res_ref[n, 2 * tokens :] = jnp.concatenate(
                [dv_s[row : row + half, :], dv_s[row + half : row + tokens, :]], axis=1
            ).astype(BF)


def run_backward(pack, grad, out_t, lse, cos_t, sin_t):
    length = cos_t.shape[1]
    blocks = length // BLOCK_Q
    columns = PER_KV * BLOCK_Q
    half = HEAD_DIM // 2
    return pl.pallas_call(
        backward_kernel,
        grid=(blocks,),
        in_specs=[
            pl.BlockSpec(pack.shape, lambda i: (0, 0, 0)),
            pl.BlockSpec(grad.shape, lambda i: (0, 0, 0)),
            pl.BlockSpec((1, HEAD_DIM, columns), lambda i: (i, 0, 0)),
            pl.BlockSpec((1, 1, columns), lambda i: (i, 0, 0)),
            pl.BlockSpec((half, length), lambda i: (0, 0)),
            pl.BlockSpec((half, length), lambda i: (0, 0)),
        ],
        out_specs=pl.BlockSpec(pack.shape, lambda i: (0, 0, 0)),
        out_shape=jax.ShapeDtypeStruct(pack.shape, BF),
        scratch_shapes=[
            pltpu.VMEM((length, ROWS_Q), BF),
            pltpu.VMEM((length, ROWS_Q), BF),
            pltpu.VMEM((length, HEAD_DIM), BF),
            pltpu.VMEM((length, HEAD_DIM), BF),
            pltpu.VMEM((HEAD_DIM, length), BF),
            pltpu.VMEM((length, HEAD_DIM), F32),
            pltpu.VMEM((length, HEAD_DIM), F32),
        ],
        compiler_params=params(60, ("arbitrary",)),
        cost_estimate=cost(20 * length * length * ROWS_Q, 8e6, length * length * PER_KV),
    )(pack, grad, out_t, lse, cos_t, sin_t)


def mid_kernel(att_ref, wo_ref, hid_ref, gain_ref, mid_ref, norm_ref, full_ref):
    for g in range(KV_HEADS):
        unpack_heads(att_ref.at[g], full_ref, 0, full_ref.shape[0], g * ROWS_Q)
    middle = hid_ref[...] + dot_nn(full_ref[...], wo_ref[...])
    mid_ref[...] = middle
    inv = lax.rsqrt(jnp.mean(middle * middle, axis=-1, keepdims=True) + EPS)
    norm_ref[...] = (middle * inv * gain_ref[...]).astype(BF)


def run_mid(att, w_output, inputs, gain):
    tokens = inputs.shape[0]
    return pl.pallas_call(
        mid_kernel,
        out_shape=(
            jax.ShapeDtypeStruct((tokens, WIDTH), F32),
            jax.ShapeDtypeStruct((tokens, WIDTH), BF),
            jax.ShapeDtypeStruct((tokens, WIDTH), BF),
        ),
        compiler_params=params(60),
        cost_estimate=cost(2 * tokens * WIDTH * WIDTH, 12e6),
    )(att, w_output, inputs, gain[None])


def expert_kernel(
    place_ref,
    x_ref,
    g_ref,
    map_ref,
    wr_ref,
    wg0_ref,
    wg1_ref,
    wu0_ref,
    wu1_ref,
    wd0_ref,
    wd1_ref,
    *refs,
    first,
):
    if first:
        mix_prior = dx_prior = None
    else:
        mix_prior, dx_prior = refs[0:2], refs[2:4]
        refs = refs[4:]
    (
    mix_keep,
    mix_send,
    dx_keep,
    dx_send,
    gate_keep,
    gate_send0,
    gate_send1,
    up_keep,
    up_send0,
    up_send1,
    down_keep,
    down_send0,
    down_send1,
    xs,
    gs,
    gate_s,
    wide_s,
    tall_s,
    ) = refs
    step = pl.program_id(0)
    sources = map_ref.shape[0]
    experts = xs.shape[0]
    low = 0 if first else experts
    tokens = x_ref.shape[1]
    rows = experts * SLOTS
    count = WIDTH // CHUNK

    def one_hot(source):
        slots = map_ref[source, low : low + experts, :]
        wide = jnp.broadcast_to(slots[:, None, :], (experts, SLOTS, tokens))
        rank = lax.broadcasted_iota(jnp.int32, (experts, SLOTS, tokens), 1).astype(F32)
        return (wide == rank).astype(F32).reshape(rows, tokens)

    @pl.when(step < sources)
    def _():
        slot_map = map_ref[step]
        chosen = slot_map >= 0.0
        logits = dot_nt(wr_ref[...], x_ref[0])[0 : slot_map.shape[0]]
        logits = jnp.where(chosen, logits, MASKED)
        raised = jnp.exp(logits - jnp.max(logits, axis=0, keepdims=True))
        raised = jnp.where(chosen, raised, 0.0)
        gates = raised / jnp.sum(raised, axis=0, keepdims=True)
        pick = one_hot(step)
        wide = jnp.broadcast_to(gates[low : low + experts, None, :], (experts, SLOTS, tokens))
        gate_rows = jnp.sum(pick * wide.reshape(rows, tokens), axis=1, keepdims=True)
        pick = pick.astype(BF)
        here = pl.ds(pl.multiple_of(step * SLOTS, SLOTS), SLOTS)
        for e in range(experts):
            gate_s[e, here, :] = gate_rows[e * SLOTS : (e + 1) * SLOTS]
        for n in range(count):
            cols = slice(n * CHUNK, (n + 1) * CHUNK)
            got = dot_nn(pick, x_ref[0, :, cols]).astype(BF)
            xs[:, here, cols] = got.reshape(experts, SLOTS, CHUNK)
            got = dot_nn(pick, g_ref[0, :, cols]).astype(BF)
            gs[:, here, cols] = got.reshape(experts, SLOTS, CHUNK)

    @pl.when((step >= sources) & (step < sources + experts))
    def _():
        e = step - sources
        x = xs[e]
        w_gate = jnp.concatenate([wg0_ref[0], wg1_ref[0]], axis=1)
        w_up = jnp.concatenate([wu0_ref[0], wu1_ref[0]], axis=1)
        gate_pre = dot_nn(x, w_gate)
        up_pre = dot_nn(x, w_up)
        sig = jax.nn.sigmoid(gate_pre)
        silu = gate_pre * sig
        hidden = (silu * up_pre).astype(BF)
        gate = gate_s[e]
        d_hidden = jnp.zeros(hidden.shape, F32)
        d_gates = jnp.zeros(gate.shape, F32)
        for n in range(count):
            cols = slice(n * CHUNK, (n + 1) * CHUNK)
            w_down = jnp.concatenate([wd0_ref[0, :, cols], wd1_ref[0, :, cols]], axis=0)
            grad = gs[e, :, cols].astype(F32)
            d_y = (gate * grad).astype(BF)
            y = dot_nn(hidden, w_down)
            d_gates += jnp.sum(y * grad, axis=1, keepdims=True)
            gs[e, :, cols] = (gate * y).astype(BF)
            d_hidden += dot_nt(d_y, w_down)
            wide_s[:, cols] = dot_tn(hidden, d_y).astype(BF)
        gate_s[e] = d_gates
        d_gate = (d_hidden * up_pre * sig * (1.0 + gate_pre * (1.0 - sig))).astype(BF)
        d_up = (d_hidden * silu).astype(BF)

        y_at, zl_at, zh_at = place_ref[1], place_ref[2], place_ref[3]
        part = down_keep.shape[2]
        for z in range(2):
            base = (zh_at ^ z) * 2
            down_keep[z, 0] = wide_s[pl.ds(pl.multiple_of((base + y_at) * part, part), part), :]
            (down_send0, down_send1)[z][0] = wide_s[
                pl.ds(pl.multiple_of((base + (1 - y_at)) * part, part), part), :
            ]

        def spread(keep, send):
            part = keep.shape[3]
            for z in range(2):
                for low in range(2):
                    base = ((zh_at ^ z) * 2 + (zl_at ^ low)) * 2
                    keep[z, low, 0] = tall_s[
                        pl.ds(pl.multiple_of((base + y_at) * part, part), part), :
                    ]
                    send[z][low, 0] = tall_s[
                        pl.ds(pl.multiple_of((base + (1 - y_at)) * part, part), part), :
                    ]

        for n in range(count):
            cols = slice(n * CHUNK, (n + 1) * CHUNK)
            tall_s[cols, :] = dot_tn(x[:, cols], d_gate).astype(BF)
        spread(gate_keep, (gate_send0, gate_send1))
        for n in range(count):
            cols = slice(n * CHUNK, (n + 1) * CHUNK)
            tall_s[cols, :] = dot_tn(x[:, cols], d_up).astype(BF)
        spread(up_keep, (up_send0, up_send1))
        for n in range(count):
            cols = slice(n * CHUNK, (n + 1) * CHUNK)
            d_x = dot_nt(d_gate, w_gate[cols]) + dot_nt(d_up, w_up[cols])
            xs[e, :, cols] = d_x.astype(BF)

    def combine(source, mix_out, dx_out, mix_in, dx_in):
        def put(out, prior, cols, values):
            if prior is not None:
                values += prior[0, :, cols].astype(F32)
            out[0, :, cols] = values.astype(BF)

        here = pl.ds(pl.multiple_of(source * SLOTS, SLOTS), SLOTS)
        pick = one_hot(source).astype(BF)
        for n in range(count):
            cols = slice(n * CHUNK, (n + 1) * CHUNK)
            put(dx_out, dx_in, cols, dot_tn(pick, xs[:, here, cols].reshape(rows, CHUNK)))
            put(mix_out, mix_in, cols, dot_tn(pick, gs[:, here, cols].reshape(rows, CHUNK)))
        values = gate_s[:, here, :].reshape(rows, 1)
        column = lax.broadcasted_iota(jnp.int32, (rows, LANES), 1)
        owner = lax.broadcasted_iota(jnp.int32, (rows, LANES), 0) // SLOTS
        spread_out = jnp.where(column == owner + (place_ref[4] + low), values, 0.0).astype(BF)
        put(dx_out, dx_in, slice(WIDTH, WIDTH + LANES), dot_tn(pick, spread_out))

    @pl.when((step >= sources + experts) & (step < sources + experts + sources // 2))
    def _():
        source = step - experts - sources // 2
        prior = (None, None) if first else (mix_prior[1], dx_prior[1])
        combine(source, mix_send, dx_send, *prior)

    @pl.when(step >= sources + experts + sources // 2)
    def _():
        source = step - experts - sources - sources // 2
        prior = (None, None) if first else (mix_prior[0], dx_prior[0])
        combine(source, mix_keep, dx_keep, *prior)


def less(shape):
    return jax.ShapeDtypeStruct(shape.shape[1:], shape.dtype)


def run_experts(place, x_all, g_all, maps, wr_t, w_gate, w_up, w_down, prior=()):
    sources, tokens, width = x_all.shape
    experts = w_gate.shape[0] // 2
    low = experts if prior else 0
    ffe = w_gate.shape[2]
    part = ffe // 8
    quarter = width // 8
    half = ffe // 2
    slots = sources * SLOTS
    extra = width + LANES
    second = sources + experts
    third = second + sources // 2

    def at(i, low, size):
        return jnp.clip(i - low, 0, size - 1)

    def expert_of(i):
        return at(i, sources, experts)

    def w_cols(block):
        return pl.BlockSpec(
            (1, width, LANES), lambda i, p: (expert_of(i) + low, 0, p[0] + 2 * block)
        )

    def w_rows(block):
        return pl.BlockSpec(
            (1, LANES, width), lambda i, p: (expert_of(i) + low, p[0] + 2 * block, 0)
        )

    token_spec = pl.BlockSpec(
        (1, tokens, width),
        lambda i, p: (at(i, 0, sources), 0, 0),
    )

    def out_tokens(low, cols):
        return pl.BlockSpec((1, tokens, cols), lambda i, p: (at(i, low, sources // 2), 0, 0))

    tall_spec = pl.BlockSpec(
        (2, 2, 1, quarter, half), lambda i, p: (0, 0, expert_of(i), 0, 0)
    )
    wide_spec = pl.BlockSpec((2, 1, part, width), lambda i, p: (0, expert_of(i), 0, 0))
    tall_half = pl.BlockSpec((2, 1, quarter, half), lambda i, p: (0, expert_of(i), 0, 0))
    wide_half = pl.BlockSpec((1, part, width), lambda i, p: (expert_of(i), 0, 0))
    tall = jax.ShapeDtypeStruct((2, 2, experts, quarter, half), BF)
    wide = jax.ShapeDtypeStruct((2, experts, part, width), BF)
    mixed = jax.ShapeDtypeStruct((sources // 2, tokens, width), BF)
    d_x = jax.ShapeDtypeStruct((sources // 2, tokens, extra), BF)
    sums = (
        out_tokens(third, width),
        out_tokens(second, width),
        out_tokens(third, extra),
        out_tokens(second, extra),
    )
    return pl.pallas_call(
        functools.partial(expert_kernel, first=not prior),
        grid_spec=pltpu.PrefetchScalarGridSpec(
            num_scalar_prefetch=1,
            grid=(third + sources // 2,),
            in_specs=[
                token_spec,
                token_spec,
                pl.BlockSpec(maps.shape, lambda i, p: (0, 0, 0)),
                pl.BlockSpec(wr_t.shape, lambda i, p: (0, 0)),
                w_cols(0),
                w_cols(1),
                w_cols(0),
                w_cols(1),
                w_rows(0),
                w_rows(1),
                *(sums if prior else ()),
            ],
            out_specs=(
                *sums,
                tall_spec,
                tall_half,
                tall_half,
                tall_spec,
                tall_half,
                tall_half,
                wide_spec,
                wide_half,
                wide_half,
            ),
            scratch_shapes=[
                pltpu.VMEM((experts, slots, width), BF),
                pltpu.VMEM((experts, slots, width), BF),
                pltpu.VMEM((experts, slots, 1), F32),
                pltpu.VMEM((half, width), BF),
                pltpu.VMEM((width, half), BF),
            ],
        ),
        out_shape=(mixed, mixed, d_x, d_x)
        + (tall, less(tall), less(tall)) * 2
        + (wide, less(wide), less(wide)),
        compiler_params=params(60, ("arbitrary",)),
        cost_estimate=cost(30e9, 60e6),
    )(place, x_all, g_all, maps, wr_t, w_gate, w_gate, w_up, w_up, w_down, w_down, *prior)


def post_kernel(
    dx_ref,
    mid_ref,
    cot_ref,
    norm_ref,
    wr_ref,
    map_ref,
    gain_ref,
    wo_ref,
    datt_ref,
    dmid_ref,
    dlow_ref,
    dlog_ref,
    ggain_ref,
):
    middle = mid_ref[...]
    inv = lax.rsqrt(jnp.mean(middle * middle, axis=-1, keepdims=True) + EPS)
    chosen = map_ref[...] >= 0.0
    logits = jnp.where(chosen, dot_nn(norm_ref[...], wr_ref[...]), MASKED)
    raised = jnp.exp(logits - jnp.max(logits, axis=-1, keepdims=True))
    raised = jnp.where(chosen, raised, 0.0)
    gates = raised / jnp.sum(raised, axis=-1, keepdims=True)
    d_gates = dx_ref[:, WIDTH:]
    d_picked = gates * (d_gates - jnp.sum(gates * d_gates, axis=-1, keepdims=True))
    d_logits = d_picked.astype(BF)
    dlog_ref[...] = d_logits
    d_norm = dx_ref[:, :WIDTH] + dot_nt(d_logits, wr_ref[...])
    scaled = d_norm * gain_ref[...]
    ggain_ref[...] = jnp.sum(d_norm * middle * inv, axis=0, keepdims=True)
    d_mid = (
        cot_ref[...]
        + inv * scaled
        - middle * inv**3 * jnp.mean(middle * scaled, axis=-1, keepdims=True)
    )
    dmid_ref[...] = d_mid
    d_low = d_mid.astype(BF)
    dlow_ref[...] = d_low
    d_att = dot_nt(d_low, wo_ref[...]).astype(BF)
    for g in range(KV_HEADS):
        pack_heads(datt_ref.at[g], d_att[:, g * ROWS_Q : (g + 1) * ROWS_Q], d_att.shape[0])


def run_post(dx_sum, middle, cotangent, normed_two, wr_pad, map_rows, gain, w_output):
    tokens = middle.shape[0]
    return pl.pallas_call(
        post_kernel,
        out_shape=(
            jax.ShapeDtypeStruct((KV_HEADS, tokens * ROWS_Q // LANES, LANES), BF),
            jax.ShapeDtypeStruct((tokens, WIDTH), F32),
            jax.ShapeDtypeStruct((tokens, WIDTH), BF),
            jax.ShapeDtypeStruct((tokens, LANES), BF),
            jax.ShapeDtypeStruct((1, WIDTH), F32),
        ),
        compiler_params=params(60),
        cost_estimate=cost(2 * tokens * WIDTH * WIDTH, 14e6),
    )(dx_sum, middle, cotangent, normed_two, wr_pad, map_rows, gain[None], w_output)


def put_rows(place_ref, held, keep, send):
    part = keep.shape[1]
    for b in range(keep.shape[0]):
        own = (2 * b) ^ place_ref[5]
        keep[b] = held[pl.ds(pl.multiple_of(own * part, part), part), :]
        other = own ^ 1
        send[b] = held[pl.ds(pl.multiple_of(other * part, part), part), :]


def qkvgrad_kernel(place_ref, a_ref, d_ref, full_ref, keep, send, held):
    step = pl.program_id(0)

    @pl.when(step == 0)
    def _():
        key_at = KV_HEADS * ROWS_Q
        value_at = key_at + KV_HEADS * HEAD_DIM
        for g in range(KV_HEADS):
            unpack_all(
                d_ref.at[g],
                full_ref,
                full_ref,
                full_ref,
                0,
                full_ref.shape[0],
                g * ROWS_Q,
                key_at + g * HEAD_DIM,
                value_at + g * HEAD_DIM,
            )

    cols = pl.ds(pl.multiple_of(step * 256, 256), 256)
    held[...] = dot_tn(a_ref[...], full_ref[:, cols]).astype(BF)
    put_rows(place_ref, held, keep, send)


def run_qkvgrad(place, normed, d_pack, blocks):
    tokens, rows = normed.shape
    cols = KV_HEADS * PACK
    part = rows // blocks
    spec = pl.BlockSpec((blocks // 2, part, 256), lambda i, p: (0, 0, i))
    shape = jax.ShapeDtypeStruct((blocks // 2, part, cols), BF)
    return pl.pallas_call(
        qkvgrad_kernel,
        grid_spec=pltpu.PrefetchScalarGridSpec(
            num_scalar_prefetch=1,
            grid=(cols // 256,),
            in_specs=[
                pl.BlockSpec((tokens, rows), lambda i, p: (0, 0)),
                pl.BlockSpec(d_pack.shape, lambda i, p: (0, 0, 0)),
            ],
            out_specs=(pl.BlockSpec((tokens, cols), lambda i, p: (0, 0)), spec, spec),
            scratch_shapes=[pltpu.VMEM((rows, 256), BF)],
        ),
        out_shape=(jax.ShapeDtypeStruct((tokens, cols), BF), shape, shape),
        compiler_params=params(60, ("arbitrary",)),
        cost_estimate=cost(2 * tokens * rows * cols, 12e6),
    )(place, normed, d_pack)


def last_work(inputs, outputs, scratch):
    gain_ref, gmlp_ref, sources = inputs[0], inputs[1], inputs[2:]
    (out_ref,) = outputs
    keep, send, held = scratch[:3]
    buffers, load_sem = scratch[3:-1], scratch[-1]
    loads = [
        pltpu.make_async_copy(source, buffer, load_sem.at[n])
        for n, (source, buffer) in enumerate(zip(sources, buffers))
    ]
    for load in loads:
        load.start()
    d_ref, wq_ref, wk_ref, wv_ref, dmid_ref, hid_ref, norm_ref, dlog_ref = buffers
    key_at = KV_HEADS * ROWS_Q
    value_at = key_at + KV_HEADS * HEAD_DIM
    device = lax.axis_index("dp") * lax.axis_size("expert") + lax.axis_index("expert")

    def compute():
        for load in loads:
            load.wait()
        tokens = hid_ref.shape[0]
        size = tokens // 4
        ggain = jnp.zeros(gain_ref.shape, F32)
        for r in range(4):
            rows = slice(r * size, (r + 1) * size)
            d_norm = dot_nt(d_ref[rows, 0:key_at], wq_ref[...])
            d_norm += dot_nt(d_ref[rows, key_at:value_at], wk_ref[...])
            d_norm += dot_nt(d_ref[rows, value_at:], wv_ref[...])
            values = hid_ref[rows, :]
            inv = lax.rsqrt(jnp.mean(values * values, axis=-1, keepdims=True) + EPS)
            scaled = d_norm * gain_ref[...]
            ggain += jnp.sum(d_norm * values * inv, axis=0, keepdims=True)
            out_ref[rows, :] = (
                dmid_ref[rows, :]
                + inv * scaled
                - values * inv**3 * jnp.mean(values * scaled, axis=-1, keepdims=True)
            )
        columns = dot_tn(norm_ref[...], dlog_ref[...])
        lane = lax.broadcasted_iota(jnp.int32, columns.shape, 1)
        for n, row in enumerate((gmlp_ref[...], ggain)):
            turned = jnp.broadcast_to(row, (8, row.shape[1])).T[:, 0:1]
            columns = jnp.where(lane == LANES - 2 + n, turned, columns)
        held[...] = columns
        part = keep.shape[1]
        for b in range(keep.shape[0]):
            own = (2 * b) ^ device
            keep[b] = held[pl.ds(pl.multiple_of(own * part, part), part), :]
            own = own ^ 1
            send[b] = held[pl.ds(pl.multiple_of(own * part, part), part), :]

    return compute


def plan_last(arrays, gain, ggain_mlp, blocks):
    vmem = pl.BlockSpec(memory_space=pltpu.VMEM)
    tokens = arrays[0].shape[0]
    small = pltpu.VMEM((blocks // 2, WIDTH // blocks, LANES), F32)
    scratch = [small, small, pltpu.VMEM((WIDTH, LANES), F32)]
    scratch += [pltpu.VMEM(array.shape, array.dtype) for array in arrays]
    scratch.append(pltpu.SemaphoreType.DMA((len(arrays),)))
    return (
        (gain[None], ggain_mlp) + arrays,
        [vmem] * 2 + [hbm] * len(arrays),
        [jax.ShapeDtypeStruct((tokens, WIDTH), F32)],
        scratch,
        last_work,
    )


def stack_swap(values, bit):
    return jnp.concatenate([values, swap_bit(values, bit)], axis=0)


MESH = pl.DeviceIdType.MESH
hbm = pl.BlockSpec(memory_space=pltpu.HBM)


def peer_of(bit):
    axis, mask = bit
    return {axis: lax.axis_index(axis) ^ mask}


def greet(ids):
    barrier = pltpu.get_barrier_semaphore()
    for device in ids:
        pl.semaphore_signal(barrier, inc=1, device_id=device, device_id_type=MESH)
    pl.semaphore_wait(barrier, len(ids))


GATHER_BITS = (X_BIT, ZL_BIT, C_BIT)


def gather_steps(x_ref, all_ref, send_sem, recv_sem, local_sem):
    half = x_ref.shape[0] // 2
    own = pltpu.make_async_copy(x_ref, all_ref.at[0], local_sem)
    own.start()
    copies = []

    def send(source, slot, rows, bit):
        n = len(copies)
        copy = pltpu.make_async_remote_copy(
            src_ref=source if rows is None else source.at[rows],
            dst_ref=all_ref.at[slot] if rows is None else all_ref.at[slot, rows],
            send_sem=send_sem.at[n],
            recv_sem=recv_sem.at[n],
            device_id=peer_of(bit),
            device_id_type=MESH,
        )
        copy.start()
        copies.append(copy)
        return copy

    top, low = pl.ds(0, half), pl.ds(half, half)
    x_top = send(x_ref, 1, top, X_BIT)
    z_low = send(x_ref, 2, low, ZL_BIT)
    x_low = send(x_ref, 1, low, X_BIT)
    z_top = send(x_ref, 2, top, ZL_BIT)
    last = [send(x_ref, 4, None, C_BIT)]
    x_top.wait_recv()
    far_top = send(all_ref.at[1], 3, top, ZL_BIT)
    z_low.wait_recv()
    far_low = send(all_ref.at[2], 3, low, X_BIT)
    x_low.wait_recv()
    last.append(send(all_ref.at[1], 5, None, C_BIT))
    z_top.wait_recv()
    last.append(send(all_ref.at[2], 6, None, C_BIT))
    far_top.wait_recv()
    far_low.wait_recv()
    last.append(send(all_ref.at[3], 7, None, C_BIT))
    for copy in last:
        copy.wait_recv()
    for copy in copies:
        copy.wait_send()
    own.wait()


def gather_kernel(x_ref, *refs):
    blocks, maps_ref = refs[0:4], refs[4]
    all_ref, other_ref, all_maps_ref = refs[5:8]
    send_sem, recv_sem, more_send, more_recv, local_sem = refs[8:]
    greet([peer_of(bit) for bit in GATHER_BITS])
    pairs = [(block, other_ref.at[n], other_ref.at[4 + n]) for n, block in enumerate(blocks)]
    pairs.append((maps_ref, all_maps_ref.at[pl.ds(0, 4)], all_maps_ref.at[pl.ds(4, 4)]))
    copies = []
    for n, (block, here, there) in enumerate(pairs):
        copy = pltpu.make_async_remote_copy(
            src_ref=block,
            dst_ref=there,
            send_sem=more_send.at[n],
            recv_sem=more_recv.at[n],
            device_id=peer_of(C_BIT),
            device_id_type=MESH,
        )
        copy.start()
        copies.append(copy)
        copy = pltpu.make_async_copy(block, here, local_sem.at[1 + n])
        copy.start()
        copies.append(copy)
    gather_steps(x_ref, all_ref, send_sem, recv_sem, local_sem.at[0])
    for copy in copies:
        copy.wait()


def run_gather(values, blocks, maps):
    shape = jax.ShapeDtypeStruct((8,) + values.shape, values.dtype)
    return pl.pallas_call(
        gather_kernel,
        in_specs=[pl.BlockSpec(memory_space=pltpu.VMEM)] * 6,
        out_specs=(hbm,) * 3,
        out_shape=(shape, shape, jax.ShapeDtypeStruct((8,) + maps.shape[1:], maps.dtype)),
        scratch_shapes=[pltpu.SemaphoreType.DMA((n,)) for n in (10, 10, 5, 5, 6)],
        compiler_params=pltpu.CompilerParams(
            collective_id=1, has_side_effects=True, vmem_limit_bytes=60 * MIB
        ),
        cost_estimate=cost(0, 150e6),
    )(values, *blocks, maps)


def trade_peers(size):
    me = lax.axis_index("dp")
    return [{"dp": me ^ k} for k in range(size - 1, 0, -1)]


def trade_start(a_ref, out_ref, send_sem, recv_sem, local_sem):
    me = lax.axis_index("dp")
    copies = []
    for n, device in enumerate(trade_peers(a_ref.shape[0])):
        copy = pltpu.make_async_remote_copy(
            src_ref=a_ref.at[device["dp"]],
            dst_ref=out_ref.at[me],
            send_sem=send_sem.at[n],
            recv_sem=recv_sem.at[n],
            device_id=device,
            device_id_type=MESH,
        )
        copy.start()
        copies.append(copy)
    own = pltpu.make_async_copy(a_ref.at[me], out_ref.at[me], local_sem)
    own.start()
    return copies, own


def trade_end(copies, own):
    own.wait()
    for copy in copies:
        copy.wait_recv()
    for copy in copies:
        copy.wait_send()


class Rider:
    def __init__(self, bit, *terms, pieces=1, turns=(0,)):
        self.bit, self.pieces, self.turns = bit, pieces, turns
        self.arrays = [term[0] if isinstance(term, tuple) else term for term in terms]
        self.parts = [term[1] if isinstance(term, tuple) else None for term in terms]
        array, part = self.arrays[0], self.parts[0]
        shape = array.shape
        if part is not None:
            kept = [len(range(n)[k]) for k, n in zip(part, shape) if not isinstance(k, int)]
            shape = tuple(kept) + shape[len(part) :]
        self.shape = jax.ShapeDtypeStruct(shape, array.dtype)
        self.direct = len(terms) == 1 and part is None

    def scratch(self):
        if self.direct:
            return []
        buffer = pltpu.VMEM(self.shape.shape, self.shape.dtype)
        return [buffer] * (len(self.arrays) + 1)

    def plan(self):
        return (self.bit, self.pieces, self.turns, tuple(self.parts), self.direct)


def rider_inputs(riders):
    return [array for rider in riders for array in rider.arrays]


def rider_shapes(riders):
    return tuple(rider.shape for rider in riders)


def rider_scratch(riders):
    remote = max(sum(rider.pieces for rider in riders), 1)
    local = max(sum(len(rider.arrays) for rider in riders), 1)
    buffers = [buffer for rider in riders for buffer in rider.scratch()]
    return buffers + [pltpu.SemaphoreType.DMA((n,)) for n in (remote, remote, local)]


def add_rows(result, buffers):
    step = 16

    @pl.loop(0, result.shape[1] // step)
    def _(r):
        rows = pl.ds(pl.multiple_of(r * step, step), step)
        for i in range(result.shape[0]):
            total = buffers[0][i, rows, :].astype(F32)
            for buffer in buffers[1:]:
                total += buffer[i, rows, :].astype(F32)
            result[i, rows, :] = total.astype(result.dtype)


def ride_pieces(sources, targets, plans, scratch):
    send_sem, recv_sem, local_sem = scratch[-3:]
    starts, finishes, loads, used, source, local = [], [], [], 0, 0, 0
    for n, (bit, pieces, turns, parts, direct) in enumerate(plans):
        arrays = sources[source : source + len(parts)]
        source += len(parts)
        if direct:
            held = arrays[0]
            prepare = None
        else:
            buffers = scratch[used : used + len(parts)]
            held = scratch[used + len(parts)]
            used += len(parts) + 1
            copies = []
            for array, part, buffer in zip(arrays, parts, buffers):
                view = array if part is None else array.at[part]
                copy = pltpu.make_async_copy(view, buffer, local_sem.at[local])
                local += 1
                loads.append(copy)
                copies.append(copy)

            def prepare(copies=copies, held=held, buffers=buffers):
                for copy in copies:
                    copy.wait()
                add_rows(held, buffers)

        size = targets[n].shape[0] // pieces
        for m in range(pieces):
            at = pl.ds(m * size, size)

            def remote(n=n, at=at, slot=len(starts), bit=bit, held=held):
                return pltpu.make_async_remote_copy(
                    src_ref=held.at[at],
                    dst_ref=targets[n].at[at],
                    send_sem=send_sem.at[slot],
                    recv_sem=recv_sem.at[slot],
                    device_id=peer_of(bit),
                    device_id_type=MESH,
                )

            def start(remote=remote):
                remote().start()

            def finish(remote=remote):
                remote().wait()

            starts.append((prepare if m == 0 else None, start, turns))
            finishes.append(finish)
    return starts, finishes, loads


def all_peers(bits):
    size = lax.axis_size("dp")
    return trade_peers(size) + [peer_of(bit) for bit in bits if bit[0] == "expert"]


def trade_kernel(*refs, plans, work):
    inputs = sum(len(plan[3]) for plan in plans)
    more = 2 if work else 0
    a_ref, sources = refs[0], refs[1 : 1 + inputs]
    work_in, refs = refs[1 + inputs : 1 + inputs + more], refs[1 + inputs + more :]
    out_ref, targets = refs[0], refs[1 : 1 + len(plans)]
    work_out, refs = refs[1 + len(plans) : 1 + len(plans) + more], refs[1 + len(plans) + more :]
    send_sem, recv_sem, local_sem, *scratch = refs
    work_scratch = scratch[-6:] if work else ()
    scratch = scratch[:-6] if work else scratch
    bits = {plan[0] for plan in plans} | ({C_BIT} if work else set())
    greet(all_peers(sorted(bits)))
    trade = trade_start(a_ref, out_ref, send_sem, recv_sem, local_sem.at[0])
    starts, finishes, loads = ride_pieces(sources, targets, plans, scratch)
    for load in loads:
        load.start()
    if work:
        finishes.append(weight_grad(work_in, work_out, work_scratch))
    for prepare, start, _ in starts:
        if prepare is not None:
            prepare()
        start()
    if work:
        finishes[-1] = finishes[-1]()
    trade_end(*trade)
    for finish in finishes:
        finish()


def weight_grad(inputs, outputs, scratch):
    keep, got = outputs
    left, right, sent, held, load_sem, cross_sem = scratch
    loads = [
        pltpu.make_async_copy(source, target, load_sem.at[n])
        for n, (source, target) in enumerate(zip(inputs, (left, right)))
    ]
    for load in loads:
        load.start()
    blocks, part, width = keep.shape
    step = held.shape[1]
    device = lax.axis_index("dp") * lax.axis_size("expert") + lax.axis_index("expert")

    def compute():
        for load in loads:
            load.wait()

        @pl.loop(0, width // step)
        def _(n):
            cols = pl.ds(pl.multiple_of(n * step, step), step)
            held[...] = dot_tn(left[...], right[:, cols]).astype(BF)
            for b in range(blocks):
                own = (2 * b) ^ device
                keep[b, :, cols] = held[pl.ds(pl.multiple_of(own * part, part), part), :]
                own = own ^ 1
                sent[b, :, cols] = held[pl.ds(pl.multiple_of(own * part, part), part), :]

        copy = pltpu.make_async_remote_copy(
            src_ref=sent,
            dst_ref=got,
            send_sem=cross_sem.at[0],
            recv_sem=cross_sem.at[1],
            device_id=peer_of(C_BIT),
            device_id_type=MESH,
        )
        copy.start()
        return copy.wait

    return compute


def run_trade(values, number, riders=(), work=(), blocks=0):
    size = values.shape[0]
    inputs = rider_inputs(riders)
    vmem = pl.BlockSpec(memory_space=pltpu.VMEM)
    shapes, specs, scratch = [], [], []
    if work:
        left, right = work
        rows, width = left.shape[1], right.shape[1]
        half = jax.ShapeDtypeStruct((blocks // 2, rows // blocks, width), BF)
        shapes, specs = [half, half], [vmem, hbm]
        scratch = [
            pltpu.VMEM(left.shape, left.dtype),
            pltpu.VMEM(right.shape, right.dtype),
            pltpu.VMEM(half.shape, BF),
            pltpu.VMEM((rows, 256), BF),
            pltpu.SemaphoreType.DMA((2,)),
            pltpu.SemaphoreType.DMA((2,)),
        ]
    out = pl.pallas_call(
        functools.partial(
            trade_kernel, plans=tuple(rider.plan() for rider in riders), work=bool(work)
        ),
        in_specs=[hbm] * (1 + len(inputs) + len(work)),
        out_specs=(hbm,) * (1 + len(riders)) + tuple(specs),
        out_shape=(jax.ShapeDtypeStruct(values.shape, values.dtype),)
        + rider_shapes(riders)
        + tuple(shapes),
        scratch_shapes=[pltpu.SemaphoreType.DMA((n,)) for n in (size - 1, size - 1, 1)]
        + rider_scratch(riders)
        + scratch,
        compiler_params=pltpu.CompilerParams(
            collective_id=number, has_side_effects=True, vmem_limit_bytes=60 * MIB
        ),
        cost_estimate=cost(0, 170e6),
    )(values, *inputs, *work)
    return out if riders or work else out[0]


def first_kernel(a_ref, rank_ref, turned_ref, out_ref, slot_ref, send_sem, recv_sem, local_sem, *, far):
    greet(trade_peers(a_ref.shape[0]))
    trade = trade_start(a_ref, out_ref, send_sem, recv_sem, local_sem.at[0])
    for e in range(rank_ref.shape[0]):
        own = rank_ref[e : e + 1, :]
        smaller = (turned_ref[:, e : e + 1] < own).astype(F32)
        before = jnp.sum(smaller, axis=0, keepdims=True)
        slot_ref[e : e + 1, :] = jnp.where(own < far, jnp.minimum(before, SLOTS), -1.0)
    trade_end(*trade)


def run_first(values, rank_map, turned, far):
    size = values.shape[0]
    vmem = pl.BlockSpec(memory_space=pltpu.VMEM)
    return pl.pallas_call(
        functools.partial(first_kernel, far=far),
        in_specs=[hbm, vmem, vmem],
        out_specs=(hbm, vmem),
        out_shape=(
            jax.ShapeDtypeStruct(values.shape, values.dtype),
            jax.ShapeDtypeStruct(rank_map.shape, F32),
        ),
        scratch_shapes=[pltpu.SemaphoreType.DMA((n,)) for n in (size - 1, size - 1, 1)],
        compiler_params=pltpu.CompilerParams(
            collective_id=2, has_side_effects=True, vmem_limit_bytes=60 * MIB
        ),
        cost_estimate=cost(0, 170e6),
    )(values, rank_map, turned)


def reduce_chain(slot, part, keep_ref, send_ref, outs, acc, got, staged, send_sem, recv_sem):
    first, bits, row, rows, column, columns, order = part
    blocks = keep_ref.shape[0]
    stages = len(bits) + 1
    low = send_ref.dtype
    at = (pl.ds(row, rows), pl.ds(column, columns))
    copies = []

    def exchange(source, target, bit):
        n = slot + len(copies)
        copy = pltpu.make_async_remote_copy(
            src_ref=source,
            dst_ref=target,
            send_sem=send_sem.at[n],
            recv_sem=recv_sem.at[n],
            device_id=peer_of(bit),
            device_id_type=MESH,
        )
        copy.start()
        copies.append(copy)

    live = list(range(blocks))
    base_got, base_sent = 0, 0
    exchange(send_ref.at[(slice(None),) + at], got.at[(pl.ds(0, blocks),) + at], first)
    yield
    for stage in range(stages):
        copies[-1].wait_recv()

        def total(position):
            index = live[position]
            kept = keep_ref[(index,) + at].astype(F32) if stage == 0 else acc[(index,) + at]
            return kept + got[(base_got + position,) + at].astype(F32)

        if stage == stages - 1:
            low_column = 0
            for out_ref in outs:
                if low_column <= column < low_column + out_ref.shape[1]:
                    out_ref[at[0], pl.ds(column - low_column, columns)] = total(0)
                low_column += out_ref.shape[1]
            break
        mask = 1 << order[stage]
        rest = [i for i in live if not i & mask]
        for m, i in enumerate(rest):
            staged[(base_sent + m,) + at] = total(live.index(i ^ mask)).astype(low)
        exchange(
            staged.at[(pl.ds(base_sent, len(rest)),) + at],
            got.at[(pl.ds(base_got + len(live), len(rest)),) + at],
            bits[order[stage]],
        )
        for i in rest:
            acc[(i,) + at] = total(live.index(i))
        base_got += len(live)
        base_sent += len(rest)
        live = rest
        yield
    for copy in copies:
        copy.wait_send()


def reduce_kernel(*refs, jobs, plans, work):
    size = len(jobs)
    given = size - 1 if work else size
    inputs = sum(len(plan[3]) for plan in plans)
    keeps, sends, refs = list(refs[:given]), list(refs[given : 2 * given]), refs[2 * given :]
    sources, refs = refs[:inputs], refs[inputs:]
    compute = None
    if work:
        counts, body = work
        work_in, refs = refs[: counts[0]], refs[counts[0] :]
        work_out, refs = refs[: counts[1]], refs[counts[1] :]
        work_scratch, refs = refs[-counts[2] :], refs[: -counts[2]]
        compute = body(work_in, work_out, work_scratch)
        keeps.append(work_scratch[0])
        sends.append(work_scratch[1])
    outs = []
    for _, _, _, widths in jobs:
        outs.append(refs[: len(widths)])
        refs = refs[len(widths) :]
    targets, scratch = refs[: len(plans)], refs[len(plans) :]
    send_sem, recv_sem = scratch[3 * size : 3 * size + 2]
    used = {bit for first, bits, *_ in jobs for bit in (first,) + bits}
    used |= {plan[0] for plan in plans}
    starts, finishes, loads = ride_pieces(sources, targets, plans, scratch[3 * size + 2 :])
    for load in loads:
        load.start()
    greet([peer_of(bit) for bit in sorted(used)])
    chains, late, slot = [], [], 0
    for n, (first, bits, parts, _) in enumerate(jobs):
        for part in parts:
            (late if n >= given else chains).append(
                reduce_chain(
                    slot,
                    (first, bits) + part,
                    keeps[n],
                    sends[n],
                    outs[n],
                    *scratch[3 * n : 3 * n + 3],
                    send_sem,
                    recv_sem,
                )
            )
            slot += len(bits) + 1
    index = lax.axis_index("dp")
    outer = (index // BIT_ZH) % 2 == (index // BIT_ZL) % 2
    turn, last = 0, max([0] + [n for _, _, turns in starts for n in turns])
    while chains or turn <= last:
        rest = []
        for chain in chains:
            try:
                next(chain)
                rest.append(chain)
            except StopIteration:
                pass
        chains = rest
        for prepare, start, turns in starts:
            if prepare is not None and min(turns) == turn:
                prepare()
            if len(set(turns)) == 1:
                if turns[0] == turn:
                    start()
            else:
                for n, side in enumerate((outer, jnp.logical_not(outer))):
                    if turns[n] == turn:
                        pl.when(side)(start)
        if turn == 0 and work:
            compute()
            chains += late
        turn += 1
    for finish in finishes:
        finish()


def run_reduce(pairs, jobs, number, riders=(), work=None):
    slots = sum(len(parts) * (len(bits) + 1) for _, bits, parts, _ in jobs)
    vmem = pl.BlockSpec(memory_space=pltpu.VMEM)
    scratch, shapes = [], []
    arrays, work_specs, work_shapes, work_scratch, body = work or ((), (), (), (), None)
    late = [(shape, shape) for shape in work_scratch[:1]]
    for (keep, send), (_, _, _, widths) in zip(list(pairs) + late, jobs):
        blocks, rows, cols = keep.shape
        scratch += [
            pltpu.VMEM((blocks, rows, cols), F32),
            pltpu.VMEM((2 * blocks - 1, rows, cols), send.dtype),
            pltpu.VMEM((max(blocks - 1, 1), rows, cols), send.dtype),
        ]
        shapes += [jax.ShapeDtypeStruct((rows, width), F32) for width in widths]
    inputs = rider_inputs(riders)
    return pl.pallas_call(
        functools.partial(
            reduce_kernel,
            jobs=jobs,
            plans=tuple(rider.plan() for rider in riders),
            work=((len(arrays), len(work_shapes), len(work_scratch)), body) if work else None,
        ),
        in_specs=[vmem] * len(pairs) + [hbm] * (len(pairs) + len(inputs)) + list(work_specs),
        out_specs=(vmem,) * (len(work_shapes) + len(shapes)) + (hbm,) * len(riders),
        out_shape=tuple(work_shapes) + tuple(shapes) + rider_shapes(riders),
        scratch_shapes=scratch
        + [pltpu.SemaphoreType.DMA((n,)) for n in (slots, slots)]
        + rider_scratch(riders)
        + list(work_scratch),
        compiler_params=pltpu.CompilerParams(
            collective_id=number, has_side_effects=True, vmem_limit_bytes=60 * MIB
        ),
        cost_estimate=cost(0, 170e6),
    )(*(keep for keep, _ in pairs), *(send for _, send in pairs), *inputs, *arrays)


def sum_pair(kept, received):
    return kept.astype(F32) + received.astype(F32)


def add_low(*terms):
    return sum(term.astype(F32) for term in terms).astype(BF)


def join_kernel(place_ref, *refs):
    outs = refs[-3:]
    zl_at = place_ref[0]

    def total(*terms):
        return sum(term.astype(F32) for term in terms)

    def flat(ref):
        return ref[(0,) * (ref.ndim - 2)]

    def work(parts, part):
        for n in range(2):
            keep, got, more, other = parts[4 * n : 4 * n + 4]
            mine = total(*(flat(term) for term in (keep, got, more)))
            across = flat(other).astype(F32)
            for m in range(2):
                cols = slice(m * LANES, (m + 1) * LANES)
                at = pl.multiple_of((2 * m + zl_at) * LANES, LANES)
                outs[n][part, 0, :, pl.ds(at, LANES)] = mine[:, cols]
                at = pl.multiple_of((2 * m + 1 - zl_at) * LANES, LANES)
                outs[n][part, 0, :, pl.ds(at, LANES)] = across[:, cols]
        keep, got, more = parts[8:]
        outs[2][part, 0] = total(*(flat(term) for term in (keep, got, more)))

    work(refs[0:11], 0)
    work(refs[11:22], 1)


def run_join(place, halves):
    _, _, experts, rows, cols = halves[0][0].shape
    wide_rows, width = halves[0][8].shape[2:]
    arrays, specs = [], []
    for half in halves:
        for operand in half:
            array, lead = operand if isinstance(operand, tuple) else (operand, 0)
            extra = array.ndim - 3
            at = (lead,) + (0,) * (extra - 1) if extra else ()
            arrays.append(array)
            specs.append(
                pl.BlockSpec(
                    (1,) * (extra + 1) + array.shape[-2:],
                    lambda i, p, at=at: at + (i, 0, 0),
                )
            )
    shapes = [(rows, 2 * cols), (rows, 2 * cols), (wide_rows, width)]
    return pl.pallas_call(
        join_kernel,
        grid_spec=pltpu.PrefetchScalarGridSpec(
            num_scalar_prefetch=1,
            grid=(experts,),
            in_specs=specs,
            out_specs=tuple(
                pl.BlockSpec((2, 1) + shape, lambda i, p: (0, i, 0, 0)) for shape in shapes
            ),
        ),
        out_shape=tuple(jax.ShapeDtypeStruct((2, experts) + shape, F32) for shape in shapes),
        compiler_params=params(60, ("arbitrary",)),
        cost_estimate=cost(1e6, 26e6),
    )(place, *arrays)


def fast_body(
    hidden_in,
    gain_attn,
    w_query,
    w_key,
    w_value,
    w_output,
    gain_mlp,
    w_router,
    w_gate,
    w_up,
    w_down,
    expert_ids,
    slot_order,
    grad_out,
):
    inputs = hidden_in[0]
    cotangent = grad_out[0]
    chosen = expert_ids[0]
    tokens = inputs.shape[0]
    top = chosen.shape[1]
    local_experts = w_gate.shape[0]
    peers = lax.axis_size("expert")
    all_experts = local_experts * peers
    shards = lax.axis_size("dp")
    length = shards * tokens
    devices = shards * peers
    index = lax.axis_index("dp")
    column = lax.axis_index("expert")
    y_at = index % 2
    zl_at = (index // 2) % 2
    zh_at = index // 4
    place = jnp.stack(
        [zl_at, y_at, zl_at, zh_at, column * local_experts, index * peers + column]
    ).astype(jnp.int32)

    ranks = slot_order[0, 0].reshape(tokens, top)
    far = tokens * top
    names = jnp.arange(all_experts, dtype=jnp.int32)
    match = chosen.T[None] == names[:, None, None]
    rank_map = jnp.min(jnp.where(match, ranks.T[None], far), axis=1).astype(F32)
    turned = rank_map.T
    map_rows = jnp.pad(
        jnp.where(turned < far, 0.0, -1.0),
        ((0, 0), (0, LANES - all_experts)),
        constant_values=-1.0,
    )
    wr_pad = jnp.pad(w_router, ((0, 0), (0, LANES - all_experts)))
    wr_t = jnp.roll(w_router.T, -column * local_experts, axis=0)
    wr_t = jnp.pad(wr_t, ((0, LANES - all_experts), (0, 0)))

    half = HEAD_DIM // 2
    frequency = jnp.exp(-math.log(10000.0) * jnp.arange(half, dtype=F32) * 2.0 / HEAD_DIM)
    own_angles = (index * tokens + jnp.arange(tokens, dtype=jnp.int32)).astype(F32)[:, None] * frequency
    cos_own, sin_own = jnp.cos(own_angles), jnp.sin(own_angles)
    cos_tab = jnp.concatenate([cos_own] * 4, axis=1)
    sin_tab = jnp.concatenate([-sin_own, sin_own] * 2, axis=1)
    angles = frequency[:, None] * jnp.arange(length, dtype=jnp.int32).astype(F32)[None]
    cos_t, sin_t = jnp.cos(angles), jnp.sin(angles)

    normed, pack, g_own = run_pre(
        inputs, gain_attn, w_query, w_key, w_value, cos_tab, sin_tab, cotangent
    )
    pack, slot_map = run_first(pack, rank_map, turned, float(far))
    pack, slot_map, g_late = fence(pack, slot_map, g_own)
    g_x = swap_bit(g_own, X_BIT)
    g_z = swap_bit(g_late, ZL_BIT)
    maps = stack_swap(slot_map[None], X_BIT)
    out, out_t, lse = run_forward(pack)
    out, g_x, g_z, maps = fence(out, g_x, g_z, maps)
    g_zx = swap_bit(g_z, X_BIT)
    maps = stack_swap(maps, ZL_BIT)
    att = run_trade(out, 3)
    att, g_zx, maps = fence(att, g_zx, maps)
    middle, normed_two, att_full = run_mid(att, w_output, inputs, gain_mlp)
    x_all, g_all, maps = run_gather(normed_two, (g_own, g_x, g_z, g_zx), maps)
    maps = jnp.roll(maps, -column * local_experts, axis=1)
    expert_args = (place, x_all, g_all, maps, wr_t, w_gate, w_up, w_down)
    first = run_experts(*expert_args)
    gate_ka, gate_s0, gate_s1, up_ka, up_s0, up_s1, down_ka, down_s0, down_s1 = first[4:]
    down_ya = swap_bit(down_s1, Y_BIT)
    gate_ya = swap_bit(gate_s1, Y_BIT)
    early = swap_bit(jnp.stack([gate_ka[1, 1], gate_s1[1]]), ZH_BIT)
    mix_keep, mix_send, dx_keep, dx_send, *second = run_experts(*expert_args, prior=first[:4])
    gate_kb, gate_t0, gate_t1, up_kb, up_t0, up_t1, down_kb, down_t0, down_t1 = second
    down_ga = swap_bit(down_s0, Y_BIT)
    dx_send, down_ya, gate_ya, early = fence(dx_send, down_ya, gate_ya, early)
    gate_s0 = jnp.stack([gate_s0[0], add_low(gate_s0[1], early[1])])
    quarter = tokens // 4
    extra = dx_keep.shape[2]
    token_parts = tuple(
        (n * quarter, quarter, 0, extra, (1, 0) if n < 2 else (0, 1)) for n in (2, 0, 3, 1)
    )
    dx_sum, up_ya, gate_ga, mix_got, down_ma = run_reduce(
        ((dx_keep, dx_send),),
        ((C_BIT, (X_BIT, ZL_BIT), token_parts, (extra,)),),
        6,
        riders=(
            Rider(Y_BIT, up_s1),
            Rider(Y_BIT, gate_s0),
            Rider(C_BIT, mix_send, turns=(1,)),
            Rider(ZH_BIT, (down_ka, (1,)), down_ya, turns=(1, 0)),
        ),
    )
    dx_sum, gate_ya, down_ga, gate_t1 = fence(dx_sum, gate_ya, down_ga, gate_t1)
    gate_ma = swap_bit(add_low(gate_ka[1, 0], gate_ya[0]), ZH_BIT)
    gate_yb = swap_bit(gate_t1, Y_BIT)
    d_att, d_middle, d_low, d_log, ggain_mlp = run_post(
        dx_sum, middle, cotangent, normed_two, wr_pad, map_rows, gain_mlp, w_output
    )
    d_att, gate_ma, gate_yb = fence(d_att, gate_ma, gate_yb)
    mix_keep = mix_keep.reshape(2, 2, tokens, WIDTH)
    mix_got = mix_got.reshape(2, 2, tokens, WIDTH)
    every = slice(None)
    d_out, up_yb, up_za, gate_oa, mix_x, out_keep, out_got = run_trade(
        d_att,
        4,
        work=(att_full, d_low),
        blocks=devices,
        riders=(
            Rider(Y_BIT, up_t1),
            Rider(ZH_BIT, (up_ka, (1, 1)), (up_ya, (1,))),
            Rider(ZL_BIT, (gate_ka, (0, 1)), (early, (0,)), (gate_ga, (1,))),
            Rider(X_BIT, (mix_keep, (every, 1)), (mix_got, (every, 1))),
        ),
    )
    split = (8, 2, WIDTH // devices, WIDTH)
    out_keep, out_got = out_keep.reshape(split), out_got.reshape(split)
    up_ga, down_yb, up_late, gate_late, _ = fence(up_s0, down_t1, up_ya, gate_yb, d_out)
    both = jnp.stack([add_low(up_ka[1, 0], up_late[0]), add_low(gate_kb[1, 1], gate_late[1])])
    both = swap_bit(both, ZH_BIT)
    up_ga = swap_bit(up_ga, Y_BIT)
    down_yb = swap_bit(down_yb, Y_BIT)
    d_pack = run_backward(pack, d_out, out_t, lse, cos_t, sin_t)
    d_pack, both, up_ga, down_yb = fence(d_pack, both, up_ga, down_yb)
    d_pack, gate_gb, up_gb, gate_mb, up_zb, mix_z, out_x, up_oa = run_trade(
        d_pack,
        5,
        riders=(
            Rider(Y_BIT, gate_t0),
            Rider(Y_BIT, up_t0),
            Rider(ZH_BIT, (gate_kb, (1, 0)), (gate_yb, (0,))),
            Rider(ZH_BIT, (up_kb, (1, 1)), (up_yb, (1,))),
            Rider(
                ZL_BIT,
                (mix_keep, (slice(1, 2), 0)),
                (mix_got, (slice(1, 2), 0)),
                (mix_x, (slice(1, 2),)),
            ),
            Rider(X_BIT, (out_keep, (every, 1)), (out_got, (every, 1))),
            Rider(ZL_BIT, (up_ka, (0, 1)), (up_ga, (1,)), (up_za, (every,))),
        ),
    )
    d_pack, up_yb, down_yb, gate_gb, down_t0, mix_z, out_x = fence(
        d_pack, up_yb, down_yb, gate_gb, down_t0, mix_z, out_x
    )
    other = jnp.stack(
        [add_low(gate_kb[0, 1], gate_gb[1], both[1]), add_low(up_kb[0, 1], up_gb[1], up_zb)]
    )
    other = swap_bit(other, ZL_BIT)
    down_mb = swap_bit(add_low(down_kb[1], down_yb), ZH_BIT)
    down_gb = swap_bit(down_t0, Y_BIT)
    d_full, qkv_keep, qkv_send = run_qkvgrad(place, normed, d_pack, devices)
    mixed = sum_pair(mix_keep[0, 0], mix_got[0, 0]) + sum_pair(mix_x[0], mix_z[0])
    hidden_out = middle + mixed
    rows = WIDTH // devices
    out_held = add_low(out_keep[:, 0], out_got[:, 0], out_x).reshape(4, 2, rows, WIDTH)
    out_first, out_second = out_held[:, 0], out_held[:, 1]
    qkv_send, out_second, hidden_out = fence(qkv_send, out_second, hidden_out)
    qkv_parts = (
        (0, rows, 0, 768, (0, 1, 2, 3)),
        (0, rows, 768, 768, (1, 0, 2, 3)),
        (0, rows, 1536, 512, (0, 1, 2, 3)),
        (0, rows, 2048, 512, (1, 0, 2, 3)),
    )
    dense_bits = (X_BIT, Y_BIT, ZL_BIT, ZH_BIT)
    last = (d_full, w_query, w_key, w_value, d_middle, inputs, normed_two, d_log)
    grad_in, query_total, key_total, value_total, output_total, small, up_mb = run_reduce(
        ((qkv_keep, qkv_send), (out_first, out_second)),
        (
            (C_BIT, dense_bits, qkv_parts, (WIDTH, KV_HEADS * HEAD_DIM, KV_HEADS * HEAD_DIM)),
            (Y_BIT, (ZL_BIT, ZH_BIT), ((0, rows, 0, WIDTH, (0, 1)),), (WIDTH,)),
            (C_BIT, dense_bits, ((0, rows, 0, LANES, (0, 1, 2, 3)),), (LANES,)),
        ),
        7,
        riders=(Rider(ZH_BIT, (up_kb, (1, 0)), (up_yb, (0,))),),
        work=plan_last(last, gain_attn, ggain_mlp, devices),
    )
    query_total, small, down_mb, down_gb, other = fence(
        query_total, small, down_mb, down_gb, other
    )
    joined = run_join(
        place,
        (
            (gate_ka, gate_ga, gate_ma, gate_oa, up_ka, up_ga, (both, 0), up_oa)
            + (down_ka, down_ga, down_ma),
            (gate_kb, gate_gb, gate_mb, (other, 0), up_kb, up_gb, up_mb, (other, 1))
            + (down_kb, down_gb, down_mb),
        ),
    )
    gate_total, up_total, down_total = [
        total.reshape((local_experts,) + total.shape[2:]) for total in joined
    ]
    return (
        hidden_out[None],
        grad_in[None],
        small[:, LANES - 1],
        query_total,
        key_total,
        value_total,
        output_total,
        small[:, LANES - 2],
        small[:, :all_experts],
        gate_total,
        up_total,
        down_total,
    )


def fits(mesh):
    return mesh.shape["dp"] == KV_HEADS and mesh.shape["expert"] == 4


def solution(mesh):
    in_specs = (
        P("expert", "dp", None),
        P(),
        P(),
        P(),
        P(),
        P(),
        P(),
        P(),
        P("expert", None, None),
        P("expert", None, None),
        P("expert", None, None),
        P("expert", "dp", None),
        P("expert", "dp", None),
        P("expert", "dp", None),
    )
    out_specs = (
        P("expert", "dp", None),
        P("expert", "dp", None),
        P(("dp", "expert")),
        P(("dp", "expert"), None),
        P(("dp", "expert"), None),
        P(("dp", "expert"), None),
        P(("dp", "expert"), None),
        P(("dp", "expert")),
        P(("dp", "expert"), None),
        P("expert", "dp", None),
        P("expert", "dp", None),
        P("expert", "dp", None),
    )
    chosen = fast_body if fits(mesh) else body
    return jax.shard_map(chosen, mesh=mesh, in_specs=in_specs, out_specs=out_specs, check_vma=False)
```

```python
import functools
import math

import jax
import jax.numpy as jnp
from jax import lax
from jax.experimental import pallas as pl
from jax.experimental.pallas import tpu as pltpu
from jax.sharding import PartitionSpec as P

HEADS = 24
KV_HEADS = 8
HEAD_DIM = 64


EPS = 1e-05
MASKED = -1e30


def rotary_tables(positions):
    half = HEAD_DIM // 2
    frequency = jnp.exp(-math.log(10000.0) * jnp.arange(half, dtype=jnp.float32) * 2.0 / HEAD_DIM)
    angles = positions.astype(jnp.float32)[:, None] * frequency[None, :]
    return (jnp.cos(angles)[:, None, :], jnp.sin(angles)[:, None, :])


def rotate(values, cosine, sine):
    half = values.shape[-1] // 2
    first = values[..., :half]
    second = values[..., half:]
    return jnp.concatenate(
        [first * cosine - second * sine, second * cosine + first * sine], axis=-1
    )


def rotate_back(values, cosine, sine):
    half = values.shape[-1] // 2
    first = values[..., :half]
    second = values[..., half:]
    return jnp.concatenate(
        [first * cosine + second * sine, second * cosine - first * sine], axis=-1
    )


def assign_slots(row_chosen, row_ranks, all_experts, capacity):
    pairs = row_chosen.shape[0]
    by_rank = jnp.zeros((pairs,), jnp.int32).at[row_ranks].set(jnp.arange(pairs, dtype=jnp.int32))
    ordered = row_chosen[by_rank]
    table = (ordered[:, None] == jnp.arange(all_experts, dtype=jnp.int32)[None, :]).astype(
        jnp.int32
    )
    before = jnp.sum(table * (jnp.cumsum(table, axis=0) - 1), axis=1)
    slot = before[row_ranks]
    target = jnp.where(slot < capacity, row_chosen * capacity + slot, all_experts * capacity)
    owner = (
        jnp.full((all_experts * capacity,), pairs, jnp.int32)
        .at[target]
        .set(jnp.arange(pairs, dtype=jnp.int32), mode="drop")
    )
    return (target, owner)


def body(
    hidden_in,
    gain_attn,
    w_query,
    w_key,
    w_value,
    w_output,
    gain_mlp,
    w_router,
    w_gate,
    w_up,
    w_down,
    expert_ids,
    slot_order,
    grad_out,
):
    inputs = hidden_in[0]
    cotangent = grad_out[0]
    chosen = expert_ids[0]
    tokens, width = inputs.shape
    top = chosen.shape[1]
    local_experts = w_gate.shape[0]
    peers = lax.axis_size("expert")
    all_experts = local_experts * peers
    pairs = tokens * top
    capacity = pairs // all_experts
    shards = lax.axis_size("dp")
    index = lax.axis_index("dp")
    length = shards * tokens
    block = math.gcd(length, 512)
    groups = HEADS // KV_HEADS
    scale = HEAD_DIM ** (-0.5)
    query_pos = index * tokens + jnp.arange(tokens, dtype=jnp.int32)
    cosine, sine = rotary_tables(query_pos)
    count = ((index + 1) * tokens + block - 1) // block
    inv_one = lax.rsqrt(jnp.mean(inputs * inputs, axis=-1, keepdims=True) + EPS)
    normed = (inputs * inv_one * gain_attn).astype(jnp.bfloat16)
    query_pre = jnp.dot(normed, w_query, preferred_element_type=jnp.float32).reshape(
        tokens, HEADS, HEAD_DIM
    )
    queries = rotate(query_pre, cosine, sine).astype(jnp.bfloat16)
    key_pre = jnp.dot(normed, w_key, preferred_element_type=jnp.float32).reshape(
        tokens, KV_HEADS, HEAD_DIM
    )
    keys_low = rotate(key_pre, cosine, sine).astype(jnp.bfloat16)
    values_low = (
        jnp.dot(normed, w_value, preferred_element_type=jnp.float32)
        .astype(jnp.bfloat16)
        .reshape(tokens, KV_HEADS, HEAD_DIM)
    )
    keys_all, values_all = (
        lax.all_gather(keys_low, "dp", axis=0, tiled=True),
        lax.all_gather(values_low, "dp", axis=0, tiled=True),
    )
    query_groups = queries.reshape(tokens, KV_HEADS, groups, HEAD_DIM)

    def block_scores(key_block, start):
        raw = (
            jnp.einsum(
                "qkgd,skd->kgqs", query_groups, key_block, preferred_element_type=jnp.float32
            )
            * scale
        )
        key_pos = start + jnp.arange(block, dtype=jnp.int32)
        allowed = key_pos[None, :] <= query_pos[:, None]
        return jnp.where(allowed, raw, MASKED)

    def stats_step(step, carry):
        running, total = carry
        scores = block_scores(
            lax.dynamic_slice_in_dim(keys_all, step * block, block, 0), step * block
        )
        newest = jnp.maximum(running, jnp.max(scores, axis=-1))
        total = total * jnp.exp(running - newest) + jnp.sum(
            jnp.exp(scores - newest[..., None]), axis=-1
        )
        return (newest, total)

    stat_init = (
        jnp.full((KV_HEADS, groups, tokens), MASKED, jnp.float32),
        jnp.zeros((KV_HEADS, groups, tokens), jnp.float32),
    )
    running, total = lax.fori_loop(0, count, stats_step, stat_init)
    log_total = running + jnp.log(total)

    def output_step(step, accum):
        start = step * block
        scores = block_scores(lax.dynamic_slice_in_dim(keys_all, start, block, 0), start)
        probs = jnp.exp(scores - log_total[..., None]).astype(jnp.bfloat16)
        value_block = lax.dynamic_slice_in_dim(values_all, start, block, 0)
        return accum + jnp.einsum(
            "kgqs,skd->qkgd", probs, value_block, preferred_element_type=jnp.float32
        )

    attended_groups = lax.fori_loop(
        0, count, output_step, jnp.zeros((tokens, KV_HEADS, groups, HEAD_DIM), jnp.float32)
    )
    attended = attended_groups.reshape(tokens, HEADS * HEAD_DIM)
    attended_low = attended.astype(jnp.bfloat16)
    branch = jnp.dot(attended_low, w_output, preferred_element_type=jnp.float32)
    middle = inputs + branch
    inv_two = lax.rsqrt(jnp.mean(middle * middle, axis=-1, keepdims=True) + EPS)
    normed_two = (middle * inv_two * gain_mlp).astype(jnp.bfloat16)
    logits = jnp.dot(normed_two, w_router, preferred_element_type=jnp.float32)
    onehot = (chosen[:, :, None] == jnp.arange(all_experts, dtype=jnp.int32)[None, None, :]).astype(
        jnp.float32
    )
    picked = jnp.sum(onehot * logits[:, None, :], axis=-1)
    gates = jax.nn.softmax(picked, axis=-1)
    target, owner = assign_slots(chosen.reshape(pairs), slot_order[0, 0], all_experts, capacity)
    valid = owner < pairs
    source = jnp.minimum(owner, pairs - 1)
    rows_send = jnp.where(valid[:, None], normed_two[source // top], 0).reshape(
        peers, local_experts, capacity, width
    )
    received = lax.all_to_all(rows_send, "expert", split_axis=0, concat_axis=0, tiled=True)
    gate_pre = jnp.einsum("necd,edf->necf", received, w_gate, preferred_element_type=jnp.float32)
    up_pre = jnp.einsum("necd,edf->necf", received, w_up, preferred_element_type=jnp.float32)
    hidden = (jax.nn.silu(gate_pre) * up_pre).astype(jnp.bfloat16)
    result = jnp.einsum(
        "necf,efd->necd", hidden, w_down, preferred_element_type=jnp.float32
    ).astype(jnp.bfloat16)
    returned = lax.all_to_all(result, "expert", split_axis=0, concat_axis=0, tiled=True)
    returned, received, gate_pre, up_pre = (returned, received, gate_pre, up_pre)
    zero_row = jnp.zeros((1, width), jnp.bfloat16)
    pair_out = jnp.concatenate([returned.reshape(all_experts * capacity, width), zero_row], axis=0)[
        target
    ].reshape(tokens, top, width)
    mixed = jnp.einsum("tk,tkd->td", gates, pair_out, preferred_element_type=jnp.float32)
    hidden_out = middle + mixed
    dy_pairs = (
        (gates[:, :, None] * cotangent[:, None, :]).astype(jnp.bfloat16).reshape(pairs, width)
    )
    dy_send = jnp.where(valid[:, None], dy_pairs[source], 0).reshape(
        peers, local_experts, capacity, width
    )
    dy_received = lax.all_to_all(dy_send, "expert", split_axis=0, concat_axis=0, tiled=True)
    sigmoid_gate = jax.nn.sigmoid(gate_pre)
    silu_gate = gate_pre * sigmoid_gate
    hidden = (silu_gate * up_pre).astype(jnp.bfloat16)
    grad_down_part = jnp.einsum(
        "necf,necd->efd", hidden, dy_received, preferred_element_type=jnp.float32
    )
    d_hidden = jnp.einsum("necd,efd->necf", dy_received, w_down, preferred_element_type=jnp.float32)
    d_gate = (d_hidden * up_pre * sigmoid_gate * (1.0 + gate_pre * (1.0 - sigmoid_gate))).astype(
        jnp.bfloat16
    )
    d_up = (d_hidden * silu_gate).astype(jnp.bfloat16)
    grad_gate_part = jnp.einsum(
        "necd,necf->edf", received, d_gate, preferred_element_type=jnp.float32
    )
    grad_up_part = jnp.einsum("necd,necf->edf", received, d_up, preferred_element_type=jnp.float32)
    gate_total, up_total, down_total = (
        lax.psum_scatter(
            grad_gate_part.astype(jnp.bfloat16), "dp", scatter_dimension=1, tiled=True
        ).astype(jnp.float32),
        lax.psum_scatter(
            grad_up_part.astype(jnp.bfloat16), "dp", scatter_dimension=1, tiled=True
        ).astype(jnp.float32),
        lax.psum_scatter(
            grad_down_part.astype(jnp.bfloat16), "dp", scatter_dimension=1, tiled=True
        ).astype(jnp.float32),
    )
    d_rows = jnp.einsum("necf,edf->necd", d_gate, w_gate, preferred_element_type=jnp.float32)
    d_rows = (
        d_rows + jnp.einsum("necf,edf->necd", d_up, w_up, preferred_element_type=jnp.float32)
    ).astype(jnp.bfloat16)
    d_back = lax.all_to_all(d_rows, "expert", split_axis=0, concat_axis=0, tiled=True)
    d_pairs = jnp.concatenate([d_back.reshape(all_experts * capacity, width), zero_row], axis=0)[
        target
    ].reshape(tokens, top, width)
    d_normed_two = jnp.sum(d_pairs, axis=1, dtype=jnp.float32)
    d_gates = jnp.einsum("td,tkd->tk", cotangent, pair_out, preferred_element_type=jnp.float32)
    d_picked = gates * (d_gates - jnp.sum(gates * d_gates, axis=-1, keepdims=True))
    d_logits = jnp.sum(onehot * d_picked[:, :, None], axis=1).astype(jnp.bfloat16)
    grad_router_part = jnp.einsum(
        "td,te->de", normed_two, d_logits, preferred_element_type=jnp.float32
    )
    d_normed_two = d_normed_two + jnp.einsum(
        "te,de->td", d_logits, w_router, preferred_element_type=jnp.float32
    )
    scaled_two = d_normed_two * gain_mlp
    grad_gain_mlp_part = jnp.sum(d_normed_two * middle * inv_two, axis=0)
    d_middle = (
        cotangent
        + inv_two * scaled_two
        - middle * inv_two**3 * jnp.mean(middle * scaled_two, axis=-1, keepdims=True)
    )
    d_branch = d_middle.astype(jnp.bfloat16)
    grad_output_part = jnp.einsum(
        "tf,td->fd", attended_low, d_branch, preferred_element_type=jnp.float32
    )
    d_attended = jnp.einsum(
        "td,fd->tf", d_branch, w_output, preferred_element_type=jnp.float32
    ).astype(jnp.bfloat16)
    d_groups = d_attended.reshape(tokens, KV_HEADS, groups, HEAD_DIM)
    delta = jnp.einsum(
        "qkgd,qkgd->kgq", d_groups, attended_groups, preferred_element_type=jnp.float32
    )
    keys_back, values_back = (
        lax.all_gather(keys_low, "dp", axis=0, tiled=True),
        lax.all_gather(values_low, "dp", axis=0, tiled=True),
    )

    def grad_step(step, carry):
        d_query, d_keys, d_values = carry
        start = step * block
        key_block = lax.dynamic_slice_in_dim(keys_back, start, block, 0)
        value_block = lax.dynamic_slice_in_dim(values_back, start, block, 0)
        scores = block_scores(key_block, start)
        probs = jnp.exp(scores - log_total[..., None])
        probs_low = probs.astype(jnp.bfloat16)
        d_probs = jnp.einsum(
            "qkgd,skd->kgqs", d_groups, value_block, preferred_element_type=jnp.float32
        )
        d_scores = (probs * (d_probs - delta[..., None])).astype(jnp.bfloat16)
        d_query = d_query + jnp.einsum(
            "kgqs,skd->qkgd", d_scores, key_block, preferred_element_type=jnp.float32
        )
        key_part = jnp.einsum(
            "kgqs,qkgd->skd", d_scores, query_groups, preferred_element_type=jnp.float32
        )
        value_part = jnp.einsum(
            "kgqs,qkgd->skd", probs_low, d_groups, preferred_element_type=jnp.float32
        )
        d_keys = lax.dynamic_update_slice_in_dim(
            d_keys, lax.dynamic_slice_in_dim(d_keys, start, block, 0) + key_part, start, 0
        )
        d_values = lax.dynamic_update_slice_in_dim(
            d_values, lax.dynamic_slice_in_dim(d_values, start, block, 0) + value_part, start, 0
        )
        return (d_query, d_keys, d_values)

    grad_init = (
        jnp.zeros((tokens, KV_HEADS, groups, HEAD_DIM), jnp.float32),
        jnp.zeros((length, KV_HEADS, HEAD_DIM), jnp.float32),
        jnp.zeros((length, KV_HEADS, HEAD_DIM), jnp.float32),
    )
    d_query, d_keys, d_values = lax.fori_loop(0, count, grad_step, grad_init)
    key_sum, value_sum = (
        lax.psum_scatter(
            (d_keys * scale).reshape(length, KV_HEADS * HEAD_DIM).astype(jnp.bfloat16),
            "dp",
            scatter_dimension=0,
            tiled=True,
        ).astype(jnp.float32),
        lax.psum_scatter(
            d_values.reshape(length, KV_HEADS * HEAD_DIM).astype(jnp.bfloat16),
            "dp",
            scatter_dimension=0,
            tiled=True,
        ).astype(jnp.float32),
    )
    d_query_low = (
        rotate_back((d_query * scale).reshape(tokens, HEADS, HEAD_DIM), cosine, sine)
        .astype(jnp.bfloat16)
        .reshape(tokens, HEADS * HEAD_DIM)
    )
    d_key_low = (
        rotate_back(key_sum.reshape(tokens, KV_HEADS, HEAD_DIM), cosine, sine)
        .astype(jnp.bfloat16)
        .reshape(tokens, KV_HEADS * HEAD_DIM)
    )
    d_value_low = value_sum.astype(jnp.bfloat16)
    grad_query_part = jnp.einsum(
        "td,tf->df", normed, d_query_low, preferred_element_type=jnp.float32
    )
    grad_key_part = jnp.einsum("td,tf->df", normed, d_key_low, preferred_element_type=jnp.float32)
    grad_value_part = jnp.einsum(
        "td,tf->df", normed, d_value_low, preferred_element_type=jnp.float32
    )
    d_normed = jnp.einsum("tf,df->td", d_query_low, w_query, preferred_element_type=jnp.float32)
    d_normed = d_normed + jnp.einsum(
        "tf,df->td", d_key_low, w_key, preferred_element_type=jnp.float32
    )
    d_normed = d_normed + jnp.einsum(
        "tf,df->td", d_value_low, w_value, preferred_element_type=jnp.float32
    )
    scaled_one = d_normed * gain_attn
    grad_gain_attn_part = jnp.sum(d_normed * inputs * inv_one, axis=0)
    grad_in = (
        d_middle
        + inv_one * scaled_one
        - inputs * inv_one**3 * jnp.mean(inputs * scaled_one, axis=-1, keepdims=True)
    )
    dense = (
        lax.psum_scatter(grad_gain_attn_part, ("dp", "expert"), scatter_dimension=0, tiled=True),
        lax.psum_scatter(grad_query_part, ("dp", "expert"), scatter_dimension=0, tiled=True),
        lax.psum_scatter(grad_key_part, ("dp", "expert"), scatter_dimension=0, tiled=True),
        lax.psum_scatter(grad_value_part, ("dp", "expert"), scatter_dimension=0, tiled=True),
        lax.psum_scatter(grad_output_part, ("dp", "expert"), scatter_dimension=0, tiled=True),
        lax.psum_scatter(grad_gain_mlp_part, ("dp", "expert"), scatter_dimension=0, tiled=True),
        lax.psum_scatter(grad_router_part, ("dp", "expert"), scatter_dimension=0, tiled=True),
    )
    return (
        hidden_out[None],
        grad_in[None],
        dense[0],
        dense[1],
        dense[2],
        dense[3],
        dense[4],
        dense[5],
        dense[6],
        gate_total,
        up_total,
        down_total,
    )

BF = jnp.bfloat16
F32 = jnp.float32
WIDTH = 1536
LANES = 128
PER_KV = HEADS // KV_HEADS
ROWS_Q = PER_KV * HEAD_DIM
PACK = ROWS_Q + 2 * HEAD_DIM
BIT_Y, BIT_ZL, BIT_ZH = 1, 2, 4
BIT_C, BIT_X = 1, 2
BLOCK_Q = 256
BLOCK_K = 512
SLOTS = 64
CHUNK = 512
MIB = 1 << 20
hbm = pl.BlockSpec(memory_space=pltpu.HBM)


def dot_nn(a, b):
    return lax.dot_general(a, b, (((1,), (0,)), ((), ())), preferred_element_type=F32)


def dot_nt(a, b):
    return lax.dot_general(a, b, (((1,), (1,)), ((), ())), preferred_element_type=F32)


def dot_tn(a, b):
    return lax.dot_general(a, b, (((0,), (0,)), ((), ())), preferred_element_type=F32)


def cost(flops, moved, transcendentals=0):
    return pl.CostEstimate(
        flops=int(flops), bytes_accessed=int(moved), transcendentals=int(transcendentals)
    )


def params(mib, dims=None):
    return pltpu.CompilerParams(vmem_limit_bytes=mib * MIB, dimension_semantics=dims)


def swap(values, axis, mask):
    size = lax.axis_size(axis)
    return lax.ppermute(values, axis, [(i, i ^ mask) for i in range(size)])


def swap_bit(values, bit):
    axis, mask = bit
    return swap(values, axis, mask)


def fence(*values):
    return lax.optimization_barrier(values)


C_BIT = ("expert", BIT_C)
X_BIT = ("expert", BIT_X)
Y_BIT = ("dp", BIT_Y)
ZL_BIT = ("dp", BIT_ZL)
ZH_BIT = ("dp", BIT_ZH)


def pre_kernel(
    hid_ref,
    gain_ref,
    wq_ref,
    wk_ref,
    wv_ref,
    cos_ref,
    sin_ref,
    cot_ref,
    norm_ref,
    pack_ref,
    low_ref,
):
    tokens = hid_ref.shape[0]
    half = tokens // 2
    low_ref[...] = cot_ref[...].astype(BF)
    inputs = hid_ref[...]
    inv = lax.rsqrt(jnp.mean(inputs * inputs, axis=-1, keepdims=True) + EPS)
    normed = (inputs * inv * gain_ref[...]).astype(BF)
    norm_ref[...] = normed
    low = (lax.broadcasted_iota(jnp.int32, (tokens, LANES), 1) % HEAD_DIM) < HEAD_DIM // 2
    cosine, sine = cos_ref[...], sin_ref[...]

    def turn(tile):
        other = jnp.where(
            low,
            pltpu.roll(tile, LANES - HEAD_DIM // 2, 1),
            pltpu.roll(tile, HEAD_DIM // 2, 1),
        )
        return (tile * cosine + other * sine).astype(BF)

    tiles = []
    for n in range(wq_ref.shape[1] // CHUNK):
        pre = dot_nn(normed, wq_ref[:, n * CHUNK : (n + 1) * CHUNK])
        tiles += [turn(pre[:, m * LANES : (m + 1) * LANES]) for m in range(CHUNK // LANES)]
    queries = jnp.concatenate(tiles, axis=1)
    pre = dot_nn(normed, wk_ref[...])
    keys = jnp.concatenate(
        [turn(pre[:, m * LANES : (m + 1) * LANES]) for m in range(pre.shape[1] // LANES)], axis=1
    )
    values = dot_nn(normed, wv_ref[...]).astype(BF)
    for g in range(KV_HEADS):
        at = g * ROWS_Q
        head = slice(g * HEAD_DIM, (g + 1) * HEAD_DIM)
        pack_ref[g, 0:tokens] = queries[:, at : at + LANES]
        pack_ref[g, tokens : 2 * tokens] = jnp.concatenate(
            [queries[:, at + LANES : at + ROWS_Q], keys[:, head]], axis=1
        )
        pack_ref[g, 2 * tokens :] = jnp.concatenate(
            [values[:half, head], values[half:, head]], axis=1
        )


def run_pre(inputs, gain, w_query, w_key, w_value, cos_tab, sin_tab, cotangent):
    tokens = inputs.shape[0]
    return pl.pallas_call(
        pre_kernel,
        out_shape=(
            jax.ShapeDtypeStruct((tokens, WIDTH), BF),
            jax.ShapeDtypeStruct((KV_HEADS, tokens * PACK // LANES, LANES), BF),
            jax.ShapeDtypeStruct((tokens, WIDTH), BF),
        ),
        compiler_params=params(60),
        cost_estimate=cost(2 * tokens * WIDTH * 2560, 14e6),
    )(inputs, gain[None], w_query, w_key, w_value, cos_tab, sin_tab, cotangent)


def unpack_heads(block_ref, out_ref, row, tokens, column):
    half = tokens // 2
    out_ref[row : row + tokens, column : column + LANES] = block_ref[0:tokens]
    rest = block_ref[tokens : tokens + half]
    out_ref[row : row + half, column + LANES : column + ROWS_Q] = rest[:, :HEAD_DIM]
    out_ref[row + half : row + tokens, column + LANES : column + ROWS_Q] = rest[:, HEAD_DIM:]


def pack_heads(block_ref, rows, tokens):
    half = tokens // 2
    block_ref[0:tokens] = rows[:, 0:LANES]
    block_ref[tokens : tokens + half] = jnp.concatenate(
        [rows[:half, LANES:ROWS_Q], rows[half:, LANES:ROWS_Q]], axis=1
    )


def unpack_all(block_ref, q_ref, k_ref, v_ref, row, tokens, q_at=0, k_at=0, v_at=0):
    half = tokens // 2
    rows = slice(row, row + tokens)
    q_ref[rows, q_at : q_at + LANES] = block_ref[0:tokens]
    two = block_ref[tokens : 2 * tokens]
    q_ref[rows, q_at + LANES : q_at + ROWS_Q] = two[:, :HEAD_DIM]
    k_ref[rows, k_at : k_at + HEAD_DIM] = two[:, HEAD_DIM:]
    rest = block_ref[2 * tokens : 2 * tokens + half]
    v_ref[row : row + half, v_at : v_at + HEAD_DIM] = rest[:, :HEAD_DIM]
    v_ref[row + half : row + tokens, v_at : v_at + HEAD_DIM] = rest[:, HEAD_DIM:]


def heads_t(block, width):
    return jnp.concatenate(
        [block[:, h * HEAD_DIM : (h + 1) * HEAD_DIM].astype(F32).T for h in range(width)], axis=1
    )


def heads_rows(block, width):
    return jnp.concatenate(
        [block[:, h * HEAD_DIM : (h + 1) * HEAD_DIM] for h in range(width)], axis=0
    )


def allowed_t(step, block):
    shape = (BLOCK_K, PER_KV * BLOCK_Q)
    key_pos = step * BLOCK_K + lax.broadcasted_iota(jnp.int32, shape, 0)
    query_pos = block * BLOCK_Q + lax.broadcasted_iota(jnp.int32, shape, 1) % BLOCK_Q
    return key_pos <= query_pos


def forward_kernel(pack_ref, out_ref, out_t_ref, lse_ref, q_s, k_s, v_s, vt_s, out_s):
    block = pl.program_id(0)
    sources = pack_ref.shape[0]
    tokens = q_s.shape[0] // sources

    @pl.when(block == 0)
    def _():
        for n in range(sources):
            unpack_all(pack_ref.at[n], q_s, k_s, v_s, n * tokens, tokens)
        vt_s[...] = v_s[...].astype(F32).T.astype(BF)

    rows = pl.ds(pl.multiple_of(block * BLOCK_Q, BLOCK_Q), BLOCK_Q)
    scale = HEAD_DIM ** (-0.5)
    q_t = (heads_t(q_s[rows, :], PER_KV) * scale).astype(BF)
    columns = PER_KV * BLOCK_Q

    def step(j, carry, masked):
        running, total, accum = carry
        keys = pl.ds(pl.multiple_of(j * BLOCK_K, BLOCK_K), BLOCK_K)
        scores = dot_nn(k_s[keys, :], q_t)
        if masked:
            scores = jnp.where(allowed_t(j, block), scores, MASKED)
        newest = jnp.maximum(running, jnp.max(scores, axis=0, keepdims=True))
        fade = jnp.exp(running - newest)
        probs = jnp.exp(scores - newest)
        total = total * fade + jnp.sum(probs, axis=0, keepdims=True)
        accum = accum * fade + dot_nn(vt_s[:, keys], probs.astype(BF))
        return newest, total, accum

    carry = (
        jnp.full((1, columns), MASKED, F32),
        jnp.zeros((1, columns), F32),
        jnp.zeros((HEAD_DIM, columns), F32),
    )
    last = (block * BLOCK_Q) // BLOCK_K
    carry = lax.fori_loop(0, last, lambda j, c: step(j, c, False), carry)
    running, total, accum = step(last, carry, True)
    out_t = accum / total
    out_t_ref[0] = out_t
    lse_ref[0] = running + jnp.log(total)
    out_s[rows, :] = jnp.concatenate(
        [out_t[:, h * BLOCK_Q : (h + 1) * BLOCK_Q].T for h in range(PER_KV)], axis=1
    ).astype(BF)

    @pl.when(block == pl.num_programs(0) - 1)
    def _():
        for n in range(sources):
            pack_heads(out_ref.at[n], out_s[n * tokens : (n + 1) * tokens, :], tokens)


def run_forward(pack):
    sources = pack.shape[0]
    length = sources * (pack.shape[1] * LANES // PACK)
    packed = (sources, length // sources * ROWS_Q // LANES, LANES)
    blocks = length // BLOCK_Q
    columns = PER_KV * BLOCK_Q
    return pl.pallas_call(
        forward_kernel,
        grid=(blocks,),
        in_specs=[pl.BlockSpec(pack.shape, lambda i: (0, 0, 0))],
        out_specs=(
            pl.BlockSpec(packed, lambda i: (0, 0, 0)),
            pl.BlockSpec((1, HEAD_DIM, columns), lambda i: (i, 0, 0)),
            pl.BlockSpec((1, 1, columns), lambda i: (i, 0, 0)),
        ),
        out_shape=(
            jax.ShapeDtypeStruct(packed, BF),
            jax.ShapeDtypeStruct((blocks, HEAD_DIM, columns), F32),
            jax.ShapeDtypeStruct((blocks, 1, columns), F32),
        ),
        scratch_shapes=[
            pltpu.VMEM((length, ROWS_Q), BF),
            pltpu.VMEM((length, HEAD_DIM), BF),
            pltpu.VMEM((length, HEAD_DIM), BF),
            pltpu.VMEM((HEAD_DIM, length), BF),
            pltpu.VMEM((length, ROWS_Q), BF),
        ],
        compiler_params=params(60, ("arbitrary",)),
        cost_estimate=cost(8 * length * length * ROWS_Q, 6e6, length * length * PER_KV),
    )(pack)


def backward_kernel(
    pack_ref,
    grad_ref,
    out_t_ref,
    lse_ref,
    cos_ref,
    sin_ref,
    res_ref,
    q_s,
    do_s,
    k_s,
    v_s,
    kt_s,
    dk_s,
    dv_s,
):
    block = pl.program_id(0)
    sources = pack_ref.shape[0]
    tokens = q_s.shape[0] // sources

    @pl.when(block == 0)
    def _():
        for n in range(sources):
            unpack_all(pack_ref.at[n], q_s, k_s, v_s, n * tokens, tokens)
            unpack_heads(grad_ref.at[n], do_s, n * tokens, tokens, 0)
        kt_s[...] = k_s[...].astype(F32).T.astype(BF)
        dk_s[...] = jnp.zeros_like(dk_s)
        dv_s[...] = jnp.zeros_like(dv_s)

    scale = HEAD_DIM ** (-0.5)
    half = HEAD_DIM // 2
    rows = pl.ds(pl.multiple_of(block * BLOCK_Q, BLOCK_Q), BLOCK_Q)
    q_block = q_s[rows, :]
    q_t = (heads_t(q_block, PER_KV) * scale).astype(BF)
    q_rows = (heads_rows(q_block, PER_KV).astype(F32) * scale).astype(BF)
    do_block = do_s[rows, :]
    do_f32 = heads_t(do_block, PER_KV)
    do_t = do_f32.astype(BF)
    do_rows = heads_rows(do_block, PER_KV)
    delta = jnp.sum(do_f32 * out_t_ref[0], axis=0, keepdims=True)
    lse = lse_ref[0]

    def step(j, dq_t, masked):
        keys = pl.ds(pl.multiple_of(j * BLOCK_K, BLOCK_K), BLOCK_K)
        scores = dot_nn(k_s[keys, :], q_t)
        if masked:
            scores = jnp.where(allowed_t(j, block), scores, MASKED)
        probs = jnp.exp(scores - lse)
        d_probs = dot_nn(v_s[keys, :], do_t)
        d_scores = (probs * (d_probs - delta)).astype(BF)
        dv_s[keys, :] += dot_nn(probs.astype(BF), do_rows)
        dk_s[keys, :] += dot_nn(d_scores, q_rows)
        return dq_t + dot_nn(kt_s[:, keys], d_scores)

    last = (block * BLOCK_Q) // BLOCK_K
    dq_t = jnp.zeros((HEAD_DIM, PER_KV * BLOCK_Q), F32)
    dq_t = lax.fori_loop(0, last, lambda j, c: step(j, c, False), dq_t)
    dq_t = step(last, dq_t, True) * scale

    def turn_back(values, cosine, sine):
        first, second = values[:half], values[half:]
        return jnp.concatenate(
            [first * cosine + second * sine, second * cosine - first * sine], axis=0
        )

    columns = pl.ds(pl.multiple_of(block * BLOCK_Q, BLOCK_Q), BLOCK_Q)
    cosine, sine = cos_ref[:, columns], sin_ref[:, columns]
    q_s[rows, :] = jnp.concatenate(
        [
            turn_back(dq_t[:, h * BLOCK_Q : (h + 1) * BLOCK_Q], cosine, sine).T
            for h in range(PER_KV)
        ],
        axis=1,
    ).astype(BF)

    @pl.when(block == pl.num_programs(0) - 1)
    def _():
        dk = turn_back(dk_s[...].T, cos_ref[...], sin_ref[...]).T.astype(BF)
        half = tokens // 2
        for n in range(sources):
            row = n * tokens
            res_ref[n, 0:tokens] = q_s[row : row + tokens, 0:LANES]
            res_ref[n, tokens : 2 * tokens] = jnp.concatenate(
                [q_s[row : row + tokens, LANES:ROWS_Q], dk[row : row + tokens]], axis=1
            )
            res_ref[n, 2 * tokens :] = jnp.concatenate(
                [dv_s[row : row + half, :], dv_s[row + half : row + tokens, :]], axis=1
            ).astype(BF)


def run_backward(pack, grad, out_t, lse, cos_t, sin_t):
    length = cos_t.shape[1]
    blocks = length // BLOCK_Q
    columns = PER_KV * BLOCK_Q
    half = HEAD_DIM // 2
    return pl.pallas_call(
        backward_kernel,
        grid=(blocks,),
        in_specs=[
            pl.BlockSpec(pack.shape, lambda i: (0, 0, 0)),
            pl.BlockSpec(grad.shape, lambda i: (0, 0, 0)),
            pl.BlockSpec((1, HEAD_DIM, columns), lambda i: (i, 0, 0)),
            pl.BlockSpec((1, 1, columns), lambda i: (i, 0, 0)),
            pl.BlockSpec((half, length), lambda i: (0, 0)),
            pl.BlockSpec((half, length), lambda i: (0, 0)),
        ],
        out_specs=pl.BlockSpec(pack.shape, lambda i: (0, 0, 0)),
        out_shape=jax.ShapeDtypeStruct(pack.shape, BF),
        scratch_shapes=[
            pltpu.VMEM((length, ROWS_Q), BF),
            pltpu.VMEM((length, ROWS_Q), BF),
            pltpu.VMEM((length, HEAD_DIM), BF),
            pltpu.VMEM((length, HEAD_DIM), BF),
            pltpu.VMEM((HEAD_DIM, length), BF),
            pltpu.VMEM((length, HEAD_DIM), F32),
            pltpu.VMEM((length, HEAD_DIM), F32),
        ],
        compiler_params=params(60, ("arbitrary",)),
        cost_estimate=cost(20 * length * length * ROWS_Q, 8e6, length * length * PER_KV),
    )(pack, grad, out_t, lse, cos_t, sin_t)


def mid_kernel(att_ref, wo_ref, hid_ref, gain_ref, mid_ref, norm_ref, full_ref):
    for g in range(KV_HEADS):
        unpack_heads(att_ref.at[g], full_ref, 0, full_ref.shape[0], g * ROWS_Q)
    middle = hid_ref[...] + dot_nn(full_ref[...], wo_ref[...])
    mid_ref[...] = middle
    inv = lax.rsqrt(jnp.mean(middle * middle, axis=-1, keepdims=True) + EPS)
    norm_ref[...] = (middle * inv * gain_ref[...]).astype(BF)


def run_mid(att, w_output, inputs, gain):
    tokens = inputs.shape[0]
    return pl.pallas_call(
        mid_kernel,
        out_shape=(
            jax.ShapeDtypeStruct((tokens, WIDTH), F32),
            jax.ShapeDtypeStruct((tokens, WIDTH), BF),
            jax.ShapeDtypeStruct((tokens, WIDTH), BF),
        ),
        compiler_params=params(60),
        cost_estimate=cost(2 * tokens * WIDTH * WIDTH, 12e6),
    )(att, w_output, inputs, gain[None])


def expert_kernel(
    place_ref,
    x_ref,
    g_ref,
    gates_ref,
    map_ref,
    wg0_ref,
    wg1_ref,
    wu0_ref,
    wu1_ref,
    wd0_ref,
    wd1_ref,
    *refs,
    first,
):
    if first:
        mix_prior = dx_prior = None
    else:
        mix_prior, dx_prior = refs[0:2], refs[2:4]
        refs = refs[4:]
    (
    mix_keep,
    mix_send,
    dx_keep,
    dx_send,
    gate_keep,
    gate_send0,
    gate_send1,
    up_keep,
    up_send0,
    up_send1,
    down_keep,
    down_send0,
    down_send1,
    xs,
    gs,
    gate_s,
    wide_s,
    tall_s,
    ) = refs
    step = pl.program_id(0)
    sources = map_ref.shape[0]
    experts = xs.shape[0]
    low = 0 if first else experts
    rows = experts * SLOTS
    count = WIDTH // CHUNK

    def pick_of(source):
        return one_hot(map_ref[source, low : low + experts, :], rows)

    @pl.when(step < experts)
    def _():
        e = step
        x = x_ref[0]
        w_gate = jnp.concatenate([wg0_ref[0], wg1_ref[0]], axis=1)
        w_up = jnp.concatenate([wu0_ref[0], wu1_ref[0]], axis=1)
        gate_pre = dot_nn(x, w_gate)
        up_pre = dot_nn(x, w_up)
        sig = jax.nn.sigmoid(gate_pre)
        silu = gate_pre * sig
        hidden = (silu * up_pre).astype(BF)
        gate = gates_ref[0]
        d_hidden = jnp.zeros(hidden.shape, F32)
        d_gates = jnp.zeros(gate.shape, F32)
        for n in range(count):
            cols = slice(n * CHUNK, (n + 1) * CHUNK)
            w_down = jnp.concatenate([wd0_ref[0, :, cols], wd1_ref[0, :, cols]], axis=0)
            grad = g_ref[0, :, cols].astype(F32)
            d_y = (gate * grad).astype(BF)
            y = dot_nn(hidden, w_down)
            d_gates += jnp.sum(y * grad, axis=1, keepdims=True)
            gs[e, :, cols] = (gate * y).astype(BF)
            d_hidden += dot_nt(d_y, w_down)
            wide_s[:, cols] = dot_tn(hidden, d_y).astype(BF)
        gate_s[e] = d_gates
        d_gate = (d_hidden * up_pre * sig * (1.0 + gate_pre * (1.0 - sig))).astype(BF)
        d_up = (d_hidden * silu).astype(BF)

        y_at, zl_at, zh_at = place_ref[1], place_ref[2], place_ref[3]
        part = down_keep.shape[2]
        for z in range(2):
            base = (zh_at ^ z) * 2
            down_keep[z, 0] = wide_s[pl.ds(pl.multiple_of((base + y_at) * part, part), part), :]
            (down_send0, down_send1)[z][0] = wide_s[
                pl.ds(pl.multiple_of((base + (1 - y_at)) * part, part), part), :
            ]

        def spread(keep, send):
            part = keep.shape[3]
            for z in range(2):
                for low in range(2):
                    base = ((zh_at ^ z) * 2 + (zl_at ^ low)) * 2
                    keep[z, low, 0] = tall_s[
                        pl.ds(pl.multiple_of((base + y_at) * part, part), part), :
                    ]
                    send[z][low, 0] = tall_s[
                        pl.ds(pl.multiple_of((base + (1 - y_at)) * part, part), part), :
                    ]

        for n in range(count):
            cols = slice(n * CHUNK, (n + 1) * CHUNK)
            tall_s[cols, :] = dot_tn(x[:, cols], d_gate).astype(BF)
        spread(gate_keep, (gate_send0, gate_send1))
        for n in range(count):
            cols = slice(n * CHUNK, (n + 1) * CHUNK)
            tall_s[cols, :] = dot_tn(x[:, cols], d_up).astype(BF)
        spread(up_keep, (up_send0, up_send1))
        for n in range(count):
            cols = slice(n * CHUNK, (n + 1) * CHUNK)
            d_x = dot_nt(d_gate, w_gate[cols]) + dot_nt(d_up, w_up[cols])
            xs[e, :, cols] = d_x.astype(BF)

    def combine(source, mix_out, dx_out, mix_in, dx_in):
        def put(out, prior, cols, values):
            if prior is not None:
                values += prior[0, :, cols].astype(F32)
            out[0, :, cols] = values.astype(BF)

        here = pl.ds(pl.multiple_of(source * SLOTS, SLOTS), SLOTS)
        pick = pick_of(source).astype(BF)
        for n in range(count):
            cols = slice(n * CHUNK, (n + 1) * CHUNK)
            put(dx_out, dx_in, cols, dot_tn(pick, xs[:, here, cols].reshape(rows, CHUNK)))
            put(mix_out, mix_in, cols, dot_tn(pick, gs[:, here, cols].reshape(rows, CHUNK)))
        values = gate_s[:, here, :].reshape(rows, 1)
        column = lax.broadcasted_iota(jnp.int32, (rows, LANES), 1)
        owner = lax.broadcasted_iota(jnp.int32, (rows, LANES), 0) // SLOTS
        spread_out = jnp.where(column == owner + (place_ref[4] + low), values, 0.0).astype(BF)
        put(dx_out, dx_in, slice(WIDTH, WIDTH + LANES), dot_tn(pick, spread_out))

    @pl.when((step >= experts) & (step < experts + sources // 2))
    def _():
        source = step - experts + sources // 2
        prior = (None, None) if first else (mix_prior[1], dx_prior[1])
        combine(source, mix_send, dx_send, *prior)

    @pl.when(step >= experts + sources // 2)
    def _():
        source = step - experts - sources // 2
        prior = (None, None) if first else (mix_prior[0], dx_prior[0])
        combine(source, mix_keep, dx_keep, *prior)


def less(shape):
    return jax.ShapeDtypeStruct(shape.shape[1:], shape.dtype)


def run_experts(place, x_slots, g_slots, gates, maps, w_gate, w_up, w_down, prior=()):
    sources, _, tokens = maps.shape
    width = x_slots.shape[2]
    experts = w_gate.shape[0] // 2
    low = experts if prior else 0
    ffe = w_gate.shape[2]
    part = ffe // 8
    quarter = width // 8
    half = ffe // 2
    slots = sources * SLOTS
    extra = width + LANES
    second = experts
    third = second + sources // 2

    def at(i, low, size):
        return jnp.clip(i - low, 0, size - 1)

    def expert_of(i):
        return at(i, 0, experts)

    def w_cols(block):
        return pl.BlockSpec(
            (1, width, LANES), lambda i, p: (expert_of(i) + low, 0, p[0] + 2 * block)
        )

    def w_rows(block):
        return pl.BlockSpec(
            (1, LANES, width), lambda i, p: (expert_of(i) + low, p[0] + 2 * block, 0)
        )

    slot_spec = pl.BlockSpec((1, slots, width), lambda i, p: (expert_of(i) + low, 0, 0))

    def out_tokens(low, cols):
        return pl.BlockSpec((1, tokens, cols), lambda i, p: (at(i, low, sources // 2), 0, 0))

    tall_spec = pl.BlockSpec(
        (2, 2, 1, quarter, half), lambda i, p: (0, 0, expert_of(i), 0, 0)
    )
    wide_spec = pl.BlockSpec((2, 1, part, width), lambda i, p: (0, expert_of(i), 0, 0))
    tall_half = pl.BlockSpec((2, 1, quarter, half), lambda i, p: (0, expert_of(i), 0, 0))
    wide_half = pl.BlockSpec((1, part, width), lambda i, p: (expert_of(i), 0, 0))
    tall = jax.ShapeDtypeStruct((2, 2, experts, quarter, half), BF)
    wide = jax.ShapeDtypeStruct((2, experts, part, width), BF)
    mixed = jax.ShapeDtypeStruct((sources // 2, tokens, width), BF)
    d_x = jax.ShapeDtypeStruct((sources // 2, tokens, extra), BF)
    sums = (
        out_tokens(third, width),
        out_tokens(second, width),
        out_tokens(third, extra),
        out_tokens(second, extra),
    )
    return pl.pallas_call(
        functools.partial(expert_kernel, first=not prior),
        grid_spec=pltpu.PrefetchScalarGridSpec(
            num_scalar_prefetch=1,
            grid=(third + sources // 2,),
            in_specs=[
                slot_spec,
                slot_spec,
                pl.BlockSpec((1, slots, 1), lambda i, p: (expert_of(i) + low, 0, 0)),
                pl.BlockSpec(maps.shape, lambda i, p: (0, 0, 0)),
                w_cols(0),
                w_cols(1),
                w_cols(0),
                w_cols(1),
                w_rows(0),
                w_rows(1),
                *(sums if prior else ()),
            ],
            out_specs=(
                *sums,
                tall_spec,
                tall_half,
                tall_half,
                tall_spec,
                tall_half,
                tall_half,
                wide_spec,
                wide_half,
                wide_half,
            ),
            scratch_shapes=[
                pltpu.VMEM((experts, slots, width), BF),
                pltpu.VMEM((experts, slots, width), BF),
                pltpu.VMEM((experts, slots, 1), F32),
                pltpu.VMEM((half, width), BF),
                pltpu.VMEM((width, half), BF),
            ],
        ),
        out_shape=(mixed, mixed, d_x, d_x)
        + (tall, less(tall), less(tall)) * 2
        + (wide, less(wide), less(wide)),
        compiler_params=params(60, ("arbitrary",)),
        cost_estimate=cost(30e9, 60e6),
    )(place, x_slots, g_slots, gates, maps, w_gate, w_gate, w_up, w_up, w_down, w_down, *prior)


def post_kernel(
    dx_ref,
    mid_ref,
    cot_ref,
    norm_ref,
    wr_ref,
    map_ref,
    gain_ref,
    wo_ref,
    datt_ref,
    dmid_ref,
    dlow_ref,
    dlog_ref,
    ggain_ref,
):
    middle = mid_ref[...]
    inv = lax.rsqrt(jnp.mean(middle * middle, axis=-1, keepdims=True) + EPS)
    chosen = map_ref[...] >= 0.0
    logits = jnp.where(chosen, dot_nn(norm_ref[...], wr_ref[...]), MASKED)
    raised = jnp.exp(logits - jnp.max(logits, axis=-1, keepdims=True))
    raised = jnp.where(chosen, raised, 0.0)
    gates = raised / jnp.sum(raised, axis=-1, keepdims=True)
    d_gates = dx_ref[:, WIDTH:]
    d_picked = gates * (d_gates - jnp.sum(gates * d_gates, axis=-1, keepdims=True))
    d_logits = d_picked.astype(BF)
    dlog_ref[...] = d_logits
    d_norm = dx_ref[:, :WIDTH] + dot_nt(d_logits, wr_ref[...])
    scaled = d_norm * gain_ref[...]
    ggain_ref[...] = jnp.sum(d_norm * middle * inv, axis=0, keepdims=True)
    d_mid = (
        cot_ref[...]
        + inv * scaled
        - middle * inv**3 * jnp.mean(middle * scaled, axis=-1, keepdims=True)
    )
    dmid_ref[...] = d_mid
    d_low = d_mid.astype(BF)
    dlow_ref[...] = d_low
    d_att = dot_nt(d_low, wo_ref[...]).astype(BF)
    for g in range(KV_HEADS):
        pack_heads(datt_ref.at[g], d_att[:, g * ROWS_Q : (g + 1) * ROWS_Q], d_att.shape[0])


def run_post(dx_sum, middle, cotangent, normed_two, wr_pad, map_rows, gain, w_output):
    tokens = middle.shape[0]
    return pl.pallas_call(
        post_kernel,
        out_shape=(
            jax.ShapeDtypeStruct((KV_HEADS, tokens * ROWS_Q // LANES, LANES), BF),
            jax.ShapeDtypeStruct((tokens, WIDTH), F32),
            jax.ShapeDtypeStruct((tokens, WIDTH), BF),
            jax.ShapeDtypeStruct((tokens, LANES), BF),
            jax.ShapeDtypeStruct((1, WIDTH), F32),
        ),
        compiler_params=params(60),
        cost_estimate=cost(2 * tokens * WIDTH * WIDTH, 14e6),
    )(dx_sum, middle, cotangent, normed_two, wr_pad, map_rows, gain[None], w_output)


def put_rows(place_ref, held, keep, send):
    part = keep.shape[1]
    for b in range(keep.shape[0]):
        own = (2 * b) ^ place_ref[5]
        keep[b] = held[pl.ds(pl.multiple_of(own * part, part), part), :]
        other = own ^ 1
        send[b] = held[pl.ds(pl.multiple_of(other * part, part), part), :]


def qkvgrad_kernel(place_ref, a_ref, d_ref, full_ref, keep, send, held):
    step = pl.program_id(0)

    @pl.when(step == 0)
    def _():
        key_at = KV_HEADS * ROWS_Q
        value_at = key_at + KV_HEADS * HEAD_DIM
        for g in range(KV_HEADS):
            unpack_all(
                d_ref.at[g],
                full_ref,
                full_ref,
                full_ref,
                0,
                full_ref.shape[0],
                g * ROWS_Q,
                key_at + g * HEAD_DIM,
                value_at + g * HEAD_DIM,
            )

    cols = pl.ds(pl.multiple_of(step * 256, 256), 256)
    held[...] = dot_tn(a_ref[...], full_ref[:, cols]).astype(BF)
    put_rows(place_ref, held, keep, send)


def run_qkvgrad(place, normed, d_pack, blocks):
    tokens, rows = normed.shape
    cols = KV_HEADS * PACK
    part = rows // blocks
    spec = pl.BlockSpec((blocks // 2, part, 256), lambda i, p: (0, 0, i))
    shape = jax.ShapeDtypeStruct((blocks // 2, part, cols), BF)
    return pl.pallas_call(
        qkvgrad_kernel,
        grid_spec=pltpu.PrefetchScalarGridSpec(
            num_scalar_prefetch=1,
            grid=(cols // 256,),
            in_specs=[
                pl.BlockSpec((tokens, rows), lambda i, p: (0, 0)),
                pl.BlockSpec(d_pack.shape, lambda i, p: (0, 0, 0)),
            ],
            out_specs=(pl.BlockSpec((tokens, cols), lambda i, p: (0, 0)), spec, spec),
            scratch_shapes=[pltpu.VMEM((rows, 256), BF)],
        ),
        out_shape=(jax.ShapeDtypeStruct((tokens, cols), BF), shape, shape),
        compiler_params=params(60, ("arbitrary",)),
        cost_estimate=cost(2 * tokens * rows * cols, 12e6),
    )(place, normed, d_pack)


def last_work(inputs, outputs, scratch):
    gain_ref, gmlp_ref, sources = inputs[0], inputs[1], inputs[2:]
    (out_ref,) = outputs
    keep, send, held = scratch[:3]
    buffers, load_sem = scratch[3:-1], scratch[-1]
    loads = [
        pltpu.make_async_copy(source, buffer, load_sem.at[n])
        for n, (source, buffer) in enumerate(zip(sources, buffers))
    ]
    for load in loads:
        load.start()
    d_ref, wq_ref, wk_ref, wv_ref, dmid_ref, hid_ref, norm_ref, dlog_ref = buffers
    key_at = KV_HEADS * ROWS_Q
    value_at = key_at + KV_HEADS * HEAD_DIM
    device = lax.axis_index("dp") * lax.axis_size("expert") + lax.axis_index("expert")

    def compute():
        for load in loads:
            load.wait()
        tokens = hid_ref.shape[0]
        size = tokens // 4
        ggain = jnp.zeros(gain_ref.shape, F32)
        for r in range(4):
            rows = slice(r * size, (r + 1) * size)
            d_norm = dot_nt(d_ref[rows, 0:key_at], wq_ref[...])
            d_norm += dot_nt(d_ref[rows, key_at:value_at], wk_ref[...])
            d_norm += dot_nt(d_ref[rows, value_at:], wv_ref[...])
            values = hid_ref[rows, :]
            inv = lax.rsqrt(jnp.mean(values * values, axis=-1, keepdims=True) + EPS)
            scaled = d_norm * gain_ref[...]
            ggain += jnp.sum(d_norm * values * inv, axis=0, keepdims=True)
            out_ref[rows, :] = (
                dmid_ref[rows, :]
                + inv * scaled
                - values * inv**3 * jnp.mean(values * scaled, axis=-1, keepdims=True)
            )
        columns = dot_tn(norm_ref[...], dlog_ref[...])
        lane = lax.broadcasted_iota(jnp.int32, columns.shape, 1)
        for n, row in enumerate((gmlp_ref[...], ggain)):
            turned = jnp.broadcast_to(row, (8, row.shape[1])).T[:, 0:1]
            columns = jnp.where(lane == LANES - 2 + n, turned, columns)
        held[...] = columns
        part = keep.shape[1]
        for b in range(keep.shape[0]):
            own = (2 * b) ^ device
            keep[b] = held[pl.ds(pl.multiple_of(own * part, part), part), :]
            own = own ^ 1
            send[b] = held[pl.ds(pl.multiple_of(own * part, part), part), :]

    return compute


def plan_last(arrays, gain, ggain_mlp, blocks):
    vmem = pl.BlockSpec(memory_space=pltpu.VMEM)
    tokens = arrays[0].shape[0]
    small = pltpu.VMEM((blocks // 2, WIDTH // blocks, LANES), F32)
    scratch = [small, small, pltpu.VMEM((WIDTH, LANES), F32)]
    scratch += [pltpu.VMEM(array.shape, array.dtype) for array in arrays]
    scratch.append(pltpu.SemaphoreType.DMA((len(arrays),)))
    return (
        (gain[None], ggain_mlp) + arrays,
        [vmem] * 2 + [hbm] * len(arrays),
        [jax.ShapeDtypeStruct((tokens, WIDTH), F32)],
        scratch,
        last_work,
    )


def stack_swap(values, bit):
    return jnp.concatenate([values, swap_bit(values, bit)], axis=0)


MESH = pl.DeviceIdType.MESH


def peer_of(bit):
    axis, mask = bit
    return {axis: lax.axis_index(axis) ^ mask}


def greet(ids):
    barrier = pltpu.get_barrier_semaphore()
    for device in ids:
        pl.semaphore_signal(barrier, inc=1, device_id=device, device_id_type=MESH)
    pl.semaphore_wait(barrier, len(ids))


GATHER_BITS = (X_BIT, ZL_BIT, C_BIT)


def one_hot(slots, rows):
    experts, tokens = slots.shape
    wide = jnp.broadcast_to(slots[:, None, :], (experts, SLOTS, tokens))
    rank = lax.broadcasted_iota(jnp.int32, (experts, SLOTS, tokens), 1).astype(F32)
    return (wide == rank).astype(F32).reshape(rows, tokens)


def gather_kernel(x_ref, *refs):
    blocks, maps_ref, wr_ref = refs[0:4], refs[4], refs[5]
    x_slots, g_slots, gates_ref, local_ref = refs[6:10]
    all_ref, other, all_maps_ref, stage = refs[10:14]
    send_sem, recv_sem, more_send, more_recv, store_sem = refs[14:]
    greet([peer_of(bit) for bit in GATHER_BITS])
    half = x_ref.shape[0] // 2
    copies = []

    def send(source, slot, rows, bit):
        n = len(copies)
        copy = pltpu.make_async_remote_copy(
            src_ref=source if rows is None else source.at[rows],
            dst_ref=all_ref.at[slot] if rows is None else all_ref.at[slot, rows],
            send_sem=send_sem.at[n],
            recv_sem=recv_sem.at[n],
            device_id=peer_of(bit),
            device_id_type=MESH,
        )
        copy.start()
        copies.append(copy)
        return copy

    top, low = pl.ds(0, half), pl.ds(half, half)
    x_top = send(x_ref, 1, top, X_BIT)
    z_low = send(x_ref, 2, low, ZL_BIT)
    x_low = send(x_ref, 1, low, X_BIT)
    z_top = send(x_ref, 2, top, ZL_BIT)
    pairs = [(maps_ref, all_maps_ref.at[pl.ds(4, 4)])]
    pairs += [(block, other.at[n]) for n, block in enumerate(blocks)]
    crossed = []
    for n, (block, there) in enumerate(pairs):
        copy = pltpu.make_async_remote_copy(
            src_ref=block,
            dst_ref=there,
            send_sem=more_send.at[n],
            recv_sem=more_recv.at[n],
            device_id=peer_of(C_BIT),
            device_id_type=MESH,
        )
        copy.start()
        crossed.append(copy)
    cross_own = send(x_ref, 4, None, C_BIT)
    all_maps_ref[0:4] = maps_ref[...]
    column = lax.axis_index("expert")
    experts = x_slots.shape[0]
    rows = experts * SLOTS
    depth = stage.shape[0]
    stores = []

    def own_rows(table):
        picked = jnp.zeros((experts, table.shape[1]), F32)
        for n in range(table.shape[0] // experts):
            picked = jnp.where(column == n, table[n * experts : (n + 1) * experts], picked)
        return picked

    def put(source, values, target, pick):
        side = len(stores) % depth
        if len(stores) >= depth:
            stores[-depth].wait()
        for n in range(WIDTH // CHUNK):
            cols = slice(n * CHUNK, (n + 1) * CHUNK)
            got = dot_nn(pick, values[:, cols]).astype(BF)
            stage[side, :, :, cols] = got.reshape(experts, SLOTS, CHUNK)
        store = pltpu.make_async_copy(
            stage.at[side], target.at[:, pl.ds(source * SLOTS, SLOTS)], store_sem.at[side]
        )
        store.start()
        stores.append(store)

    def put_g(source, values):
        pick = one_hot(own_rows(all_maps_ref[source]), rows)
        put(source, values, g_slots, pick.astype(BF))

    def put_x(source, values):
        slot_map = all_maps_ref[source]
        chosen = slot_map >= 0.0
        logits = dot_nt(wr_ref[...], values[...])[0 : slot_map.shape[0]]
        logits = jnp.where(chosen, logits, MASKED)
        raised = jnp.exp(logits - jnp.max(logits, axis=0, keepdims=True))
        raised = jnp.where(chosen, raised, 0.0)
        gates = own_rows(raised / jnp.sum(raised, axis=0, keepdims=True))
        slots = own_rows(slot_map)
        local_ref[source] = slots
        pick = one_hot(slots, rows)
        wide = jnp.broadcast_to(gates[:, None, :], (experts, SLOTS, gates.shape[1]))
        of_rows = jnp.sum(pick * wide.reshape(rows, gates.shape[1]), axis=1, keepdims=True)
        gates_ref[:, source * SLOTS : (source + 1) * SLOTS, :] = of_rows.reshape(experts, SLOTS, 1)
        put(source, values, x_slots, pick.astype(BF))

    put_x(0, x_ref)
    put_g(0, blocks[0])
    put_g(1, blocks[1])
    x_top.wait_recv()
    far_top = send(all_ref.at[1], 3, top, ZL_BIT)
    z_low.wait_recv()
    far_low = send(all_ref.at[2], 3, low, X_BIT)
    put_g(2, blocks[2])
    put_g(3, blocks[3])
    for copy in crossed:
        copy.wait_recv()
    cross_own.wait_recv()
    put_x(4, all_ref.at[4])
    put_g(4, other.at[0])
    x_low.wait_recv()
    cross_x = send(all_ref.at[1], 5, None, C_BIT)
    z_top.wait_recv()
    cross_z = send(all_ref.at[2], 6, None, C_BIT)
    put_x(1, all_ref.at[1])
    put_x(2, all_ref.at[2])
    put_g(5, other.at[1])
    cross_x.wait_recv()
    cross_z.wait_recv()
    put_x(5, all_ref.at[5])
    far_top.wait_recv()
    far_low.wait_recv()
    cross_far = send(all_ref.at[3], 7, None, C_BIT)
    put_x(6, all_ref.at[6])
    put_g(6, other.at[2])
    put_g(7, other.at[3])
    put_x(3, all_ref.at[3])
    cross_far.wait_recv()
    put_x(7, all_ref.at[7])
    for store in stores[-depth:]:
        store.wait()
    for copy in copies + crossed:
        copy.wait_send()


def run_gather(values, blocks, maps, wr_t, experts):
    vmem = pl.BlockSpec(memory_space=pltpu.VMEM)
    tokens, width = values.shape
    slots = jax.ShapeDtypeStruct((experts, 8 * SLOTS, width), values.dtype)
    return pl.pallas_call(
        gather_kernel,
        in_specs=[vmem] * 7,
        out_specs=(hbm, hbm, vmem, vmem),
        out_shape=(
            slots,
            slots,
            jax.ShapeDtypeStruct((experts, 8 * SLOTS, 1), F32),
            jax.ShapeDtypeStruct((8, experts, tokens), F32),
        ),
        scratch_shapes=[
            pltpu.VMEM((8, tokens, width), values.dtype),
            pltpu.VMEM((4, tokens, width), values.dtype),
            pltpu.VMEM((8,) + maps.shape[1:], maps.dtype),
            pltpu.VMEM((4, experts, SLOTS, width), values.dtype),
        ]
        + [pltpu.SemaphoreType.DMA((n,)) for n in (10, 10, 5, 5, 4)],
        compiler_params=pltpu.CompilerParams(
            collective_id=1, has_side_effects=True, vmem_limit_bytes=60 * MIB
        ),
        cost_estimate=cost(0, 150e6),
    )(values, *blocks, maps, wr_t)


def trade_peers(size):
    me = lax.axis_index("dp")
    return [{"dp": me ^ k} for k in range(size - 1, 0, -1)]


def trade_start(a_ref, out_ref, send_sem, recv_sem, local_sem):
    me = lax.axis_index("dp")
    copies = []
    for n, device in enumerate(trade_peers(a_ref.shape[0])):
        copy = pltpu.make_async_remote_copy(
            src_ref=a_ref.at[device["dp"]],
            dst_ref=out_ref.at[me],
            send_sem=send_sem.at[n],
            recv_sem=recv_sem.at[n],
            device_id=device,
            device_id_type=MESH,
        )
        copy.start()
        copies.append(copy)
    own = pltpu.make_async_copy(a_ref.at[me], out_ref.at[me], local_sem)
    own.start()
    return copies, own


def trade_end(copies, own):
    own.wait()
    for copy in copies:
        copy.wait_recv()
    for copy in copies:
        copy.wait_send()


class Rider:
    def __init__(self, bit, *terms, pieces=1, turns=(0,)):
        self.bit, self.pieces, self.turns = bit, pieces, turns
        self.arrays = [term[0] if isinstance(term, tuple) else term for term in terms]
        self.parts = [term[1] if isinstance(term, tuple) else None for term in terms]
        array, part = self.arrays[0], self.parts[0]
        shape = array.shape
        if part is not None:
            kept = [len(range(n)[k]) for k, n in zip(part, shape) if not isinstance(k, int)]
            shape = tuple(kept) + shape[len(part) :]
        self.shape = jax.ShapeDtypeStruct(shape, array.dtype)
        self.direct = len(terms) == 1 and part is None

    def scratch(self):
        if self.direct:
            return []
        buffer = pltpu.VMEM(self.shape.shape, self.shape.dtype)
        return [buffer] * (len(self.arrays) + 1)

    def plan(self):
        return (self.bit, self.pieces, self.turns, tuple(self.parts), self.direct)


def rider_inputs(riders):
    return [array for rider in riders for array in rider.arrays]


def rider_shapes(riders):
    return tuple(rider.shape for rider in riders)


def rider_scratch(riders):
    remote = max(sum(rider.pieces for rider in riders), 1)
    local = max(sum(len(rider.arrays) for rider in riders), 1)
    buffers = [buffer for rider in riders for buffer in rider.scratch()]
    return buffers + [pltpu.SemaphoreType.DMA((n,)) for n in (remote, remote, local)]


def add_rows(result, buffers):
    step = 16

    @pl.loop(0, result.shape[1] // step)
    def _(r):
        rows = pl.ds(pl.multiple_of(r * step, step), step)
        for i in range(result.shape[0]):
            total = buffers[0][i, rows, :].astype(F32)
            for buffer in buffers[1:]:
                total += buffer[i, rows, :].astype(F32)
            result[i, rows, :] = total.astype(result.dtype)


def ride_pieces(sources, targets, plans, scratch):
    send_sem, recv_sem, local_sem = scratch[-3:]
    starts, finishes, loads, used, source, local = [], [], [], 0, 0, 0
    for n, (bit, pieces, turns, parts, direct) in enumerate(plans):
        arrays = sources[source : source + len(parts)]
        source += len(parts)
        if direct:
            held = arrays[0]
            prepare = None
        else:
            buffers = scratch[used : used + len(parts)]
            held = scratch[used + len(parts)]
            used += len(parts) + 1
            copies = []
            for array, part, buffer in zip(arrays, parts, buffers):
                view = array if part is None else array.at[part]
                copy = pltpu.make_async_copy(view, buffer, local_sem.at[local])
                local += 1
                loads.append(copy)
                copies.append(copy)

            def prepare(copies=copies, held=held, buffers=buffers):
                for copy in copies:
                    copy.wait()
                add_rows(held, buffers)

        size = targets[n].shape[0] // pieces
        for m in range(pieces):
            at = pl.ds(m * size, size)

            def remote(n=n, at=at, slot=len(starts), bit=bit, held=held):
                return pltpu.make_async_remote_copy(
                    src_ref=held.at[at],
                    dst_ref=targets[n].at[at],
                    send_sem=send_sem.at[slot],
                    recv_sem=recv_sem.at[slot],
                    device_id=peer_of(bit),
                    device_id_type=MESH,
                )

            def start(remote=remote):
                remote().start()

            def finish(remote=remote):
                remote().wait()

            starts.append((prepare if m == 0 else None, start, turns))
            finishes.append(finish)
    return starts, finishes, loads


def all_peers(bits):
    size = lax.axis_size("dp")
    return trade_peers(size) + [peer_of(bit) for bit in bits if bit[0] == "expert"]


def trade_kernel(*refs, plans, work):
    inputs = sum(len(plan[3]) for plan in plans)
    more = 2 if work else 0
    a_ref, sources = refs[0], refs[1 : 1 + inputs]
    work_in, refs = refs[1 + inputs : 1 + inputs + more], refs[1 + inputs + more :]
    out_ref, targets = refs[0], refs[1 : 1 + len(plans)]
    work_out, refs = refs[1 + len(plans) : 1 + len(plans) + more], refs[1 + len(plans) + more :]
    send_sem, recv_sem, local_sem, *scratch = refs
    work_scratch = scratch[-6:] if work else ()
    scratch = scratch[:-6] if work else scratch
    bits = {plan[0] for plan in plans} | ({C_BIT} if work else set())
    greet(all_peers(sorted(bits)))
    trade = trade_start(a_ref, out_ref, send_sem, recv_sem, local_sem.at[0])
    starts, finishes, loads = ride_pieces(sources, targets, plans, scratch)
    for load in loads:
        load.start()
    if work:
        finishes.append(weight_grad(work_in, work_out, work_scratch))
    for prepare, start, _ in starts:
        if prepare is not None:
            prepare()
        start()
    if work:
        finishes[-1] = finishes[-1]()
    trade_end(*trade)
    for finish in finishes:
        finish()


def weight_grad(inputs, outputs, scratch):
    keep, got = outputs
    left, right, sent, held, load_sem, cross_sem = scratch
    loads = [
        pltpu.make_async_copy(source, target, load_sem.at[n])
        for n, (source, target) in enumerate(zip(inputs, (left, right)))
    ]
    for load in loads:
        load.start()
    blocks, part, width = keep.shape
    step = held.shape[1]
    device = lax.axis_index("dp") * lax.axis_size("expert") + lax.axis_index("expert")

    def compute():
        for load in loads:
            load.wait()

        @pl.loop(0, width // step)
        def _(n):
            cols = pl.ds(pl.multiple_of(n * step, step), step)
            held[...] = dot_tn(left[...], right[:, cols]).astype(BF)
            for b in range(blocks):
                own = (2 * b) ^ device
                keep[b, :, cols] = held[pl.ds(pl.multiple_of(own * part, part), part), :]
                own = own ^ 1
                sent[b, :, cols] = held[pl.ds(pl.multiple_of(own * part, part), part), :]

        copy = pltpu.make_async_remote_copy(
            src_ref=sent,
            dst_ref=got,
            send_sem=cross_sem.at[0],
            recv_sem=cross_sem.at[1],
            device_id=peer_of(C_BIT),
            device_id_type=MESH,
        )
        copy.start()
        return copy.wait

    return compute


def run_trade(values, number, riders=(), work=(), blocks=0):
    size = values.shape[0]
    inputs = rider_inputs(riders)
    vmem = pl.BlockSpec(memory_space=pltpu.VMEM)
    shapes, specs, scratch = [], [], []
    if work:
        left, right = work
        rows, width = left.shape[1], right.shape[1]
        half = jax.ShapeDtypeStruct((blocks // 2, rows // blocks, width), BF)
        shapes, specs = [half, half], [vmem, hbm]
        scratch = [
            pltpu.VMEM(left.shape, left.dtype),
            pltpu.VMEM(right.shape, right.dtype),
            pltpu.VMEM(half.shape, BF),
            pltpu.VMEM((rows, 256), BF),
            pltpu.SemaphoreType.DMA((2,)),
            pltpu.SemaphoreType.DMA((2,)),
        ]
    out = pl.pallas_call(
        functools.partial(
            trade_kernel, plans=tuple(rider.plan() for rider in riders), work=bool(work)
        ),
        in_specs=[hbm] * (1 + len(inputs) + len(work)),
        out_specs=(hbm,) * (1 + len(riders)) + tuple(specs),
        out_shape=(jax.ShapeDtypeStruct(values.shape, values.dtype),)
        + rider_shapes(riders)
        + tuple(shapes),
        scratch_shapes=[pltpu.SemaphoreType.DMA((n,)) for n in (size - 1, size - 1, 1)]
        + rider_scratch(riders)
        + scratch,
        compiler_params=pltpu.CompilerParams(
            collective_id=number, has_side_effects=True, vmem_limit_bytes=60 * MIB
        ),
        cost_estimate=cost(0, 170e6),
    )(values, *inputs, *work)
    return out if riders or work else out[0]


def first_kernel(a_ref, rank_ref, turned_ref, out_ref, slot_ref, send_sem, recv_sem, local_sem, *, far):
    greet(trade_peers(a_ref.shape[0]))
    trade = trade_start(a_ref, out_ref, send_sem, recv_sem, local_sem.at[0])
    for e in range(rank_ref.shape[0]):
        own = rank_ref[e : e + 1, :]
        smaller = (turned_ref[:, e : e + 1] < own).astype(F32)
        before = jnp.sum(smaller, axis=0, keepdims=True)
        slot_ref[e : e + 1, :] = jnp.where(own < far, jnp.minimum(before, SLOTS), -1.0)
    trade_end(*trade)


def run_first(values, rank_map, turned, far):
    size = values.shape[0]
    vmem = pl.BlockSpec(memory_space=pltpu.VMEM)
    return pl.pallas_call(
        functools.partial(first_kernel, far=far),
        in_specs=[hbm, vmem, vmem],
        out_specs=(hbm, vmem),
        out_shape=(
            jax.ShapeDtypeStruct(values.shape, values.dtype),
            jax.ShapeDtypeStruct(rank_map.shape, F32),
        ),
        scratch_shapes=[pltpu.SemaphoreType.DMA((n,)) for n in (size - 1, size - 1, 1)],
        compiler_params=pltpu.CompilerParams(
            collective_id=2, has_side_effects=True, vmem_limit_bytes=60 * MIB
        ),
        cost_estimate=cost(0, 170e6),
    )(values, rank_map, turned)


def reduce_chain(slot, part, keep_ref, send_ref, outs, acc, got, staged, send_sem, recv_sem):
    first, bits, row, rows, column, columns, order = part
    blocks = keep_ref.shape[0]
    stages = len(bits) + 1
    low = send_ref.dtype
    at = (pl.ds(row, rows), pl.ds(column, columns))
    copies = []

    def exchange(source, target, bit):
        n = slot + len(copies)
        copy = pltpu.make_async_remote_copy(
            src_ref=source,
            dst_ref=target,
            send_sem=send_sem.at[n],
            recv_sem=recv_sem.at[n],
            device_id=peer_of(bit),
            device_id_type=MESH,
        )
        copy.start()
        copies.append(copy)

    live = list(range(blocks))
    base_got, base_sent = 0, 0
    exchange(send_ref.at[(slice(None),) + at], got.at[(pl.ds(0, blocks),) + at], first)
    yield
    for stage in range(stages):
        copies[-1].wait_recv()

        def total(position):
            index = live[position]
            kept = keep_ref[(index,) + at].astype(F32) if stage == 0 else acc[(index,) + at]
            return kept + got[(base_got + position,) + at].astype(F32)

        if stage == stages - 1:
            low_column = 0
            for out_ref in outs:
                if low_column <= column < low_column + out_ref.shape[1]:
                    out_ref[at[0], pl.ds(column - low_column, columns)] = total(0)
                low_column += out_ref.shape[1]
            break
        mask = 1 << order[stage]
        rest = [i for i in live if not i & mask]
        for m, i in enumerate(rest):
            staged[(base_sent + m,) + at] = total(live.index(i ^ mask)).astype(low)
        exchange(
            staged.at[(pl.ds(base_sent, len(rest)),) + at],
            got.at[(pl.ds(base_got + len(live), len(rest)),) + at],
            bits[order[stage]],
        )
        for i in rest:
            acc[(i,) + at] = total(live.index(i))
        base_got += len(live)
        base_sent += len(rest)
        live = rest
        yield
    for copy in copies:
        copy.wait_send()


def reduce_kernel(*refs, jobs, plans, work):
    size = len(jobs)
    given = size - 1 if work else size
    inputs = sum(len(plan[3]) for plan in plans)
    keeps, sends, refs = list(refs[:given]), list(refs[given : 2 * given]), refs[2 * given :]
    sources, refs = refs[:inputs], refs[inputs:]
    compute = None
    if work:
        counts, body = work
        work_in, refs = refs[: counts[0]], refs[counts[0] :]
        work_out, refs = refs[: counts[1]], refs[counts[1] :]
        work_scratch, refs = refs[-counts[2] :], refs[: -counts[2]]
        compute = body(work_in, work_out, work_scratch)
        keeps.append(work_scratch[0])
        sends.append(work_scratch[1])
    outs = []
    for _, _, _, widths in jobs:
        outs.append(refs[: len(widths)])
        refs = refs[len(widths) :]
    targets, scratch = refs[: len(plans)], refs[len(plans) :]
    send_sem, recv_sem = scratch[3 * size : 3 * size + 2]
    used = {bit for first, bits, *_ in jobs for bit in (first,) + bits}
    used |= {plan[0] for plan in plans}
    starts, finishes, loads = ride_pieces(sources, targets, plans, scratch[3 * size + 2 :])
    for load in loads:
        load.start()
    greet([peer_of(bit) for bit in sorted(used)])
    chains, late, slot = [], [], 0
    for n, (first, bits, parts, _) in enumerate(jobs):
        for part in parts:
            (late if n >= given else chains).append(
                reduce_chain(
                    slot,
                    (first, bits) + part,
                    keeps[n],
                    sends[n],
                    outs[n],
                    *scratch[3 * n : 3 * n + 3],
                    send_sem,
                    recv_sem,
                )
            )
            slot += len(bits) + 1
    index = lax.axis_index("dp")
    outer = (index // BIT_ZH) % 2 == (index // BIT_ZL) % 2
    turn, last = 0, max([0] + [n for _, _, turns in starts for n in turns])
    while chains or turn <= last:
        rest = []
        for chain in chains:
            try:
                next(chain)
                rest.append(chain)
            except StopIteration:
                pass
        chains = rest
        for prepare, start, turns in starts:
            if prepare is not None and min(turns) == turn:
                prepare()
            if len(set(turns)) == 1:
                if turns[0] == turn:
                    start()
            else:
                for n, side in enumerate((outer, jnp.logical_not(outer))):
                    if turns[n] == turn:
                        pl.when(side)(start)
        if turn == 0 and work:
            compute()
            chains += late
        turn += 1
    for finish in finishes:
        finish()


def run_reduce(pairs, jobs, number, riders=(), work=None):
    slots = sum(len(parts) * (len(bits) + 1) for _, bits, parts, _ in jobs)
    vmem = pl.BlockSpec(memory_space=pltpu.VMEM)
    scratch, shapes = [], []
    arrays, work_specs, work_shapes, work_scratch, body = work or ((), (), (), (), None)
    late = [(shape, shape) for shape in work_scratch[:1]]
    for (keep, send), (_, _, _, widths) in zip(list(pairs) + late, jobs):
        blocks, rows, cols = keep.shape
        scratch += [
            pltpu.VMEM((blocks, rows, cols), F32),
            pltpu.VMEM((2 * blocks - 1, rows, cols), send.dtype),
            pltpu.VMEM((max(blocks - 1, 1), rows, cols), send.dtype),
        ]
        shapes += [jax.ShapeDtypeStruct((rows, width), F32) for width in widths]
    inputs = rider_inputs(riders)
    return pl.pallas_call(
        functools.partial(
            reduce_kernel,
            jobs=jobs,
            plans=tuple(rider.plan() for rider in riders),
            work=((len(arrays), len(work_shapes), len(work_scratch)), body) if work else None,
        ),
        in_specs=[vmem] * len(pairs) + [hbm] * (len(pairs) + len(inputs)) + list(work_specs),
        out_specs=(vmem,) * (len(work_shapes) + len(shapes)) + (hbm,) * len(riders),
        out_shape=tuple(work_shapes) + tuple(shapes) + rider_shapes(riders),
        scratch_shapes=scratch
        + [pltpu.SemaphoreType.DMA((n,)) for n in (slots, slots)]
        + rider_scratch(riders)
        + list(work_scratch),
        compiler_params=pltpu.CompilerParams(
            collective_id=number, has_side_effects=True, vmem_limit_bytes=60 * MIB
        ),
        cost_estimate=cost(0, 170e6),
    )(*(keep for keep, _ in pairs), *(send for _, send in pairs), *inputs, *arrays)


def sum_pair(kept, received):
    return kept.astype(F32) + received.astype(F32)


def add_low(*terms):
    return sum(term.astype(F32) for term in terms).astype(BF)


def join_kernel(place_ref, *refs):
    outs = refs[-3:]
    zl_at = place_ref[0]

    def total(*terms):
        return sum(term.astype(F32) for term in terms)

    def flat(ref):
        return ref[(0,) * (ref.ndim - 2)]

    def work(parts, part):
        for n in range(2):
            keep, got, more, other = parts[4 * n : 4 * n + 4]
            mine = total(*(flat(term) for term in (keep, got, more)))
            across = flat(other).astype(F32)
            for m in range(2):
                cols = slice(m * LANES, (m + 1) * LANES)
                at = pl.multiple_of((2 * m + zl_at) * LANES, LANES)
                outs[n][part, 0, :, pl.ds(at, LANES)] = mine[:, cols]
                at = pl.multiple_of((2 * m + 1 - zl_at) * LANES, LANES)
                outs[n][part, 0, :, pl.ds(at, LANES)] = across[:, cols]
        keep, got, more = parts[8:]
        outs[2][part, 0] = total(*(flat(term) for term in (keep, got, more)))

    work(refs[0:11], 0)
    work(refs[11:22], 1)


def run_join(place, halves):
    _, _, experts, rows, cols = halves[0][0].shape
    wide_rows, width = halves[0][8].shape[2:]
    arrays, specs = [], []
    for half in halves:
        for operand in half:
            array, lead = operand if isinstance(operand, tuple) else (operand, 0)
            extra = array.ndim - 3
            at = (lead,) + (0,) * (extra - 1) if extra else ()
            arrays.append(array)
            specs.append(
                pl.BlockSpec(
                    (1,) * (extra + 1) + array.shape[-2:],
                    lambda i, p, at=at: at + (i, 0, 0),
                )
            )
    shapes = [(rows, 2 * cols), (rows, 2 * cols), (wide_rows, width)]
    return pl.pallas_call(
        join_kernel,
        grid_spec=pltpu.PrefetchScalarGridSpec(
            num_scalar_prefetch=1,
            grid=(experts,),
            in_specs=specs,
            out_specs=tuple(
                pl.BlockSpec((2, 1) + shape, lambda i, p: (0, i, 0, 0)) for shape in shapes
            ),
        ),
        out_shape=tuple(jax.ShapeDtypeStruct((2, experts) + shape, F32) for shape in shapes),
        compiler_params=params(60, ("arbitrary",)),
        cost_estimate=cost(1e6, 26e6),
    )(place, *arrays)


def fast_body(
    hidden_in,
    gain_attn,
    w_query,
    w_key,
    w_value,
    w_output,
    gain_mlp,
    w_router,
    w_gate,
    w_up,
    w_down,
    expert_ids,
    slot_order,
    grad_out,
):
    inputs = hidden_in[0]
    cotangent = grad_out[0]
    chosen = expert_ids[0]
    tokens = inputs.shape[0]
    top = chosen.shape[1]
    local_experts = w_gate.shape[0]
    peers = lax.axis_size("expert")
    all_experts = local_experts * peers
    shards = lax.axis_size("dp")
    length = shards * tokens
    devices = shards * peers
    index = lax.axis_index("dp")
    column = lax.axis_index("expert")
    y_at = index % 2
    zl_at = (index // 2) % 2
    zh_at = index // 4
    place = jnp.stack(
        [zl_at, y_at, zl_at, zh_at, column * local_experts, index * peers + column]
    ).astype(jnp.int32)

    ranks = slot_order[0, 0].reshape(tokens, top)
    far = tokens * top
    names = jnp.arange(all_experts, dtype=jnp.int32)
    match = chosen.T[None] == names[:, None, None]
    rank_map = jnp.min(jnp.where(match, ranks.T[None], far), axis=1).astype(F32)
    turned = rank_map.T
    map_rows = jnp.pad(
        jnp.where(turned < far, 0.0, -1.0),
        ((0, 0), (0, LANES - all_experts)),
        constant_values=-1.0,
    )
    wr_pad = jnp.pad(w_router, ((0, 0), (0, LANES - all_experts)))
    wr_t = jnp.pad(w_router.T, ((0, LANES - all_experts), (0, 0)))

    half = HEAD_DIM // 2
    frequency = jnp.exp(-math.log(10000.0) * jnp.arange(half, dtype=F32) * 2.0 / HEAD_DIM)
    own_angles = (index * tokens + jnp.arange(tokens, dtype=jnp.int32)).astype(F32)[:, None] * frequency
    cos_own, sin_own = jnp.cos(own_angles), jnp.sin(own_angles)
    cos_tab = jnp.concatenate([cos_own] * 4, axis=1)
    sin_tab = jnp.concatenate([-sin_own, sin_own] * 2, axis=1)
    angles = frequency[:, None] * jnp.arange(length, dtype=jnp.int32).astype(F32)[None]
    cos_t, sin_t = jnp.cos(angles), jnp.sin(angles)

    normed, pack, g_own = run_pre(
        inputs, gain_attn, w_query, w_key, w_value, cos_tab, sin_tab, cotangent
    )
    pack, slot_map = run_first(pack, rank_map, turned, float(far))
    pack, slot_map, g_late = fence(pack, slot_map, g_own)
    g_x = swap_bit(g_own, X_BIT)
    g_z = swap_bit(g_late, ZL_BIT)
    maps = stack_swap(slot_map[None], X_BIT)
    out, out_t, lse = run_forward(pack)
    out, g_x, g_z, maps = fence(out, g_x, g_z, maps)
    g_zx = swap_bit(g_z, X_BIT)
    maps = stack_swap(maps, ZL_BIT)
    att = run_trade(out, 3)
    att, g_zx, maps = fence(att, g_zx, maps)
    middle, normed_two, att_full = run_mid(att, w_output, inputs, gain_mlp)
    x_slots, g_slots, gates, maps = run_gather(
        normed_two, (g_own, g_x, g_z, g_zx), maps, wr_t, local_experts
    )
    expert_args = (place, x_slots, g_slots, gates, maps, w_gate, w_up, w_down)
    first = run_experts(*expert_args)
    gate_ka, gate_s0, gate_s1, up_ka, up_s0, up_s1, down_ka, down_s0, down_s1 = first[4:]
    down_ya = swap_bit(down_s1, Y_BIT)
    gate_ya = swap_bit(gate_s1, Y_BIT)
    early = swap_bit(jnp.stack([gate_ka[1, 1], gate_s1[1]]), ZH_BIT)
    mix_keep, mix_send, dx_keep, dx_send, *second = run_experts(*expert_args, prior=first[:4])
    gate_kb, gate_t0, gate_t1, up_kb, up_t0, up_t1, down_kb, down_t0, down_t1 = second
    down_ga = swap_bit(down_s0, Y_BIT)
    dx_send, down_ya, gate_ya, early = fence(dx_send, down_ya, gate_ya, early)
    gate_s0 = jnp.stack([gate_s0[0], add_low(gate_s0[1], early[1])])
    quarter = tokens // 4
    extra = dx_keep.shape[2]
    token_parts = tuple(
        (n * quarter, quarter, 0, extra, (1, 0) if n < 2 else (0, 1)) for n in (2, 0, 3, 1)
    )
    dx_sum, up_ya, gate_ga, mix_got, down_ma = run_reduce(
        ((dx_keep, dx_send),),
        ((C_BIT, (X_BIT, ZL_BIT), token_parts, (extra,)),),
        6,
        riders=(
            Rider(Y_BIT, up_s1),
            Rider(Y_BIT, gate_s0),
            Rider(C_BIT, mix_send, turns=(1,)),
            Rider(ZH_BIT, (down_ka, (1,)), down_ya, turns=(1, 0)),
        ),
    )
    dx_sum, gate_ya, down_ga, gate_t1 = fence(dx_sum, gate_ya, down_ga, gate_t1)
    gate_ma = swap_bit(add_low(gate_ka[1, 0], gate_ya[0]), ZH_BIT)
    gate_yb = swap_bit(gate_t1, Y_BIT)
    d_att, d_middle, d_low, d_log, ggain_mlp = run_post(
        dx_sum, middle, cotangent, normed_two, wr_pad, map_rows, gain_mlp, w_output
    )
    d_att, gate_ma, gate_yb = fence(d_att, gate_ma, gate_yb)
    mix_keep = mix_keep.reshape(2, 2, tokens, WIDTH)
    mix_got = mix_got.reshape(2, 2, tokens, WIDTH)
    every = slice(None)
    d_out, up_yb, up_za, gate_oa, mix_x, out_keep, out_got = run_trade(
        d_att,
        4,
        work=(att_full, d_low),
        blocks=devices,
        riders=(
            Rider(Y_BIT, up_t1),
            Rider(ZH_BIT, (up_ka, (1, 1)), (up_ya, (1,))),
            Rider(ZL_BIT, (gate_ka, (0, 1)), (early, (0,)), (gate_ga, (1,))),
            Rider(X_BIT, (mix_keep, (every, 1)), (mix_got, (every, 1))),
        ),
    )
    split = (8, 2, WIDTH // devices, WIDTH)
    out_keep, out_got = out_keep.reshape(split), out_got.reshape(split)
    up_ga, down_yb, up_late, gate_late, _ = fence(up_s0, down_t1, up_ya, gate_yb, d_out)
    both = jnp.stack([add_low(up_ka[1, 0], up_late[0]), add_low(gate_kb[1, 1], gate_late[1])])
    both = swap_bit(both, ZH_BIT)
    up_ga = swap_bit(up_ga, Y_BIT)
    down_yb = swap_bit(down_yb, Y_BIT)
    d_pack = run_backward(pack, d_out, out_t, lse, cos_t, sin_t)
    d_pack, both, up_ga, down_yb = fence(d_pack, both, up_ga, down_yb)
    d_pack, gate_gb, up_gb, gate_mb, up_zb, mix_z, out_x, up_oa = run_trade(
        d_pack,
        5,
        riders=(
            Rider(Y_BIT, gate_t0),
            Rider(Y_BIT, up_t0),
            Rider(ZH_BIT, (gate_kb, (1, 0)), (gate_yb, (0,))),
            Rider(ZH_BIT, (up_kb, (1, 1)), (up_yb, (1,))),
            Rider(
                ZL_BIT,
                (mix_keep, (slice(1, 2), 0)),
                (mix_got, (slice(1, 2), 0)),
                (mix_x, (slice(1, 2),)),
            ),
            Rider(X_BIT, (out_keep, (every, 1)), (out_got, (every, 1))),
            Rider(ZL_BIT, (up_ka, (0, 1)), (up_ga, (1,)), (up_za, (every,))),
        ),
    )
    d_pack, up_yb, down_yb, gate_gb, down_t0, mix_z, out_x = fence(
        d_pack, up_yb, down_yb, gate_gb, down_t0, mix_z, out_x
    )
    other = jnp.stack(
        [add_low(gate_kb[0, 1], gate_gb[1], both[1]), add_low(up_kb[0, 1], up_gb[1], up_zb)]
    )
    other = swap_bit(other, ZL_BIT)
    down_mb = swap_bit(add_low(down_kb[1], down_yb), ZH_BIT)
    down_gb = swap_bit(down_t0, Y_BIT)
    d_full, qkv_keep, qkv_send = run_qkvgrad(place, normed, d_pack, devices)
    mixed = sum_pair(mix_keep[0, 0], mix_got[0, 0]) + sum_pair(mix_x[0], mix_z[0])
    hidden_out = middle + mixed
    rows = WIDTH // devices
    out_held = add_low(out_keep[:, 0], out_got[:, 0], out_x).reshape(4, 2, rows, WIDTH)
    out_first, out_second = out_held[:, 0], out_held[:, 1]
    qkv_send, out_second, hidden_out = fence(qkv_send, out_second, hidden_out)
    qkv_parts = (
        (0, rows, 0, 768, (0, 1, 2, 3)),
        (0, rows, 768, 768, (1, 0, 2, 3)),
        (0, rows, 1536, 512, (0, 1, 2, 3)),
        (0, rows, 2048, 512, (1, 0, 2, 3)),
    )
    dense_bits = (X_BIT, Y_BIT, ZL_BIT, ZH_BIT)
    last = (d_full, w_query, w_key, w_value, d_middle, inputs, normed_two, d_log)
    grad_in, query_total, key_total, value_total, output_total, small, up_mb = run_reduce(
        ((qkv_keep, qkv_send), (out_first, out_second)),
        (
            (C_BIT, dense_bits, qkv_parts, (WIDTH, KV_HEADS * HEAD_DIM, KV_HEADS * HEAD_DIM)),
            (Y_BIT, (ZL_BIT, ZH_BIT), ((0, rows, 0, WIDTH, (0, 1)),), (WIDTH,)),
            (C_BIT, dense_bits, ((0, rows, 0, LANES, (0, 1, 2, 3)),), (LANES,)),
        ),
        7,
        riders=(Rider(ZH_BIT, (up_kb, (1, 0)), (up_yb, (0,))),),
        work=plan_last(last, gain_attn, ggain_mlp, devices),
    )
    query_total, small, down_mb, down_gb, other = fence(
        query_total, small, down_mb, down_gb, other
    )
    joined = run_join(
        place,
        (
            (gate_ka, gate_ga, gate_ma, gate_oa, up_ka, up_ga, (both, 0), up_oa)
            + (down_ka, down_ga, down_ma),
            (gate_kb, gate_gb, gate_mb, (other, 0), up_kb, up_gb, up_mb, (other, 1))
            + (down_kb, down_gb, down_mb),
        ),
    )
    gate_total, up_total, down_total = [
        total.reshape((local_experts,) + total.shape[2:]) for total in joined
    ]
    return (
        hidden_out[None],
        grad_in[None],
        small[:, LANES - 1],
        query_total,
        key_total,
        value_total,
        output_total,
        small[:, LANES - 2],
        small[:, :all_experts],
        gate_total,
        up_total,
        down_total,
    )


def fits(mesh):
    return mesh.shape["dp"] == KV_HEADS and mesh.shape["expert"] == 4


def solution(mesh):
    in_specs = (
        P("expert", "dp", None),
        P(),
        P(),
        P(),
        P(),
        P(),
        P(),
        P(),
        P("expert", None, None),
        P("expert", None, None),
        P("expert", None, None),
        P("expert", "dp", None),
        P("expert", "dp", None),
        P("expert", "dp", None),
    )
    out_specs = (
        P("expert", "dp", None),
        P("expert", "dp", None),
        P(("dp", "expert")),
        P(("dp", "expert"), None),
        P(("dp", "expert"), None),
        P(("dp", "expert"), None),
        P(("dp", "expert"), None),
        P(("dp", "expert")),
        P(("dp", "expert"), None),
        P("expert", "dp", None),
        P("expert", "dp", None),
        P("expert", "dp", None),
    )
    chosen = fast_body if fits(mesh) else body
    return jax.shard_map(chosen, mesh=mesh, in_specs=in_specs, out_specs=out_specs, check_vma=False)
```

```python
import functools
import math

import jax
import jax.numpy as jnp
from jax import lax
from jax.experimental import pallas as pl
from jax.experimental.pallas import tpu as pltpu
from jax.sharding import PartitionSpec as P

HEADS = 24
KV_HEADS = 8
HEAD_DIM = 64


EPS = 1e-05
MASKED = -1e30


def rotary_tables(positions):
    half = HEAD_DIM // 2
    frequency = jnp.exp(-math.log(10000.0) * jnp.arange(half, dtype=jnp.float32) * 2.0 / HEAD_DIM)
    angles = positions.astype(jnp.float32)[:, None] * frequency[None, :]
    return (jnp.cos(angles)[:, None, :], jnp.sin(angles)[:, None, :])


def rotate(values, cosine, sine):
    half = values.shape[-1] // 2
    first = values[..., :half]
    second = values[..., half:]
    return jnp.concatenate(
        [first * cosine - second * sine, second * cosine + first * sine], axis=-1
    )


def rotate_back(values, cosine, sine):
    half = values.shape[-1] // 2
    first = values[..., :half]
    second = values[..., half:]
    return jnp.concatenate(
        [first * cosine + second * sine, second * cosine - first * sine], axis=-1
    )


def assign_slots(row_chosen, row_ranks, all_experts, capacity):
    pairs = row_chosen.shape[0]
    by_rank = jnp.zeros((pairs,), jnp.int32).at[row_ranks].set(jnp.arange(pairs, dtype=jnp.int32))
    ordered = row_chosen[by_rank]
    table = (ordered[:, None] == jnp.arange(all_experts, dtype=jnp.int32)[None, :]).astype(
        jnp.int32
    )
    before = jnp.sum(table * (jnp.cumsum(table, axis=0) - 1), axis=1)
    slot = before[row_ranks]
    target = jnp.where(slot < capacity, row_chosen * capacity + slot, all_experts * capacity)
    owner = (
        jnp.full((all_experts * capacity,), pairs, jnp.int32)
        .at[target]
        .set(jnp.arange(pairs, dtype=jnp.int32), mode="drop")
    )
    return (target, owner)


def body(
    hidden_in,
    gain_attn,
    w_query,
    w_key,
    w_value,
    w_output,
    gain_mlp,
    w_router,
    w_gate,
    w_up,
    w_down,
    expert_ids,
    slot_order,
    grad_out,
):
    inputs = hidden_in[0]
    cotangent = grad_out[0]
    chosen = expert_ids[0]
    tokens, width = inputs.shape
    top = chosen.shape[1]
    local_experts = w_gate.shape[0]
    peers = lax.axis_size("expert")
    all_experts = local_experts * peers
    pairs = tokens * top
    capacity = pairs // all_experts
    shards = lax.axis_size("dp")
    index = lax.axis_index("dp")
    length = shards * tokens
    block = math.gcd(length, 512)
    groups = HEADS // KV_HEADS
    scale = HEAD_DIM ** (-0.5)
    query_pos = index * tokens + jnp.arange(tokens, dtype=jnp.int32)
    cosine, sine = rotary_tables(query_pos)
    count = ((index + 1) * tokens + block - 1) // block
    inv_one = lax.rsqrt(jnp.mean(inputs * inputs, axis=-1, keepdims=True) + EPS)
    normed = (inputs * inv_one * gain_attn).astype(jnp.bfloat16)
    query_pre = jnp.dot(normed, w_query, preferred_element_type=jnp.float32).reshape(
        tokens, HEADS, HEAD_DIM
    )
    queries = rotate(query_pre, cosine, sine).astype(jnp.bfloat16)
    key_pre = jnp.dot(normed, w_key, preferred_element_type=jnp.float32).reshape(
        tokens, KV_HEADS, HEAD_DIM
    )
    keys_low = rotate(key_pre, cosine, sine).astype(jnp.bfloat16)
    values_low = (
        jnp.dot(normed, w_value, preferred_element_type=jnp.float32)
        .astype(jnp.bfloat16)
        .reshape(tokens, KV_HEADS, HEAD_DIM)
    )
    keys_all, values_all = (
        lax.all_gather(keys_low, "dp", axis=0, tiled=True),
        lax.all_gather(values_low, "dp", axis=0, tiled=True),
    )
    query_groups = queries.reshape(tokens, KV_HEADS, groups, HEAD_DIM)

    def block_scores(key_block, start):
        raw = (
            jnp.einsum(
                "qkgd,skd->kgqs", query_groups, key_block, preferred_element_type=jnp.float32
            )
            * scale
        )
        key_pos = start + jnp.arange(block, dtype=jnp.int32)
        allowed = key_pos[None, :] <= query_pos[:, None]
        return jnp.where(allowed, raw, MASKED)

    def stats_step(step, carry):
        running, total = carry
        scores = block_scores(
            lax.dynamic_slice_in_dim(keys_all, step * block, block, 0), step * block
        )
        newest = jnp.maximum(running, jnp.max(scores, axis=-1))
        total = total * jnp.exp(running - newest) + jnp.sum(
            jnp.exp(scores - newest[..., None]), axis=-1
        )
        return (newest, total)

    stat_init = (
        jnp.full((KV_HEADS, groups, tokens), MASKED, jnp.float32),
        jnp.zeros((KV_HEADS, groups, tokens), jnp.float32),
    )
    running, total = lax.fori_loop(0, count, stats_step, stat_init)
    log_total = running + jnp.log(total)

    def output_step(step, accum):
        start = step * block
        scores = block_scores(lax.dynamic_slice_in_dim(keys_all, start, block, 0), start)
        probs = jnp.exp(scores - log_total[..., None]).astype(jnp.bfloat16)
        value_block = lax.dynamic_slice_in_dim(values_all, start, block, 0)
        return accum + jnp.einsum(
            "kgqs,skd->qkgd", probs, value_block, preferred_element_type=jnp.float32
        )

    attended_groups = lax.fori_loop(
        0, count, output_step, jnp.zeros((tokens, KV_HEADS, groups, HEAD_DIM), jnp.float32)
    )
    attended = attended_groups.reshape(tokens, HEADS * HEAD_DIM)
    attended_low = attended.astype(jnp.bfloat16)
    branch = jnp.dot(attended_low, w_output, preferred_element_type=jnp.float32)
    middle = inputs + branch
    inv_two = lax.rsqrt(jnp.mean(middle * middle, axis=-1, keepdims=True) + EPS)
    normed_two = (middle * inv_two * gain_mlp).astype(jnp.bfloat16)
    logits = jnp.dot(normed_two, w_router, preferred_element_type=jnp.float32)
    onehot = (chosen[:, :, None] == jnp.arange(all_experts, dtype=jnp.int32)[None, None, :]).astype(
        jnp.float32
    )
    picked = jnp.sum(onehot * logits[:, None, :], axis=-1)
    gates = jax.nn.softmax(picked, axis=-1)
    target, owner = assign_slots(chosen.reshape(pairs), slot_order[0, 0], all_experts, capacity)
    valid = owner < pairs
    source = jnp.minimum(owner, pairs - 1)
    rows_send = jnp.where(valid[:, None], normed_two[source // top], 0).reshape(
        peers, local_experts, capacity, width
    )
    received = lax.all_to_all(rows_send, "expert", split_axis=0, concat_axis=0, tiled=True)
    gate_pre = jnp.einsum("necd,edf->necf", received, w_gate, preferred_element_type=jnp.float32)
    up_pre = jnp.einsum("necd,edf->necf", received, w_up, preferred_element_type=jnp.float32)
    hidden = (jax.nn.silu(gate_pre) * up_pre).astype(jnp.bfloat16)
    result = jnp.einsum(
        "necf,efd->necd", hidden, w_down, preferred_element_type=jnp.float32
    ).astype(jnp.bfloat16)
    returned = lax.all_to_all(result, "expert", split_axis=0, concat_axis=0, tiled=True)
    returned, received, gate_pre, up_pre = (returned, received, gate_pre, up_pre)
    zero_row = jnp.zeros((1, width), jnp.bfloat16)
    pair_out = jnp.concatenate([returned.reshape(all_experts * capacity, width), zero_row], axis=0)[
        target
    ].reshape(tokens, top, width)
    mixed = jnp.einsum("tk,tkd->td", gates, pair_out, preferred_element_type=jnp.float32)
    hidden_out = middle + mixed
    dy_pairs = (
        (gates[:, :, None] * cotangent[:, None, :]).astype(jnp.bfloat16).reshape(pairs, width)
    )
    dy_send = jnp.where(valid[:, None], dy_pairs[source], 0).reshape(
        peers, local_experts, capacity, width
    )
    dy_received = lax.all_to_all(dy_send, "expert", split_axis=0, concat_axis=0, tiled=True)
    sigmoid_gate = jax.nn.sigmoid(gate_pre)
    silu_gate = gate_pre * sigmoid_gate
    hidden = (silu_gate * up_pre).astype(jnp.bfloat16)
    grad_down_part = jnp.einsum(
        "necf,necd->efd", hidden, dy_received, preferred_element_type=jnp.float32
    )
    d_hidden = jnp.einsum("necd,efd->necf", dy_received, w_down, preferred_element_type=jnp.float32)
    d_gate = (d_hidden * up_pre * sigmoid_gate * (1.0 + gate_pre * (1.0 - sigmoid_gate))).astype(
        jnp.bfloat16
    )
    d_up = (d_hidden * silu_gate).astype(jnp.bfloat16)
    grad_gate_part = jnp.einsum(
        "necd,necf->edf", received, d_gate, preferred_element_type=jnp.float32
    )
    grad_up_part = jnp.einsum("necd,necf->edf", received, d_up, preferred_element_type=jnp.float32)
    gate_total, up_total, down_total = (
        lax.psum_scatter(
            grad_gate_part.astype(jnp.bfloat16), "dp", scatter_dimension=1, tiled=True
        ).astype(jnp.float32),
        lax.psum_scatter(
            grad_up_part.astype(jnp.bfloat16), "dp", scatter_dimension=1, tiled=True
        ).astype(jnp.float32),
        lax.psum_scatter(
            grad_down_part.astype(jnp.bfloat16), "dp", scatter_dimension=1, tiled=True
        ).astype(jnp.float32),
    )
    d_rows = jnp.einsum("necf,edf->necd", d_gate, w_gate, preferred_element_type=jnp.float32)
    d_rows = (
        d_rows + jnp.einsum("necf,edf->necd", d_up, w_up, preferred_element_type=jnp.float32)
    ).astype(jnp.bfloat16)
    d_back = lax.all_to_all(d_rows, "expert", split_axis=0, concat_axis=0, tiled=True)
    d_pairs = jnp.concatenate([d_back.reshape(all_experts * capacity, width), zero_row], axis=0)[
        target
    ].reshape(tokens, top, width)
    d_normed_two = jnp.sum(d_pairs, axis=1, dtype=jnp.float32)
    d_gates = jnp.einsum("td,tkd->tk", cotangent, pair_out, preferred_element_type=jnp.float32)
    d_picked = gates * (d_gates - jnp.sum(gates * d_gates, axis=-1, keepdims=True))
    d_logits = jnp.sum(onehot * d_picked[:, :, None], axis=1).astype(jnp.bfloat16)
    grad_router_part = jnp.einsum(
        "td,te->de", normed_two, d_logits, preferred_element_type=jnp.float32
    )
    d_normed_two = d_normed_two + jnp.einsum(
        "te,de->td", d_logits, w_router, preferred_element_type=jnp.float32
    )
    scaled_two = d_normed_two * gain_mlp
    grad_gain_mlp_part = jnp.sum(d_normed_two * middle * inv_two, axis=0)
    d_middle = (
        cotangent
        + inv_two * scaled_two
        - middle * inv_two**3 * jnp.mean(middle * scaled_two, axis=-1, keepdims=True)
    )
    d_branch = d_middle.astype(jnp.bfloat16)
    grad_output_part = jnp.einsum(
        "tf,td->fd", attended_low, d_branch, preferred_element_type=jnp.float32
    )
    d_attended = jnp.einsum(
        "td,fd->tf", d_branch, w_output, preferred_element_type=jnp.float32
    ).astype(jnp.bfloat16)
    d_groups = d_attended.reshape(tokens, KV_HEADS, groups, HEAD_DIM)
    delta = jnp.einsum(
        "qkgd,qkgd->kgq", d_groups, attended_groups, preferred_element_type=jnp.float32
    )
    keys_back, values_back = (
        lax.all_gather(keys_low, "dp", axis=0, tiled=True),
        lax.all_gather(values_low, "dp", axis=0, tiled=True),
    )

    def grad_step(step, carry):
        d_query, d_keys, d_values = carry
        start = step * block
        key_block = lax.dynamic_slice_in_dim(keys_back, start, block, 0)
        value_block = lax.dynamic_slice_in_dim(values_back, start, block, 0)
        scores = block_scores(key_block, start)
        probs = jnp.exp(scores - log_total[..., None])
        probs_low = probs.astype(jnp.bfloat16)
        d_probs = jnp.einsum(
            "qkgd,skd->kgqs", d_groups, value_block, preferred_element_type=jnp.float32
        )
        d_scores = (probs * (d_probs - delta[..., None])).astype(jnp.bfloat16)
        d_query = d_query + jnp.einsum(
            "kgqs,skd->qkgd", d_scores, key_block, preferred_element_type=jnp.float32
        )
        key_part = jnp.einsum(
            "kgqs,qkgd->skd", d_scores, query_groups, preferred_element_type=jnp.float32
        )
        value_part = jnp.einsum(
            "kgqs,qkgd->skd", probs_low, d_groups, preferred_element_type=jnp.float32
        )
        d_keys = lax.dynamic_update_slice_in_dim(
            d_keys, lax.dynamic_slice_in_dim(d_keys, start, block, 0) + key_part, start, 0
        )
        d_values = lax.dynamic_update_slice_in_dim(
            d_values, lax.dynamic_slice_in_dim(d_values, start, block, 0) + value_part, start, 0
        )
        return (d_query, d_keys, d_values)

    grad_init = (
        jnp.zeros((tokens, KV_HEADS, groups, HEAD_DIM), jnp.float32),
        jnp.zeros((length, KV_HEADS, HEAD_DIM), jnp.float32),
        jnp.zeros((length, KV_HEADS, HEAD_DIM), jnp.float32),
    )
    d_query, d_keys, d_values = lax.fori_loop(0, count, grad_step, grad_init)
    key_sum, value_sum = (
        lax.psum_scatter(
            (d_keys * scale).reshape(length, KV_HEADS * HEAD_DIM).astype(jnp.bfloat16),
            "dp",
            scatter_dimension=0,
            tiled=True,
        ).astype(jnp.float32),
        lax.psum_scatter(
            d_values.reshape(length, KV_HEADS * HEAD_DIM).astype(jnp.bfloat16),
            "dp",
            scatter_dimension=0,
            tiled=True,
        ).astype(jnp.float32),
    )
    d_query_low = (
        rotate_back((d_query * scale).reshape(tokens, HEADS, HEAD_DIM), cosine, sine)
        .astype(jnp.bfloat16)
        .reshape(tokens, HEADS * HEAD_DIM)
    )
    d_key_low = (
        rotate_back(key_sum.reshape(tokens, KV_HEADS, HEAD_DIM), cosine, sine)
        .astype(jnp.bfloat16)
        .reshape(tokens, KV_HEADS * HEAD_DIM)
    )
    d_value_low = value_sum.astype(jnp.bfloat16)
    grad_query_part = jnp.einsum(
        "td,tf->df", normed, d_query_low, preferred_element_type=jnp.float32
    )
    grad_key_part = jnp.einsum("td,tf->df", normed, d_key_low, preferred_element_type=jnp.float32)
    grad_value_part = jnp.einsum(
        "td,tf->df", normed, d_value_low, preferred_element_type=jnp.float32
    )
    d_normed = jnp.einsum("tf,df->td", d_query_low, w_query, preferred_element_type=jnp.float32)
    d_normed = d_normed + jnp.einsum(
        "tf,df->td", d_key_low, w_key, preferred_element_type=jnp.float32
    )
    d_normed = d_normed + jnp.einsum(
        "tf,df->td", d_value_low, w_value, preferred_element_type=jnp.float32
    )
    scaled_one = d_normed * gain_attn
    grad_gain_attn_part = jnp.sum(d_normed * inputs * inv_one, axis=0)
    grad_in = (
        d_middle
        + inv_one * scaled_one
        - inputs * inv_one**3 * jnp.mean(inputs * scaled_one, axis=-1, keepdims=True)
    )
    dense = (
        lax.psum_scatter(grad_gain_attn_part, ("dp", "expert"), scatter_dimension=0, tiled=True),
        lax.psum_scatter(grad_query_part, ("dp", "expert"), scatter_dimension=0, tiled=True),
        lax.psum_scatter(grad_key_part, ("dp", "expert"), scatter_dimension=0, tiled=True),
        lax.psum_scatter(grad_value_part, ("dp", "expert"), scatter_dimension=0, tiled=True),
        lax.psum_scatter(grad_output_part, ("dp", "expert"), scatter_dimension=0, tiled=True),
        lax.psum_scatter(grad_gain_mlp_part, ("dp", "expert"), scatter_dimension=0, tiled=True),
        lax.psum_scatter(grad_router_part, ("dp", "expert"), scatter_dimension=0, tiled=True),
    )
    return (
        hidden_out[None],
        grad_in[None],
        dense[0],
        dense[1],
        dense[2],
        dense[3],
        dense[4],
        dense[5],
        dense[6],
        gate_total,
        up_total,
        down_total,
    )

BF = jnp.bfloat16
F32 = jnp.float32
WIDTH = 1536
LANES = 128
PER_KV = HEADS // KV_HEADS
ROWS_Q = PER_KV * HEAD_DIM
PACK = ROWS_Q + 2 * HEAD_DIM
BIT_Y, BIT_ZL, BIT_ZH = 1, 2, 4
BIT_C, BIT_X = 1, 2
BLOCK_Q = 256
BLOCK_K = 512
SLOTS = 64
CHUNK = 512
MIB = 1 << 20
hbm = pl.BlockSpec(memory_space=pltpu.HBM)


def dot_nn(a, b):
    return lax.dot_general(a, b, (((1,), (0,)), ((), ())), preferred_element_type=F32)


def dot_nt(a, b):
    return lax.dot_general(a, b, (((1,), (1,)), ((), ())), preferred_element_type=F32)


def dot_tn(a, b):
    return lax.dot_general(a, b, (((0,), (0,)), ((), ())), preferred_element_type=F32)


def cost(flops, moved, transcendentals=0):
    return pl.CostEstimate(
        flops=int(flops), bytes_accessed=int(moved), transcendentals=int(transcendentals)
    )


def params(mib, dims=None):
    return pltpu.CompilerParams(vmem_limit_bytes=mib * MIB, dimension_semantics=dims)


def swap(values, axis, mask):
    size = lax.axis_size(axis)
    return lax.ppermute(values, axis, [(i, i ^ mask) for i in range(size)])


def swap_bit(values, bit):
    axis, mask = bit
    return swap(values, axis, mask)


def fence(*values):
    return lax.optimization_barrier(values)


C_BIT = ("expert", BIT_C)
X_BIT = ("expert", BIT_X)
Y_BIT = ("dp", BIT_Y)
ZL_BIT = ("dp", BIT_ZL)
ZH_BIT = ("dp", BIT_ZH)


def pre_kernel(
    hid_ref,
    gain_ref,
    wq_ref,
    wk_ref,
    wv_ref,
    cos_ref,
    sin_ref,
    cot_ref,
    norm_ref,
    pack_ref,
    low_ref,
):
    tokens = hid_ref.shape[0]
    half = tokens // 2
    low_ref[...] = cot_ref[...].astype(BF)
    inputs = hid_ref[...]
    inv = lax.rsqrt(jnp.mean(inputs * inputs, axis=-1, keepdims=True) + EPS)
    normed = (inputs * inv * gain_ref[...]).astype(BF)
    norm_ref[...] = normed
    low = (lax.broadcasted_iota(jnp.int32, (tokens, LANES), 1) % HEAD_DIM) < HEAD_DIM // 2
    cosine, sine = cos_ref[...], sin_ref[...]

    def turn(tile):
        other = jnp.where(
            low,
            pltpu.roll(tile, LANES - HEAD_DIM // 2, 1),
            pltpu.roll(tile, HEAD_DIM // 2, 1),
        )
        return (tile * cosine + other * sine).astype(BF)

    tiles = []
    for n in range(wq_ref.shape[1] // CHUNK):
        pre = dot_nn(normed, wq_ref[:, n * CHUNK : (n + 1) * CHUNK])
        tiles += [turn(pre[:, m * LANES : (m + 1) * LANES]) for m in range(CHUNK // LANES)]
    queries = jnp.concatenate(tiles, axis=1)
    pre = dot_nn(normed, wk_ref[...])
    keys = jnp.concatenate(
        [turn(pre[:, m * LANES : (m + 1) * LANES]) for m in range(pre.shape[1] // LANES)], axis=1
    )
    values = dot_nn(normed, wv_ref[...]).astype(BF)
    for g in range(KV_HEADS):
        at = g * ROWS_Q
        head = slice(g * HEAD_DIM, (g + 1) * HEAD_DIM)
        pack_ref[g, 0:tokens] = queries[:, at : at + LANES]
        pack_ref[g, tokens : 2 * tokens] = jnp.concatenate(
            [queries[:, at + LANES : at + ROWS_Q], keys[:, head]], axis=1
        )
        pack_ref[g, 2 * tokens :] = jnp.concatenate(
            [values[:half, head], values[half:, head]], axis=1
        )


def run_pre(inputs, gain, w_query, w_key, w_value, cos_tab, sin_tab, cotangent):
    tokens = inputs.shape[0]
    return pl.pallas_call(
        pre_kernel,
        out_shape=(
            jax.ShapeDtypeStruct((tokens, WIDTH), BF),
            jax.ShapeDtypeStruct((KV_HEADS, tokens * PACK // LANES, LANES), BF),
            jax.ShapeDtypeStruct((tokens, WIDTH), BF),
        ),
        compiler_params=params(60),
        cost_estimate=cost(2 * tokens * WIDTH * 2560, 14e6),
    )(inputs, gain[None], w_query, w_key, w_value, cos_tab, sin_tab, cotangent)


def unpack_heads(block_ref, out_ref, row, tokens, column):
    half = tokens // 2
    out_ref[row : row + tokens, column : column + LANES] = block_ref[0:tokens]
    rest = block_ref[tokens : tokens + half]
    out_ref[row : row + half, column + LANES : column + ROWS_Q] = rest[:, :HEAD_DIM]
    out_ref[row + half : row + tokens, column + LANES : column + ROWS_Q] = rest[:, HEAD_DIM:]


def pack_heads(block_ref, rows, tokens):
    half = tokens // 2
    block_ref[0:tokens] = rows[:, 0:LANES]
    block_ref[tokens : tokens + half] = jnp.concatenate(
        [rows[:half, LANES:ROWS_Q], rows[half:, LANES:ROWS_Q]], axis=1
    )


def unpack_all(block_ref, q_ref, k_ref, v_ref, row, tokens, q_at=0, k_at=0, v_at=0):
    half = tokens // 2
    rows = slice(row, row + tokens)
    q_ref[rows, q_at : q_at + LANES] = block_ref[0:tokens]
    two = block_ref[tokens : 2 * tokens]
    q_ref[rows, q_at + LANES : q_at + ROWS_Q] = two[:, :HEAD_DIM]
    k_ref[rows, k_at : k_at + HEAD_DIM] = two[:, HEAD_DIM:]
    rest = block_ref[2 * tokens : 2 * tokens + half]
    v_ref[row : row + half, v_at : v_at + HEAD_DIM] = rest[:, :HEAD_DIM]
    v_ref[row + half : row + tokens, v_at : v_at + HEAD_DIM] = rest[:, HEAD_DIM:]


def heads_t(block, width):
    return jnp.concatenate(
        [block[:, h * HEAD_DIM : (h + 1) * HEAD_DIM].astype(F32).T for h in range(width)], axis=1
    )


def heads_rows(block, width):
    return jnp.concatenate(
        [block[:, h * HEAD_DIM : (h + 1) * HEAD_DIM] for h in range(width)], axis=0
    )


def allowed_t(step, block):
    shape = (BLOCK_K, PER_KV * BLOCK_Q)
    key_pos = step * BLOCK_K + lax.broadcasted_iota(jnp.int32, shape, 0)
    query_pos = block * BLOCK_Q + lax.broadcasted_iota(jnp.int32, shape, 1) % BLOCK_Q
    return key_pos <= query_pos


def forward_kernel(pack_ref, out_ref, out_t_ref, lse_ref, q_s, k_s, v_s, vt_s, out_s):
    block = pl.program_id(0)
    sources = pack_ref.shape[0]
    tokens = q_s.shape[0] // sources

    @pl.when(block == 0)
    def _():
        for n in range(sources):
            unpack_all(pack_ref.at[n], q_s, k_s, v_s, n * tokens, tokens)
        vt_s[...] = v_s[...].astype(F32).T.astype(BF)

    rows = pl.ds(pl.multiple_of(block * BLOCK_Q, BLOCK_Q), BLOCK_Q)
    scale = HEAD_DIM ** (-0.5)
    q_t = (heads_t(q_s[rows, :], PER_KV) * scale).astype(BF)
    columns = PER_KV * BLOCK_Q

    def step(j, carry, masked):
        running, total, accum = carry
        keys = pl.ds(pl.multiple_of(j * BLOCK_K, BLOCK_K), BLOCK_K)
        scores = dot_nn(k_s[keys, :], q_t)
        if masked:
            scores = jnp.where(allowed_t(j, block), scores, MASKED)
        newest = jnp.maximum(running, jnp.max(scores, axis=0, keepdims=True))
        fade = jnp.exp(running - newest)
        probs = jnp.exp(scores - newest)
        total = total * fade + jnp.sum(probs, axis=0, keepdims=True)
        accum = accum * fade + dot_nn(vt_s[:, keys], probs.astype(BF))
        return newest, total, accum

    carry = (
        jnp.full((1, columns), MASKED, F32),
        jnp.zeros((1, columns), F32),
        jnp.zeros((HEAD_DIM, columns), F32),
    )
    last = (block * BLOCK_Q) // BLOCK_K
    carry = lax.fori_loop(0, last, lambda j, c: step(j, c, False), carry)
    running, total, accum = step(last, carry, True)
    out_t = accum / total
    out_t_ref[0] = out_t
    lse_ref[0] = running + jnp.log(total)
    out_s[rows, :] = jnp.concatenate(
        [out_t[:, h * BLOCK_Q : (h + 1) * BLOCK_Q].T for h in range(PER_KV)], axis=1
    ).astype(BF)

    @pl.when(block == pl.num_programs(0) - 1)
    def _():
        for n in range(sources):
            pack_heads(out_ref.at[n], out_s[n * tokens : (n + 1) * tokens, :], tokens)


def run_forward(pack):
    sources = pack.shape[0]
    length = sources * (pack.shape[1] * LANES // PACK)
    packed = (sources, length // sources * ROWS_Q // LANES, LANES)
    blocks = length // BLOCK_Q
    columns = PER_KV * BLOCK_Q
    return pl.pallas_call(
        forward_kernel,
        grid=(blocks,),
        in_specs=[pl.BlockSpec(pack.shape, lambda i: (0, 0, 0))],
        out_specs=(
            pl.BlockSpec(packed, lambda i: (0, 0, 0)),
            pl.BlockSpec((1, HEAD_DIM, columns), lambda i: (i, 0, 0)),
            pl.BlockSpec((1, 1, columns), lambda i: (i, 0, 0)),
        ),
        out_shape=(
            jax.ShapeDtypeStruct(packed, BF),
            jax.ShapeDtypeStruct((blocks, HEAD_DIM, columns), F32),
            jax.ShapeDtypeStruct((blocks, 1, columns), F32),
        ),
        scratch_shapes=[
            pltpu.VMEM((length, ROWS_Q), BF),
            pltpu.VMEM((length, HEAD_DIM), BF),
            pltpu.VMEM((length, HEAD_DIM), BF),
            pltpu.VMEM((HEAD_DIM, length), BF),
            pltpu.VMEM((length, ROWS_Q), BF),
        ],
        compiler_params=params(60, ("arbitrary",)),
        cost_estimate=cost(8 * length * length * ROWS_Q, 6e6, length * length * PER_KV),
    )(pack)


def backward_kernel(
    pack_ref,
    grad_ref,
    out_t_ref,
    lse_ref,
    cos_ref,
    sin_ref,
    res_ref,
    q_s,
    do_s,
    k_s,
    v_s,
    kt_s,
    dk_s,
    dv_s,
):
    block = pl.program_id(0)
    sources = pack_ref.shape[0]
    tokens = q_s.shape[0] // sources

    @pl.when(block == 0)
    def _():
        for n in range(sources):
            unpack_all(pack_ref.at[n], q_s, k_s, v_s, n * tokens, tokens)
            unpack_heads(grad_ref.at[n], do_s, n * tokens, tokens, 0)
        kt_s[...] = k_s[...].astype(F32).T.astype(BF)
        dk_s[...] = jnp.zeros_like(dk_s)
        dv_s[...] = jnp.zeros_like(dv_s)

    scale = HEAD_DIM ** (-0.5)
    half = HEAD_DIM // 2
    rows = pl.ds(pl.multiple_of(block * BLOCK_Q, BLOCK_Q), BLOCK_Q)
    q_block = q_s[rows, :]
    q_t = (heads_t(q_block, PER_KV) * scale).astype(BF)
    q_rows = (heads_rows(q_block, PER_KV).astype(F32) * scale).astype(BF)
    do_block = do_s[rows, :]
    do_f32 = heads_t(do_block, PER_KV)
    do_t = do_f32.astype(BF)
    do_rows = heads_rows(do_block, PER_KV)
    delta = jnp.sum(do_f32 * out_t_ref[0], axis=0, keepdims=True)
    lse = lse_ref[0]

    def step(j, dq_t, masked):
        keys = pl.ds(pl.multiple_of(j * BLOCK_K, BLOCK_K), BLOCK_K)
        scores = dot_nn(k_s[keys, :], q_t)
        if masked:
            scores = jnp.where(allowed_t(j, block), scores, MASKED)
        probs = jnp.exp(scores - lse)
        d_probs = dot_nn(v_s[keys, :], do_t)
        d_scores = (probs * (d_probs - delta)).astype(BF)
        dv_s[keys, :] += dot_nn(probs.astype(BF), do_rows)
        dk_s[keys, :] += dot_nn(d_scores, q_rows)
        return dq_t + dot_nn(kt_s[:, keys], d_scores)

    last = (block * BLOCK_Q) // BLOCK_K
    dq_t = jnp.zeros((HEAD_DIM, PER_KV * BLOCK_Q), F32)
    dq_t = lax.fori_loop(0, last, lambda j, c: step(j, c, False), dq_t)
    dq_t = step(last, dq_t, True) * scale

    def turn_back(values, cosine, sine):
        first, second = values[:half], values[half:]
        return jnp.concatenate(
            [first * cosine + second * sine, second * cosine - first * sine], axis=0
        )

    columns = pl.ds(pl.multiple_of(block * BLOCK_Q, BLOCK_Q), BLOCK_Q)
    cosine, sine = cos_ref[:, columns], sin_ref[:, columns]
    q_s[rows, :] = jnp.concatenate(
        [
            turn_back(dq_t[:, h * BLOCK_Q : (h + 1) * BLOCK_Q], cosine, sine).T
            for h in range(PER_KV)
        ],
        axis=1,
    ).astype(BF)

    @pl.when(block == pl.num_programs(0) - 1)
    def _():
        dk = turn_back(dk_s[...].T, cos_ref[...], sin_ref[...]).T.astype(BF)
        half = tokens // 2
        for n in range(sources):
            row = n * tokens
            res_ref[n, 0:tokens] = q_s[row : row + tokens, 0:LANES]
            res_ref[n, tokens : 2 * tokens] = jnp.concatenate(
                [q_s[row : row + tokens, LANES:ROWS_Q], dk[row : row + tokens]], axis=1
            )
            res_ref[n, 2 * tokens :] = jnp.concatenate(
                [dv_s[row : row + half, :], dv_s[row + half : row + tokens, :]], axis=1
            ).astype(BF)


def run_backward(pack, grad, out_t, lse, cos_t, sin_t):
    length = cos_t.shape[1]
    blocks = length // BLOCK_Q
    columns = PER_KV * BLOCK_Q
    half = HEAD_DIM // 2
    return pl.pallas_call(
        backward_kernel,
        grid=(blocks,),
        in_specs=[
            pl.BlockSpec(pack.shape, lambda i: (0, 0, 0)),
            pl.BlockSpec(grad.shape, lambda i: (0, 0, 0)),
            pl.BlockSpec((1, HEAD_DIM, columns), lambda i: (i, 0, 0)),
            pl.BlockSpec((1, 1, columns), lambda i: (i, 0, 0)),
            pl.BlockSpec((half, length), lambda i: (0, 0)),
            pl.BlockSpec((half, length), lambda i: (0, 0)),
        ],
        out_specs=pl.BlockSpec(pack.shape, lambda i: (0, 0, 0)),
        out_shape=jax.ShapeDtypeStruct(pack.shape, BF),
        scratch_shapes=[
            pltpu.VMEM((length, ROWS_Q), BF),
            pltpu.VMEM((length, ROWS_Q), BF),
            pltpu.VMEM((length, HEAD_DIM), BF),
            pltpu.VMEM((length, HEAD_DIM), BF),
            pltpu.VMEM((HEAD_DIM, length), BF),
            pltpu.VMEM((length, HEAD_DIM), F32),
            pltpu.VMEM((length, HEAD_DIM), F32),
        ],
        compiler_params=params(60, ("arbitrary",)),
        cost_estimate=cost(20 * length * length * ROWS_Q, 8e6, length * length * PER_KV),
    )(pack, grad, out_t, lse, cos_t, sin_t)


def mid_kernel(att_ref, wo_ref, hid_ref, gain_ref, mid_ref, norm_ref, full_ref):
    for g in range(KV_HEADS):
        unpack_heads(att_ref.at[g], full_ref, 0, full_ref.shape[0], g * ROWS_Q)
    middle = hid_ref[...] + dot_nn(full_ref[...], wo_ref[...])
    mid_ref[...] = middle
    inv = lax.rsqrt(jnp.mean(middle * middle, axis=-1, keepdims=True) + EPS)
    norm_ref[...] = (middle * inv * gain_ref[...]).astype(BF)


def run_mid(att, w_output, inputs, gain):
    tokens = inputs.shape[0]
    return pl.pallas_call(
        mid_kernel,
        out_shape=(
            jax.ShapeDtypeStruct((tokens, WIDTH), F32),
            jax.ShapeDtypeStruct((tokens, WIDTH), BF),
            jax.ShapeDtypeStruct((tokens, WIDTH), BF),
        ),
        compiler_params=params(60),
        cost_estimate=cost(2 * tokens * WIDTH * WIDTH, 12e6),
    )(att, w_output, inputs, gain[None])


def expert_kernel(
    place_ref,
    x_ref,
    g_ref,
    gates_ref,
    map_ref,
    wg0_ref,
    wg1_ref,
    wu0_ref,
    wu1_ref,
    wd0_ref,
    wd1_ref,
    *refs,
    first,
):
    if first:
        mix_prior = dx_prior = None
    else:
        mix_prior, dx_prior = refs[0:2], refs[2:4]
        refs = refs[4:]
    (
    mix_keep,
    mix_send,
    dx_keep,
    dx_send,
    gate_keep,
    gate_send0,
    gate_send1,
    early,
    up_keep,
    up_send0,
    up_send1,
    down_keep,
    down_send0,
    down_send1,
    xs,
    gs,
    gate_s,
    wide_s,
    tall_s,
    ) = refs
    step = pl.program_id(0)
    sources = map_ref.shape[0]
    experts = xs.shape[0]
    low = 0 if first else experts
    rows = experts * SLOTS
    count = WIDTH // CHUNK

    def pick_of(source):
        return one_hot(map_ref[source, low : low + experts, :], rows)

    @pl.when(step < experts)
    def _():
        e = step
        x = x_ref[0]
        w_gate = jnp.concatenate([wg0_ref[0], wg1_ref[0]], axis=1)
        w_up = jnp.concatenate([wu0_ref[0], wu1_ref[0]], axis=1)
        gate_pre = dot_nn(x, w_gate)
        up_pre = dot_nn(x, w_up)
        sig = jax.nn.sigmoid(gate_pre)
        silu = gate_pre * sig
        hidden = (silu * up_pre).astype(BF)
        gate = gates_ref[0]
        d_hidden = jnp.zeros(hidden.shape, F32)
        d_gates = jnp.zeros(gate.shape, F32)
        for n in range(count):
            cols = slice(n * CHUNK, (n + 1) * CHUNK)
            w_down = jnp.concatenate([wd0_ref[0, :, cols], wd1_ref[0, :, cols]], axis=0)
            grad = g_ref[0, :, cols].astype(F32)
            d_y = (gate * grad).astype(BF)
            y = dot_nn(hidden, w_down)
            d_gates += jnp.sum(y * grad, axis=1, keepdims=True)
            gs[e, :, cols] = (gate * y).astype(BF)
            d_hidden += dot_nt(d_y, w_down)
            wide_s[:, cols] = dot_tn(hidden, d_y).astype(BF)
        gate_s[e] = d_gates
        d_gate = (d_hidden * up_pre * sig * (1.0 + gate_pre * (1.0 - sig))).astype(BF)
        d_up = (d_hidden * silu).astype(BF)

        y_at, zl_at, zh_at = place_ref[1], place_ref[2], place_ref[3]
        part = down_keep.shape[2]
        for z in range(2):
            base = (zh_at ^ z) * 2
            down_keep[z, 0] = wide_s[pl.ds(pl.multiple_of((base + y_at) * part, part), part), :]
            (down_send0, down_send1)[z][0] = wide_s[
                pl.ds(pl.multiple_of((base + (1 - y_at)) * part, part), part), :
            ]

        def spread(keep, send):
            part = keep.shape[3]
            for z in range(2):
                for low in range(2):
                    base = ((zh_at ^ z) * 2 + (zl_at ^ low)) * 2
                    keep[z, low, 0] = tall_s[
                        pl.ds(pl.multiple_of((base + y_at) * part, part), part), :
                    ]
                    send[z][low, 0] = tall_s[
                        pl.ds(pl.multiple_of((base + (1 - y_at)) * part, part), part), :
                    ]

        for n in range(count):
            cols = slice(n * CHUNK, (n + 1) * CHUNK)
            tall_s[cols, :] = dot_tn(x[:, cols], d_gate).astype(BF)
        spread(gate_keep, (gate_send0, gate_send1))
        early[0, 0] = gate_keep[1, 1, 0]
        early[1, 0] = gate_send1[1, 0]
        for n in range(count):
            cols = slice(n * CHUNK, (n + 1) * CHUNK)
            tall_s[cols, :] = dot_tn(x[:, cols], d_up).astype(BF)
        spread(up_keep, (up_send0, up_send1))
        for n in range(count):
            cols = slice(n * CHUNK, (n + 1) * CHUNK)
            d_x = dot_nt(d_gate, w_gate[cols]) + dot_nt(d_up, w_up[cols])
            xs[e, :, cols] = d_x.astype(BF)

    def combine(source, mix_out, dx_out, mix_in, dx_in):
        def put(out, prior, cols, values):
            if prior is not None:
                values += prior[0, :, cols].astype(F32)
            out[0, :, cols] = values.astype(BF)

        here = pl.ds(pl.multiple_of(source * SLOTS, SLOTS), SLOTS)
        pick = pick_of(source).astype(BF)
        for n in range(count):
            cols = slice(n * CHUNK, (n + 1) * CHUNK)
            put(dx_out, dx_in, cols, dot_tn(pick, xs[:, here, cols].reshape(rows, CHUNK)))
            put(mix_out, mix_in, cols, dot_tn(pick, gs[:, here, cols].reshape(rows, CHUNK)))
        values = gate_s[:, here, :].reshape(rows, 1)
        column = lax.broadcasted_iota(jnp.int32, (rows, LANES), 1)
        owner = lax.broadcasted_iota(jnp.int32, (rows, LANES), 0) // SLOTS
        spread_out = jnp.where(column == owner + (place_ref[4] + low), values, 0.0).astype(BF)
        put(dx_out, dx_in, slice(WIDTH, WIDTH + LANES), dot_tn(pick, spread_out))

    @pl.when((step >= experts) & (step < experts + sources // 2))
    def _():
        source = step - experts + sources // 2
        prior = (None, None) if first else (mix_prior[1], dx_prior[1])
        combine(source, mix_send, dx_send, *prior)

    @pl.when(step >= experts + sources // 2)
    def _():
        source = step - experts - sources // 2
        prior = (None, None) if first else (mix_prior[0], dx_prior[0])
        combine(source, mix_keep, dx_keep, *prior)


def less(shape):
    return jax.ShapeDtypeStruct(shape.shape[1:], shape.dtype)


def run_experts(place, x_slots, g_slots, gates, maps, w_gate, w_up, w_down, prior=()):
    sources, _, tokens = maps.shape
    width = x_slots.shape[2]
    experts = w_gate.shape[0] // 2
    low = experts if prior else 0
    ffe = w_gate.shape[2]
    part = ffe // 8
    quarter = width // 8
    half = ffe // 2
    slots = sources * SLOTS
    extra = width + LANES
    second = experts
    third = second + sources // 2

    def at(i, low, size):
        return jnp.clip(i - low, 0, size - 1)

    def expert_of(i):
        return at(i, 0, experts)

    def w_cols(block):
        return pl.BlockSpec(
            (1, width, LANES), lambda i, p: (expert_of(i) + low, 0, p[0] + 2 * block)
        )

    def w_rows(block):
        return pl.BlockSpec(
            (1, LANES, width), lambda i, p: (expert_of(i) + low, p[0] + 2 * block, 0)
        )

    slot_spec = pl.BlockSpec((1, slots, width), lambda i, p: (expert_of(i) + low, 0, 0))

    def out_tokens(low, cols):
        return pl.BlockSpec((1, tokens, cols), lambda i, p: (at(i, low, sources // 2), 0, 0))

    tall_spec = pl.BlockSpec(
        (2, 2, 1, quarter, half), lambda i, p: (0, 0, expert_of(i), 0, 0)
    )
    wide_spec = pl.BlockSpec((2, 1, part, width), lambda i, p: (0, expert_of(i), 0, 0))
    tall_half = pl.BlockSpec((2, 1, quarter, half), lambda i, p: (0, expert_of(i), 0, 0))
    wide_half = pl.BlockSpec((1, part, width), lambda i, p: (expert_of(i), 0, 0))
    tall = jax.ShapeDtypeStruct((2, 2, experts, quarter, half), BF)
    wide = jax.ShapeDtypeStruct((2, experts, part, width), BF)
    mixed = jax.ShapeDtypeStruct((sources // 2, tokens, width), BF)
    d_x = jax.ShapeDtypeStruct((sources // 2, tokens, extra), BF)
    sums = (
        out_tokens(third, width),
        out_tokens(second, width),
        out_tokens(third, extra),
        out_tokens(second, extra),
    )
    return pl.pallas_call(
        functools.partial(expert_kernel, first=not prior),
        grid_spec=pltpu.PrefetchScalarGridSpec(
            num_scalar_prefetch=1,
            grid=(third + sources // 2,),
            in_specs=[
                slot_spec,
                slot_spec,
                pl.BlockSpec((1, slots, 1), lambda i, p: (expert_of(i) + low, 0, 0)),
                pl.BlockSpec(maps.shape, lambda i, p: (0, 0, 0)),
                w_cols(0),
                w_cols(1),
                w_cols(0),
                w_cols(1),
                w_rows(0),
                w_rows(1),
                *(sums if prior else ()),
            ],
            out_specs=(
                *sums,
                tall_spec,
                tall_half,
                tall_half,
                tall_half,
                tall_spec,
                tall_half,
                tall_half,
                wide_spec,
                wide_half,
                wide_half,
            ),
            scratch_shapes=[
                pltpu.VMEM((experts, slots, width), BF),
                pltpu.VMEM((experts, slots, width), BF),
                pltpu.VMEM((experts, slots, 1), F32),
                pltpu.VMEM((half, width), BF),
                pltpu.VMEM((width, half), BF),
            ],
        ),
        out_shape=(mixed, mixed, d_x, d_x)
        + (tall, less(tall), less(tall), less(tall))
        + (tall, less(tall), less(tall))
        + (wide, less(wide), less(wide)),
        compiler_params=params(60, ("arbitrary",)),
        cost_estimate=cost(30e9, 60e6),
    )(place, x_slots, g_slots, gates, maps, w_gate, w_gate, w_up, w_up, w_down, w_down, *prior)


def post_kernel(
    dx_ref,
    mid_ref,
    cot_ref,
    norm_ref,
    wr_ref,
    map_ref,
    gain_ref,
    wo_ref,
    datt_ref,
    dmid_ref,
    dlow_ref,
    dlog_ref,
    ggain_ref,
):
    middle = mid_ref[...]
    inv = lax.rsqrt(jnp.mean(middle * middle, axis=-1, keepdims=True) + EPS)
    chosen = map_ref[...] >= 0.0
    logits = jnp.where(chosen, dot_nn(norm_ref[...], wr_ref[...]), MASKED)
    raised = jnp.exp(logits - jnp.max(logits, axis=-1, keepdims=True))
    raised = jnp.where(chosen, raised, 0.0)
    gates = raised / jnp.sum(raised, axis=-1, keepdims=True)
    d_gates = dx_ref[:, WIDTH:]
    d_picked = gates * (d_gates - jnp.sum(gates * d_gates, axis=-1, keepdims=True))
    d_logits = d_picked.astype(BF)
    dlog_ref[...] = d_logits
    d_norm = dx_ref[:, :WIDTH] + dot_nt(d_logits, wr_ref[...])
    scaled = d_norm * gain_ref[...]
    ggain_ref[...] = jnp.sum(d_norm * middle * inv, axis=0, keepdims=True)
    d_mid = (
        cot_ref[...]
        + inv * scaled
        - middle * inv**3 * jnp.mean(middle * scaled, axis=-1, keepdims=True)
    )
    dmid_ref[...] = d_mid
    d_low = d_mid.astype(BF)
    dlow_ref[...] = d_low
    d_att = dot_nt(d_low, wo_ref[...]).astype(BF)
    for g in range(KV_HEADS):
        pack_heads(datt_ref.at[g], d_att[:, g * ROWS_Q : (g + 1) * ROWS_Q], d_att.shape[0])


def run_post(dx_sum, middle, cotangent, normed_two, wr_pad, map_rows, gain, w_output):
    tokens = middle.shape[0]
    return pl.pallas_call(
        post_kernel,
        out_shape=(
            jax.ShapeDtypeStruct((KV_HEADS, tokens * ROWS_Q // LANES, LANES), BF),
            jax.ShapeDtypeStruct((tokens, WIDTH), F32),
            jax.ShapeDtypeStruct((tokens, WIDTH), BF),
            jax.ShapeDtypeStruct((tokens, LANES), BF),
            jax.ShapeDtypeStruct((1, WIDTH), F32),
        ),
        compiler_params=params(60),
        cost_estimate=cost(2 * tokens * WIDTH * WIDTH, 14e6),
    )(dx_sum, middle, cotangent, normed_two, wr_pad, map_rows, gain[None], w_output)


def put_rows(place_ref, held, keep, send):
    part = keep.shape[1]
    for b in range(keep.shape[0]):
        own = (2 * b) ^ place_ref[5]
        keep[b] = held[pl.ds(pl.multiple_of(own * part, part), part), :]
        other = own ^ 1
        send[b] = held[pl.ds(pl.multiple_of(other * part, part), part), :]


def qkvgrad_kernel(place_ref, a_ref, d_ref, full_ref, keep, send, held):
    step = pl.program_id(0)

    @pl.when(step == 0)
    def _():
        key_at = KV_HEADS * ROWS_Q
        value_at = key_at + KV_HEADS * HEAD_DIM
        for g in range(KV_HEADS):
            unpack_all(
                d_ref.at[g],
                full_ref,
                full_ref,
                full_ref,
                0,
                full_ref.shape[0],
                g * ROWS_Q,
                key_at + g * HEAD_DIM,
                value_at + g * HEAD_DIM,
            )

    cols = pl.ds(pl.multiple_of(step * 256, 256), 256)
    held[...] = dot_tn(a_ref[...], full_ref[:, cols]).astype(BF)
    put_rows(place_ref, held, keep, send)


def run_qkvgrad(place, normed, d_pack, blocks):
    tokens, rows = normed.shape
    cols = KV_HEADS * PACK
    part = rows // blocks
    spec = pl.BlockSpec((blocks // 2, part, 256), lambda i, p: (0, 0, i))
    shape = jax.ShapeDtypeStruct((blocks // 2, part, cols), BF)
    return pl.pallas_call(
        qkvgrad_kernel,
        grid_spec=pltpu.PrefetchScalarGridSpec(
            num_scalar_prefetch=1,
            grid=(cols // 256,),
            in_specs=[
                pl.BlockSpec((tokens, rows), lambda i, p: (0, 0)),
                pl.BlockSpec(d_pack.shape, lambda i, p: (0, 0, 0)),
            ],
            out_specs=(pl.BlockSpec((tokens, cols), lambda i, p: (0, 0)), spec, spec),
            scratch_shapes=[pltpu.VMEM((rows, 256), BF)],
        ),
        out_shape=(jax.ShapeDtypeStruct((tokens, cols), BF), shape, shape),
        compiler_params=params(60, ("arbitrary",)),
        cost_estimate=cost(2 * tokens * rows * cols, 12e6),
    )(place, normed, d_pack)


def last_work(inputs, outputs, scratch):
    gain_ref, gmlp_ref, sources = inputs[0], inputs[1], inputs[2:]
    (out_ref,) = outputs
    keep, send, held = scratch[:3]
    buffers, load_sem = scratch[3:-1], scratch[-1]
    loads = [
        pltpu.make_async_copy(source, buffer, load_sem.at[n])
        for n, (source, buffer) in enumerate(zip(sources, buffers))
    ]
    for load in loads:
        load.start()
    d_ref, wq_ref, wk_ref, wv_ref, dmid_ref, hid_ref, norm_ref, dlog_ref = buffers
    key_at = KV_HEADS * ROWS_Q
    value_at = key_at + KV_HEADS * HEAD_DIM
    device = lax.axis_index("dp") * lax.axis_size("expert") + lax.axis_index("expert")

    def compute():
        for load in loads:
            load.wait()
        tokens = hid_ref.shape[0]
        size = tokens // 4
        ggain = jnp.zeros(gain_ref.shape, F32)
        for r in range(4):
            rows = slice(r * size, (r + 1) * size)
            d_norm = dot_nt(d_ref[rows, 0:key_at], wq_ref[...])
            d_norm += dot_nt(d_ref[rows, key_at:value_at], wk_ref[...])
            d_norm += dot_nt(d_ref[rows, value_at:], wv_ref[...])
            values = hid_ref[rows, :]
            inv = lax.rsqrt(jnp.mean(values * values, axis=-1, keepdims=True) + EPS)
            scaled = d_norm * gain_ref[...]
            ggain += jnp.sum(d_norm * values * inv, axis=0, keepdims=True)
            out_ref[rows, :] = (
                dmid_ref[rows, :]
                + inv * scaled
                - values * inv**3 * jnp.mean(values * scaled, axis=-1, keepdims=True)
            )
        columns = dot_tn(norm_ref[...], dlog_ref[...])
        lane = lax.broadcasted_iota(jnp.int32, columns.shape, 1)
        for n, row in enumerate((gmlp_ref[...], ggain)):
            turned = jnp.broadcast_to(row, (8, row.shape[1])).T[:, 0:1]
            columns = jnp.where(lane == LANES - 2 + n, turned, columns)
        held[...] = columns
        part = keep.shape[1]
        for b in range(keep.shape[0]):
            own = (2 * b) ^ device
            keep[b] = held[pl.ds(pl.multiple_of(own * part, part), part), :]
            own = own ^ 1
            send[b] = held[pl.ds(pl.multiple_of(own * part, part), part), :]

    return compute


def plan_last(arrays, gain, ggain_mlp, blocks):
    vmem = pl.BlockSpec(memory_space=pltpu.VMEM)
    tokens = arrays[0].shape[0]
    small = pltpu.VMEM((blocks // 2, WIDTH // blocks, LANES), F32)
    scratch = [small, small, pltpu.VMEM((WIDTH, LANES), F32)]
    scratch += [pltpu.VMEM(array.shape, array.dtype) for array in arrays]
    scratch.append(pltpu.SemaphoreType.DMA((len(arrays),)))
    return (
        (gain[None], ggain_mlp) + arrays,
        [vmem] * 2 + [hbm] * len(arrays),
        [jax.ShapeDtypeStruct((tokens, WIDTH), F32)],
        scratch,
        last_work,
    )


def stack_swap(values, bit):
    return jnp.concatenate([values, swap_bit(values, bit)], axis=0)


MESH = pl.DeviceIdType.MESH


def peer_of(bit):
    axis, mask = bit
    return {axis: lax.axis_index(axis) ^ mask}


def greet(ids):
    barrier = pltpu.get_barrier_semaphore()
    for device in ids:
        pl.semaphore_signal(barrier, inc=1, device_id=device, device_id_type=MESH)
    pl.semaphore_wait(barrier, len(ids))


GATHER_BITS = (X_BIT, ZL_BIT, C_BIT)


def one_hot(slots, rows):
    experts, tokens = slots.shape
    wide = jnp.broadcast_to(slots[:, None, :], (experts, SLOTS, tokens))
    rank = lax.broadcasted_iota(jnp.int32, (experts, SLOTS, tokens), 1).astype(F32)
    return (wide == rank).astype(F32).reshape(rows, tokens)


def gather_kernel(x_ref, *refs):
    blocks, maps_ref, wr_ref = refs[0:4], refs[4], refs[5]
    x_slots, g_slots, gates_ref, local_ref = refs[6:10]
    all_ref, other, all_maps_ref, stage = refs[10:14]
    send_sem, recv_sem, more_send, more_recv, store_sem = refs[14:]
    greet([peer_of(bit) for bit in GATHER_BITS])
    half = x_ref.shape[0] // 2
    copies = []

    def send(source, slot, rows, bit):
        n = len(copies)
        copy = pltpu.make_async_remote_copy(
            src_ref=source if rows is None else source.at[rows],
            dst_ref=all_ref.at[slot] if rows is None else all_ref.at[slot, rows],
            send_sem=send_sem.at[n],
            recv_sem=recv_sem.at[n],
            device_id=peer_of(bit),
            device_id_type=MESH,
        )
        copy.start()
        copies.append(copy)
        return copy

    top, low = pl.ds(0, half), pl.ds(half, half)
    x_top = send(x_ref, 1, top, X_BIT)
    z_low = send(x_ref, 2, low, ZL_BIT)
    x_low = send(x_ref, 1, low, X_BIT)
    z_top = send(x_ref, 2, top, ZL_BIT)
    pairs = [(maps_ref, all_maps_ref.at[pl.ds(4, 4)])]
    pairs += [(block, other.at[n]) for n, block in enumerate(blocks)]
    crossed = []
    for n, (block, there) in enumerate(pairs):
        copy = pltpu.make_async_remote_copy(
            src_ref=block,
            dst_ref=there,
            send_sem=more_send.at[n],
            recv_sem=more_recv.at[n],
            device_id=peer_of(C_BIT),
            device_id_type=MESH,
        )
        copy.start()
        crossed.append(copy)
    cross_own = send(x_ref, 4, None, C_BIT)
    all_maps_ref[0:4] = maps_ref[...]
    column = lax.axis_index("expert")
    experts = x_slots.shape[0]
    rows = experts * SLOTS
    depth = stage.shape[0]
    stores = []

    def own_rows(table):
        picked = jnp.zeros((experts, table.shape[1]), F32)
        for n in range(table.shape[0] // experts):
            picked = jnp.where(column == n, table[n * experts : (n + 1) * experts], picked)
        return picked

    def put(source, values, target, pick):
        side = len(stores) % depth
        if len(stores) >= depth:
            stores[-depth].wait()
        for n in range(WIDTH // CHUNK):
            cols = slice(n * CHUNK, (n + 1) * CHUNK)
            got = dot_nn(pick, values[:, cols]).astype(BF)
            stage[side, :, :, cols] = got.reshape(experts, SLOTS, CHUNK)
        store = pltpu.make_async_copy(
            stage.at[side], target.at[:, pl.ds(source * SLOTS, SLOTS)], store_sem.at[side]
        )
        store.start()
        stores.append(store)

    def put_g(source, values):
        pick = one_hot(own_rows(all_maps_ref[source]), rows)
        put(source, values, g_slots, pick.astype(BF))

    def put_x(source, values):
        slot_map = all_maps_ref[source]
        chosen = slot_map >= 0.0
        logits = dot_nt(wr_ref[...], values[...])[0 : slot_map.shape[0]]
        logits = jnp.where(chosen, logits, MASKED)
        raised = jnp.exp(logits - jnp.max(logits, axis=0, keepdims=True))
        raised = jnp.where(chosen, raised, 0.0)
        gates = own_rows(raised / jnp.sum(raised, axis=0, keepdims=True))
        slots = own_rows(slot_map)
        local_ref[source] = slots
        pick = one_hot(slots, rows)
        wide = jnp.broadcast_to(gates[:, None, :], (experts, SLOTS, gates.shape[1]))
        of_rows = jnp.sum(pick * wide.reshape(rows, gates.shape[1]), axis=1, keepdims=True)
        gates_ref[:, source * SLOTS : (source + 1) * SLOTS, :] = of_rows.reshape(experts, SLOTS, 1)
        put(source, values, x_slots, pick.astype(BF))

    put_x(0, x_ref)
    put_g(0, blocks[0])
    put_g(1, blocks[1])
    x_top.wait_recv()
    far_top = send(all_ref.at[1], 3, top, ZL_BIT)
    z_low.wait_recv()
    far_low = send(all_ref.at[2], 3, low, X_BIT)
    put_g(2, blocks[2])
    put_g(3, blocks[3])
    for copy in crossed:
        copy.wait_recv()
    cross_own.wait_recv()
    put_x(4, all_ref.at[4])
    put_g(4, other.at[0])
    x_low.wait_recv()
    cross_x = send(all_ref.at[1], 5, None, C_BIT)
    z_top.wait_recv()
    cross_z = send(all_ref.at[2], 6, None, C_BIT)
    put_x(1, all_ref.at[1])
    put_x(2, all_ref.at[2])
    put_g(5, other.at[1])
    cross_x.wait_recv()
    cross_z.wait_recv()
    put_x(5, all_ref.at[5])
    far_top.wait_recv()
    far_low.wait_recv()
    cross_far = send(all_ref.at[3], 7, None, C_BIT)
    put_x(6, all_ref.at[6])
    put_g(6, other.at[2])
    put_g(7, other.at[3])
    put_x(3, all_ref.at[3])
    cross_far.wait_recv()
    put_x(7, all_ref.at[7])
    for store in stores[-depth:]:
        store.wait()
    for copy in copies + crossed:
        copy.wait_send()


def run_gather(values, blocks, maps, wr_t, experts):
    vmem = pl.BlockSpec(memory_space=pltpu.VMEM)
    tokens, width = values.shape
    slots = jax.ShapeDtypeStruct((experts, 8 * SLOTS, width), values.dtype)
    return pl.pallas_call(
        gather_kernel,
        in_specs=[vmem] * 7,
        out_specs=(hbm, hbm, vmem, vmem),
        out_shape=(
            slots,
            slots,
            jax.ShapeDtypeStruct((experts, 8 * SLOTS, 1), F32),
            jax.ShapeDtypeStruct((8, experts, tokens), F32),
        ),
        scratch_shapes=[
            pltpu.VMEM((8, tokens, width), values.dtype),
            pltpu.VMEM((4, tokens, width), values.dtype),
            pltpu.VMEM((8,) + maps.shape[1:], maps.dtype),
            pltpu.VMEM((4, experts, SLOTS, width), values.dtype),
        ]
        + [pltpu.SemaphoreType.DMA((n,)) for n in (10, 10, 5, 5, 4)],
        compiler_params=pltpu.CompilerParams(
            collective_id=1, has_side_effects=True, vmem_limit_bytes=60 * MIB
        ),
        cost_estimate=cost(0, 150e6),
    )(values, *blocks, maps, wr_t)


def trade_peers(size):
    me = lax.axis_index("dp")
    return [{"dp": me ^ k} for k in range(size - 1, 0, -1)]


def trade_start(a_ref, out_ref, send_sem, recv_sem, local_sem):
    me = lax.axis_index("dp")
    copies = []
    for n, device in enumerate(trade_peers(a_ref.shape[0])):
        copy = pltpu.make_async_remote_copy(
            src_ref=a_ref.at[device["dp"]],
            dst_ref=out_ref.at[me],
            send_sem=send_sem.at[n],
            recv_sem=recv_sem.at[n],
            device_id=device,
            device_id_type=MESH,
        )
        copy.start()
        copies.append(copy)
    own = pltpu.make_async_copy(a_ref.at[me], out_ref.at[me], local_sem)
    own.start()
    return copies, own


def trade_end(copies, own):
    own.wait()
    for copy in copies:
        copy.wait_recv()
    for copy in copies:
        copy.wait_send()


class Rider:
    def __init__(self, bit, *terms, pieces=1, turns=(0,)):
        self.bit, self.pieces, self.turns = bit, pieces, turns
        self.arrays = [term[0] if isinstance(term, tuple) else term for term in terms]
        self.parts = [term[1] if isinstance(term, tuple) else None for term in terms]
        array, part = self.arrays[0], self.parts[0]
        shape = array.shape
        if part is not None:
            kept = [len(range(n)[k]) for k, n in zip(part, shape) if not isinstance(k, int)]
            shape = tuple(kept) + shape[len(part) :]
        self.shape = jax.ShapeDtypeStruct(shape, array.dtype)
        self.direct = len(terms) == 1 and part is None

    def scratch(self):
        if self.direct:
            return []
        buffer = pltpu.VMEM(self.shape.shape, self.shape.dtype)
        return [buffer] * (len(self.arrays) + 1)

    def plan(self):
        return (self.bit, self.pieces, self.turns, tuple(self.parts), self.direct)


def rider_inputs(riders):
    return [array for rider in riders for array in rider.arrays]


def rider_shapes(riders):
    return tuple(rider.shape for rider in riders)


def rider_scratch(riders):
    remote = max(sum(rider.pieces for rider in riders), 1)
    local = max(sum(len(rider.arrays) for rider in riders), 1)
    buffers = [buffer for rider in riders for buffer in rider.scratch()]
    return buffers + [pltpu.SemaphoreType.DMA((n,)) for n in (remote, remote, local)]


def add_rows(result, buffers):
    step = 16

    @pl.loop(0, result.shape[1] // step)
    def _(r):
        rows = pl.ds(pl.multiple_of(r * step, step), step)
        for i in range(result.shape[0]):
            total = buffers[0][i, rows, :].astype(F32)
            for buffer in buffers[1:]:
                total += buffer[i, rows, :].astype(F32)
            result[i, rows, :] = total.astype(result.dtype)


def ride_pieces(sources, targets, plans, scratch):
    send_sem, recv_sem, local_sem = scratch[-3:]
    starts, finishes, loads, used, source, local = [], [], [], 0, 0, 0
    for n, (bit, pieces, turns, parts, direct) in enumerate(plans):
        arrays = sources[source : source + len(parts)]
        source += len(parts)
        if direct:
            held = arrays[0]
            prepare = None
        else:
            buffers = scratch[used : used + len(parts)]
            held = scratch[used + len(parts)]
            used += len(parts) + 1
            copies = []
            for array, part, buffer in zip(arrays, parts, buffers):
                view = array if part is None else array.at[part]
                copy = pltpu.make_async_copy(view, buffer, local_sem.at[local])
                local += 1
                loads.append(copy)
                copies.append(copy)

            def prepare(copies=copies, held=held, buffers=buffers):
                for copy in copies:
                    copy.wait()
                add_rows(held, buffers)

        size = targets[n].shape[0] // pieces
        for m in range(pieces):
            at = pl.ds(m * size, size)

            def remote(n=n, at=at, slot=len(starts), bit=bit, held=held):
                return pltpu.make_async_remote_copy(
                    src_ref=held.at[at],
                    dst_ref=targets[n].at[at],
                    send_sem=send_sem.at[slot],
                    recv_sem=recv_sem.at[slot],
                    device_id=peer_of(bit),
                    device_id_type=MESH,
                )

            def start(remote=remote):
                remote().start()

            def finish(remote=remote):
                remote().wait()

            starts.append((prepare if m == 0 else None, start, turns))
            finishes.append(finish)
    return starts, finishes, loads


def all_peers(bits):
    size = lax.axis_size("dp")
    return trade_peers(size) + [peer_of(bit) for bit in bits if bit[0] == "expert"]


def trade_kernel(*refs, plans, work):
    inputs = sum(len(plan[3]) for plan in plans)
    more = 2 if work else 0
    a_ref, sources = refs[0], refs[1 : 1 + inputs]
    work_in, refs = refs[1 + inputs : 1 + inputs + more], refs[1 + inputs + more :]
    out_ref, targets = refs[0], refs[1 : 1 + len(plans)]
    work_out, refs = refs[1 + len(plans) : 1 + len(plans) + more], refs[1 + len(plans) + more :]
    send_sem, recv_sem, local_sem, *scratch = refs
    work_scratch = scratch[-6:] if work else ()
    scratch = scratch[:-6] if work else scratch
    bits = {plan[0] for plan in plans} | ({C_BIT} if work else set())
    greet(all_peers(sorted(bits)))
    trade = trade_start(a_ref, out_ref, send_sem, recv_sem, local_sem.at[0])
    starts, finishes, loads = ride_pieces(sources, targets, plans, scratch)
    for load in loads:
        load.start()
    if work:
        finishes.append(weight_grad(work_in, work_out, work_scratch))
    for prepare, start, _ in starts:
        if prepare is not None:
            prepare()
        start()
    if work:
        finishes[-1] = finishes[-1]()
    trade_end(*trade)
    for finish in finishes:
        finish()


def weight_grad(inputs, outputs, scratch):
    keep, got = outputs
    left, right, sent, held, load_sem, cross_sem = scratch
    loads = [
        pltpu.make_async_copy(source, target, load_sem.at[n])
        for n, (source, target) in enumerate(zip(inputs, (left, right)))
    ]
    for load in loads:
        load.start()
    blocks, part, width = keep.shape
    step = held.shape[1]
    device = lax.axis_index("dp") * lax.axis_size("expert") + lax.axis_index("expert")

    def compute():
        for load in loads:
            load.wait()

        @pl.loop(0, width // step)
        def _(n):
            cols = pl.ds(pl.multiple_of(n * step, step), step)
            held[...] = dot_tn(left[...], right[:, cols]).astype(BF)
            for b in range(blocks):
                own = (2 * b) ^ device
                keep[b, :, cols] = held[pl.ds(pl.multiple_of(own * part, part), part), :]
                own = own ^ 1
                sent[b, :, cols] = held[pl.ds(pl.multiple_of(own * part, part), part), :]

        copy = pltpu.make_async_remote_copy(
            src_ref=sent,
            dst_ref=got,
            send_sem=cross_sem.at[0],
            recv_sem=cross_sem.at[1],
            device_id=peer_of(C_BIT),
            device_id_type=MESH,
        )
        copy.start()
        return copy.wait

    return compute


def run_trade(values, number, riders=(), work=(), blocks=0):
    size = values.shape[0]
    inputs = rider_inputs(riders)
    vmem = pl.BlockSpec(memory_space=pltpu.VMEM)
    shapes, specs, scratch = [], [], []
    if work:
        left, right = work
        rows, width = left.shape[1], right.shape[1]
        half = jax.ShapeDtypeStruct((blocks // 2, rows // blocks, width), BF)
        shapes, specs = [half, half], [vmem, hbm]
        scratch = [
            pltpu.VMEM(left.shape, left.dtype),
            pltpu.VMEM(right.shape, right.dtype),
            pltpu.VMEM(half.shape, BF),
            pltpu.VMEM((rows, 256), BF),
            pltpu.SemaphoreType.DMA((2,)),
            pltpu.SemaphoreType.DMA((2,)),
        ]
    out = pl.pallas_call(
        functools.partial(
            trade_kernel, plans=tuple(rider.plan() for rider in riders), work=bool(work)
        ),
        in_specs=[hbm] * (1 + len(inputs) + len(work)),
        out_specs=(hbm,) * (1 + len(riders)) + tuple(specs),
        out_shape=(jax.ShapeDtypeStruct(values.shape, values.dtype),)
        + rider_shapes(riders)
        + tuple(shapes),
        scratch_shapes=[pltpu.SemaphoreType.DMA((n,)) for n in (size - 1, size - 1, 1)]
        + rider_scratch(riders)
        + scratch,
        compiler_params=pltpu.CompilerParams(
            collective_id=number, has_side_effects=True, vmem_limit_bytes=60 * MIB
        ),
        cost_estimate=cost(0, 170e6),
    )(values, *inputs, *work)
    return out if riders or work else out[0]


def first_kernel(a_ref, rank_ref, turned_ref, out_ref, slot_ref, send_sem, recv_sem, local_sem, *, far):
    greet(trade_peers(a_ref.shape[0]))
    trade = trade_start(a_ref, out_ref, send_sem, recv_sem, local_sem.at[0])
    for e in range(rank_ref.shape[0]):
        own = rank_ref[e : e + 1, :]
        smaller = (turned_ref[:, e : e + 1] < own).astype(F32)
        before = jnp.sum(smaller, axis=0, keepdims=True)
        slot_ref[e : e + 1, :] = jnp.where(own < far, jnp.minimum(before, SLOTS), -1.0)
    trade_end(*trade)


def run_first(values, rank_map, turned, far):
    size = values.shape[0]
    vmem = pl.BlockSpec(memory_space=pltpu.VMEM)
    return pl.pallas_call(
        functools.partial(first_kernel, far=far),
        in_specs=[hbm, vmem, vmem],
        out_specs=(hbm, vmem),
        out_shape=(
            jax.ShapeDtypeStruct(values.shape, values.dtype),
            jax.ShapeDtypeStruct(rank_map.shape, F32),
        ),
        scratch_shapes=[pltpu.SemaphoreType.DMA((n,)) for n in (size - 1, size - 1, 1)],
        compiler_params=pltpu.CompilerParams(
            collective_id=2, has_side_effects=True, vmem_limit_bytes=60 * MIB
        ),
        cost_estimate=cost(0, 170e6),
    )(values, rank_map, turned)


def reduce_chain(slot, part, keep_ref, send_ref, outs, acc, got, staged, send_sem, recv_sem):
    first, bits, row, rows, column, columns, order = part
    blocks = keep_ref.shape[0]
    stages = len(bits) + 1
    low = send_ref.dtype
    at = (pl.ds(row, rows), pl.ds(column, columns))
    copies = []

    def exchange(source, target, bit):
        n = slot + len(copies)
        copy = pltpu.make_async_remote_copy(
            src_ref=source,
            dst_ref=target,
            send_sem=send_sem.at[n],
            recv_sem=recv_sem.at[n],
            device_id=peer_of(bit),
            device_id_type=MESH,
        )
        copy.start()
        copies.append(copy)

    live = list(range(blocks))
    base_got, base_sent = 0, 0
    exchange(send_ref.at[(slice(None),) + at], got.at[(pl.ds(0, blocks),) + at], first)
    yield
    for stage in range(stages):
        copies[-1].wait_recv()

        def total(position):
            index = live[position]
            kept = keep_ref[(index,) + at].astype(F32) if stage == 0 else acc[(index,) + at]
            return kept + got[(base_got + position,) + at].astype(F32)

        if stage == stages - 1:
            low_column = 0
            for out_ref in outs:
                if low_column <= column < low_column + out_ref.shape[1]:
                    out_ref[at[0], pl.ds(column - low_column, columns)] = total(0)
                low_column += out_ref.shape[1]
            break
        mask = 1 << order[stage]
        rest = [i for i in live if not i & mask]
        for m, i in enumerate(rest):
            staged[(base_sent + m,) + at] = total(live.index(i ^ mask)).astype(low)
        exchange(
            staged.at[(pl.ds(base_sent, len(rest)),) + at],
            got.at[(pl.ds(base_got + len(live), len(rest)),) + at],
            bits[order[stage]],
        )
        for i in rest:
            acc[(i,) + at] = total(live.index(i))
        base_got += len(live)
        base_sent += len(rest)
        live = rest
        yield
    for copy in copies:
        copy.wait_send()


def reduce_kernel(*refs, jobs, plans, work):
    size = len(jobs)
    given = size - 1 if work else size
    inputs = sum(len(plan[3]) for plan in plans)
    keeps, sends, refs = list(refs[:given]), list(refs[given : 2 * given]), refs[2 * given :]
    sources, refs = refs[:inputs], refs[inputs:]
    compute = None
    if work:
        counts, body = work
        work_in, refs = refs[: counts[0]], refs[counts[0] :]
        work_out, refs = refs[: counts[1]], refs[counts[1] :]
        work_scratch, refs = refs[-counts[2] :], refs[: -counts[2]]
        compute = body(work_in, work_out, work_scratch)
        keeps.append(work_scratch[0])
        sends.append(work_scratch[1])
    outs = []
    for _, _, _, widths in jobs:
        outs.append(refs[: len(widths)])
        refs = refs[len(widths) :]
    targets, scratch = refs[: len(plans)], refs[len(plans) :]
    send_sem, recv_sem = scratch[3 * size : 3 * size + 2]
    used = {bit for first, bits, *_ in jobs for bit in (first,) + bits}
    used |= {plan[0] for plan in plans}
    starts, finishes, loads = ride_pieces(sources, targets, plans, scratch[3 * size + 2 :])
    for load in loads:
        load.start()
    greet([peer_of(bit) for bit in sorted(used)])
    chains, late, slot = [], [], 0
    for n, (first, bits, parts, _) in enumerate(jobs):
        for part in parts:
            (late if n >= given else chains).append(
                reduce_chain(
                    slot,
                    (first, bits) + part,
                    keeps[n],
                    sends[n],
                    outs[n],
                    *scratch[3 * n : 3 * n + 3],
                    send_sem,
                    recv_sem,
                )
            )
            slot += len(bits) + 1
    index = lax.axis_index("dp")
    outer = (index // BIT_ZH) % 2 == (index // BIT_ZL) % 2
    turn, last = 0, max([0] + [n for _, _, turns in starts for n in turns])
    while chains or turn <= last:
        rest = []
        for chain in chains:
            try:
                next(chain)
                rest.append(chain)
            except StopIteration:
                pass
        chains = rest
        for prepare, start, turns in starts:
            if prepare is not None and min(turns) == turn:
                prepare()
            if len(set(turns)) == 1:
                if turns[0] == turn:
                    start()
            else:
                for n, side in enumerate((outer, jnp.logical_not(outer))):
                    if turns[n] == turn:
                        pl.when(side)(start)
        if turn == 0 and work:
            compute()
            chains += late
        turn += 1
    for finish in finishes:
        finish()


def run_reduce(pairs, jobs, number, riders=(), work=None):
    slots = sum(len(parts) * (len(bits) + 1) for _, bits, parts, _ in jobs)
    vmem = pl.BlockSpec(memory_space=pltpu.VMEM)
    scratch, shapes = [], []
    arrays, work_specs, work_shapes, work_scratch, body = work or ((), (), (), (), None)
    late = [(shape, shape) for shape in work_scratch[:1]]
    for (keep, send), (_, _, _, widths) in zip(list(pairs) + late, jobs):
        blocks, rows, cols = keep.shape
        scratch += [
            pltpu.VMEM((blocks, rows, cols), F32),
            pltpu.VMEM((2 * blocks - 1, rows, cols), send.dtype),
            pltpu.VMEM((max(blocks - 1, 1), rows, cols), send.dtype),
        ]
        shapes += [jax.ShapeDtypeStruct((rows, width), F32) for width in widths]
    inputs = rider_inputs(riders)
    return pl.pallas_call(
        functools.partial(
            reduce_kernel,
            jobs=jobs,
            plans=tuple(rider.plan() for rider in riders),
            work=((len(arrays), len(work_shapes), len(work_scratch)), body) if work else None,
        ),
        in_specs=[vmem] * len(pairs) + [hbm] * (len(pairs) + len(inputs)) + list(work_specs),
        out_specs=(vmem,) * (len(work_shapes) + len(shapes)) + (hbm,) * len(riders),
        out_shape=tuple(work_shapes) + tuple(shapes) + rider_shapes(riders),
        scratch_shapes=scratch
        + [pltpu.SemaphoreType.DMA((n,)) for n in (slots, slots)]
        + rider_scratch(riders)
        + list(work_scratch),
        compiler_params=pltpu.CompilerParams(
            collective_id=number, has_side_effects=True, vmem_limit_bytes=60 * MIB
        ),
        cost_estimate=cost(0, 170e6),
    )(*(keep for keep, _ in pairs), *(send for _, send in pairs), *inputs, *arrays)


def sum_pair(kept, received):
    return kept.astype(F32) + received.astype(F32)


def add_low(*terms):
    return sum(term.astype(F32) for term in terms).astype(BF)


def join_kernel(place_ref, *refs):
    outs = refs[-3:]
    zl_at = place_ref[0]

    def total(*terms):
        return sum(term.astype(F32) for term in terms)

    def flat(ref):
        return ref[(0,) * (ref.ndim - 2)]

    def work(parts, part):
        for n in range(2):
            keep, got, more, other = parts[4 * n : 4 * n + 4]
            mine = total(*(flat(term) for term in (keep, got, more)))
            across = flat(other).astype(F32)
            for m in range(2):
                cols = slice(m * LANES, (m + 1) * LANES)
                at = pl.multiple_of((2 * m + zl_at) * LANES, LANES)
                outs[n][part, 0, :, pl.ds(at, LANES)] = mine[:, cols]
                at = pl.multiple_of((2 * m + 1 - zl_at) * LANES, LANES)
                outs[n][part, 0, :, pl.ds(at, LANES)] = across[:, cols]
        keep, got, more = parts[8:]
        outs[2][part, 0] = total(*(flat(term) for term in (keep, got, more)))

    work(refs[0:11], 0)
    work(refs[11:22], 1)


def run_join(place, halves):
    _, _, experts, rows, cols = halves[0][0].shape
    wide_rows, width = halves[0][8].shape[2:]
    arrays, specs = [], []
    for half in halves:
        for operand in half:
            array, lead = operand if isinstance(operand, tuple) else (operand, 0)
            extra = array.ndim - 3
            at = (lead,) + (0,) * (extra - 1) if extra else ()
            arrays.append(array)
            specs.append(
                pl.BlockSpec(
                    (1,) * (extra + 1) + array.shape[-2:],
                    lambda i, p, at=at: at + (i, 0, 0),
                )
            )
    shapes = [(rows, 2 * cols), (rows, 2 * cols), (wide_rows, width)]
    return pl.pallas_call(
        join_kernel,
        grid_spec=pltpu.PrefetchScalarGridSpec(
            num_scalar_prefetch=1,
            grid=(experts,),
            in_specs=specs,
            out_specs=tuple(
                pl.BlockSpec((2, 1) + shape, lambda i, p: (0, i, 0, 0)) for shape in shapes
            ),
        ),
        out_shape=tuple(jax.ShapeDtypeStruct((2, experts) + shape, F32) for shape in shapes),
        compiler_params=params(60, ("arbitrary",)),
        cost_estimate=cost(1e6, 26e6),
    )(place, *arrays)


def fast_body(
    hidden_in,
    gain_attn,
    w_query,
    w_key,
    w_value,
    w_output,
    gain_mlp,
    w_router,
    w_gate,
    w_up,
    w_down,
    expert_ids,
    slot_order,
    grad_out,
):
    inputs = hidden_in[0]
    cotangent = grad_out[0]
    chosen = expert_ids[0]
    tokens = inputs.shape[0]
    top = chosen.shape[1]
    local_experts = w_gate.shape[0]
    peers = lax.axis_size("expert")
    all_experts = local_experts * peers
    shards = lax.axis_size("dp")
    length = shards * tokens
    devices = shards * peers
    index = lax.axis_index("dp")
    column = lax.axis_index("expert")
    y_at = index % 2
    zl_at = (index // 2) % 2
    zh_at = index // 4
    place = jnp.stack(
        [zl_at, y_at, zl_at, zh_at, column * local_experts, index * peers + column]
    ).astype(jnp.int32)

    ranks = slot_order[0, 0].reshape(tokens, top)
    far = tokens * top
    names = jnp.arange(all_experts, dtype=jnp.int32)
    match = chosen.T[None] == names[:, None, None]
    rank_map = jnp.min(jnp.where(match, ranks.T[None], far), axis=1).astype(F32)
    turned = rank_map.T
    map_rows = jnp.pad(
        jnp.where(turned < far, 0.0, -1.0),
        ((0, 0), (0, LANES - all_experts)),
        constant_values=-1.0,
    )
    wr_pad = jnp.pad(w_router, ((0, 0), (0, LANES - all_experts)))
    wr_t = jnp.pad(w_router.T, ((0, LANES - all_experts), (0, 0)))

    half = HEAD_DIM // 2
    frequency = jnp.exp(-math.log(10000.0) * jnp.arange(half, dtype=F32) * 2.0 / HEAD_DIM)
    own_angles = (index * tokens + jnp.arange(tokens, dtype=jnp.int32)).astype(F32)[:, None] * frequency
    cos_own, sin_own = jnp.cos(own_angles), jnp.sin(own_angles)
    cos_tab = jnp.concatenate([cos_own] * 4, axis=1)
    sin_tab = jnp.concatenate([-sin_own, sin_own] * 2, axis=1)
    angles = frequency[:, None] * jnp.arange(length, dtype=jnp.int32).astype(F32)[None]
    cos_t, sin_t = jnp.cos(angles), jnp.sin(angles)

    normed, pack, g_own = run_pre(
        inputs, gain_attn, w_query, w_key, w_value, cos_tab, sin_tab, cotangent
    )
    pack, slot_map = run_first(pack, rank_map, turned, float(far))
    pack, slot_map, g_late = fence(pack, slot_map, g_own)
    g_x = swap_bit(g_own, X_BIT)
    g_z = swap_bit(g_late, ZL_BIT)
    maps = stack_swap(slot_map[None], X_BIT)
    out, out_t, lse = run_forward(pack)
    out, g_x, g_z, maps = fence(out, g_x, g_z, maps)
    g_zx = swap_bit(g_z, X_BIT)
    maps = stack_swap(maps, ZL_BIT)
    att = run_trade(out, 3)
    att, g_zx, maps = fence(att, g_zx, maps)
    middle, normed_two, att_full = run_mid(att, w_output, inputs, gain_mlp)
    x_slots, g_slots, gates, maps = run_gather(
        normed_two, (g_own, g_x, g_z, g_zx), maps, wr_t, local_experts
    )
    expert_args = (place, x_slots, g_slots, gates, maps, w_gate, w_up, w_down)
    first = run_experts(*expert_args)
    gate_ka, gate_s0, gate_s1, early, up_ka, up_s0, up_s1, down_ka, down_s0, down_s1 = first[4:]
    down_ya = swap_bit(down_s1, Y_BIT)
    gate_ya = swap_bit(gate_s1, Y_BIT)
    early = swap_bit(early, ZH_BIT)
    mix_keep, mix_send, dx_keep, dx_send, *second = run_experts(*expert_args, prior=first[:4])
    gate_kb, gate_t0, gate_t1, _, up_kb, up_t0, up_t1, down_kb, down_t0, down_t1 = second
    down_ga = swap_bit(down_s0, Y_BIT)
    dx_send, down_ya, gate_ya, early = fence(dx_send, down_ya, gate_ya, early)
    gate_s0 = jnp.stack([gate_s0[0], add_low(gate_s0[1], early[1])])
    quarter = tokens // 4
    extra = dx_keep.shape[2]
    token_parts = tuple(
        (n * quarter, quarter, 0, extra, (1, 0) if n < 2 else (0, 1)) for n in (2, 0, 3, 1)
    )
    dx_sum, up_ya, gate_ga, mix_got, down_ma = run_reduce(
        ((dx_keep, dx_send),),
        ((C_BIT, (X_BIT, ZL_BIT), token_parts, (extra,)),),
        6,
        riders=(
            Rider(Y_BIT, up_s1),
            Rider(Y_BIT, gate_s0),
            Rider(C_BIT, mix_send, turns=(1,)),
            Rider(ZH_BIT, (down_ka, (1,)), down_ya, turns=(1, 0)),
        ),
    )
    dx_sum, gate_ya, down_ga, gate_t1 = fence(dx_sum, gate_ya, down_ga, gate_t1)
    gate_ma = swap_bit(add_low(gate_ka[1, 0], gate_ya[0]), ZH_BIT)
    gate_yb = swap_bit(gate_t1, Y_BIT)
    d_att, d_middle, d_low, d_log, ggain_mlp = run_post(
        dx_sum, middle, cotangent, normed_two, wr_pad, map_rows, gain_mlp, w_output
    )
    mix_keep = mix_keep.reshape(2, 2, tokens, WIDTH)
    mix_got = mix_got.reshape(2, 2, tokens, WIDTH)
    every = slice(None)
    d_out, up_yb, up_za, gate_oa, mix_x, out_keep, out_got = run_trade(
        d_att,
        4,
        work=(att_full, d_low),
        blocks=devices,
        riders=(
            Rider(Y_BIT, up_t1),
            Rider(ZH_BIT, (up_ka, (1, 1)), (up_ya, (1,))),
            Rider(ZL_BIT, (gate_ka, (0, 1)), (early, (0,)), (gate_ga, (1,))),
            Rider(X_BIT, (mix_keep, (every, 1)), (mix_got, (every, 1))),
        ),
    )
    split = (8, 2, WIDTH // devices, WIDTH)
    out_keep, out_got = out_keep.reshape(split), out_got.reshape(split)
    up_ga, down_yb, up_late, gate_late, gate_ma, d_out = fence(
        up_s0, down_t1, up_ya, gate_yb, gate_ma, d_out
    )
    both = jnp.stack([add_low(up_ka[1, 0], up_late[0]), add_low(gate_kb[1, 1], gate_late[1])])
    both = swap_bit(both, ZH_BIT)
    up_ga = swap_bit(up_ga, Y_BIT)
    down_yb = swap_bit(down_yb, Y_BIT)
    d_pack = run_backward(pack, d_out, out_t, lse, cos_t, sin_t)
    d_pack, both, up_ga, down_yb = fence(d_pack, both, up_ga, down_yb)
    d_pack, gate_gb, up_gb, gate_mb, up_zb, mix_z, out_x, up_oa = run_trade(
        d_pack,
        5,
        riders=(
            Rider(Y_BIT, gate_t0),
            Rider(Y_BIT, up_t0),
            Rider(ZH_BIT, (gate_kb, (1, 0)), (gate_yb, (0,))),
            Rider(ZH_BIT, (up_kb, (1, 1)), (up_yb, (1,))),
            Rider(
                ZL_BIT,
                (mix_keep, (slice(1, 2), 0)),
                (mix_got, (slice(1, 2), 0)),
                (mix_x, (slice(1, 2),)),
            ),
            Rider(X_BIT, (out_keep, (every, 1)), (out_got, (every, 1))),
            Rider(ZL_BIT, (up_ka, (0, 1)), (up_ga, (1,)), (up_za, (every,))),
        ),
    )
    d_pack, up_yb, down_yb, gate_gb, down_t0, mix_z, out_x = fence(
        d_pack, up_yb, down_yb, gate_gb, down_t0, mix_z, out_x
    )
    other = jnp.stack(
        [add_low(gate_kb[0, 1], gate_gb[1], both[1]), add_low(up_kb[0, 1], up_gb[1], up_zb)]
    )
    other = swap_bit(other, ZL_BIT)
    down_mb = swap_bit(add_low(down_kb[1], down_yb), ZH_BIT)
    down_gb = swap_bit(down_t0, Y_BIT)
    d_full, qkv_keep, qkv_send = run_qkvgrad(place, normed, d_pack, devices)
    mixed = sum_pair(mix_keep[0, 0], mix_got[0, 0]) + sum_pair(mix_x[0], mix_z[0])
    hidden_out = middle + mixed
    rows = WIDTH // devices
    out_held = add_low(out_keep[:, 0], out_got[:, 0], out_x).reshape(4, 2, rows, WIDTH)
    out_first, out_second = out_held[:, 0], out_held[:, 1]
    qkv_send, out_second, hidden_out = fence(qkv_send, out_second, hidden_out)
    qkv_parts = (
        (0, rows, 0, 768, (0, 1, 2, 3)),
        (0, rows, 768, 768, (1, 0, 2, 3)),
        (0, rows, 1536, 512, (0, 1, 2, 3)),
        (0, rows, 2048, 512, (1, 0, 2, 3)),
    )
    dense_bits = (X_BIT, Y_BIT, ZL_BIT, ZH_BIT)
    last = (d_full, w_query, w_key, w_value, d_middle, inputs, normed_two, d_log)
    grad_in, query_total, key_total, value_total, output_total, small, up_mb = run_reduce(
        ((qkv_keep, qkv_send), (out_first, out_second)),
        (
            (C_BIT, dense_bits, qkv_parts, (WIDTH, KV_HEADS * HEAD_DIM, KV_HEADS * HEAD_DIM)),
            (Y_BIT, (ZL_BIT, ZH_BIT), ((0, rows, 0, WIDTH, (0, 1)),), (WIDTH,)),
            (C_BIT, dense_bits, ((0, rows, 0, LANES, (0, 1, 2, 3)),), (LANES,)),
        ),
        7,
        riders=(Rider(ZH_BIT, (up_kb, (1, 0)), (up_yb, (0,))),),
        work=plan_last(last, gain_attn, ggain_mlp, devices),
    )
    query_total, small, down_mb, down_gb, other = fence(
        query_total, small, down_mb, down_gb, other
    )
    joined = run_join(
        place,
        (
            (gate_ka, gate_ga, gate_ma, gate_oa, up_ka, up_ga, (both, 0), up_oa)
            + (down_ka, down_ga, down_ma),
            (gate_kb, gate_gb, gate_mb, (other, 0), up_kb, up_gb, up_mb, (other, 1))
            + (down_kb, down_gb, down_mb),
        ),
    )
    gate_total, up_total, down_total = [
        total.reshape((local_experts,) + total.shape[2:]) for total in joined
    ]
    return (
        hidden_out[None],
        grad_in[None],
        small[:, LANES - 1],
        query_total,
        key_total,
        value_total,
        output_total,
        small[:, LANES - 2],
        small[:, :all_experts],
        gate_total,
        up_total,
        down_total,
    )


def fits(mesh):
    return mesh.shape["dp"] == KV_HEADS and mesh.shape["expert"] == 4


def solution(mesh):
    in_specs = (
        P("expert", "dp", None),
        P(),
        P(),
        P(),
        P(),
        P(),
        P(),
        P(),
        P("expert", None, None),
        P("expert", None, None),
        P("expert", None, None),
        P("expert", "dp", None),
        P("expert", "dp", None),
        P("expert", "dp", None),
    )
    out_specs = (
        P("expert", "dp", None),
        P("expert", "dp", None),
        P(("dp", "expert")),
        P(("dp", "expert"), None),
        P(("dp", "expert"), None),
        P(("dp", "expert"), None),
        P(("dp", "expert"), None),
        P(("dp", "expert")),
        P(("dp", "expert"), None),
        P("expert", "dp", None),
        P("expert", "dp", None),
        P("expert", "dp", None),
    )
    chosen = fast_body if fits(mesh) else body
    return jax.shard_map(chosen, mesh=mesh, in_specs=in_specs, out_specs=out_specs, check_vma=False)
```

```python
import functools
import math

import jax
import jax.numpy as jnp
from jax import lax
from jax.experimental import pallas as pl
from jax.experimental.pallas import tpu as pltpu
from jax.sharding import PartitionSpec as P

HEADS = 24
KV_HEADS = 8
HEAD_DIM = 64


EPS = 1e-05
MASKED = -1e30


def rotary_tables(positions):
    half = HEAD_DIM // 2
    frequency = jnp.exp(-math.log(10000.0) * jnp.arange(half, dtype=jnp.float32) * 2.0 / HEAD_DIM)
    angles = positions.astype(jnp.float32)[:, None] * frequency[None, :]
    return (jnp.cos(angles)[:, None, :], jnp.sin(angles)[:, None, :])


def rotate(values, cosine, sine):
    half = values.shape[-1] // 2
    first = values[..., :half]
    second = values[..., half:]
    return jnp.concatenate(
        [first * cosine - second * sine, second * cosine + first * sine], axis=-1
    )


def rotate_back(values, cosine, sine):
    half = values.shape[-1] // 2
    first = values[..., :half]
    second = values[..., half:]
    return jnp.concatenate(
        [first * cosine + second * sine, second * cosine - first * sine], axis=-1
    )


def assign_slots(row_chosen, row_ranks, all_experts, capacity):
    pairs = row_chosen.shape[0]
    by_rank = jnp.zeros((pairs,), jnp.int32).at[row_ranks].set(jnp.arange(pairs, dtype=jnp.int32))
    ordered = row_chosen[by_rank]
    table = (ordered[:, None] == jnp.arange(all_experts, dtype=jnp.int32)[None, :]).astype(
        jnp.int32
    )
    before = jnp.sum(table * (jnp.cumsum(table, axis=0) - 1), axis=1)
    slot = before[row_ranks]
    target = jnp.where(slot < capacity, row_chosen * capacity + slot, all_experts * capacity)
    owner = (
        jnp.full((all_experts * capacity,), pairs, jnp.int32)
        .at[target]
        .set(jnp.arange(pairs, dtype=jnp.int32), mode="drop")
    )
    return (target, owner)


def body(
    hidden_in,
    gain_attn,
    w_query,
    w_key,
    w_value,
    w_output,
    gain_mlp,
    w_router,
    w_gate,
    w_up,
    w_down,
    expert_ids,
    slot_order,
    grad_out,
):
    inputs = hidden_in[0]
    cotangent = grad_out[0]
    chosen = expert_ids[0]
    tokens, width = inputs.shape
    top = chosen.shape[1]
    local_experts = w_gate.shape[0]
    peers = lax.axis_size("expert")
    all_experts = local_experts * peers
    pairs = tokens * top
    capacity = pairs // all_experts
    shards = lax.axis_size("dp")
    index = lax.axis_index("dp")
    length = shards * tokens
    block = math.gcd(length, 512)
    groups = HEADS // KV_HEADS
    scale = HEAD_DIM ** (-0.5)
    query_pos = index * tokens + jnp.arange(tokens, dtype=jnp.int32)
    cosine, sine = rotary_tables(query_pos)
    count = ((index + 1) * tokens + block - 1) // block
    inv_one = lax.rsqrt(jnp.mean(inputs * inputs, axis=-1, keepdims=True) + EPS)
    normed = (inputs * inv_one * gain_attn).astype(jnp.bfloat16)
    query_pre = jnp.dot(normed, w_query, preferred_element_type=jnp.float32).reshape(
        tokens, HEADS, HEAD_DIM
    )
    queries = rotate(query_pre, cosine, sine).astype(jnp.bfloat16)
    key_pre = jnp.dot(normed, w_key, preferred_element_type=jnp.float32).reshape(
        tokens, KV_HEADS, HEAD_DIM
    )
    keys_low = rotate(key_pre, cosine, sine).astype(jnp.bfloat16)
    values_low = (
        jnp.dot(normed, w_value, preferred_element_type=jnp.float32)
        .astype(jnp.bfloat16)
        .reshape(tokens, KV_HEADS, HEAD_DIM)
    )
    keys_all, values_all = (
        lax.all_gather(keys_low, "dp", axis=0, tiled=True),
        lax.all_gather(values_low, "dp", axis=0, tiled=True),
    )
    query_groups = queries.reshape(tokens, KV_HEADS, groups, HEAD_DIM)

    def block_scores(key_block, start):
        raw = (
            jnp.einsum(
                "qkgd,skd->kgqs", query_groups, key_block, preferred_element_type=jnp.float32
            )
            * scale
        )
        key_pos = start + jnp.arange(block, dtype=jnp.int32)
        allowed = key_pos[None, :] <= query_pos[:, None]
        return jnp.where(allowed, raw, MASKED)

    def stats_step(step, carry):
        running, total = carry
        scores = block_scores(
            lax.dynamic_slice_in_dim(keys_all, step * block, block, 0), step * block
        )
        newest = jnp.maximum(running, jnp.max(scores, axis=-1))
        total = total * jnp.exp(running - newest) + jnp.sum(
            jnp.exp(scores - newest[..., None]), axis=-1
        )
        return (newest, total)

    stat_init = (
        jnp.full((KV_HEADS, groups, tokens), MASKED, jnp.float32),
        jnp.zeros((KV_HEADS, groups, tokens), jnp.float32),
    )
    running, total = lax.fori_loop(0, count, stats_step, stat_init)
    log_total = running + jnp.log(total)

    def output_step(step, accum):
        start = step * block
        scores = block_scores(lax.dynamic_slice_in_dim(keys_all, start, block, 0), start)
        probs = jnp.exp(scores - log_total[..., None]).astype(jnp.bfloat16)
        value_block = lax.dynamic_slice_in_dim(values_all, start, block, 0)
        return accum + jnp.einsum(
            "kgqs,skd->qkgd", probs, value_block, preferred_element_type=jnp.float32
        )

    attended_groups = lax.fori_loop(
        0, count, output_step, jnp.zeros((tokens, KV_HEADS, groups, HEAD_DIM), jnp.float32)
    )
    attended = attended_groups.reshape(tokens, HEADS * HEAD_DIM)
    attended_low = attended.astype(jnp.bfloat16)
    branch = jnp.dot(attended_low, w_output, preferred_element_type=jnp.float32)
    middle = inputs + branch
    inv_two = lax.rsqrt(jnp.mean(middle * middle, axis=-1, keepdims=True) + EPS)
    normed_two = (middle * inv_two * gain_mlp).astype(jnp.bfloat16)
    logits = jnp.dot(normed_two, w_router, preferred_element_type=jnp.float32)
    onehot = (chosen[:, :, None] == jnp.arange(all_experts, dtype=jnp.int32)[None, None, :]).astype(
        jnp.float32
    )
    picked = jnp.sum(onehot * logits[:, None, :], axis=-1)
    gates = jax.nn.softmax(picked, axis=-1)
    target, owner = assign_slots(chosen.reshape(pairs), slot_order[0, 0], all_experts, capacity)
    valid = owner < pairs
    source = jnp.minimum(owner, pairs - 1)
    rows_send = jnp.where(valid[:, None], normed_two[source // top], 0).reshape(
        peers, local_experts, capacity, width
    )
    received = lax.all_to_all(rows_send, "expert", split_axis=0, concat_axis=0, tiled=True)
    gate_pre = jnp.einsum("necd,edf->necf", received, w_gate, preferred_element_type=jnp.float32)
    up_pre = jnp.einsum("necd,edf->necf", received, w_up, preferred_element_type=jnp.float32)
    hidden = (jax.nn.silu(gate_pre) * up_pre).astype(jnp.bfloat16)
    result = jnp.einsum(
        "necf,efd->necd", hidden, w_down, preferred_element_type=jnp.float32
    ).astype(jnp.bfloat16)
    returned = lax.all_to_all(result, "expert", split_axis=0, concat_axis=0, tiled=True)
    returned, received, gate_pre, up_pre = (returned, received, gate_pre, up_pre)
    zero_row = jnp.zeros((1, width), jnp.bfloat16)
    pair_out = jnp.concatenate([returned.reshape(all_experts * capacity, width), zero_row], axis=0)[
        target
    ].reshape(tokens, top, width)
    mixed = jnp.einsum("tk,tkd->td", gates, pair_out, preferred_element_type=jnp.float32)
    hidden_out = middle + mixed
    dy_pairs = (
        (gates[:, :, None] * cotangent[:, None, :]).astype(jnp.bfloat16).reshape(pairs, width)
    )
    dy_send = jnp.where(valid[:, None], dy_pairs[source], 0).reshape(
        peers, local_experts, capacity, width
    )
    dy_received = lax.all_to_all(dy_send, "expert", split_axis=0, concat_axis=0, tiled=True)
    sigmoid_gate = jax.nn.sigmoid(gate_pre)
    silu_gate = gate_pre * sigmoid_gate
    hidden = (silu_gate * up_pre).astype(jnp.bfloat16)
    grad_down_part = jnp.einsum(
        "necf,necd->efd", hidden, dy_received, preferred_element_type=jnp.float32
    )
    d_hidden = jnp.einsum("necd,efd->necf", dy_received, w_down, preferred_element_type=jnp.float32)
    d_gate = (d_hidden * up_pre * sigmoid_gate * (1.0 + gate_pre * (1.0 - sigmoid_gate))).astype(
        jnp.bfloat16
    )
    d_up = (d_hidden * silu_gate).astype(jnp.bfloat16)
    grad_gate_part = jnp.einsum(
        "necd,necf->edf", received, d_gate, preferred_element_type=jnp.float32
    )
    grad_up_part = jnp.einsum("necd,necf->edf", received, d_up, preferred_element_type=jnp.float32)
    gate_total, up_total, down_total = (
        lax.psum_scatter(
            grad_gate_part.astype(jnp.bfloat16), "dp", scatter_dimension=1, tiled=True
        ).astype(jnp.float32),
        lax.psum_scatter(
            grad_up_part.astype(jnp.bfloat16), "dp", scatter_dimension=1, tiled=True
        ).astype(jnp.float32),
        lax.psum_scatter(
            grad_down_part.astype(jnp.bfloat16), "dp", scatter_dimension=1, tiled=True
        ).astype(jnp.float32),
    )
    d_rows = jnp.einsum("necf,edf->necd", d_gate, w_gate, preferred_element_type=jnp.float32)
    d_rows = (
        d_rows + jnp.einsum("necf,edf->necd", d_up, w_up, preferred_element_type=jnp.float32)
    ).astype(jnp.bfloat16)
    d_back = lax.all_to_all(d_rows, "expert", split_axis=0, concat_axis=0, tiled=True)
    d_pairs = jnp.concatenate([d_back.reshape(all_experts * capacity, width), zero_row], axis=0)[
        target
    ].reshape(tokens, top, width)
    d_normed_two = jnp.sum(d_pairs, axis=1, dtype=jnp.float32)
    d_gates = jnp.einsum("td,tkd->tk", cotangent, pair_out, preferred_element_type=jnp.float32)
    d_picked = gates * (d_gates - jnp.sum(gates * d_gates, axis=-1, keepdims=True))
    d_logits = jnp.sum(onehot * d_picked[:, :, None], axis=1).astype(jnp.bfloat16)
    grad_router_part = jnp.einsum(
        "td,te->de", normed_two, d_logits, preferred_element_type=jnp.float32
    )
    d_normed_two = d_normed_two + jnp.einsum(
        "te,de->td", d_logits, w_router, preferred_element_type=jnp.float32
    )
    scaled_two = d_normed_two * gain_mlp
    grad_gain_mlp_part = jnp.sum(d_normed_two * middle * inv_two, axis=0)
    d_middle = (
        cotangent
        + inv_two * scaled_two
        - middle * inv_two**3 * jnp.mean(middle * scaled_two, axis=-1, keepdims=True)
    )
    d_branch = d_middle.astype(jnp.bfloat16)
    grad_output_part = jnp.einsum(
        "tf,td->fd", attended_low, d_branch, preferred_element_type=jnp.float32
    )
    d_attended = jnp.einsum(
        "td,fd->tf", d_branch, w_output, preferred_element_type=jnp.float32
    ).astype(jnp.bfloat16)
    d_groups = d_attended.reshape(tokens, KV_HEADS, groups, HEAD_DIM)
    delta = jnp.einsum(
        "qkgd,qkgd->kgq", d_groups, attended_groups, preferred_element_type=jnp.float32
    )
    keys_back, values_back = (
        lax.all_gather(keys_low, "dp", axis=0, tiled=True),
        lax.all_gather(values_low, "dp", axis=0, tiled=True),
    )

    def grad_step(step, carry):
        d_query, d_keys, d_values = carry
        start = step * block
        key_block = lax.dynamic_slice_in_dim(keys_back, start, block, 0)
        value_block = lax.dynamic_slice_in_dim(values_back, start, block, 0)
        scores = block_scores(key_block, start)
        probs = jnp.exp(scores - log_total[..., None])
        probs_low = probs.astype(jnp.bfloat16)
        d_probs = jnp.einsum(
            "qkgd,skd->kgqs", d_groups, value_block, preferred_element_type=jnp.float32
        )
        d_scores = (probs * (d_probs - delta[..., None])).astype(jnp.bfloat16)
        d_query = d_query + jnp.einsum(
            "kgqs,skd->qkgd", d_scores, key_block, preferred_element_type=jnp.float32
        )
        key_part = jnp.einsum(
            "kgqs,qkgd->skd", d_scores, query_groups, preferred_element_type=jnp.float32
        )
        value_part = jnp.einsum(
            "kgqs,qkgd->skd", probs_low, d_groups, preferred_element_type=jnp.float32
        )
        d_keys = lax.dynamic_update_slice_in_dim(
            d_keys, lax.dynamic_slice_in_dim(d_keys, start, block, 0) + key_part, start, 0
        )
        d_values = lax.dynamic_update_slice_in_dim(
            d_values, lax.dynamic_slice_in_dim(d_values, start, block, 0) + value_part, start, 0
        )
        return (d_query, d_keys, d_values)

    grad_init = (
        jnp.zeros((tokens, KV_HEADS, groups, HEAD_DIM), jnp.float32),
        jnp.zeros((length, KV_HEADS, HEAD_DIM), jnp.float32),
        jnp.zeros((length, KV_HEADS, HEAD_DIM), jnp.float32),
    )
    d_query, d_keys, d_values = lax.fori_loop(0, count, grad_step, grad_init)
    key_sum, value_sum = (
        lax.psum_scatter(
            (d_keys * scale).reshape(length, KV_HEADS * HEAD_DIM).astype(jnp.bfloat16),
            "dp",
            scatter_dimension=0,
            tiled=True,
        ).astype(jnp.float32),
        lax.psum_scatter(
            d_values.reshape(length, KV_HEADS * HEAD_DIM).astype(jnp.bfloat16),
            "dp",
            scatter_dimension=0,
            tiled=True,
        ).astype(jnp.float32),
    )
    d_query_low = (
        rotate_back((d_query * scale).reshape(tokens, HEADS, HEAD_DIM), cosine, sine)
        .astype(jnp.bfloat16)
        .reshape(tokens, HEADS * HEAD_DIM)
    )
    d_key_low = (
        rotate_back(key_sum.reshape(tokens, KV_HEADS, HEAD_DIM), cosine, sine)
        .astype(jnp.bfloat16)
        .reshape(tokens, KV_HEADS * HEAD_DIM)
    )
    d_value_low = value_sum.astype(jnp.bfloat16)
    grad_query_part = jnp.einsum(
        "td,tf->df", normed, d_query_low, preferred_element_type=jnp.float32
    )
    grad_key_part = jnp.einsum("td,tf->df", normed, d_key_low, preferred_element_type=jnp.float32)
    grad_value_part = jnp.einsum(
        "td,tf->df", normed, d_value_low, preferred_element_type=jnp.float32
    )
    d_normed = jnp.einsum("tf,df->td", d_query_low, w_query, preferred_element_type=jnp.float32)
    d_normed = d_normed + jnp.einsum(
        "tf,df->td", d_key_low, w_key, preferred_element_type=jnp.float32
    )
    d_normed = d_normed + jnp.einsum(
        "tf,df->td", d_value_low, w_value, preferred_element_type=jnp.float32
    )
    scaled_one = d_normed * gain_attn
    grad_gain_attn_part = jnp.sum(d_normed * inputs * inv_one, axis=0)
    grad_in = (
        d_middle
        + inv_one * scaled_one
        - inputs * inv_one**3 * jnp.mean(inputs * scaled_one, axis=-1, keepdims=True)
    )
    dense = (
        lax.psum_scatter(grad_gain_attn_part, ("dp", "expert"), scatter_dimension=0, tiled=True),
        lax.psum_scatter(grad_query_part, ("dp", "expert"), scatter_dimension=0, tiled=True),
        lax.psum_scatter(grad_key_part, ("dp", "expert"), scatter_dimension=0, tiled=True),
        lax.psum_scatter(grad_value_part, ("dp", "expert"), scatter_dimension=0, tiled=True),
        lax.psum_scatter(grad_output_part, ("dp", "expert"), scatter_dimension=0, tiled=True),
        lax.psum_scatter(grad_gain_mlp_part, ("dp", "expert"), scatter_dimension=0, tiled=True),
        lax.psum_scatter(grad_router_part, ("dp", "expert"), scatter_dimension=0, tiled=True),
    )
    return (
        hidden_out[None],
        grad_in[None],
        dense[0],
        dense[1],
        dense[2],
        dense[3],
        dense[4],
        dense[5],
        dense[6],
        gate_total,
        up_total,
        down_total,
    )

BF = jnp.bfloat16
F32 = jnp.float32
WIDTH = 1536
LANES = 128
PER_KV = HEADS // KV_HEADS
ROWS_Q = PER_KV * HEAD_DIM
PACK = ROWS_Q + 2 * HEAD_DIM
BIT_Y, BIT_ZL, BIT_ZH = 1, 2, 4
BIT_C, BIT_X = 1, 2
BLOCK_Q = 256
BLOCK_K = 512
SLOTS = 64
CHUNK = 512
MIB = 1 << 20
hbm = pl.BlockSpec(memory_space=pltpu.HBM)


def dot_nn(a, b):
    return lax.dot_general(a, b, (((1,), (0,)), ((), ())), preferred_element_type=F32)


def dot_nt(a, b):
    return lax.dot_general(a, b, (((1,), (1,)), ((), ())), preferred_element_type=F32)


def dot_tn(a, b):
    return lax.dot_general(a, b, (((0,), (0,)), ((), ())), preferred_element_type=F32)


def cost(flops, moved, transcendentals=0):
    return pl.CostEstimate(
        flops=int(flops), bytes_accessed=int(moved), transcendentals=int(transcendentals)
    )


def params(mib, dims=None):
    return pltpu.CompilerParams(vmem_limit_bytes=mib * MIB, dimension_semantics=dims)


def swap(values, axis, mask):
    size = lax.axis_size(axis)
    return lax.ppermute(values, axis, [(i, i ^ mask) for i in range(size)])


def swap_bit(values, bit):
    axis, mask = bit
    return swap(values, axis, mask)


def fence(*values):
    return lax.optimization_barrier(values)


C_BIT = ("expert", BIT_C)
X_BIT = ("expert", BIT_X)
Y_BIT = ("dp", BIT_Y)
ZL_BIT = ("dp", BIT_ZL)
ZH_BIT = ("dp", BIT_ZH)


def pre_kernel(
    hid_ref,
    gain_ref,
    wq_ref,
    wk_ref,
    wv_ref,
    cos_ref,
    sin_ref,
    cot_ref,
    norm_ref,
    pack_ref,
    low_ref,
):
    tokens = hid_ref.shape[0]
    half = tokens // 2
    low_ref[...] = cot_ref[...].astype(BF)
    inputs = hid_ref[...]
    inv = lax.rsqrt(jnp.mean(inputs * inputs, axis=-1, keepdims=True) + EPS)
    normed = (inputs * inv * gain_ref[...]).astype(BF)
    norm_ref[...] = normed
    low = (lax.broadcasted_iota(jnp.int32, (tokens, LANES), 1) % HEAD_DIM) < HEAD_DIM // 2
    cosine, sine = cos_ref[...], sin_ref[...]

    def turn(tile):
        other = jnp.where(
            low,
            pltpu.roll(tile, LANES - HEAD_DIM // 2, 1),
            pltpu.roll(tile, HEAD_DIM // 2, 1),
        )
        return (tile * cosine + other * sine).astype(BF)

    tiles = []
    for n in range(wq_ref.shape[1] // CHUNK):
        pre = dot_nn(normed, wq_ref[:, n * CHUNK : (n + 1) * CHUNK])
        tiles += [turn(pre[:, m * LANES : (m + 1) * LANES]) for m in range(CHUNK // LANES)]
    queries = jnp.concatenate(tiles, axis=1)
    pre = dot_nn(normed, wk_ref[...])
    keys = jnp.concatenate(
        [turn(pre[:, m * LANES : (m + 1) * LANES]) for m in range(pre.shape[1] // LANES)], axis=1
    )
    values = dot_nn(normed, wv_ref[...]).astype(BF)
    for g in range(KV_HEADS):
        at = g * ROWS_Q
        head = slice(g * HEAD_DIM, (g + 1) * HEAD_DIM)
        pack_ref[g, 0:tokens] = queries[:, at : at + LANES]
        pack_ref[g, tokens : 2 * tokens] = jnp.concatenate(
            [queries[:, at + LANES : at + ROWS_Q], keys[:, head]], axis=1
        )
        pack_ref[g, 2 * tokens :] = jnp.concatenate(
            [values[:half, head], values[half:, head]], axis=1
        )


def run_pre(inputs, gain, w_query, w_key, w_value, cos_tab, sin_tab, cotangent):
    tokens = inputs.shape[0]
    return pl.pallas_call(
        pre_kernel,
        out_shape=(
            jax.ShapeDtypeStruct((tokens, WIDTH), BF),
            jax.ShapeDtypeStruct((KV_HEADS, tokens * PACK // LANES, LANES), BF),
            jax.ShapeDtypeStruct((tokens, WIDTH), BF),
        ),
        compiler_params=params(60),
        cost_estimate=cost(2 * tokens * WIDTH * 2560, 14e6),
    )(inputs, gain[None], w_query, w_key, w_value, cos_tab, sin_tab, cotangent)


def unpack_heads(block_ref, out_ref, row, tokens, column):
    half = tokens // 2
    out_ref[row : row + tokens, column : column + LANES] = block_ref[0:tokens]
    rest = block_ref[tokens : tokens + half]
    out_ref[row : row + half, column + LANES : column + ROWS_Q] = rest[:, :HEAD_DIM]
    out_ref[row + half : row + tokens, column + LANES : column + ROWS_Q] = rest[:, HEAD_DIM:]


def pack_heads(block_ref, rows, tokens):
    half = tokens // 2
    block_ref[0:tokens] = rows[:, 0:LANES]
    block_ref[tokens : tokens + half] = jnp.concatenate(
        [rows[:half, LANES:ROWS_Q], rows[half:, LANES:ROWS_Q]], axis=1
    )


def unpack_all(block_ref, q_ref, k_ref, v_ref, row, tokens, q_at=0, k_at=0, v_at=0):
    half = tokens // 2
    rows = slice(row, row + tokens)
    q_ref[rows, q_at : q_at + LANES] = block_ref[0:tokens]
    two = block_ref[tokens : 2 * tokens]
    q_ref[rows, q_at + LANES : q_at + ROWS_Q] = two[:, :HEAD_DIM]
    k_ref[rows, k_at : k_at + HEAD_DIM] = two[:, HEAD_DIM:]
    rest = block_ref[2 * tokens : 2 * tokens + half]
    v_ref[row : row + half, v_at : v_at + HEAD_DIM] = rest[:, :HEAD_DIM]
    v_ref[row + half : row + tokens, v_at : v_at + HEAD_DIM] = rest[:, HEAD_DIM:]


def heads_t(block, width):
    return jnp.concatenate(
        [block[:, h * HEAD_DIM : (h + 1) * HEAD_DIM].astype(F32).T for h in range(width)], axis=1
    )


def heads_rows(block, width):
    return jnp.concatenate(
        [block[:, h * HEAD_DIM : (h + 1) * HEAD_DIM] for h in range(width)], axis=0
    )


def allowed_t(step, block):
    shape = (BLOCK_K, PER_KV * BLOCK_Q)
    key_pos = step * BLOCK_K + lax.broadcasted_iota(jnp.int32, shape, 0)
    query_pos = block * BLOCK_Q + lax.broadcasted_iota(jnp.int32, shape, 1) % BLOCK_Q
    return key_pos <= query_pos


def forward_kernel(pack_ref, out_ref, out_t_ref, lse_ref, q_s, k_s, v_s, vt_s, out_s):
    block = pl.program_id(0)
    sources = pack_ref.shape[0]
    tokens = q_s.shape[0] // sources

    @pl.when(block == 0)
    def _():
        for n in range(sources):
            unpack_all(pack_ref.at[n], q_s, k_s, v_s, n * tokens, tokens)
        vt_s[...] = v_s[...].astype(F32).T.astype(BF)

    rows = pl.ds(pl.multiple_of(block * BLOCK_Q, BLOCK_Q), BLOCK_Q)
    scale = HEAD_DIM ** (-0.5)
    q_t = (heads_t(q_s[rows, :], PER_KV) * scale).astype(BF)
    columns = PER_KV * BLOCK_Q

    def step(j, carry, masked):
        running, total, accum = carry
        keys = pl.ds(pl.multiple_of(j * BLOCK_K, BLOCK_K), BLOCK_K)
        scores = dot_nn(k_s[keys, :], q_t)
        if masked:
            scores = jnp.where(allowed_t(j, block), scores, MASKED)
        newest = jnp.maximum(running, jnp.max(scores, axis=0, keepdims=True))
        fade = jnp.exp(running - newest)
        probs = jnp.exp(scores - newest)
        total = total * fade + jnp.sum(probs, axis=0, keepdims=True)
        accum = accum * fade + dot_nn(vt_s[:, keys], probs.astype(BF))
        return newest, total, accum

    carry = (
        jnp.full((1, columns), MASKED, F32),
        jnp.zeros((1, columns), F32),
        jnp.zeros((HEAD_DIM, columns), F32),
    )
    last = (block * BLOCK_Q) // BLOCK_K
    carry = lax.fori_loop(0, last, lambda j, c: step(j, c, False), carry)
    running, total, accum = step(last, carry, True)
    out_t = accum / total
    out_t_ref[0] = out_t
    lse_ref[0] = running + jnp.log(total)
    out_s[rows, :] = jnp.concatenate(
        [out_t[:, h * BLOCK_Q : (h + 1) * BLOCK_Q].T for h in range(PER_KV)], axis=1
    ).astype(BF)

    @pl.when(block == pl.num_programs(0) - 1)
    def _():
        for n in range(sources):
            pack_heads(out_ref.at[n], out_s[n * tokens : (n + 1) * tokens, :], tokens)


def run_forward(pack):
    sources = pack.shape[0]
    length = sources * (pack.shape[1] * LANES // PACK)
    packed = (sources, length // sources * ROWS_Q // LANES, LANES)
    blocks = length // BLOCK_Q
    columns = PER_KV * BLOCK_Q
    return pl.pallas_call(
        forward_kernel,
        grid=(blocks,),
        in_specs=[pl.BlockSpec(pack.shape, lambda i: (0, 0, 0))],
        out_specs=(
            pl.BlockSpec(packed, lambda i: (0, 0, 0)),
            pl.BlockSpec((1, HEAD_DIM, columns), lambda i: (i, 0, 0)),
            pl.BlockSpec((1, 1, columns), lambda i: (i, 0, 0)),
        ),
        out_shape=(
            jax.ShapeDtypeStruct(packed, BF),
            jax.ShapeDtypeStruct((blocks, HEAD_DIM, columns), F32),
            jax.ShapeDtypeStruct((blocks, 1, columns), F32),
        ),
        scratch_shapes=[
            pltpu.VMEM((length, ROWS_Q), BF),
            pltpu.VMEM((length, HEAD_DIM), BF),
            pltpu.VMEM((length, HEAD_DIM), BF),
            pltpu.VMEM((HEAD_DIM, length), BF),
            pltpu.VMEM((length, ROWS_Q), BF),
        ],
        compiler_params=params(60, ("arbitrary",)),
        cost_estimate=cost(8 * length * length * ROWS_Q, 6e6, length * length * PER_KV),
    )(pack)


def backward_kernel(
    pack_ref,
    grad_ref,
    out_t_ref,
    lse_ref,
    cos_ref,
    sin_ref,
    res_ref,
    q_s,
    do_s,
    k_s,
    v_s,
    kt_s,
    dk_s,
    dv_s,
):
    block = pl.program_id(0)
    sources = pack_ref.shape[0]
    tokens = q_s.shape[0] // sources

    @pl.when(block == 0)
    def _():
        for n in range(sources):
            unpack_all(pack_ref.at[n], q_s, k_s, v_s, n * tokens, tokens)
            unpack_heads(grad_ref.at[n], do_s, n * tokens, tokens, 0)
        kt_s[...] = k_s[...].astype(F32).T.astype(BF)
        dk_s[...] = jnp.zeros_like(dk_s)
        dv_s[...] = jnp.zeros_like(dv_s)

    scale = HEAD_DIM ** (-0.5)
    half = HEAD_DIM // 2
    rows = pl.ds(pl.multiple_of(block * BLOCK_Q, BLOCK_Q), BLOCK_Q)
    q_block = q_s[rows, :]
    q_t = (heads_t(q_block, PER_KV) * scale).astype(BF)
    q_rows = (heads_rows(q_block, PER_KV).astype(F32) * scale).astype(BF)
    do_block = do_s[rows, :]
    do_f32 = heads_t(do_block, PER_KV)
    do_t = do_f32.astype(BF)
    do_rows = heads_rows(do_block, PER_KV)
    delta = jnp.sum(do_f32 * out_t_ref[0], axis=0, keepdims=True)
    lse = lse_ref[0]

    def step(j, dq_t, masked):
        keys = pl.ds(pl.multiple_of(j * BLOCK_K, BLOCK_K), BLOCK_K)
        scores = dot_nn(k_s[keys, :], q_t)
        if masked:
            scores = jnp.where(allowed_t(j, block), scores, MASKED)
        probs = jnp.exp(scores - lse)
        d_probs = dot_nn(v_s[keys, :], do_t)
        d_scores = (probs * (d_probs - delta)).astype(BF)
        dv_s[keys, :] += dot_nn(probs.astype(BF), do_rows)
        dk_s[keys, :] += dot_nn(d_scores, q_rows)
        return dq_t + dot_nn(kt_s[:, keys], d_scores)

    last = (block * BLOCK_Q) // BLOCK_K
    dq_t = jnp.zeros((HEAD_DIM, PER_KV * BLOCK_Q), F32)
    dq_t = lax.fori_loop(0, last, lambda j, c: step(j, c, False), dq_t)
    dq_t = step(last, dq_t, True) * scale

    def turn_back(values, cosine, sine):
        first, second = values[:half], values[half:]
        return jnp.concatenate(
            [first * cosine + second * sine, second * cosine - first * sine], axis=0
        )

    columns = pl.ds(pl.multiple_of(block * BLOCK_Q, BLOCK_Q), BLOCK_Q)
    cosine, sine = cos_ref[:, columns], sin_ref[:, columns]
    q_s[rows, :] = jnp.concatenate(
        [
            turn_back(dq_t[:, h * BLOCK_Q : (h + 1) * BLOCK_Q], cosine, sine).T
            for h in range(PER_KV)
        ],
        axis=1,
    ).astype(BF)

    @pl.when(block == pl.num_programs(0) - 1)
    def _():
        dk = turn_back(dk_s[...].T, cos_ref[...], sin_ref[...]).T.astype(BF)
        half = tokens // 2
        for n in range(sources):
            row = n * tokens
            res_ref[n, 0:tokens] = q_s[row : row + tokens, 0:LANES]
            res_ref[n, tokens : 2 * tokens] = jnp.concatenate(
                [q_s[row : row + tokens, LANES:ROWS_Q], dk[row : row + tokens]], axis=1
            )
            res_ref[n, 2 * tokens :] = jnp.concatenate(
                [dv_s[row : row + half, :], dv_s[row + half : row + tokens, :]], axis=1
            ).astype(BF)


def run_backward(pack, grad, out_t, lse, cos_t, sin_t):
    length = cos_t.shape[1]
    blocks = length // BLOCK_Q
    columns = PER_KV * BLOCK_Q
    half = HEAD_DIM // 2
    return pl.pallas_call(
        backward_kernel,
        grid=(blocks,),
        in_specs=[
            pl.BlockSpec(pack.shape, lambda i: (0, 0, 0)),
            pl.BlockSpec(grad.shape, lambda i: (0, 0, 0)),
            pl.BlockSpec((1, HEAD_DIM, columns), lambda i: (i, 0, 0)),
            pl.BlockSpec((1, 1, columns), lambda i: (i, 0, 0)),
            pl.BlockSpec((half, length), lambda i: (0, 0)),
            pl.BlockSpec((half, length), lambda i: (0, 0)),
        ],
        out_specs=pl.BlockSpec(pack.shape, lambda i: (0, 0, 0)),
        out_shape=jax.ShapeDtypeStruct(pack.shape, BF),
        scratch_shapes=[
            pltpu.VMEM((length, ROWS_Q), BF),
            pltpu.VMEM((length, ROWS_Q), BF),
            pltpu.VMEM((length, HEAD_DIM), BF),
            pltpu.VMEM((length, HEAD_DIM), BF),
            pltpu.VMEM((HEAD_DIM, length), BF),
            pltpu.VMEM((length, HEAD_DIM), F32),
            pltpu.VMEM((length, HEAD_DIM), F32),
        ],
        compiler_params=params(60, ("arbitrary",)),
        cost_estimate=cost(20 * length * length * ROWS_Q, 8e6, length * length * PER_KV),
    )(pack, grad, out_t, lse, cos_t, sin_t)


def mid_kernel(att_ref, wo_ref, hid_ref, gain_ref, mid_ref, norm_ref, full_ref):
    for g in range(KV_HEADS):
        unpack_heads(att_ref.at[g], full_ref, 0, full_ref.shape[0], g * ROWS_Q)
    middle = hid_ref[...] + dot_nn(full_ref[...], wo_ref[...])
    mid_ref[...] = middle
    inv = lax.rsqrt(jnp.mean(middle * middle, axis=-1, keepdims=True) + EPS)
    norm_ref[...] = (middle * inv * gain_ref[...]).astype(BF)


def run_mid(att, w_output, inputs, gain):
    tokens = inputs.shape[0]
    return pl.pallas_call(
        mid_kernel,
        out_shape=(
            jax.ShapeDtypeStruct((tokens, WIDTH), F32),
            jax.ShapeDtypeStruct((tokens, WIDTH), BF),
            jax.ShapeDtypeStruct((tokens, WIDTH), BF),
        ),
        compiler_params=params(24),
        cost_estimate=cost(2 * tokens * WIDTH * WIDTH, 12e6),
    )(att, w_output, inputs, gain[None])


def expert_kernel(
    place_ref,
    x_ref,
    g_ref,
    gates_ref,
    map_ref,
    wg0_ref,
    wg1_ref,
    wu0_ref,
    wu1_ref,
    wd0_ref,
    wd1_ref,
    *refs,
    first,
):
    if first:
        mix_prior = dx_prior = None
    else:
        mix_prior, dx_prior = refs[0:2], refs[2:4]
        refs = refs[4:]
    (
    mix_keep,
    mix_send,
    dx_keep,
    dx_send,
    gate_keep,
    gate_send0,
    gate_send1,
    early,
    up_keep,
    up_send0,
    up_send1,
    down_keep,
    down_send0,
    down_send1,
    xs,
    gs,
    gate_s,
    wide_s,
    tall_s,
    ) = refs
    step = pl.program_id(0)
    sources = map_ref.shape[0]
    experts = xs.shape[0]
    low = 0 if first else experts
    rows = experts * SLOTS
    count = WIDTH // CHUNK

    def pick_of(source):
        return one_hot(map_ref[source, low : low + experts, :], rows)

    @pl.when(step < experts)
    def _():
        e = step
        x = x_ref[0]
        w_gate = jnp.concatenate([wg0_ref[0], wg1_ref[0]], axis=1)
        w_up = jnp.concatenate([wu0_ref[0], wu1_ref[0]], axis=1)
        gate_pre = dot_nn(x, w_gate)
        up_pre = dot_nn(x, w_up)
        sig = jax.nn.sigmoid(gate_pre)
        silu = gate_pre * sig
        hidden = (silu * up_pre).astype(BF)
        gate = gates_ref[0]
        d_hidden = jnp.zeros(hidden.shape, F32)
        d_gates = jnp.zeros(gate.shape, F32)
        for n in range(count):
            cols = slice(n * CHUNK, (n + 1) * CHUNK)
            w_down = jnp.concatenate([wd0_ref[0, :, cols], wd1_ref[0, :, cols]], axis=0)
            grad = g_ref[0, :, cols].astype(F32)
            d_y = (gate * grad).astype(BF)
            y = dot_nn(hidden, w_down)
            d_gates += jnp.sum(y * grad, axis=1, keepdims=True)
            gs[e, :, cols] = (gate * y).astype(BF)
            d_hidden += dot_nt(d_y, w_down)
            wide_s[:, cols] = dot_tn(hidden, d_y).astype(BF)
        gate_s[e] = d_gates
        d_gate = (d_hidden * up_pre * sig * (1.0 + gate_pre * (1.0 - sig))).astype(BF)
        d_up = (d_hidden * silu).astype(BF)

        y_at, zl_at, zh_at = place_ref[1], place_ref[2], place_ref[3]
        part = down_keep.shape[2]
        for z in range(2):
            base = (zh_at ^ z) * 2
            down_keep[z, 0] = wide_s[pl.ds(pl.multiple_of((base + y_at) * part, part), part), :]
            (down_send0, down_send1)[z][0] = wide_s[
                pl.ds(pl.multiple_of((base + (1 - y_at)) * part, part), part), :
            ]

        def spread(keep, send):
            part = keep.shape[3]
            for z in range(2):
                for low in range(2):
                    base = ((zh_at ^ z) * 2 + (zl_at ^ low)) * 2
                    keep[z, low, 0] = tall_s[
                        pl.ds(pl.multiple_of((base + y_at) * part, part), part), :
                    ]
                    send[z][low, 0] = tall_s[
                        pl.ds(pl.multiple_of((base + (1 - y_at)) * part, part), part), :
                    ]

        for n in range(count):
            cols = slice(n * CHUNK, (n + 1) * CHUNK)
            tall_s[cols, :] = dot_tn(x[:, cols], d_gate).astype(BF)
        spread(gate_keep, (gate_send0, gate_send1))
        early[0, 0] = gate_keep[1, 1, 0]
        early[1, 0] = gate_send1[1, 0]
        for n in range(count):
            cols = slice(n * CHUNK, (n + 1) * CHUNK)
            tall_s[cols, :] = dot_tn(x[:, cols], d_up).astype(BF)
        spread(up_keep, (up_send0, up_send1))
        for n in range(count):
            cols = slice(n * CHUNK, (n + 1) * CHUNK)
            d_x = dot_nt(d_gate, w_gate[cols]) + dot_nt(d_up, w_up[cols])
            xs[e, :, cols] = d_x.astype(BF)

    def combine(source, mix_out, dx_out, mix_in, dx_in):
        def put(out, prior, cols, values):
            if prior is not None:
                values += prior[0, :, cols].astype(F32)
            out[0, :, cols] = values.astype(BF)

        here = pl.ds(pl.multiple_of(source * SLOTS, SLOTS), SLOTS)
        pick = pick_of(source).astype(BF)
        for n in range(count):
            cols = slice(n * CHUNK, (n + 1) * CHUNK)
            put(dx_out, dx_in, cols, dot_tn(pick, xs[:, here, cols].reshape(rows, CHUNK)))
            put(mix_out, mix_in, cols, dot_tn(pick, gs[:, here, cols].reshape(rows, CHUNK)))
        values = gate_s[:, here, :].reshape(rows, 1)
        column = lax.broadcasted_iota(jnp.int32, (rows, LANES), 1)
        owner = lax.broadcasted_iota(jnp.int32, (rows, LANES), 0) // SLOTS
        spread_out = jnp.where(column == owner + (place_ref[4] + low), values, 0.0).astype(BF)
        put(dx_out, dx_in, slice(WIDTH, WIDTH + LANES), dot_tn(pick, spread_out))

    @pl.when((step >= experts) & (step < experts + sources // 2))
    def _():
        source = step - experts + sources // 2
        prior = (None, None) if first else (mix_prior[1], dx_prior[1])
        combine(source, mix_send, dx_send, *prior)

    @pl.when(step >= experts + sources // 2)
    def _():
        source = step - experts - sources // 2
        prior = (None, None) if first else (mix_prior[0], dx_prior[0])
        combine(source, mix_keep, dx_keep, *prior)


def less(shape):
    return jax.ShapeDtypeStruct(shape.shape[1:], shape.dtype)


def run_experts(place, x_slots, g_slots, gates, maps, w_gate, w_up, w_down, prior=()):
    sources, _, tokens = maps.shape
    width = x_slots.shape[2]
    experts = w_gate.shape[0] // 2
    low = experts if prior else 0
    ffe = w_gate.shape[2]
    part = ffe // 8
    quarter = width // 8
    half = ffe // 2
    slots = sources * SLOTS
    extra = width + LANES
    second = experts
    third = second + sources // 2

    def at(i, low, size):
        return jnp.clip(i - low, 0, size - 1)

    def expert_of(i):
        return at(i, 0, experts)

    def w_cols(block):
        return pl.BlockSpec(
            (1, width, LANES), lambda i, p: (expert_of(i) + low, 0, p[0] + 2 * block)
        )

    def w_rows(block):
        return pl.BlockSpec(
            (1, LANES, width), lambda i, p: (expert_of(i) + low, p[0] + 2 * block, 0)
        )

    slot_spec = pl.BlockSpec((1, slots, width), lambda i, p: (expert_of(i) + low, 0, 0))

    def out_tokens(low, cols):
        return pl.BlockSpec((1, tokens, cols), lambda i, p: (at(i, low, sources // 2), 0, 0))

    tall_spec = pl.BlockSpec(
        (2, 2, 1, quarter, half), lambda i, p: (0, 0, expert_of(i), 0, 0)
    )
    wide_spec = pl.BlockSpec((2, 1, part, width), lambda i, p: (0, expert_of(i), 0, 0))
    tall_half = pl.BlockSpec((2, 1, quarter, half), lambda i, p: (0, expert_of(i), 0, 0))
    wide_half = pl.BlockSpec((1, part, width), lambda i, p: (expert_of(i), 0, 0))
    tall = jax.ShapeDtypeStruct((2, 2, experts, quarter, half), BF)
    wide = jax.ShapeDtypeStruct((2, experts, part, width), BF)
    mixed = jax.ShapeDtypeStruct((sources // 2, tokens, width), BF)
    d_x = jax.ShapeDtypeStruct((sources // 2, tokens, extra), BF)
    sums = (
        out_tokens(third, width),
        out_tokens(second, width),
        out_tokens(third, extra),
        out_tokens(second, extra),
    )
    return pl.pallas_call(
        functools.partial(expert_kernel, first=not prior),
        grid_spec=pltpu.PrefetchScalarGridSpec(
            num_scalar_prefetch=1,
            grid=(third + sources // 2,),
            in_specs=[
                slot_spec,
                slot_spec,
                pl.BlockSpec((1, slots, 1), lambda i, p: (expert_of(i) + low, 0, 0)),
                pl.BlockSpec(maps.shape, lambda i, p: (0, 0, 0)),
                w_cols(0),
                w_cols(1),
                w_cols(0),
                w_cols(1),
                w_rows(0),
                w_rows(1),
                *(sums if prior else ()),
            ],
            out_specs=(
                *sums,
                tall_spec,
                tall_half,
                tall_half,
                tall_half,
                tall_spec,
                tall_half,
                tall_half,
                wide_spec,
                wide_half,
                wide_half,
            ),
            scratch_shapes=[
                pltpu.VMEM((experts, slots, width), BF),
                pltpu.VMEM((experts, slots, width), BF),
                pltpu.VMEM((experts, slots, 1), F32),
                pltpu.VMEM((half, width), BF),
                pltpu.VMEM((width, half), BF),
            ],
        ),
        out_shape=(mixed, mixed, d_x, d_x)
        + (tall, less(tall), less(tall), less(tall))
        + (tall, less(tall), less(tall))
        + (wide, less(wide), less(wide)),
        compiler_params=params(60, ("arbitrary",)),
        cost_estimate=cost(30e9, 60e6),
    )(place, x_slots, g_slots, gates, maps, w_gate, w_gate, w_up, w_up, w_down, w_down, *prior)


def post_kernel(
    dx_ref,
    mid_ref,
    cot_ref,
    norm_ref,
    wr_ref,
    map_ref,
    gain_ref,
    wo_ref,
    datt_ref,
    dmid_ref,
    dlow_ref,
    dlog_ref,
    ggain_ref,
):
    middle = mid_ref[...]
    inv = lax.rsqrt(jnp.mean(middle * middle, axis=-1, keepdims=True) + EPS)
    chosen = map_ref[...] >= 0.0
    logits = jnp.where(chosen, dot_nn(norm_ref[...], wr_ref[...]), MASKED)
    raised = jnp.exp(logits - jnp.max(logits, axis=-1, keepdims=True))
    raised = jnp.where(chosen, raised, 0.0)
    gates = raised / jnp.sum(raised, axis=-1, keepdims=True)
    d_gates = dx_ref[:, WIDTH:]
    d_picked = gates * (d_gates - jnp.sum(gates * d_gates, axis=-1, keepdims=True))
    d_logits = d_picked.astype(BF)
    dlog_ref[...] = d_logits
    d_norm = dx_ref[:, :WIDTH] + dot_nt(d_logits, wr_ref[...])
    scaled = d_norm * gain_ref[...]
    ggain_ref[...] = jnp.sum(d_norm * middle * inv, axis=0, keepdims=True)
    d_mid = (
        cot_ref[...]
        + inv * scaled
        - middle * inv**3 * jnp.mean(middle * scaled, axis=-1, keepdims=True)
    )
    dmid_ref[...] = d_mid
    d_low = d_mid.astype(BF)
    dlow_ref[...] = d_low
    d_att = dot_nt(d_low, wo_ref[...]).astype(BF)
    for g in range(KV_HEADS):
        pack_heads(datt_ref.at[g], d_att[:, g * ROWS_Q : (g + 1) * ROWS_Q], d_att.shape[0])


def run_post(dx_sum, middle, cotangent, normed_two, wr_pad, map_rows, gain, w_output):
    tokens = middle.shape[0]
    return pl.pallas_call(
        post_kernel,
        out_shape=(
            jax.ShapeDtypeStruct((KV_HEADS, tokens * ROWS_Q // LANES, LANES), BF),
            jax.ShapeDtypeStruct((tokens, WIDTH), F32),
            jax.ShapeDtypeStruct((tokens, WIDTH), BF),
            jax.ShapeDtypeStruct((tokens, LANES), BF),
            jax.ShapeDtypeStruct((1, WIDTH), F32),
        ),
        compiler_params=params(60),
        cost_estimate=cost(2 * tokens * WIDTH * WIDTH, 14e6),
    )(dx_sum, middle, cotangent, normed_two, wr_pad, map_rows, gain[None], w_output)


def put_rows(place_ref, held, keep, send):
    part = keep.shape[1]
    for b in range(keep.shape[0]):
        own = (2 * b) ^ place_ref[5]
        keep[b] = held[pl.ds(pl.multiple_of(own * part, part), part), :]
        other = own ^ 1
        send[b] = held[pl.ds(pl.multiple_of(other * part, part), part), :]


def qkvgrad_kernel(place_ref, a_ref, d_ref, full_ref, keep, send, held):
    step = pl.program_id(0)

    @pl.when(step == 0)
    def _():
        key_at = KV_HEADS * ROWS_Q
        value_at = key_at + KV_HEADS * HEAD_DIM
        for g in range(KV_HEADS):
            unpack_all(
                d_ref.at[g],
                full_ref,
                full_ref,
                full_ref,
                0,
                full_ref.shape[0],
                g * ROWS_Q,
                key_at + g * HEAD_DIM,
                value_at + g * HEAD_DIM,
            )

    cols = pl.ds(pl.multiple_of(step * 256, 256), 256)
    held[...] = dot_tn(a_ref[...], full_ref[:, cols]).astype(BF)
    put_rows(place_ref, held, keep, send)


def run_qkvgrad(place, normed, d_pack, blocks):
    tokens, rows = normed.shape
    cols = KV_HEADS * PACK
    part = rows // blocks
    spec = pl.BlockSpec((blocks // 2, part, 256), lambda i, p: (0, 0, i))
    shape = jax.ShapeDtypeStruct((blocks // 2, part, cols), BF)
    return pl.pallas_call(
        qkvgrad_kernel,
        grid_spec=pltpu.PrefetchScalarGridSpec(
            num_scalar_prefetch=1,
            grid=(cols // 256,),
            in_specs=[
                pl.BlockSpec((tokens, rows), lambda i, p: (0, 0)),
                pl.BlockSpec(d_pack.shape, lambda i, p: (0, 0, 0)),
            ],
            out_specs=(pl.BlockSpec((tokens, cols), lambda i, p: (0, 0)), spec, spec),
            scratch_shapes=[pltpu.VMEM((rows, 256), BF)],
        ),
        out_shape=(jax.ShapeDtypeStruct((tokens, cols), BF), shape, shape),
        compiler_params=params(60, ("arbitrary",)),
        cost_estimate=cost(2 * tokens * rows * cols, 12e6),
    )(place, normed, d_pack)


def last_work(inputs, outputs, scratch):
    gain_ref, gmlp_ref, sources = inputs[0], inputs[1], inputs[2:]
    (out_ref,) = outputs
    keep, send, held = scratch[:3]
    buffers, load_sem = scratch[3:-1], scratch[-1]
    loads = [
        pltpu.make_async_copy(source, buffer, load_sem.at[n])
        for n, (source, buffer) in enumerate(zip(sources, buffers))
    ]
    for load in loads:
        load.start()
    d_ref, wq_ref, wk_ref, wv_ref, dmid_ref, hid_ref, norm_ref, dlog_ref = buffers
    key_at = KV_HEADS * ROWS_Q
    value_at = key_at + KV_HEADS * HEAD_DIM
    device = lax.axis_index("dp") * lax.axis_size("expert") + lax.axis_index("expert")

    def compute():
        for load in loads:
            load.wait()
        tokens = hid_ref.shape[0]
        size = tokens // 4
        ggain = jnp.zeros(gain_ref.shape, F32)
        for r in range(4):
            rows = slice(r * size, (r + 1) * size)
            d_norm = dot_nt(d_ref[rows, 0:key_at], wq_ref[...])
            d_norm += dot_nt(d_ref[rows, key_at:value_at], wk_ref[...])
            d_norm += dot_nt(d_ref[rows, value_at:], wv_ref[...])
            values = hid_ref[rows, :]
            inv = lax.rsqrt(jnp.mean(values * values, axis=-1, keepdims=True) + EPS)
            scaled = d_norm * gain_ref[...]
            ggain += jnp.sum(d_norm * values * inv, axis=0, keepdims=True)
            out_ref[rows, :] = (
                dmid_ref[rows, :]
                + inv * scaled
                - values * inv**3 * jnp.mean(values * scaled, axis=-1, keepdims=True)
            )
        columns = dot_tn(norm_ref[...], dlog_ref[...])
        lane = lax.broadcasted_iota(jnp.int32, columns.shape, 1)
        for n, row in enumerate((gmlp_ref[...], ggain)):
            turned = jnp.broadcast_to(row, (8, row.shape[1])).T[:, 0:1]
            columns = jnp.where(lane == LANES - 2 + n, turned, columns)
        held[...] = columns
        part = keep.shape[1]
        for b in range(keep.shape[0]):
            own = (2 * b) ^ device
            keep[b] = held[pl.ds(pl.multiple_of(own * part, part), part), :]
            own = own ^ 1
            send[b] = held[pl.ds(pl.multiple_of(own * part, part), part), :]

    return compute


def plan_last(arrays, gain, ggain_mlp, blocks):
    vmem = pl.BlockSpec(memory_space=pltpu.VMEM)
    tokens = arrays[0].shape[0]
    small = pltpu.VMEM((blocks // 2, WIDTH // blocks, LANES), F32)
    scratch = [small, small, pltpu.VMEM((WIDTH, LANES), F32)]
    scratch += [pltpu.VMEM(array.shape, array.dtype) for array in arrays]
    scratch.append(pltpu.SemaphoreType.DMA((len(arrays),)))
    return (
        (gain[None], ggain_mlp) + arrays,
        [vmem] * 2 + [hbm] * len(arrays),
        [jax.ShapeDtypeStruct((tokens, WIDTH), F32)],
        scratch,
        last_work,
    )


def stack_swap(values, bit):
    return jnp.concatenate([values, swap_bit(values, bit)], axis=0)


MESH = pl.DeviceIdType.MESH


def peer_of(bit):
    axis, mask = bit
    return {axis: lax.axis_index(axis) ^ mask}


def greet(ids):
    barrier = pltpu.get_barrier_semaphore()
    for device in ids:
        pl.semaphore_signal(barrier, inc=1, device_id=device, device_id_type=MESH)
    pl.semaphore_wait(barrier, len(ids))


GATHER_BITS = (X_BIT, ZL_BIT, C_BIT)


def one_hot(slots, rows):
    experts, tokens = slots.shape
    wide = jnp.broadcast_to(slots[:, None, :], (experts, SLOTS, tokens))
    rank = lax.broadcasted_iota(jnp.int32, (experts, SLOTS, tokens), 1).astype(F32)
    return (wide == rank).astype(F32).reshape(rows, tokens)


def gather_kernel(x_ref, *refs):
    blocks, maps_ref, wr_ref = refs[0:4], refs[4], refs[5]
    x_slots, g_slots, gates_ref, local_ref = refs[6:10]
    all_ref, other, all_maps_ref, stage = refs[10:14]
    send_sem, recv_sem, more_send, more_recv, store_sem = refs[14:]
    greet([peer_of(bit) for bit in GATHER_BITS])
    half = x_ref.shape[0] // 2
    copies = []

    def send(source, slot, rows, bit):
        n = len(copies)
        copy = pltpu.make_async_remote_copy(
            src_ref=source if rows is None else source.at[rows],
            dst_ref=all_ref.at[slot] if rows is None else all_ref.at[slot, rows],
            send_sem=send_sem.at[n],
            recv_sem=recv_sem.at[n],
            device_id=peer_of(bit),
            device_id_type=MESH,
        )
        copy.start()
        copies.append(copy)
        return copy

    top, low = pl.ds(0, half), pl.ds(half, half)
    x_top = send(x_ref, 1, top, X_BIT)
    z_low = send(x_ref, 2, low, ZL_BIT)
    x_low = send(x_ref, 1, low, X_BIT)
    z_top = send(x_ref, 2, top, ZL_BIT)
    pairs = [(maps_ref, all_maps_ref.at[pl.ds(4, 4)])]
    pairs += [(block, other.at[n]) for n, block in enumerate(blocks)]
    crossed = []
    for n, (block, there) in enumerate(pairs):
        copy = pltpu.make_async_remote_copy(
            src_ref=block,
            dst_ref=there,
            send_sem=more_send.at[n],
            recv_sem=more_recv.at[n],
            device_id=peer_of(C_BIT),
            device_id_type=MESH,
        )
        copy.start()
        crossed.append(copy)
    cross_own = send(x_ref, 4, None, C_BIT)
    all_maps_ref[0:4] = maps_ref[...]
    column = lax.axis_index("expert")
    experts = x_slots.shape[0]
    rows = experts * SLOTS
    depth = stage.shape[0]
    stores = []

    def own_rows(table):
        picked = jnp.zeros((experts, table.shape[1]), F32)
        for n in range(table.shape[0] // experts):
            picked = jnp.where(column == n, table[n * experts : (n + 1) * experts], picked)
        return picked

    def put(source, values, target, pick):
        side = len(stores) % depth
        if len(stores) >= depth:
            stores[-depth].wait()
        for n in range(WIDTH // CHUNK):
            cols = slice(n * CHUNK, (n + 1) * CHUNK)
            got = dot_nn(pick, values[:, cols]).astype(BF)
            stage[side, :, :, cols] = got.reshape(experts, SLOTS, CHUNK)
        store = pltpu.make_async_copy(
            stage.at[side], target.at[:, pl.ds(source * SLOTS, SLOTS)], store_sem.at[side]
        )
        store.start()
        stores.append(store)

    def put_g(source, values):
        pick = one_hot(own_rows(all_maps_ref[source]), rows)
        put(source, values, g_slots, pick.astype(BF))

    def put_x(source, values):
        slot_map = all_maps_ref[source]
        chosen = slot_map >= 0.0
        logits = dot_nt(wr_ref[...], values[...])[0 : slot_map.shape[0]]
        logits = jnp.where(chosen, logits, MASKED)
        raised = jnp.exp(logits - jnp.max(logits, axis=0, keepdims=True))
        raised = jnp.where(chosen, raised, 0.0)
        gates = own_rows(raised / jnp.sum(raised, axis=0, keepdims=True))
        slots = own_rows(slot_map)
        local_ref[source] = slots
        pick = one_hot(slots, rows)
        wide = jnp.broadcast_to(gates[:, None, :], (experts, SLOTS, gates.shape[1]))
        of_rows = jnp.sum(pick * wide.reshape(rows, gates.shape[1]), axis=1, keepdims=True)
        gates_ref[:, source * SLOTS : (source + 1) * SLOTS, :] = of_rows.reshape(experts, SLOTS, 1)
        put(source, values, x_slots, pick.astype(BF))

    put_x(0, x_ref)
    put_g(0, blocks[0])
    put_g(1, blocks[1])
    x_top.wait_recv()
    far_top = send(all_ref.at[1], 3, top, ZL_BIT)
    z_low.wait_recv()
    far_low = send(all_ref.at[2], 3, low, X_BIT)
    put_g(2, blocks[2])
    put_g(3, blocks[3])
    for copy in crossed:
        copy.wait_recv()
    cross_own.wait_recv()
    put_x(4, all_ref.at[4])
    put_g(4, other.at[0])
    put_g(5, other.at[1])
    put_g(6, other.at[2])
    x_low.wait_recv()
    cross_x = send(all_ref.at[1], 5, None, C_BIT)
    z_top.wait_recv()
    cross_z = send(all_ref.at[2], 6, None, C_BIT)
    put_x(1, all_ref.at[1])
    put_x(2, all_ref.at[2])
    cross_x.wait_recv()
    cross_z.wait_recv()
    put_x(5, all_ref.at[5])
    put_x(6, all_ref.at[6])
    put_g(7, other.at[3])
    far_top.wait_recv()
    far_low.wait_recv()
    cross_far = send(all_ref.at[3], 7, None, C_BIT)
    put_x(3, all_ref.at[3])
    cross_far.wait_recv()
    put_x(7, all_ref.at[7])
    for store in stores[-depth:]:
        store.wait()
    for copy in copies + crossed:
        copy.wait_send()


def run_gather(values, blocks, maps, wr_t, experts):
    vmem = pl.BlockSpec(memory_space=pltpu.VMEM)
    tokens, width = values.shape
    slots = jax.ShapeDtypeStruct((experts, 8 * SLOTS, width), values.dtype)
    return pl.pallas_call(
        gather_kernel,
        in_specs=[vmem] * 7,
        out_specs=(hbm, hbm, vmem, vmem),
        out_shape=(
            slots,
            slots,
            jax.ShapeDtypeStruct((experts, 8 * SLOTS, 1), F32),
            jax.ShapeDtypeStruct((8, experts, tokens), F32),
        ),
        scratch_shapes=[
            pltpu.VMEM((8, tokens, width), values.dtype),
            pltpu.VMEM((4, tokens, width), values.dtype),
            pltpu.VMEM((8,) + maps.shape[1:], maps.dtype),
            pltpu.VMEM((4, experts, SLOTS, width), values.dtype),
        ]
        + [pltpu.SemaphoreType.DMA((n,)) for n in (10, 10, 5, 5, 4)],
        compiler_params=pltpu.CompilerParams(
            collective_id=1, has_side_effects=True, vmem_limit_bytes=60 * MIB
        ),
        cost_estimate=cost(0, 150e6),
    )(values, *blocks, maps, wr_t)


def trade_peers(size):
    me = lax.axis_index("dp")
    return [{"dp": me ^ k} for k in range(size - 1, 0, -1)]


def trade_start(a_ref, out_ref, send_sem, recv_sem, local_sem):
    me = lax.axis_index("dp")
    copies = []
    for n, device in enumerate(trade_peers(a_ref.shape[0])):
        copy = pltpu.make_async_remote_copy(
            src_ref=a_ref.at[device["dp"]],
            dst_ref=out_ref.at[me],
            send_sem=send_sem.at[n],
            recv_sem=recv_sem.at[n],
            device_id=device,
            device_id_type=MESH,
        )
        copy.start()
        copies.append(copy)
    own = pltpu.make_async_copy(a_ref.at[me], out_ref.at[me], local_sem)
    own.start()
    return copies, own


def trade_end(copies, own):
    own.wait()
    for copy in copies:
        copy.wait_recv()
    for copy in copies:
        copy.wait_send()


class Rider:
    def __init__(self, bit, *terms, pieces=1, turns=(0,)):
        self.bit, self.pieces, self.turns = bit, pieces, turns
        self.arrays = [term[0] if isinstance(term, tuple) else term for term in terms]
        self.parts = [term[1] if isinstance(term, tuple) else None for term in terms]
        array, part = self.arrays[0], self.parts[0]
        shape = array.shape
        if part is not None:
            kept = [len(range(n)[k]) for k, n in zip(part, shape) if not isinstance(k, int)]
            shape = tuple(kept) + shape[len(part) :]
        self.shape = jax.ShapeDtypeStruct(shape, array.dtype)
        self.direct = len(terms) == 1 and part is None

    def scratch(self):
        if self.direct:
            return []
        buffer = pltpu.VMEM(self.shape.shape, self.shape.dtype)
        return [buffer] * (len(self.arrays) + 1)

    def plan(self):
        return (self.bit, self.pieces, self.turns, tuple(self.parts), self.direct)


def rider_inputs(riders):
    return [array for rider in riders for array in rider.arrays]


def rider_shapes(riders):
    return tuple(rider.shape for rider in riders)


def rider_scratch(riders):
    remote = max(sum(rider.pieces for rider in riders), 1)
    local = max(sum(len(rider.arrays) for rider in riders), 1)
    buffers = [buffer for rider in riders for buffer in rider.scratch()]
    return buffers + [pltpu.SemaphoreType.DMA((n,)) for n in (remote, remote, local)]


def add_rows(result, buffers):
    step = 16

    @pl.loop(0, result.shape[1] // step)
    def _(r):
        rows = pl.ds(pl.multiple_of(r * step, step), step)
        for i in range(result.shape[0]):
            total = buffers[0][i, rows, :].astype(F32)
            for buffer in buffers[1:]:
                total += buffer[i, rows, :].astype(F32)
            result[i, rows, :] = total.astype(result.dtype)


def ride_pieces(sources, targets, plans, scratch):
    send_sem, recv_sem, local_sem = scratch[-3:]
    starts, finishes, loads, used, source, local = [], [], [], 0, 0, 0
    for n, (bit, pieces, turns, parts, direct) in enumerate(plans):
        arrays = sources[source : source + len(parts)]
        source += len(parts)
        if direct:
            held = arrays[0]
            prepare = None
        else:
            buffers = scratch[used : used + len(parts)]
            held = scratch[used + len(parts)]
            used += len(parts) + 1
            copies = []
            for array, part, buffer in zip(arrays, parts, buffers):
                view = array if part is None else array.at[part]
                copy = pltpu.make_async_copy(view, buffer, local_sem.at[local])
                local += 1
                loads.append(copy)
                copies.append(copy)

            def prepare(copies=copies, held=held, buffers=buffers):
                for copy in copies:
                    copy.wait()
                add_rows(held, buffers)

        size = targets[n].shape[0] // pieces
        for m in range(pieces):
            at = pl.ds(m * size, size)

            def remote(n=n, at=at, slot=len(starts), bit=bit, held=held):
                return pltpu.make_async_remote_copy(
                    src_ref=held.at[at],
                    dst_ref=targets[n].at[at],
                    send_sem=send_sem.at[slot],
                    recv_sem=recv_sem.at[slot],
                    device_id=peer_of(bit),
                    device_id_type=MESH,
                )

            def start(remote=remote):
                remote().start()

            def finish(remote=remote):
                remote().wait()

            starts.append((prepare if m == 0 else None, start, turns))
            finishes.append(finish)
    return starts, finishes, loads


def all_peers(bits):
    size = lax.axis_size("dp")
    return trade_peers(size) + [peer_of(bit) for bit in bits if bit[0] == "expert"]


def trade_kernel(*refs, plans, work):
    inputs = sum(len(plan[3]) for plan in plans)
    more = 2 if work else 0
    a_ref, sources = refs[0], refs[1 : 1 + inputs]
    work_in, refs = refs[1 + inputs : 1 + inputs + more], refs[1 + inputs + more :]
    out_ref, targets = refs[0], refs[1 : 1 + len(plans)]
    work_out, refs = refs[1 + len(plans) : 1 + len(plans) + more], refs[1 + len(plans) + more :]
    send_sem, recv_sem, local_sem, *scratch = refs
    work_scratch = scratch[-6:] if work else ()
    scratch = scratch[:-6] if work else scratch
    bits = {plan[0] for plan in plans} | ({C_BIT} if work else set())
    greet(all_peers(sorted(bits)))
    trade = trade_start(a_ref, out_ref, send_sem, recv_sem, local_sem.at[0])
    starts, finishes, loads = ride_pieces(sources, targets, plans, scratch)
    for load in loads:
        load.start()
    if work:
        finishes.append(weight_grad(work_in, work_out, work_scratch))
    for prepare, start, _ in starts:
        if prepare is not None:
            prepare()
        start()
    if work:
        finishes[-1] = finishes[-1]()
    trade_end(*trade)
    for finish in finishes:
        finish()


def weight_grad(inputs, outputs, scratch):
    keep, got = outputs
    left, right, sent, held, load_sem, cross_sem = scratch
    loads = [
        pltpu.make_async_copy(source, target, load_sem.at[n])
        for n, (source, target) in enumerate(zip(inputs, (left, right)))
    ]
    for load in loads:
        load.start()
    blocks, part, width = keep.shape
    step = held.shape[1]
    device = lax.axis_index("dp") * lax.axis_size("expert") + lax.axis_index("expert")

    def compute():
        for load in loads:
            load.wait()

        @pl.loop(0, width // step)
        def _(n):
            cols = pl.ds(pl.multiple_of(n * step, step), step)
            held[...] = dot_tn(left[...], right[:, cols]).astype(BF)
            for b in range(blocks):
                own = (2 * b) ^ device
                keep[b, :, cols] = held[pl.ds(pl.multiple_of(own * part, part), part), :]
                own = own ^ 1
                sent[b, :, cols] = held[pl.ds(pl.multiple_of(own * part, part), part), :]

        copy = pltpu.make_async_remote_copy(
            src_ref=sent,
            dst_ref=got,
            send_sem=cross_sem.at[0],
            recv_sem=cross_sem.at[1],
            device_id=peer_of(C_BIT),
            device_id_type=MESH,
        )
        copy.start()
        return copy.wait

    return compute


def run_trade(values, number, riders=(), work=(), blocks=0, mib=60):
    size = values.shape[0]
    inputs = rider_inputs(riders)
    vmem = pl.BlockSpec(memory_space=pltpu.VMEM)
    shapes, specs, scratch = [], [], []
    if work:
        left, right = work
        rows, width = left.shape[1], right.shape[1]
        half = jax.ShapeDtypeStruct((blocks // 2, rows // blocks, width), BF)
        shapes, specs = [half, half], [vmem, hbm]
        scratch = [
            pltpu.VMEM(left.shape, left.dtype),
            pltpu.VMEM(right.shape, right.dtype),
            pltpu.VMEM(half.shape, BF),
            pltpu.VMEM((rows, 256), BF),
            pltpu.SemaphoreType.DMA((2,)),
            pltpu.SemaphoreType.DMA((2,)),
        ]
    out = pl.pallas_call(
        functools.partial(
            trade_kernel, plans=tuple(rider.plan() for rider in riders), work=bool(work)
        ),
        in_specs=[hbm] * (1 + len(inputs) + len(work)),
        out_specs=(hbm,) * (1 + len(riders)) + tuple(specs),
        out_shape=(jax.ShapeDtypeStruct(values.shape, values.dtype),)
        + rider_shapes(riders)
        + tuple(shapes),
        scratch_shapes=[pltpu.SemaphoreType.DMA((n,)) for n in (size - 1, size - 1, 1)]
        + rider_scratch(riders)
        + scratch,
        compiler_params=pltpu.CompilerParams(
            collective_id=number, has_side_effects=True, vmem_limit_bytes=mib * MIB
        ),
        cost_estimate=cost(0, 170e6),
    )(values, *inputs, *work)
    return out if riders or work else out[0]


def first_kernel(a_ref, rank_ref, turned_ref, out_ref, slot_ref, send_sem, recv_sem, local_sem, *, far):
    greet(trade_peers(a_ref.shape[0]))
    trade = trade_start(a_ref, out_ref, send_sem, recv_sem, local_sem.at[0])
    for e in range(rank_ref.shape[0]):
        own = rank_ref[e : e + 1, :]
        smaller = (turned_ref[:, e : e + 1] < own).astype(F32)
        before = jnp.sum(smaller, axis=0, keepdims=True)
        slot_ref[e : e + 1, :] = jnp.where(own < far, jnp.minimum(before, SLOTS), -1.0)
    trade_end(*trade)


def run_first(values, rank_map, turned, far):
    size = values.shape[0]
    vmem = pl.BlockSpec(memory_space=pltpu.VMEM)
    return pl.pallas_call(
        functools.partial(first_kernel, far=far),
        in_specs=[hbm, vmem, vmem],
        out_specs=(hbm, vmem),
        out_shape=(
            jax.ShapeDtypeStruct(values.shape, values.dtype),
            jax.ShapeDtypeStruct(rank_map.shape, F32),
        ),
        scratch_shapes=[pltpu.SemaphoreType.DMA((n,)) for n in (size - 1, size - 1, 1)],
        compiler_params=pltpu.CompilerParams(
            collective_id=2, has_side_effects=True, vmem_limit_bytes=60 * MIB
        ),
        cost_estimate=cost(0, 170e6),
    )(values, rank_map, turned)


def reduce_chain(slot, part, keep_ref, send_ref, outs, acc, got, staged, send_sem, recv_sem):
    first, bits, row, rows, column, columns, order = part
    blocks = keep_ref.shape[0]
    stages = len(bits) + 1
    low = send_ref.dtype
    at = (pl.ds(row, rows), pl.ds(column, columns))
    copies = []

    def exchange(source, target, bit):
        n = slot + len(copies)
        copy = pltpu.make_async_remote_copy(
            src_ref=source,
            dst_ref=target,
            send_sem=send_sem.at[n],
            recv_sem=recv_sem.at[n],
            device_id=peer_of(bit),
            device_id_type=MESH,
        )
        copy.start()
        copies.append(copy)

    live = list(range(blocks))
    base_got, base_sent = 0, 0
    exchange(send_ref.at[(slice(None),) + at], got.at[(pl.ds(0, blocks),) + at], first)
    yield
    for stage in range(stages):
        copies[-1].wait_recv()

        def total(position):
            index = live[position]
            kept = keep_ref[(index,) + at].astype(F32) if stage == 0 else acc[(index,) + at]
            return kept + got[(base_got + position,) + at].astype(F32)

        if stage == stages - 1:
            low_column = 0
            for out_ref in outs:
                if low_column <= column < low_column + out_ref.shape[1]:
                    out_ref[at[0], pl.ds(column - low_column, columns)] = total(0)
                low_column += out_ref.shape[1]
            break
        mask = 1 << order[stage]
        rest = [i for i in live if not i & mask]
        for m, i in enumerate(rest):
            staged[(base_sent + m,) + at] = total(live.index(i ^ mask)).astype(low)
        exchange(
            staged.at[(pl.ds(base_sent, len(rest)),) + at],
            got.at[(pl.ds(base_got + len(live), len(rest)),) + at],
            bits[order[stage]],
        )
        for i in rest:
            acc[(i,) + at] = total(live.index(i))
        base_got += len(live)
        base_sent += len(rest)
        live = rest
        yield
    for copy in copies:
        copy.wait_send()


def reduce_kernel(*refs, jobs, plans, work):
    size = len(jobs)
    given = size - 1 if work else size
    inputs = sum(len(plan[3]) for plan in plans)
    keeps, sends, refs = list(refs[:given]), list(refs[given : 2 * given]), refs[2 * given :]
    sources, refs = refs[:inputs], refs[inputs:]
    compute = None
    if work:
        counts, body = work
        work_in, refs = refs[: counts[0]], refs[counts[0] :]
        work_out, refs = refs[: counts[1]], refs[counts[1] :]
        work_scratch, refs = refs[-counts[2] :], refs[: -counts[2]]
        compute = body(work_in, work_out, work_scratch)
        keeps.append(work_scratch[0])
        sends.append(work_scratch[1])
    outs = []
    for _, _, _, widths in jobs:
        outs.append(refs[: len(widths)])
        refs = refs[len(widths) :]
    targets, scratch = refs[: len(plans)], refs[len(plans) :]
    send_sem, recv_sem = scratch[3 * size : 3 * size + 2]
    used = {bit for first, bits, *_ in jobs for bit in (first,) + bits}
    used |= {plan[0] for plan in plans}
    starts, finishes, loads = ride_pieces(sources, targets, plans, scratch[3 * size + 2 :])
    for load in loads:
        load.start()
    greet([peer_of(bit) for bit in sorted(used)])
    chains, late, slot = [], [], 0
    for n, (first, bits, parts, _) in enumerate(jobs):
        for part in parts:
            (late if n >= given else chains).append(
                reduce_chain(
                    slot,
                    (first, bits) + part,
                    keeps[n],
                    sends[n],
                    outs[n],
                    *scratch[3 * n : 3 * n + 3],
                    send_sem,
                    recv_sem,
                )
            )
            slot += len(bits) + 1
    index = lax.axis_index("dp")
    outer = (index // BIT_ZH) % 2 == (index // BIT_ZL) % 2
    turn, last = 0, max([0] + [n for _, _, turns in starts for n in turns])
    while chains or turn <= last:
        rest = []
        for chain in chains:
            try:
                next(chain)
                rest.append(chain)
            except StopIteration:
                pass
        chains = rest
        for prepare, start, turns in starts:
            if prepare is not None and min(turns) == turn:
                prepare()
            if len(set(turns)) == 1:
                if turns[0] == turn:
                    start()
            else:
                for n, side in enumerate((outer, jnp.logical_not(outer))):
                    if turns[n] == turn:
                        pl.when(side)(start)
        if turn == 0 and work:
            compute()
            chains += late
        turn += 1
    for finish in finishes:
        finish()


def run_reduce(pairs, jobs, number, riders=(), work=None):
    slots = sum(len(parts) * (len(bits) + 1) for _, bits, parts, _ in jobs)
    vmem = pl.BlockSpec(memory_space=pltpu.VMEM)
    scratch, shapes = [], []
    arrays, work_specs, work_shapes, work_scratch, body = work or ((), (), (), (), None)
    late = [(shape, shape) for shape in work_scratch[:1]]
    for (keep, send), (_, _, _, widths) in zip(list(pairs) + late, jobs):
        blocks, rows, cols = keep.shape
        scratch += [
            pltpu.VMEM((blocks, rows, cols), F32),
            pltpu.VMEM((2 * blocks - 1, rows, cols), send.dtype),
            pltpu.VMEM((max(blocks - 1, 1), rows, cols), send.dtype),
        ]
        shapes += [jax.ShapeDtypeStruct((rows, width), F32) for width in widths]
    inputs = rider_inputs(riders)
    return pl.pallas_call(
        functools.partial(
            reduce_kernel,
            jobs=jobs,
            plans=tuple(rider.plan() for rider in riders),
            work=((len(arrays), len(work_shapes), len(work_scratch)), body) if work else None,
        ),
        in_specs=[vmem] * len(pairs) + [hbm] * (len(pairs) + len(inputs)) + list(work_specs),
        out_specs=(vmem,) * (len(work_shapes) + len(shapes)) + (hbm,) * len(riders),
        out_shape=tuple(work_shapes) + tuple(shapes) + rider_shapes(riders),
        scratch_shapes=scratch
        + [pltpu.SemaphoreType.DMA((n,)) for n in (slots, slots)]
        + rider_scratch(riders)
        + list(work_scratch),
        compiler_params=pltpu.CompilerParams(
            collective_id=number, has_side_effects=True, vmem_limit_bytes=60 * MIB
        ),
        cost_estimate=cost(0, 170e6),
    )(*(keep for keep, _ in pairs), *(send for _, send in pairs), *inputs, *arrays)


def sum_pair(kept, received):
    return kept.astype(F32) + received.astype(F32)


def add_low(*terms):
    return sum(term.astype(F32) for term in terms).astype(BF)


def join_kernel(place_ref, *refs):
    outs = refs[-3:]
    zl_at = place_ref[0]

    def total(*terms):
        return sum(term.astype(F32) for term in terms)

    def flat(ref):
        return ref[(0,) * (ref.ndim - 2)]

    def work(parts, part):
        for n in range(2):
            keep, got, more, other = parts[4 * n : 4 * n + 4]
            mine = total(*(flat(term) for term in (keep, got, more)))
            across = flat(other).astype(F32)
            for m in range(2):
                cols = slice(m * LANES, (m + 1) * LANES)
                at = pl.multiple_of((2 * m + zl_at) * LANES, LANES)
                outs[n][part, 0, :, pl.ds(at, LANES)] = mine[:, cols]
                at = pl.multiple_of((2 * m + 1 - zl_at) * LANES, LANES)
                outs[n][part, 0, :, pl.ds(at, LANES)] = across[:, cols]
        keep, got, more = parts[8:]
        outs[2][part, 0] = total(*(flat(term) for term in (keep, got, more)))

    work(refs[0:11], 0)
    work(refs[11:22], 1)


def run_join(place, halves):
    _, _, experts, rows, cols = halves[0][0].shape
    wide_rows, width = halves[0][8].shape[2:]
    arrays, specs = [], []
    for half in halves:
        for operand in half:
            array, lead = operand if isinstance(operand, tuple) else (operand, 0)
            extra = array.ndim - 3
            at = (lead,) + (0,) * (extra - 1) if extra else ()
            arrays.append(array)
            specs.append(
                pl.BlockSpec(
                    (1,) * (extra + 1) + array.shape[-2:],
                    lambda i, p, at=at: at + (i, 0, 0),
                )
            )
    shapes = [(rows, 2 * cols), (rows, 2 * cols), (wide_rows, width)]
    return pl.pallas_call(
        join_kernel,
        grid_spec=pltpu.PrefetchScalarGridSpec(
            num_scalar_prefetch=1,
            grid=(experts,),
            in_specs=specs,
            out_specs=tuple(
                pl.BlockSpec((2, 1) + shape, lambda i, p: (0, i, 0, 0)) for shape in shapes
            ),
        ),
        out_shape=tuple(jax.ShapeDtypeStruct((2, experts) + shape, F32) for shape in shapes),
        compiler_params=params(60, ("arbitrary",)),
        cost_estimate=cost(1e6, 26e6),
    )(place, *arrays)


def fast_body(
    hidden_in,
    gain_attn,
    w_query,
    w_key,
    w_value,
    w_output,
    gain_mlp,
    w_router,
    w_gate,
    w_up,
    w_down,
    expert_ids,
    slot_order,
    grad_out,
):
    inputs = hidden_in[0]
    cotangent = grad_out[0]
    chosen = expert_ids[0]
    tokens = inputs.shape[0]
    top = chosen.shape[1]
    local_experts = w_gate.shape[0]
    peers = lax.axis_size("expert")
    all_experts = local_experts * peers
    shards = lax.axis_size("dp")
    length = shards * tokens
    devices = shards * peers
    index = lax.axis_index("dp")
    column = lax.axis_index("expert")
    y_at = index % 2
    zl_at = (index // 2) % 2
    zh_at = index // 4
    place = jnp.stack(
        [zl_at, y_at, zl_at, zh_at, column * local_experts, index * peers + column]
    ).astype(jnp.int32)

    ranks = slot_order[0, 0].reshape(tokens, top)
    far = tokens * top
    names = jnp.arange(all_experts, dtype=jnp.int32)
    match = chosen.T[None] == names[:, None, None]
    rank_map = jnp.min(jnp.where(match, ranks.T[None], far), axis=1).astype(F32)
    turned = rank_map.T
    map_rows = jnp.pad(
        jnp.where(turned < far, 0.0, -1.0),
        ((0, 0), (0, LANES - all_experts)),
        constant_values=-1.0,
    )
    wr_pad = jnp.pad(w_router, ((0, 0), (0, LANES - all_experts)))
    wr_t = jnp.pad(w_router.T, ((0, LANES - all_experts), (0, 0)))

    half = HEAD_DIM // 2
    frequency = jnp.exp(-math.log(10000.0) * jnp.arange(half, dtype=F32) * 2.0 / HEAD_DIM)
    own_angles = (index * tokens + jnp.arange(tokens, dtype=jnp.int32)).astype(F32)[:, None] * frequency
    cos_own, sin_own = jnp.cos(own_angles), jnp.sin(own_angles)
    cos_tab = jnp.concatenate([cos_own] * 4, axis=1)
    sin_tab = jnp.concatenate([-sin_own, sin_own] * 2, axis=1)
    angles = frequency[:, None] * jnp.arange(length, dtype=jnp.int32).astype(F32)[None]
    cos_t, sin_t = jnp.cos(angles), jnp.sin(angles)

    normed, pack, g_own = run_pre(
        inputs, gain_attn, w_query, w_key, w_value, cos_tab, sin_tab, cotangent
    )
    pack, slot_map = run_first(pack, rank_map, turned, float(far))
    pack, slot_map, g_late = fence(pack, slot_map, g_own)
    g_x = swap_bit(g_own, X_BIT)
    g_z = swap_bit(g_late, ZL_BIT)
    maps = stack_swap(slot_map[None], X_BIT)
    out, out_t, lse = run_forward(pack)
    out, g_x, g_z, maps = fence(out, g_x, g_z, maps)
    g_zx = swap_bit(g_z, X_BIT)
    maps = stack_swap(maps, ZL_BIT)
    att = run_trade(out, 3, mib=16)
    att, g_zx, maps = fence(att, g_zx, maps)
    middle, normed_two, att_full = run_mid(att, w_output, inputs, gain_mlp)
    x_slots, g_slots, gates, maps = run_gather(
        normed_two, (g_own, g_x, g_z, g_zx), maps, wr_t, local_experts
    )
    expert_args = (place, x_slots, g_slots, gates, maps, w_gate, w_up, w_down)
    first = run_experts(*expert_args)
    gate_ka, gate_s0, gate_s1, early, up_ka, up_s0, up_s1, down_ka, down_s0, down_s1 = first[4:]
    down_ya = swap_bit(down_s1, Y_BIT)
    gate_ya = swap_bit(gate_s1, Y_BIT)
    early = swap_bit(early, ZH_BIT)
    mix_keep, mix_send, dx_keep, dx_send, *second = run_experts(*expert_args, prior=first[:4])
    gate_kb, gate_t0, gate_t1, _, up_kb, up_t0, up_t1, down_kb, down_t0, down_t1 = second
    down_ga = swap_bit(down_s0, Y_BIT)
    dx_send, down_ya, gate_ya, early = fence(dx_send, down_ya, gate_ya, early)
    gate_s0 = jnp.stack([gate_s0[0], add_low(gate_s0[1], early[1])])
    quarter = tokens // 4
    extra = dx_keep.shape[2]
    token_parts = tuple(
        (n * quarter, quarter, 0, extra, (1, 0) if n < 2 else (0, 1)) for n in (2, 0, 3, 1)
    )
    dx_sum, up_ya, gate_ga, mix_got, down_ma = run_reduce(
        ((dx_keep, dx_send),),
        ((C_BIT, (X_BIT, ZL_BIT), token_parts, (extra,)),),
        6,
        riders=(
            Rider(Y_BIT, up_s1),
            Rider(Y_BIT, gate_s0),
            Rider(C_BIT, mix_send, turns=(1,)),
            Rider(ZH_BIT, (down_ka, (1,)), down_ya, turns=(1, 0)),
        ),
    )
    dx_sum, gate_ya, down_ga, gate_t1 = fence(dx_sum, gate_ya, down_ga, gate_t1)
    gate_ma = swap_bit(add_low(gate_ka[1, 0], gate_ya[0]), ZH_BIT)
    gate_yb = swap_bit(gate_t1, Y_BIT)
    d_att, d_middle, d_low, d_log, ggain_mlp = run_post(
        dx_sum, middle, cotangent, normed_two, wr_pad, map_rows, gain_mlp, w_output
    )
    mix_keep = mix_keep.reshape(2, 2, tokens, WIDTH)
    mix_got = mix_got.reshape(2, 2, tokens, WIDTH)
    every = slice(None)
    d_out, up_yb, up_za, gate_oa, mix_x, out_keep, out_got = run_trade(
        d_att,
        4,
        work=(att_full, d_low),
        blocks=devices,
        riders=(
            Rider(Y_BIT, up_t1),
            Rider(ZH_BIT, (up_ka, (1, 1)), (up_ya, (1,))),
            Rider(ZL_BIT, (gate_ka, (0, 1)), (early, (0,)), (gate_ga, (1,))),
            Rider(X_BIT, (mix_keep, (every, 1)), (mix_got, (every, 1))),
        ),
    )
    split = (8, 2, WIDTH // devices, WIDTH)
    out_keep, out_got = out_keep.reshape(split), out_got.reshape(split)
    up_ga, down_yb, up_late, gate_late, gate_ma, d_out = fence(
        up_s0, down_t1, up_ya, gate_yb, gate_ma, d_out
    )
    both = jnp.stack([add_low(up_ka[1, 0], up_late[0]), add_low(gate_kb[1, 1], gate_late[1])])
    both = swap_bit(both, ZH_BIT)
    up_ga = swap_bit(up_ga, Y_BIT)
    down_yb = swap_bit(down_yb, Y_BIT)
    d_pack = run_backward(pack, d_out, out_t, lse, cos_t, sin_t)
    d_pack, both, up_ga, down_yb = fence(d_pack, both, up_ga, down_yb)
    d_pack, gate_gb, up_gb, gate_mb, up_zb, mix_z, out_x, up_oa = run_trade(
        d_pack,
        5,
        riders=(
            Rider(Y_BIT, gate_t0),
            Rider(Y_BIT, up_t0),
            Rider(ZH_BIT, (gate_kb, (1, 0)), (gate_yb, (0,))),
            Rider(ZH_BIT, (up_kb, (1, 1)), (up_yb, (1,))),
            Rider(
                ZL_BIT,
                (mix_keep, (slice(1, 2), 0)),
                (mix_got, (slice(1, 2), 0)),
                (mix_x, (slice(1, 2),)),
            ),
            Rider(X_BIT, (out_keep, (every, 1)), (out_got, (every, 1))),
            Rider(ZL_BIT, (up_ka, (0, 1)), (up_ga, (1,)), (up_za, (every,))),
        ),
    )
    d_pack, up_yb, down_yb, gate_gb, down_t0, mix_z, out_x = fence(
        d_pack, up_yb, down_yb, gate_gb, down_t0, mix_z, out_x
    )
    other = jnp.stack(
        [add_low(gate_kb[0, 1], gate_gb[1], both[1]), add_low(up_kb[0, 1], up_gb[1], up_zb)]
    )
    other = swap_bit(other, ZL_BIT)
    down_mb = swap_bit(add_low(down_kb[1], down_yb), ZH_BIT)
    down_gb = swap_bit(down_t0, Y_BIT)
    d_full, qkv_keep, qkv_send = run_qkvgrad(place, normed, d_pack, devices)
    mixed = sum_pair(mix_keep[0, 0], mix_got[0, 0]) + sum_pair(mix_x[0], mix_z[0])
    hidden_out = middle + mixed
    rows = WIDTH // devices
    out_held = add_low(out_keep[:, 0], out_got[:, 0], out_x).reshape(4, 2, rows, WIDTH)
    out_first, out_second = out_held[:, 0], out_held[:, 1]
    qkv_send, out_second, hidden_out = fence(qkv_send, out_second, hidden_out)
    qkv_parts = (
        (0, rows, 0, 768, (0, 1, 2, 3)),
        (0, rows, 768, 768, (1, 0, 2, 3)),
        (0, rows, 1536, 512, (0, 1, 2, 3)),
        (0, rows, 2048, 512, (1, 0, 2, 3)),
    )
    dense_bits = (X_BIT, Y_BIT, ZL_BIT, ZH_BIT)
    last = (d_full, w_query, w_key, w_value, d_middle, inputs, normed_two, d_log)
    grad_in, query_total, key_total, value_total, output_total, small, up_mb = run_reduce(
        ((qkv_keep, qkv_send), (out_first, out_second)),
        (
            (C_BIT, dense_bits, qkv_parts, (WIDTH, KV_HEADS * HEAD_DIM, KV_HEADS * HEAD_DIM)),
            (Y_BIT, (ZL_BIT, ZH_BIT), ((0, rows, 0, WIDTH, (0, 1)),), (WIDTH,)),
            (C_BIT, dense_bits, ((0, rows, 0, LANES, (0, 1, 2, 3)),), (LANES,)),
        ),
        7,
        riders=(Rider(ZH_BIT, (up_kb, (1, 0)), (up_yb, (0,))),),
        work=plan_last(last, gain_attn, ggain_mlp, devices),
    )
    query_total, small, down_mb, down_gb, other = fence(
        query_total, small, down_mb, down_gb, other
    )
    joined = run_join(
        place,
        (
            (gate_ka, gate_ga, gate_ma, gate_oa, up_ka, up_ga, (both, 0), up_oa)
            + (down_ka, down_ga, down_ma),
            (gate_kb, gate_gb, gate_mb, (other, 0), up_kb, up_gb, up_mb, (other, 1))
            + (down_kb, down_gb, down_mb),
        ),
    )
    gate_total, up_total, down_total = [
        total.reshape((local_experts,) + total.shape[2:]) for total in joined
    ]
    return (
        hidden_out[None],
        grad_in[None],
        small[:, LANES - 1],
        query_total,
        key_total,
        value_total,
        output_total,
        small[:, LANES - 2],
        small[:, :all_experts],
        gate_total,
        up_total,
        down_total,
    )


def fits(mesh):
    return mesh.shape["dp"] == KV_HEADS and mesh.shape["expert"] == 4


def solution(mesh):
    in_specs = (
        P("expert", "dp", None),
        P(),
        P(),
        P(),
        P(),
        P(),
        P(),
        P(),
        P("expert", None, None),
        P("expert", None, None),
        P("expert", None, None),
        P("expert", "dp", None),
        P("expert", "dp", None),
        P("expert", "dp", None),
    )
    out_specs = (
        P("expert", "dp", None),
        P("expert", "dp", None),
        P(("dp", "expert")),
        P(("dp", "expert"), None),
        P(("dp", "expert"), None),
        P(("dp", "expert"), None),
        P(("dp", "expert"), None),
        P(("dp", "expert")),
        P(("dp", "expert"), None),
        P("expert", "dp", None),
        P("expert", "dp", None),
        P("expert", "dp", None),
    )
    chosen = fast_body if fits(mesh) else body
    return jax.shard_map(chosen, mesh=mesh, in_specs=in_specs, out_specs=out_specs, check_vma=False)
```

```python
import functools
import math

import jax
import jax.numpy as jnp
from jax import lax
from jax.experimental import pallas as pl
from jax.experimental.pallas import tpu as pltpu
from jax.sharding import PartitionSpec as P

HEADS = 24
KV_HEADS = 8
HEAD_DIM = 64


EPS = 1e-05
MASKED = -1e30


def rotary_tables(positions):
    half = HEAD_DIM // 2
    frequency = jnp.exp(-math.log(10000.0) * jnp.arange(half, dtype=jnp.float32) * 2.0 / HEAD_DIM)
    angles = positions.astype(jnp.float32)[:, None] * frequency[None, :]
    return (jnp.cos(angles)[:, None, :], jnp.sin(angles)[:, None, :])


def rotate(values, cosine, sine):
    half = values.shape[-1] // 2
    first = values[..., :half]
    second = values[..., half:]
    return jnp.concatenate(
        [first * cosine - second * sine, second * cosine + first * sine], axis=-1
    )


def rotate_back(values, cosine, sine):
    half = values.shape[-1] // 2
    first = values[..., :half]
    second = values[..., half:]
    return jnp.concatenate(
        [first * cosine + second * sine, second * cosine - first * sine], axis=-1
    )


def assign_slots(row_chosen, row_ranks, all_experts, capacity):
    pairs = row_chosen.shape[0]
    by_rank = jnp.zeros((pairs,), jnp.int32).at[row_ranks].set(jnp.arange(pairs, dtype=jnp.int32))
    ordered = row_chosen[by_rank]
    table = (ordered[:, None] == jnp.arange(all_experts, dtype=jnp.int32)[None, :]).astype(
        jnp.int32
    )
    before = jnp.sum(table * (jnp.cumsum(table, axis=0) - 1), axis=1)
    slot = before[row_ranks]
    target = jnp.where(slot < capacity, row_chosen * capacity + slot, all_experts * capacity)
    owner = (
        jnp.full((all_experts * capacity,), pairs, jnp.int32)
        .at[target]
        .set(jnp.arange(pairs, dtype=jnp.int32), mode="drop")
    )
    return (target, owner)


def body(
    hidden_in,
    gain_attn,
    w_query,
    w_key,
    w_value,
    w_output,
    gain_mlp,
    w_router,
    w_gate,
    w_up,
    w_down,
    expert_ids,
    slot_order,
    grad_out,
):
    inputs = hidden_in[0]
    cotangent = grad_out[0]
    chosen = expert_ids[0]
    tokens, width = inputs.shape
    top = chosen.shape[1]
    local_experts = w_gate.shape[0]
    peers = lax.axis_size("expert")
    all_experts = local_experts * peers
    pairs = tokens * top
    capacity = pairs // all_experts
    shards = lax.axis_size("dp")
    index = lax.axis_index("dp")
    length = shards * tokens
    block = math.gcd(length, 512)
    groups = HEADS // KV_HEADS
    scale = HEAD_DIM ** (-0.5)
    query_pos = index * tokens + jnp.arange(tokens, dtype=jnp.int32)
    cosine, sine = rotary_tables(query_pos)
    count = ((index + 1) * tokens + block - 1) // block
    inv_one = lax.rsqrt(jnp.mean(inputs * inputs, axis=-1, keepdims=True) + EPS)
    normed = (inputs * inv_one * gain_attn).astype(jnp.bfloat16)
    query_pre = jnp.dot(normed, w_query, preferred_element_type=jnp.float32).reshape(
        tokens, HEADS, HEAD_DIM
    )
    queries = rotate(query_pre, cosine, sine).astype(jnp.bfloat16)
    key_pre = jnp.dot(normed, w_key, preferred_element_type=jnp.float32).reshape(
        tokens, KV_HEADS, HEAD_DIM
    )
    keys_low = rotate(key_pre, cosine, sine).astype(jnp.bfloat16)
    values_low = (
        jnp.dot(normed, w_value, preferred_element_type=jnp.float32)
        .astype(jnp.bfloat16)
        .reshape(tokens, KV_HEADS, HEAD_DIM)
    )
    keys_all, values_all = (
        lax.all_gather(keys_low, "dp", axis=0, tiled=True),
        lax.all_gather(values_low, "dp", axis=0, tiled=True),
    )
    query_groups = queries.reshape(tokens, KV_HEADS, groups, HEAD_DIM)

    def block_scores(key_block, start):
        raw = (
            jnp.einsum(
                "qkgd,skd->kgqs", query_groups, key_block, preferred_element_type=jnp.float32
            )
            * scale
        )
        key_pos = start + jnp.arange(block, dtype=jnp.int32)
        allowed = key_pos[None, :] <= query_pos[:, None]
        return jnp.where(allowed, raw, MASKED)

    def stats_step(step, carry):
        running, total = carry
        scores = block_scores(
            lax.dynamic_slice_in_dim(keys_all, step * block, block, 0), step * block
        )
        newest = jnp.maximum(running, jnp.max(scores, axis=-1))
        total = total * jnp.exp(running - newest) + jnp.sum(
            jnp.exp(scores - newest[..., None]), axis=-1
        )
        return (newest, total)

    stat_init = (
        jnp.full((KV_HEADS, groups, tokens), MASKED, jnp.float32),
        jnp.zeros((KV_HEADS, groups, tokens), jnp.float32),
    )
    running, total = lax.fori_loop(0, count, stats_step, stat_init)
    log_total = running + jnp.log(total)

    def output_step(step, accum):
        start = step * block
        scores = block_scores(lax.dynamic_slice_in_dim(keys_all, start, block, 0), start)
        probs = jnp.exp(scores - log_total[..., None]).astype(jnp.bfloat16)
        value_block = lax.dynamic_slice_in_dim(values_all, start, block, 0)
        return accum + jnp.einsum(
            "kgqs,skd->qkgd", probs, value_block, preferred_element_type=jnp.float32
        )

    attended_groups = lax.fori_loop(
        0, count, output_step, jnp.zeros((tokens, KV_HEADS, groups, HEAD_DIM), jnp.float32)
    )
    attended = attended_groups.reshape(tokens, HEADS * HEAD_DIM)
    attended_low = attended.astype(jnp.bfloat16)
    branch = jnp.dot(attended_low, w_output, preferred_element_type=jnp.float32)
    middle = inputs + branch
    inv_two = lax.rsqrt(jnp.mean(middle * middle, axis=-1, keepdims=True) + EPS)
    normed_two = (middle * inv_two * gain_mlp).astype(jnp.bfloat16)
    logits = jnp.dot(normed_two, w_router, preferred_element_type=jnp.float32)
    onehot = (chosen[:, :, None] == jnp.arange(all_experts, dtype=jnp.int32)[None, None, :]).astype(
        jnp.float32
    )
    picked = jnp.sum(onehot * logits[:, None, :], axis=-1)
    gates = jax.nn.softmax(picked, axis=-1)
    target, owner = assign_slots(chosen.reshape(pairs), slot_order[0, 0], all_experts, capacity)
    valid = owner < pairs
    source = jnp.minimum(owner, pairs - 1)
    rows_send = jnp.where(valid[:, None], normed_two[source // top], 0).reshape(
        peers, local_experts, capacity, width
    )
    received = lax.all_to_all(rows_send, "expert", split_axis=0, concat_axis=0, tiled=True)
    gate_pre = jnp.einsum("necd,edf->necf", received, w_gate, preferred_element_type=jnp.float32)
    up_pre = jnp.einsum("necd,edf->necf", received, w_up, preferred_element_type=jnp.float32)
    hidden = (jax.nn.silu(gate_pre) * up_pre).astype(jnp.bfloat16)
    result = jnp.einsum(
        "necf,efd->necd", hidden, w_down, preferred_element_type=jnp.float32
    ).astype(jnp.bfloat16)
    returned = lax.all_to_all(result, "expert", split_axis=0, concat_axis=0, tiled=True)
    returned, received, gate_pre, up_pre = (returned, received, gate_pre, up_pre)
    zero_row = jnp.zeros((1, width), jnp.bfloat16)
    pair_out = jnp.concatenate([returned.reshape(all_experts * capacity, width), zero_row], axis=0)[
        target
    ].reshape(tokens, top, width)
    mixed = jnp.einsum("tk,tkd->td", gates, pair_out, preferred_element_type=jnp.float32)
    hidden_out = middle + mixed
    dy_pairs = (
        (gates[:, :, None] * cotangent[:, None, :]).astype(jnp.bfloat16).reshape(pairs, width)
    )
    dy_send = jnp.where(valid[:, None], dy_pairs[source], 0).reshape(
        peers, local_experts, capacity, width
    )
    dy_received = lax.all_to_all(dy_send, "expert", split_axis=0, concat_axis=0, tiled=True)
    sigmoid_gate = jax.nn.sigmoid(gate_pre)
    silu_gate = gate_pre * sigmoid_gate
    hidden = (silu_gate * up_pre).astype(jnp.bfloat16)
    grad_down_part = jnp.einsum(
        "necf,necd->efd", hidden, dy_received, preferred_element_type=jnp.float32
    )
    d_hidden = jnp.einsum("necd,efd->necf", dy_received, w_down, preferred_element_type=jnp.float32)
    d_gate = (d_hidden * up_pre * sigmoid_gate * (1.0 + gate_pre * (1.0 - sigmoid_gate))).astype(
        jnp.bfloat16
    )
    d_up = (d_hidden * silu_gate).astype(jnp.bfloat16)
    grad_gate_part = jnp.einsum(
        "necd,necf->edf", received, d_gate, preferred_element_type=jnp.float32
    )
    grad_up_part = jnp.einsum("necd,necf->edf", received, d_up, preferred_element_type=jnp.float32)
    gate_total, up_total, down_total = (
        lax.psum_scatter(
            grad_gate_part.astype(jnp.bfloat16), "dp", scatter_dimension=1, tiled=True
        ).astype(jnp.float32),
        lax.psum_scatter(
            grad_up_part.astype(jnp.bfloat16), "dp", scatter_dimension=1, tiled=True
        ).astype(jnp.float32),
        lax.psum_scatter(
            grad_down_part.astype(jnp.bfloat16), "dp", scatter_dimension=1, tiled=True
        ).astype(jnp.float32),
    )
    d_rows = jnp.einsum("necf,edf->necd", d_gate, w_gate, preferred_element_type=jnp.float32)
    d_rows = (
        d_rows + jnp.einsum("necf,edf->necd", d_up, w_up, preferred_element_type=jnp.float32)
    ).astype(jnp.bfloat16)
    d_back = lax.all_to_all(d_rows, "expert", split_axis=0, concat_axis=0, tiled=True)
    d_pairs = jnp.concatenate([d_back.reshape(all_experts * capacity, width), zero_row], axis=0)[
        target
    ].reshape(tokens, top, width)
    d_normed_two = jnp.sum(d_pairs, axis=1, dtype=jnp.float32)
    d_gates = jnp.einsum("td,tkd->tk", cotangent, pair_out, preferred_element_type=jnp.float32)
    d_picked = gates * (d_gates - jnp.sum(gates * d_gates, axis=-1, keepdims=True))
    d_logits = jnp.sum(onehot * d_picked[:, :, None], axis=1).astype(jnp.bfloat16)
    grad_router_part = jnp.einsum(
        "td,te->de", normed_two, d_logits, preferred_element_type=jnp.float32
    )
    d_normed_two = d_normed_two + jnp.einsum(
        "te,de->td", d_logits, w_router, preferred_element_type=jnp.float32
    )
    scaled_two = d_normed_two * gain_mlp
    grad_gain_mlp_part = jnp.sum(d_normed_two * middle * inv_two, axis=0)
    d_middle = (
        cotangent
        + inv_two * scaled_two
        - middle * inv_two**3 * jnp.mean(middle * scaled_two, axis=-1, keepdims=True)
    )
    d_branch = d_middle.astype(jnp.bfloat16)
    grad_output_part = jnp.einsum(
        "tf,td->fd", attended_low, d_branch, preferred_element_type=jnp.float32
    )
    d_attended = jnp.einsum(
        "td,fd->tf", d_branch, w_output, preferred_element_type=jnp.float32
    ).astype(jnp.bfloat16)
    d_groups = d_attended.reshape(tokens, KV_HEADS, groups, HEAD_DIM)
    delta = jnp.einsum(
        "qkgd,qkgd->kgq", d_groups, attended_groups, preferred_element_type=jnp.float32
    )
    keys_back, values_back = (
        lax.all_gather(keys_low, "dp", axis=0, tiled=True),
        lax.all_gather(values_low, "dp", axis=0, tiled=True),
    )

    def grad_step(step, carry):
        d_query, d_keys, d_values = carry
        start = step * block
        key_block = lax.dynamic_slice_in_dim(keys_back, start, block, 0)
        value_block = lax.dynamic_slice_in_dim(values_back, start, block, 0)
        scores = block_scores(key_block, start)
        probs = jnp.exp(scores - log_total[..., None])
        probs_low = probs.astype(jnp.bfloat16)
        d_probs = jnp.einsum(
            "qkgd,skd->kgqs", d_groups, value_block, preferred_element_type=jnp.float32
        )
        d_scores = (probs * (d_probs - delta[..., None])).astype(jnp.bfloat16)
        d_query = d_query + jnp.einsum(
            "kgqs,skd->qkgd", d_scores, key_block, preferred_element_type=jnp.float32
        )
        key_part = jnp.einsum(
            "kgqs,qkgd->skd", d_scores, query_groups, preferred_element_type=jnp.float32
        )
        value_part = jnp.einsum(
            "kgqs,qkgd->skd", probs_low, d_groups, preferred_element_type=jnp.float32
        )
        d_keys = lax.dynamic_update_slice_in_dim(
            d_keys, lax.dynamic_slice_in_dim(d_keys, start, block, 0) + key_part, start, 0
        )
        d_values = lax.dynamic_update_slice_in_dim(
            d_values, lax.dynamic_slice_in_dim(d_values, start, block, 0) + value_part, start, 0
        )
        return (d_query, d_keys, d_values)

    grad_init = (
        jnp.zeros((tokens, KV_HEADS, groups, HEAD_DIM), jnp.float32),
        jnp.zeros((length, KV_HEADS, HEAD_DIM), jnp.float32),
        jnp.zeros((length, KV_HEADS, HEAD_DIM), jnp.float32),
    )
    d_query, d_keys, d_values = lax.fori_loop(0, count, grad_step, grad_init)
    key_sum, value_sum = (
        lax.psum_scatter(
            (d_keys * scale).reshape(length, KV_HEADS * HEAD_DIM).astype(jnp.bfloat16),
            "dp",
            scatter_dimension=0,
            tiled=True,
        ).astype(jnp.float32),
        lax.psum_scatter(
            d_values.reshape(length, KV_HEADS * HEAD_DIM).astype(jnp.bfloat16),
            "dp",
            scatter_dimension=0,
            tiled=True,
        ).astype(jnp.float32),
    )
    d_query_low = (
        rotate_back((d_query * scale).reshape(tokens, HEADS, HEAD_DIM), cosine, sine)
        .astype(jnp.bfloat16)
        .reshape(tokens, HEADS * HEAD_DIM)
    )
    d_key_low = (
        rotate_back(key_sum.reshape(tokens, KV_HEADS, HEAD_DIM), cosine, sine)
        .astype(jnp.bfloat16)
        .reshape(tokens, KV_HEADS * HEAD_DIM)
    )
    d_value_low = value_sum.astype(jnp.bfloat16)
    grad_query_part = jnp.einsum(
        "td,tf->df", normed, d_query_low, preferred_element_type=jnp.float32
    )
    grad_key_part = jnp.einsum("td,tf->df", normed, d_key_low, preferred_element_type=jnp.float32)
    grad_value_part = jnp.einsum(
        "td,tf->df", normed, d_value_low, preferred_element_type=jnp.float32
    )
    d_normed = jnp.einsum("tf,df->td", d_query_low, w_query, preferred_element_type=jnp.float32)
    d_normed = d_normed + jnp.einsum(
        "tf,df->td", d_key_low, w_key, preferred_element_type=jnp.float32
    )
    d_normed = d_normed + jnp.einsum(
        "tf,df->td", d_value_low, w_value, preferred_element_type=jnp.float32
    )
    scaled_one = d_normed * gain_attn
    grad_gain_attn_part = jnp.sum(d_normed * inputs * inv_one, axis=0)
    grad_in = (
        d_middle
        + inv_one * scaled_one
        - inputs * inv_one**3 * jnp.mean(inputs * scaled_one, axis=-1, keepdims=True)
    )
    dense = (
        lax.psum_scatter(grad_gain_attn_part, ("dp", "expert"), scatter_dimension=0, tiled=True),
        lax.psum_scatter(grad_query_part, ("dp", "expert"), scatter_dimension=0, tiled=True),
        lax.psum_scatter(grad_key_part, ("dp", "expert"), scatter_dimension=0, tiled=True),
        lax.psum_scatter(grad_value_part, ("dp", "expert"), scatter_dimension=0, tiled=True),
        lax.psum_scatter(grad_output_part, ("dp", "expert"), scatter_dimension=0, tiled=True),
        lax.psum_scatter(grad_gain_mlp_part, ("dp", "expert"), scatter_dimension=0, tiled=True),
        lax.psum_scatter(grad_router_part, ("dp", "expert"), scatter_dimension=0, tiled=True),
    )
    return (
        hidden_out[None],
        grad_in[None],
        dense[0],
        dense[1],
        dense[2],
        dense[3],
        dense[4],
        dense[5],
        dense[6],
        gate_total,
        up_total,
        down_total,
    )

BF = jnp.bfloat16
F32 = jnp.float32
WIDTH = 1536
LANES = 128
PER_KV = HEADS // KV_HEADS
ROWS_Q = PER_KV * HEAD_DIM
PACK = ROWS_Q + 2 * HEAD_DIM
BIT_Y, BIT_ZL, BIT_ZH = 1, 2, 4
BIT_C, BIT_X = 1, 2
BLOCK_Q = 256
BLOCK_K = 512
SLOTS = 64
CHUNK = 512
MIB = 1 << 20
hbm = pl.BlockSpec(memory_space=pltpu.HBM)


def dot_nn(a, b):
    return lax.dot_general(a, b, (((1,), (0,)), ((), ())), preferred_element_type=F32)


def dot_nt(a, b):
    return lax.dot_general(a, b, (((1,), (1,)), ((), ())), preferred_element_type=F32)


def dot_tn(a, b):
    return lax.dot_general(a, b, (((0,), (0,)), ((), ())), preferred_element_type=F32)


def cost(flops, moved, transcendentals=0):
    return pl.CostEstimate(
        flops=int(flops), bytes_accessed=int(moved), transcendentals=int(transcendentals)
    )


def params(mib, dims=None):
    return pltpu.CompilerParams(vmem_limit_bytes=mib * MIB, dimension_semantics=dims)


def swap(values, axis, mask):
    size = lax.axis_size(axis)
    return lax.ppermute(values, axis, [(i, i ^ mask) for i in range(size)])


def swap_bit(values, bit):
    axis, mask = bit
    return swap(values, axis, mask)


def fence(*values):
    return lax.optimization_barrier(values)


C_BIT = ("expert", BIT_C)
X_BIT = ("expert", BIT_X)
Y_BIT = ("dp", BIT_Y)
ZL_BIT = ("dp", BIT_ZL)
ZH_BIT = ("dp", BIT_ZH)


def pre_kernel(
    hid_ref,
    gain_ref,
    wq_ref,
    wk_ref,
    wv_ref,
    cos_ref,
    sin_ref,
    cot_ref,
    norm_ref,
    pack_ref,
    low_ref,
):
    tokens = hid_ref.shape[0]
    half = tokens // 2
    low_ref[...] = cot_ref[...].astype(BF)
    inputs = hid_ref[...]
    inv = lax.rsqrt(jnp.mean(inputs * inputs, axis=-1, keepdims=True) + EPS)
    normed = (inputs * inv * gain_ref[...]).astype(BF)
    norm_ref[...] = normed
    low = (lax.broadcasted_iota(jnp.int32, (tokens, LANES), 1) % HEAD_DIM) < HEAD_DIM // 2
    cosine, sine = cos_ref[...], sin_ref[...]

    def turn(tile):
        other = jnp.where(
            low,
            pltpu.roll(tile, LANES - HEAD_DIM // 2, 1),
            pltpu.roll(tile, HEAD_DIM // 2, 1),
        )
        return (tile * cosine + other * sine).astype(BF)

    tiles = []
    for n in range(wq_ref.shape[1] // CHUNK):
        pre = dot_nn(normed, wq_ref[:, n * CHUNK : (n + 1) * CHUNK])
        tiles += [turn(pre[:, m * LANES : (m + 1) * LANES]) for m in range(CHUNK // LANES)]
    queries = jnp.concatenate(tiles, axis=1)
    pre = dot_nn(normed, wk_ref[...])
    keys = jnp.concatenate(
        [turn(pre[:, m * LANES : (m + 1) * LANES]) for m in range(pre.shape[1] // LANES)], axis=1
    )
    values = dot_nn(normed, wv_ref[...]).astype(BF)
    for g in range(KV_HEADS):
        at = g * ROWS_Q
        head = slice(g * HEAD_DIM, (g + 1) * HEAD_DIM)
        pack_ref[g, 0:tokens] = queries[:, at : at + LANES]
        pack_ref[g, tokens : 2 * tokens] = jnp.concatenate(
            [queries[:, at + LANES : at + ROWS_Q], keys[:, head]], axis=1
        )
        pack_ref[g, 2 * tokens :] = jnp.concatenate(
            [values[:half, head], values[half:, head]], axis=1
        )


def run_pre(inputs, gain, w_query, w_key, w_value, cos_tab, sin_tab, cotangent):
    tokens = inputs.shape[0]
    return pl.pallas_call(
        pre_kernel,
        out_shape=(
            jax.ShapeDtypeStruct((tokens, WIDTH), BF),
            jax.ShapeDtypeStruct((KV_HEADS, tokens * PACK // LANES, LANES), BF),
            jax.ShapeDtypeStruct((tokens, WIDTH), BF),
        ),
        compiler_params=params(60),
        cost_estimate=cost(2 * tokens * WIDTH * 2560, 14e6),
    )(inputs, gain[None], w_query, w_key, w_value, cos_tab, sin_tab, cotangent)


def unpack_heads(block_ref, out_ref, row, tokens, column):
    half = tokens // 2
    out_ref[row : row + tokens, column : column + LANES] = block_ref[0:tokens]
    rest = block_ref[tokens : tokens + half]
    out_ref[row : row + half, column + LANES : column + ROWS_Q] = rest[:, :HEAD_DIM]
    out_ref[row + half : row + tokens, column + LANES : column + ROWS_Q] = rest[:, HEAD_DIM:]


def pack_heads(block_ref, rows, tokens):
    half = tokens // 2
    block_ref[0:tokens] = rows[:, 0:LANES]
    block_ref[tokens : tokens + half] = jnp.concatenate(
        [rows[:half, LANES:ROWS_Q], rows[half:, LANES:ROWS_Q]], axis=1
    )


def unpack_all(block_ref, q_ref, k_ref, v_ref, row, tokens, q_at=0, k_at=0, v_at=0):
    half = tokens // 2
    rows = slice(row, row + tokens)
    q_ref[rows, q_at : q_at + LANES] = block_ref[0:tokens]
    two = block_ref[tokens : 2 * tokens]
    q_ref[rows, q_at + LANES : q_at + ROWS_Q] = two[:, :HEAD_DIM]
    k_ref[rows, k_at : k_at + HEAD_DIM] = two[:, HEAD_DIM:]
    rest = block_ref[2 * tokens : 2 * tokens + half]
    v_ref[row : row + half, v_at : v_at + HEAD_DIM] = rest[:, :HEAD_DIM]
    v_ref[row + half : row + tokens, v_at : v_at + HEAD_DIM] = rest[:, HEAD_DIM:]


def heads_t(block, width):
    return jnp.concatenate(
        [block[:, h * HEAD_DIM : (h + 1) * HEAD_DIM].astype(F32).T for h in range(width)], axis=1
    )


def heads_rows(block, width):
    return jnp.concatenate(
        [block[:, h * HEAD_DIM : (h + 1) * HEAD_DIM] for h in range(width)], axis=0
    )


def allowed_t(step, block):
    shape = (BLOCK_K, PER_KV * BLOCK_Q)
    key_pos = step * BLOCK_K + lax.broadcasted_iota(jnp.int32, shape, 0)
    query_pos = block * BLOCK_Q + lax.broadcasted_iota(jnp.int32, shape, 1) % BLOCK_Q
    return key_pos <= query_pos


def forward_kernel(pack_ref, out_ref, out_t_ref, lse_ref, q_s, k_s, v_s, vt_s, out_s):
    block = pl.program_id(0)
    sources = pack_ref.shape[0]
    tokens = q_s.shape[0] // sources

    @pl.when(block == 0)
    def _():
        for n in range(sources):
            unpack_all(pack_ref.at[n], q_s, k_s, v_s, n * tokens, tokens)
        vt_s[...] = v_s[...].astype(F32).T.astype(BF)

    rows = pl.ds(pl.multiple_of(block * BLOCK_Q, BLOCK_Q), BLOCK_Q)
    scale = HEAD_DIM ** (-0.5)
    q_t = (heads_t(q_s[rows, :], PER_KV) * scale).astype(BF)
    columns = PER_KV * BLOCK_Q

    def step(j, carry, masked):
        running, total, accum = carry
        keys = pl.ds(pl.multiple_of(j * BLOCK_K, BLOCK_K), BLOCK_K)
        scores = dot_nn(k_s[keys, :], q_t)
        if masked:
            scores = jnp.where(allowed_t(j, block), scores, MASKED)
        newest = jnp.maximum(running, jnp.max(scores, axis=0, keepdims=True))
        fade = jnp.exp(running - newest)
        probs = jnp.exp(scores - newest)
        total = total * fade + jnp.sum(probs, axis=0, keepdims=True)
        accum = accum * fade + dot_nn(vt_s[:, keys], probs.astype(BF))
        return newest, total, accum

    carry = (
        jnp.full((1, columns), MASKED, F32),
        jnp.zeros((1, columns), F32),
        jnp.zeros((HEAD_DIM, columns), F32),
    )
    last = (block * BLOCK_Q) // BLOCK_K
    carry = lax.fori_loop(0, last, lambda j, c: step(j, c, False), carry)
    running, total, accum = step(last, carry, True)
    out_t = accum / total
    out_t_ref[0] = out_t
    lse_ref[0] = running + jnp.log(total)
    out_s[rows, :] = jnp.concatenate(
        [out_t[:, h * BLOCK_Q : (h + 1) * BLOCK_Q].T for h in range(PER_KV)], axis=1
    ).astype(BF)

    @pl.when(block == pl.num_programs(0) - 1)
    def _():
        for n in range(sources):
            pack_heads(out_ref.at[n], out_s[n * tokens : (n + 1) * tokens, :], tokens)


def run_forward(pack):
    sources = pack.shape[0]
    length = sources * (pack.shape[1] * LANES // PACK)
    packed = (sources, length // sources * ROWS_Q // LANES, LANES)
    blocks = length // BLOCK_Q
    columns = PER_KV * BLOCK_Q
    return pl.pallas_call(
        forward_kernel,
        grid=(blocks,),
        in_specs=[pl.BlockSpec(pack.shape, lambda i: (0, 0, 0))],
        out_specs=(
            pl.BlockSpec(packed, lambda i: (0, 0, 0)),
            pl.BlockSpec((1, HEAD_DIM, columns), lambda i: (i, 0, 0)),
            pl.BlockSpec((1, 1, columns), lambda i: (i, 0, 0)),
        ),
        out_shape=(
            jax.ShapeDtypeStruct(packed, BF),
            jax.ShapeDtypeStruct((blocks, HEAD_DIM, columns), F32),
            jax.ShapeDtypeStruct((blocks, 1, columns), F32),
        ),
        scratch_shapes=[
            pltpu.VMEM((length, ROWS_Q), BF),
            pltpu.VMEM((length, HEAD_DIM), BF),
            pltpu.VMEM((length, HEAD_DIM), BF),
            pltpu.VMEM((HEAD_DIM, length), BF),
            pltpu.VMEM((length, ROWS_Q), BF),
        ],
        compiler_params=params(60, ("arbitrary",)),
        cost_estimate=cost(8 * length * length * ROWS_Q, 6e6, length * length * PER_KV),
    )(pack)


def backward_kernel(
    pack_ref,
    grad_ref,
    out_t_ref,
    lse_ref,
    cos_ref,
    sin_ref,
    res_ref,
    q_s,
    do_s,
    k_s,
    v_s,
    kt_s,
    dk_s,
    dv_s,
):
    block = pl.program_id(0)
    sources = pack_ref.shape[0]
    tokens = q_s.shape[0] // sources

    @pl.when(block == 0)
    def _():
        for n in range(sources):
            unpack_all(pack_ref.at[n], q_s, k_s, v_s, n * tokens, tokens)
            unpack_heads(grad_ref.at[n], do_s, n * tokens, tokens, 0)
        kt_s[...] = k_s[...].astype(F32).T.astype(BF)
        dk_s[...] = jnp.zeros_like(dk_s)
        dv_s[...] = jnp.zeros_like(dv_s)

    scale = HEAD_DIM ** (-0.5)
    half = HEAD_DIM // 2
    rows = pl.ds(pl.multiple_of(block * BLOCK_Q, BLOCK_Q), BLOCK_Q)
    q_block = q_s[rows, :]
    q_t = (heads_t(q_block, PER_KV) * scale).astype(BF)
    q_rows = (heads_rows(q_block, PER_KV).astype(F32) * scale).astype(BF)
    do_block = do_s[rows, :]
    do_f32 = heads_t(do_block, PER_KV)
    do_t = do_f32.astype(BF)
    do_rows = heads_rows(do_block, PER_KV)
    delta = jnp.sum(do_f32 * out_t_ref[0], axis=0, keepdims=True)
    lse = lse_ref[0]

    def step(j, dq_t, masked):
        keys = pl.ds(pl.multiple_of(j * BLOCK_K, BLOCK_K), BLOCK_K)
        scores = dot_nn(k_s[keys, :], q_t)
        if masked:
            scores = jnp.where(allowed_t(j, block), scores, MASKED)
        probs = jnp.exp(scores - lse)
        d_probs = dot_nn(v_s[keys, :], do_t)
        d_scores = (probs * (d_probs - delta)).astype(BF)
        dv_s[keys, :] += dot_nn(probs.astype(BF), do_rows)
        dk_s[keys, :] += dot_nn(d_scores, q_rows)
        return dq_t + dot_nn(kt_s[:, keys], d_scores)

    last = (block * BLOCK_Q) // BLOCK_K
    dq_t = jnp.zeros((HEAD_DIM, PER_KV * BLOCK_Q), F32)
    dq_t = lax.fori_loop(0, last, lambda j, c: step(j, c, False), dq_t)
    dq_t = step(last, dq_t, True) * scale

    def turn_back(values, cosine, sine):
        first, second = values[:half], values[half:]
        return jnp.concatenate(
            [first * cosine + second * sine, second * cosine - first * sine], axis=0
        )

    columns = pl.ds(pl.multiple_of(block * BLOCK_Q, BLOCK_Q), BLOCK_Q)
    cosine, sine = cos_ref[:, columns], sin_ref[:, columns]
    q_s[rows, :] = jnp.concatenate(
        [
            turn_back(dq_t[:, h * BLOCK_Q : (h + 1) * BLOCK_Q], cosine, sine).T
            for h in range(PER_KV)
        ],
        axis=1,
    ).astype(BF)

    @pl.when(block == pl.num_programs(0) - 1)
    def _():
        dk = turn_back(dk_s[...].T, cos_ref[...], sin_ref[...]).T.astype(BF)
        half = tokens // 2
        for n in range(sources):
            row = n * tokens
            res_ref[n, 0:tokens] = q_s[row : row + tokens, 0:LANES]
            res_ref[n, tokens : 2 * tokens] = jnp.concatenate(
                [q_s[row : row + tokens, LANES:ROWS_Q], dk[row : row + tokens]], axis=1
            )
            res_ref[n, 2 * tokens :] = jnp.concatenate(
                [dv_s[row : row + half, :], dv_s[row + half : row + tokens, :]], axis=1
            ).astype(BF)


def run_backward(pack, grad, out_t, lse, cos_t, sin_t):
    length = cos_t.shape[1]
    blocks = length // BLOCK_Q
    columns = PER_KV * BLOCK_Q
    half = HEAD_DIM // 2
    return pl.pallas_call(
        backward_kernel,
        grid=(blocks,),
        in_specs=[
            pl.BlockSpec(pack.shape, lambda i: (0, 0, 0)),
            pl.BlockSpec(grad.shape, lambda i: (0, 0, 0)),
            pl.BlockSpec((1, HEAD_DIM, columns), lambda i: (i, 0, 0)),
            pl.BlockSpec((1, 1, columns), lambda i: (i, 0, 0)),
            pl.BlockSpec((half, length), lambda i: (0, 0)),
            pl.BlockSpec((half, length), lambda i: (0, 0)),
        ],
        out_specs=pl.BlockSpec(pack.shape, lambda i: (0, 0, 0)),
        out_shape=jax.ShapeDtypeStruct(pack.shape, BF),
        scratch_shapes=[
            pltpu.VMEM((length, ROWS_Q), BF),
            pltpu.VMEM((length, ROWS_Q), BF),
            pltpu.VMEM((length, HEAD_DIM), BF),
            pltpu.VMEM((length, HEAD_DIM), BF),
            pltpu.VMEM((HEAD_DIM, length), BF),
            pltpu.VMEM((length, HEAD_DIM), F32),
            pltpu.VMEM((length, HEAD_DIM), F32),
        ],
        compiler_params=params(60, ("arbitrary",)),
        cost_estimate=cost(20 * length * length * ROWS_Q, 8e6, length * length * PER_KV),
    )(pack, grad, out_t, lse, cos_t, sin_t)


def mid_kernel(att_ref, wo_ref, hid_ref, gain_ref, mid_ref, norm_ref, full_ref):
    for g in range(KV_HEADS):
        unpack_heads(att_ref.at[g], full_ref, 0, full_ref.shape[0], g * ROWS_Q)
    middle = hid_ref[...] + dot_nn(full_ref[...], wo_ref[...])
    mid_ref[...] = middle
    inv = lax.rsqrt(jnp.mean(middle * middle, axis=-1, keepdims=True) + EPS)
    norm_ref[...] = (middle * inv * gain_ref[...]).astype(BF)


def run_mid(att, w_output, inputs, gain):
    tokens = inputs.shape[0]
    return pl.pallas_call(
        mid_kernel,
        out_shape=(
            jax.ShapeDtypeStruct((tokens, WIDTH), F32),
            jax.ShapeDtypeStruct((tokens, WIDTH), BF),
            jax.ShapeDtypeStruct((tokens, WIDTH), BF),
        ),
        compiler_params=params(24),
        cost_estimate=cost(2 * tokens * WIDTH * WIDTH, 12e6),
    )(att, w_output, inputs, gain[None])


def expert_kernel(
    place_ref,
    x_ref,
    g_ref,
    gates_ref,
    map_ref,
    wg0_ref,
    wg1_ref,
    wu0_ref,
    wu1_ref,
    wd0_ref,
    wd1_ref,
    *refs,
    first,
):
    if first:
        mix_prior = dx_prior = None
    else:
        mix_prior, dx_prior = refs[0:2], refs[2:4]
        refs = refs[4:]
    (
    mix_keep,
    mix_send,
    dx_keep,
    dx_send,
    gate_keep,
    gate_send0,
    gate_send1,
    early,
    up_keep,
    up_send0,
    up_send1,
    down_keep,
    down_send0,
    down_send1,
    xs,
    gs,
    gate_s,
    wide_s,
    tall_s,
    ) = refs
    step = pl.program_id(0)
    sources = map_ref.shape[0]
    experts = xs.shape[0]
    low = 0 if first else experts
    rows = experts * SLOTS
    count = WIDTH // CHUNK

    def pick_of(source):
        return one_hot(map_ref[source, low : low + experts, :], rows)

    @pl.when(step < experts)
    def _():
        e = step
        x = x_ref[0]
        w_gate = jnp.concatenate([wg0_ref[0], wg1_ref[0]], axis=1)
        w_up = jnp.concatenate([wu0_ref[0], wu1_ref[0]], axis=1)
        gate_pre = dot_nn(x, w_gate)
        up_pre = dot_nn(x, w_up)
        sig = jax.nn.sigmoid(gate_pre)
        silu = gate_pre * sig
        hidden = (silu * up_pre).astype(BF)
        gate = gates_ref[0]
        d_hidden = jnp.zeros(hidden.shape, F32)
        d_gates = jnp.zeros(gate.shape, F32)
        for n in range(count):
            cols = slice(n * CHUNK, (n + 1) * CHUNK)
            w_down = jnp.concatenate([wd0_ref[0, :, cols], wd1_ref[0, :, cols]], axis=0)
            grad = g_ref[0, :, cols].astype(F32)
            d_y = (gate * grad).astype(BF)
            y = dot_nn(hidden, w_down)
            d_gates += jnp.sum(y * grad, axis=1, keepdims=True)
            gs[e, :, cols] = (gate * y).astype(BF)
            d_hidden += dot_nt(d_y, w_down)
            wide_s[:, cols] = dot_tn(hidden, d_y).astype(BF)
        gate_s[e] = d_gates
        d_gate = (d_hidden * up_pre * sig * (1.0 + gate_pre * (1.0 - sig))).astype(BF)
        d_up = (d_hidden * silu).astype(BF)

        y_at, zl_at, zh_at = place_ref[1], place_ref[2], place_ref[3]
        part = down_keep.shape[2]
        for z in range(2):
            base = (zh_at ^ z) * 2
            down_keep[z, 0] = wide_s[pl.ds(pl.multiple_of((base + y_at) * part, part), part), :]
            (down_send0, down_send1)[z][0] = wide_s[
                pl.ds(pl.multiple_of((base + (1 - y_at)) * part, part), part), :
            ]

        def spread(keep, send):
            part = keep.shape[3]
            for z in range(2):
                for low in range(2):
                    base = ((zh_at ^ z) * 2 + (zl_at ^ low)) * 2
                    keep[z, low, 0] = tall_s[
                        pl.ds(pl.multiple_of((base + y_at) * part, part), part), :
                    ]
                    send[z][low, 0] = tall_s[
                        pl.ds(pl.multiple_of((base + (1 - y_at)) * part, part), part), :
                    ]

        for n in range(count):
            cols = slice(n * CHUNK, (n + 1) * CHUNK)
            tall_s[cols, :] = dot_tn(x[:, cols], d_gate).astype(BF)
        spread(gate_keep, (gate_send0, gate_send1))
        early[0, 0] = gate_keep[1, 1, 0]
        early[1, 0] = gate_send1[1, 0]
        for n in range(count):
            cols = slice(n * CHUNK, (n + 1) * CHUNK)
            tall_s[cols, :] = dot_tn(x[:, cols], d_up).astype(BF)
        spread(up_keep, (up_send0, up_send1))
        for n in range(count):
            cols = slice(n * CHUNK, (n + 1) * CHUNK)
            d_x = dot_nt(d_gate, w_gate[cols]) + dot_nt(d_up, w_up[cols])
            xs[e, :, cols] = d_x.astype(BF)

    def combine(source, mix_out, dx_out, mix_in, dx_in):
        def put(out, prior, cols, values):
            if prior is not None:
                values += prior[0, :, cols].astype(F32)
            out[0, :, cols] = values.astype(BF)

        here = pl.ds(pl.multiple_of(source * SLOTS, SLOTS), SLOTS)
        pick = pick_of(source).astype(BF)
        for n in range(count):
            cols = slice(n * CHUNK, (n + 1) * CHUNK)
            put(dx_out, dx_in, cols, dot_tn(pick, xs[:, here, cols].reshape(rows, CHUNK)))
            put(mix_out, mix_in, cols, dot_tn(pick, gs[:, here, cols].reshape(rows, CHUNK)))
        values = gate_s[:, here, :].reshape(rows, 1)
        column = lax.broadcasted_iota(jnp.int32, (rows, LANES), 1)
        owner = lax.broadcasted_iota(jnp.int32, (rows, LANES), 0) // SLOTS
        spread_out = jnp.where(column == owner + (place_ref[4] + low), values, 0.0).astype(BF)
        put(dx_out, dx_in, slice(WIDTH, WIDTH + LANES), dot_tn(pick, spread_out))

    @pl.when((step >= experts) & (step < experts + sources // 2))
    def _():
        source = step - experts + sources // 2
        prior = (None, None) if first else (mix_prior[1], dx_prior[1])
        combine(source, mix_send, dx_send, *prior)

    @pl.when(step >= experts + sources // 2)
    def _():
        source = step - experts - sources // 2
        prior = (None, None) if first else (mix_prior[0], dx_prior[0])
        combine(source, mix_keep, dx_keep, *prior)


def less(shape):
    return jax.ShapeDtypeStruct(shape.shape[1:], shape.dtype)


def run_experts(place, x_slots, g_slots, gates, maps, w_gate, w_up, w_down, prior=()):
    sources, _, tokens = maps.shape
    width = x_slots.shape[2]
    experts = w_gate.shape[0] // 2
    low = experts if prior else 0
    ffe = w_gate.shape[2]
    part = ffe // 8
    quarter = width // 8
    half = ffe // 2
    slots = sources * SLOTS
    extra = width + LANES
    second = experts
    third = second + sources // 2

    def at(i, low, size):
        return jnp.clip(i - low, 0, size - 1)

    def expert_of(i):
        return at(i, 0, experts)

    def w_cols(block):
        return pl.BlockSpec(
            (1, width, LANES), lambda i, p: (expert_of(i) + low, 0, p[0] + 2 * block)
        )

    def w_rows(block):
        return pl.BlockSpec(
            (1, LANES, width), lambda i, p: (expert_of(i) + low, p[0] + 2 * block, 0)
        )

    slot_spec = pl.BlockSpec((1, slots, width), lambda i, p: (expert_of(i) + low, 0, 0))

    def out_tokens(low, cols):
        return pl.BlockSpec((1, tokens, cols), lambda i, p: (at(i, low, sources // 2), 0, 0))

    tall_spec = pl.BlockSpec(
        (2, 2, 1, quarter, half), lambda i, p: (0, 0, expert_of(i), 0, 0)
    )
    wide_spec = pl.BlockSpec((2, 1, part, width), lambda i, p: (0, expert_of(i), 0, 0))
    tall_half = pl.BlockSpec((2, 1, quarter, half), lambda i, p: (0, expert_of(i), 0, 0))
    wide_half = pl.BlockSpec((1, part, width), lambda i, p: (expert_of(i), 0, 0))
    tall = jax.ShapeDtypeStruct((2, 2, experts, quarter, half), BF)
    wide = jax.ShapeDtypeStruct((2, experts, part, width), BF)
    mixed = jax.ShapeDtypeStruct((sources // 2, tokens, width), BF)
    d_x = jax.ShapeDtypeStruct((sources // 2, tokens, extra), BF)
    sums = (
        out_tokens(third, width),
        out_tokens(second, width),
        out_tokens(third, extra),
        out_tokens(second, extra),
    )
    return pl.pallas_call(
        functools.partial(expert_kernel, first=not prior),
        grid_spec=pltpu.PrefetchScalarGridSpec(
            num_scalar_prefetch=1,
            grid=(third + sources // 2,),
            in_specs=[
                slot_spec,
                slot_spec,
                pl.BlockSpec((1, slots, 1), lambda i, p: (expert_of(i) + low, 0, 0)),
                pl.BlockSpec(maps.shape, lambda i, p: (0, 0, 0)),
                w_cols(0),
                w_cols(1),
                w_cols(0),
                w_cols(1),
                w_rows(0),
                w_rows(1),
                *(sums if prior else ()),
            ],
            out_specs=(
                *sums,
                tall_spec,
                tall_half,
                tall_half,
                tall_half,
                tall_spec,
                tall_half,
                tall_half,
                wide_spec,
                wide_half,
                wide_half,
            ),
            scratch_shapes=[
                pltpu.VMEM((experts, slots, width), BF),
                pltpu.VMEM((experts, slots, width), BF),
                pltpu.VMEM((experts, slots, 1), F32),
                pltpu.VMEM((half, width), BF),
                pltpu.VMEM((width, half), BF),
            ],
        ),
        out_shape=(mixed, mixed, d_x, d_x)
        + (tall, less(tall), less(tall), less(tall))
        + (tall, less(tall), less(tall))
        + (wide, less(wide), less(wide)),
        compiler_params=params(60, ("arbitrary",)),
        cost_estimate=cost(30e9, 60e6),
    )(place, x_slots, g_slots, gates, maps, w_gate, w_gate, w_up, w_up, w_down, w_down, *prior)


def post_kernel(
    dx_ref,
    mid_ref,
    cot_ref,
    norm_ref,
    wr_ref,
    map_ref,
    gain_ref,
    wo_ref,
    datt_ref,
    dmid_ref,
    dlow_ref,
    dlog_ref,
    ggain_ref,
):
    middle = mid_ref[...]
    inv = lax.rsqrt(jnp.mean(middle * middle, axis=-1, keepdims=True) + EPS)
    chosen = map_ref[...] >= 0.0
    logits = jnp.where(chosen, dot_nn(norm_ref[...], wr_ref[...]), MASKED)
    raised = jnp.exp(logits - jnp.max(logits, axis=-1, keepdims=True))
    raised = jnp.where(chosen, raised, 0.0)
    gates = raised / jnp.sum(raised, axis=-1, keepdims=True)
    d_gates = dx_ref[:, WIDTH:]
    d_picked = gates * (d_gates - jnp.sum(gates * d_gates, axis=-1, keepdims=True))
    d_logits = d_picked.astype(BF)
    dlog_ref[...] = d_logits
    d_norm = dx_ref[:, :WIDTH] + dot_nt(d_logits, wr_ref[...])
    scaled = d_norm * gain_ref[...]
    ggain_ref[...] = jnp.sum(d_norm * middle * inv, axis=0, keepdims=True)
    d_mid = (
        cot_ref[...]
        + inv * scaled
        - middle * inv**3 * jnp.mean(middle * scaled, axis=-1, keepdims=True)
    )
    dmid_ref[...] = d_mid
    d_low = d_mid.astype(BF)
    dlow_ref[...] = d_low
    d_att = dot_nt(d_low, wo_ref[...]).astype(BF)
    for g in range(KV_HEADS):
        pack_heads(datt_ref.at[g], d_att[:, g * ROWS_Q : (g + 1) * ROWS_Q], d_att.shape[0])


def run_post(dx_sum, middle, cotangent, normed_two, wr_pad, map_rows, gain, w_output):
    tokens = middle.shape[0]
    return pl.pallas_call(
        post_kernel,
        out_shape=(
            jax.ShapeDtypeStruct((KV_HEADS, tokens * ROWS_Q // LANES, LANES), BF),
            jax.ShapeDtypeStruct((tokens, WIDTH), F32),
            jax.ShapeDtypeStruct((tokens, WIDTH), BF),
            jax.ShapeDtypeStruct((tokens, LANES), BF),
            jax.ShapeDtypeStruct((1, WIDTH), F32),
        ),
        compiler_params=params(60),
        cost_estimate=cost(2 * tokens * WIDTH * WIDTH, 14e6),
    )(dx_sum, middle, cotangent, normed_two, wr_pad, map_rows, gain[None], w_output)


def put_rows(place_ref, held, keep, send):
    part = keep.shape[1]
    for b in range(keep.shape[0]):
        own = (2 * b) ^ place_ref[5]
        keep[b] = held[pl.ds(pl.multiple_of(own * part, part), part), :]
        other = own ^ 1
        send[b] = held[pl.ds(pl.multiple_of(other * part, part), part), :]


def qkvgrad_kernel(place_ref, a_ref, d_ref, full_ref, keep, send, held):
    step = pl.program_id(0)

    @pl.when(step == 0)
    def _():
        key_at = KV_HEADS * ROWS_Q
        value_at = key_at + KV_HEADS * HEAD_DIM
        for g in range(KV_HEADS):
            unpack_all(
                d_ref.at[g],
                full_ref,
                full_ref,
                full_ref,
                0,
                full_ref.shape[0],
                g * ROWS_Q,
                key_at + g * HEAD_DIM,
                value_at + g * HEAD_DIM,
            )

    cols = pl.ds(pl.multiple_of(step * 256, 256), 256)
    held[...] = dot_tn(a_ref[...], full_ref[:, cols]).astype(BF)
    put_rows(place_ref, held, keep, send)


def run_qkvgrad(place, normed, d_pack, blocks):
    tokens, rows = normed.shape
    cols = KV_HEADS * PACK
    part = rows // blocks
    spec = pl.BlockSpec((blocks // 2, part, 256), lambda i, p: (0, 0, i))
    shape = jax.ShapeDtypeStruct((blocks // 2, part, cols), BF)
    return pl.pallas_call(
        qkvgrad_kernel,
        grid_spec=pltpu.PrefetchScalarGridSpec(
            num_scalar_prefetch=1,
            grid=(cols // 256,),
            in_specs=[
                pl.BlockSpec((tokens, rows), lambda i, p: (0, 0)),
                pl.BlockSpec(d_pack.shape, lambda i, p: (0, 0, 0)),
            ],
            out_specs=(pl.BlockSpec((tokens, cols), lambda i, p: (0, 0)), spec, spec),
            scratch_shapes=[pltpu.VMEM((rows, 256), BF)],
        ),
        out_shape=(jax.ShapeDtypeStruct((tokens, cols), BF), shape, shape),
        compiler_params=params(60, ("arbitrary",)),
        cost_estimate=cost(2 * tokens * rows * cols, 12e6),
    )(place, normed, d_pack)


def last_work(inputs, outputs, scratch):
    gain_ref, gmlp_ref, sources = inputs[0], inputs[1], inputs[2:]
    (out_ref,) = outputs
    keep, send, held = scratch[:3]
    buffers, load_sem = scratch[3:-1], scratch[-1]
    loads = [
        pltpu.make_async_copy(source, buffer, load_sem.at[n])
        for n, (source, buffer) in enumerate(zip(sources, buffers))
    ]
    for load in loads:
        load.start()
    d_ref, wq_ref, wk_ref, wv_ref, dmid_ref, hid_ref, norm_ref, dlog_ref = buffers
    key_at = KV_HEADS * ROWS_Q
    value_at = key_at + KV_HEADS * HEAD_DIM
    device = lax.axis_index("dp") * lax.axis_size("expert") + lax.axis_index("expert")

    def compute():
        for load in loads:
            load.wait()
        tokens = hid_ref.shape[0]
        size = tokens // 4
        ggain = jnp.zeros(gain_ref.shape, F32)
        for r in range(4):
            rows = slice(r * size, (r + 1) * size)
            d_norm = dot_nt(d_ref[rows, 0:key_at], wq_ref[...])
            d_norm += dot_nt(d_ref[rows, key_at:value_at], wk_ref[...])
            d_norm += dot_nt(d_ref[rows, value_at:], wv_ref[...])
            values = hid_ref[rows, :]
            inv = lax.rsqrt(jnp.mean(values * values, axis=-1, keepdims=True) + EPS)
            scaled = d_norm * gain_ref[...]
            ggain += jnp.sum(d_norm * values * inv, axis=0, keepdims=True)
            out_ref[rows, :] = (
                dmid_ref[rows, :]
                + inv * scaled
                - values * inv**3 * jnp.mean(values * scaled, axis=-1, keepdims=True)
            )
        columns = dot_tn(norm_ref[...], dlog_ref[...])
        lane = lax.broadcasted_iota(jnp.int32, columns.shape, 1)
        for n, row in enumerate((gmlp_ref[...], ggain)):
            turned = jnp.broadcast_to(row, (8, row.shape[1])).T[:, 0:1]
            columns = jnp.where(lane == LANES - 2 + n, turned, columns)
        held[...] = columns
        part = keep.shape[1]
        for b in range(keep.shape[0]):
            own = (2 * b) ^ device
            keep[b] = held[pl.ds(pl.multiple_of(own * part, part), part), :]
            own = own ^ 1
            send[b] = held[pl.ds(pl.multiple_of(own * part, part), part), :]

    return compute


def plan_last(arrays, gain, ggain_mlp, blocks):
    vmem = pl.BlockSpec(memory_space=pltpu.VMEM)
    tokens = arrays[0].shape[0]
    small = pltpu.VMEM((blocks // 2, WIDTH // blocks, LANES), F32)
    scratch = [small, small, pltpu.VMEM((WIDTH, LANES), F32)]
    scratch += [pltpu.VMEM(array.shape, array.dtype) for array in arrays]
    scratch.append(pltpu.SemaphoreType.DMA((len(arrays),)))
    return (
        (gain[None], ggain_mlp) + arrays,
        [vmem] * 2 + [hbm] * len(arrays),
        [jax.ShapeDtypeStruct((tokens, WIDTH), F32)],
        scratch,
        last_work,
    )


def stack_swap(values, bit):
    return jnp.concatenate([values, swap_bit(values, bit)], axis=0)


MESH = pl.DeviceIdType.MESH


def peer_of(bit):
    axis, mask = bit
    return {axis: lax.axis_index(axis) ^ mask}


def greet(ids):
    barrier = pltpu.get_barrier_semaphore()
    for device in ids:
        pl.semaphore_signal(barrier, inc=1, device_id=device, device_id_type=MESH)
    pl.semaphore_wait(barrier, len(ids))


GATHER_BITS = (X_BIT, ZL_BIT, C_BIT)


def one_hot(slots, rows):
    experts, tokens = slots.shape
    wide = jnp.broadcast_to(slots[:, None, :], (experts, SLOTS, tokens))
    rank = lax.broadcasted_iota(jnp.int32, (experts, SLOTS, tokens), 1).astype(F32)
    return (wide == rank).astype(F32).reshape(rows, tokens)


def gather_kernel(x_ref, *refs):
    blocks, maps_ref, wr_ref = refs[0:4], refs[4], refs[5]
    x_slots, g_slots, gates_ref, local_ref = refs[6:10]
    all_ref, other, all_maps_ref, stage = refs[10:14]
    send_sem, recv_sem, more_send, more_recv, store_sem = refs[14:]
    greet([peer_of(bit) for bit in GATHER_BITS])
    half = x_ref.shape[0] // 2
    copies = []

    def send(source, slot, rows, bit):
        n = len(copies)
        copy = pltpu.make_async_remote_copy(
            src_ref=source if rows is None else source.at[rows],
            dst_ref=all_ref.at[slot] if rows is None else all_ref.at[slot, rows],
            send_sem=send_sem.at[n],
            recv_sem=recv_sem.at[n],
            device_id=peer_of(bit),
            device_id_type=MESH,
        )
        copy.start()
        copies.append(copy)
        return copy

    top, low = pl.ds(0, half), pl.ds(half, half)
    x_top = send(x_ref, 1, top, X_BIT)
    z_low = send(x_ref, 2, low, ZL_BIT)
    x_low = send(x_ref, 1, low, X_BIT)
    z_top = send(x_ref, 2, top, ZL_BIT)
    pairs = [(maps_ref, all_maps_ref.at[pl.ds(4, 4)])]
    pairs += [(block, other.at[n]) for n, block in enumerate(blocks)]
    crossed = []
    for n, (block, there) in enumerate(pairs):
        copy = pltpu.make_async_remote_copy(
            src_ref=block,
            dst_ref=there,
            send_sem=more_send.at[n],
            recv_sem=more_recv.at[n],
            device_id=peer_of(C_BIT),
            device_id_type=MESH,
        )
        copy.start()
        crossed.append(copy)
    cross_own = send(x_ref, 4, None, C_BIT)
    all_maps_ref[0:4] = maps_ref[...]
    column = lax.axis_index("expert")
    experts = x_slots.shape[0]
    rows = experts * SLOTS
    depth = stage.shape[0]
    stores = []

    def own_rows(table):
        picked = jnp.zeros((experts, table.shape[1]), F32)
        for n in range(table.shape[0] // experts):
            picked = jnp.where(column == n, table[n * experts : (n + 1) * experts], picked)
        return picked

    def put(source, values, target, pick):
        side = len(stores) % depth
        if len(stores) >= depth:
            stores[-depth].wait()
        for n in range(WIDTH // CHUNK):
            cols = slice(n * CHUNK, (n + 1) * CHUNK)
            got = dot_nn(pick, values[:, cols]).astype(BF)
            stage[side, :, :, cols] = got.reshape(experts, SLOTS, CHUNK)
        store = pltpu.make_async_copy(
            stage.at[side], target.at[:, pl.ds(source * SLOTS, SLOTS)], store_sem.at[side]
        )
        store.start()
        stores.append(store)

    def put_g(source, values):
        pick = one_hot(own_rows(all_maps_ref[source]), rows)
        put(source, values, g_slots, pick.astype(BF))

    def put_x(source, values):
        slot_map = all_maps_ref[source]
        chosen = slot_map >= 0.0
        logits = dot_nt(wr_ref[...], values[...])[0 : slot_map.shape[0]]
        logits = jnp.where(chosen, logits, MASKED)
        raised = jnp.exp(logits - jnp.max(logits, axis=0, keepdims=True))
        raised = jnp.where(chosen, raised, 0.0)
        gates = own_rows(raised / jnp.sum(raised, axis=0, keepdims=True))
        slots = own_rows(slot_map)
        local_ref[source] = slots
        pick = one_hot(slots, rows)
        wide = jnp.broadcast_to(gates[:, None, :], (experts, SLOTS, gates.shape[1]))
        of_rows = jnp.sum(pick * wide.reshape(rows, gates.shape[1]), axis=1, keepdims=True)
        gates_ref[:, source * SLOTS : (source + 1) * SLOTS, :] = of_rows.reshape(experts, SLOTS, 1)
        put(source, values, x_slots, pick.astype(BF))

    put_x(0, x_ref)
    put_g(0, blocks[0])
    put_g(1, blocks[1])
    x_top.wait_recv()
    far_top = send(all_ref.at[1], 3, top, ZL_BIT)
    z_low.wait_recv()
    far_low = send(all_ref.at[2], 3, low, X_BIT)
    put_g(2, blocks[2])
    put_g(3, blocks[3])
    for copy in crossed:
        copy.wait_recv()
    cross_own.wait_recv()
    put_x(4, all_ref.at[4])
    put_g(4, other.at[0])
    put_g(5, other.at[1])
    put_g(6, other.at[2])
    x_low.wait_recv()
    cross_x = send(all_ref.at[1], 5, None, C_BIT)
    z_top.wait_recv()
    cross_z = send(all_ref.at[2], 6, None, C_BIT)
    put_x(1, all_ref.at[1])
    put_x(2, all_ref.at[2])
    cross_x.wait_recv()
    cross_z.wait_recv()
    put_x(5, all_ref.at[5])
    put_x(6, all_ref.at[6])
    put_g(7, other.at[3])
    far_top.wait_recv()
    far_low.wait_recv()
    cross_far = send(all_ref.at[3], 7, None, C_BIT)
    put_x(3, all_ref.at[3])
    cross_far.wait_recv()
    put_x(7, all_ref.at[7])
    for store in stores[-depth:]:
        store.wait()
    for copy in copies + crossed:
        copy.wait_send()


def run_gather(values, blocks, maps, wr_t, experts):
    vmem = pl.BlockSpec(memory_space=pltpu.VMEM)
    tokens, width = values.shape
    slots = jax.ShapeDtypeStruct((experts, 8 * SLOTS, width), values.dtype)
    return pl.pallas_call(
        gather_kernel,
        in_specs=[vmem] * 7,
        out_specs=(hbm, hbm, vmem, vmem),
        out_shape=(
            slots,
            slots,
            jax.ShapeDtypeStruct((experts, 8 * SLOTS, 1), F32),
            jax.ShapeDtypeStruct((8, experts, tokens), F32),
        ),
        scratch_shapes=[
            pltpu.VMEM((8, tokens, width), values.dtype),
            pltpu.VMEM((4, tokens, width), values.dtype),
            pltpu.VMEM((8,) + maps.shape[1:], maps.dtype),
            pltpu.VMEM((4, experts, SLOTS, width), values.dtype),
        ]
        + [pltpu.SemaphoreType.DMA((n,)) for n in (10, 10, 5, 5, 4)],
        compiler_params=pltpu.CompilerParams(
            collective_id=1, has_side_effects=True, vmem_limit_bytes=60 * MIB
        ),
        cost_estimate=cost(0, 150e6),
    )(values, *blocks, maps, wr_t)


def trade_peers(size):
    me = lax.axis_index("dp")
    return [{"dp": me ^ k} for k in range(size - 1, 0, -1)]


def trade_start(a_ref, out_ref, send_sem, recv_sem, local_sem):
    me = lax.axis_index("dp")
    copies = []
    for n, device in enumerate(trade_peers(a_ref.shape[0])):
        copy = pltpu.make_async_remote_copy(
            src_ref=a_ref.at[device["dp"]],
            dst_ref=out_ref.at[me],
            send_sem=send_sem.at[n],
            recv_sem=recv_sem.at[n],
            device_id=device,
            device_id_type=MESH,
        )
        copy.start()
        copies.append(copy)
    own = pltpu.make_async_copy(a_ref.at[me], out_ref.at[me], local_sem)
    own.start()
    return copies, own


def trade_end(copies, own):
    own.wait()
    for copy in copies:
        copy.wait_recv()
    for copy in copies:
        copy.wait_send()


class Rider:
    def __init__(self, bit, *terms, pieces=1, turns=(0,)):
        self.bit, self.pieces, self.turns = bit, pieces, turns
        self.arrays = [term[0] if isinstance(term, tuple) else term for term in terms]
        self.parts = [term[1] if isinstance(term, tuple) else None for term in terms]
        array, part = self.arrays[0], self.parts[0]
        shape = array.shape
        if part is not None:
            kept = [len(range(n)[k]) for k, n in zip(part, shape) if not isinstance(k, int)]
            shape = tuple(kept) + shape[len(part) :]
        self.shape = jax.ShapeDtypeStruct(shape, array.dtype)
        self.direct = len(terms) == 1 and part is None

    def scratch(self):
        if self.direct:
            return []
        buffer = pltpu.VMEM(self.shape.shape, self.shape.dtype)
        return [buffer] * (len(self.arrays) + 1)

    def plan(self):
        return (self.bit, self.pieces, self.turns, tuple(self.parts), self.direct)


def rider_inputs(riders):
    return [array for rider in riders for array in rider.arrays]


def rider_shapes(riders):
    return tuple(rider.shape for rider in riders)


def rider_scratch(riders):
    remote = max(sum(rider.pieces for rider in riders), 1)
    local = max(sum(len(rider.arrays) for rider in riders), 1)
    buffers = [buffer for rider in riders for buffer in rider.scratch()]
    return buffers + [pltpu.SemaphoreType.DMA((n,)) for n in (remote, remote, local)]


def add_rows(result, buffers):
    step = 16

    @pl.loop(0, result.shape[1] // step)
    def _(r):
        rows = pl.ds(pl.multiple_of(r * step, step), step)
        for i in range(result.shape[0]):
            total = buffers[0][i, rows, :].astype(F32)
            for buffer in buffers[1:]:
                total += buffer[i, rows, :].astype(F32)
            result[i, rows, :] = total.astype(result.dtype)


def ride_pieces(sources, targets, plans, scratch):
    send_sem, recv_sem, local_sem = scratch[-3:]
    starts, finishes, loads, used, source, local = [], [], [], 0, 0, 0
    for n, (bit, pieces, turns, parts, direct) in enumerate(plans):
        arrays = sources[source : source + len(parts)]
        source += len(parts)
        if direct:
            held = arrays[0]
            prepare = None
        else:
            buffers = scratch[used : used + len(parts)]
            held = scratch[used + len(parts)]
            used += len(parts) + 1
            copies = []
            for array, part, buffer in zip(arrays, parts, buffers):
                view = array if part is None else array.at[part]
                copy = pltpu.make_async_copy(view, buffer, local_sem.at[local])
                local += 1
                loads.append(copy)
                copies.append(copy)

            def prepare(copies=copies, held=held, buffers=buffers):
                for copy in copies:
                    copy.wait()
                add_rows(held, buffers)

        size = targets[n].shape[0] // pieces
        for m in range(pieces):
            at = pl.ds(m * size, size)

            def remote(n=n, at=at, slot=len(starts), bit=bit, held=held):
                return pltpu.make_async_remote_copy(
                    src_ref=held.at[at],
                    dst_ref=targets[n].at[at],
                    send_sem=send_sem.at[slot],
                    recv_sem=recv_sem.at[slot],
                    device_id=peer_of(bit),
                    device_id_type=MESH,
                )

            def start(remote=remote):
                remote().start()

            def finish(remote=remote):
                remote().wait()

            starts.append((prepare if m == 0 else None, start, turns))
            finishes.append(finish)
    return starts, finishes, loads


def all_peers(bits):
    size = lax.axis_size("dp")
    return trade_peers(size) + [peer_of(bit) for bit in bits if bit[0] == "expert"]


def trade_kernel(*refs, plans, work):
    inputs = sum(len(plan[3]) for plan in plans)
    more = 2 if work else 0
    a_ref, sources = refs[0], refs[1 : 1 + inputs]
    work_in, refs = refs[1 + inputs : 1 + inputs + more], refs[1 + inputs + more :]
    out_ref, targets = refs[0], refs[1 : 1 + len(plans)]
    work_out, refs = refs[1 + len(plans) : 1 + len(plans) + more], refs[1 + len(plans) + more :]
    send_sem, recv_sem, local_sem, *scratch = refs
    work_scratch = scratch[-6:] if work else ()
    scratch = scratch[:-6] if work else scratch
    bits = {plan[0] for plan in plans} | ({C_BIT} if work else set())
    greet(all_peers(sorted(bits)))
    trade = trade_start(a_ref, out_ref, send_sem, recv_sem, local_sem.at[0])
    starts, finishes, loads = ride_pieces(sources, targets, plans, scratch)
    for load in loads:
        load.start()
    if work:
        finishes.append(weight_grad(work_in, work_out, work_scratch))
    for prepare, start, _ in starts:
        if prepare is not None:
            prepare()
        start()
    if work:
        finishes[-1] = finishes[-1]()
    trade_end(*trade)
    for finish in finishes:
        finish()


def weight_grad(inputs, outputs, scratch):
    keep, got = outputs
    left, right, sent, held, load_sem, cross_sem = scratch
    loads = [
        pltpu.make_async_copy(source, target, load_sem.at[n])
        for n, (source, target) in enumerate(zip(inputs, (left, right)))
    ]
    for load in loads:
        load.start()
    blocks, part, width = keep.shape
    step = held.shape[1]
    device = lax.axis_index("dp") * lax.axis_size("expert") + lax.axis_index("expert")

    def compute():
        for load in loads:
            load.wait()

        @pl.loop(0, width // step)
        def _(n):
            cols = pl.ds(pl.multiple_of(n * step, step), step)
            held[...] = dot_tn(left[...], right[:, cols]).astype(BF)
            for b in range(blocks):
                own = (2 * b) ^ device
                keep[b, :, cols] = held[pl.ds(pl.multiple_of(own * part, part), part), :]
                own = own ^ 1
                sent[b, :, cols] = held[pl.ds(pl.multiple_of(own * part, part), part), :]

        copy = pltpu.make_async_remote_copy(
            src_ref=sent,
            dst_ref=got,
            send_sem=cross_sem.at[0],
            recv_sem=cross_sem.at[1],
            device_id=peer_of(C_BIT),
            device_id_type=MESH,
        )
        copy.start()
        return copy.wait

    return compute


def run_trade(values, number, riders=(), work=(), blocks=0, mib=60):
    size = values.shape[0]
    inputs = rider_inputs(riders)
    vmem = pl.BlockSpec(memory_space=pltpu.VMEM)
    shapes, specs, scratch = [], [], []
    if work:
        left, right = work
        rows, width = left.shape[1], right.shape[1]
        half = jax.ShapeDtypeStruct((blocks // 2, rows // blocks, width), BF)
        shapes, specs = [half, half], [vmem, hbm]
        scratch = [
            pltpu.VMEM(left.shape, left.dtype),
            pltpu.VMEM(right.shape, right.dtype),
            pltpu.VMEM(half.shape, BF),
            pltpu.VMEM((rows, 256), BF),
            pltpu.SemaphoreType.DMA((2,)),
            pltpu.SemaphoreType.DMA((2,)),
        ]
    out = pl.pallas_call(
        functools.partial(
            trade_kernel, plans=tuple(rider.plan() for rider in riders), work=bool(work)
        ),
        in_specs=[hbm] * (1 + len(inputs) + len(work)),
        out_specs=(hbm,) * (1 + len(riders)) + tuple(specs),
        out_shape=(jax.ShapeDtypeStruct(values.shape, values.dtype),)
        + rider_shapes(riders)
        + tuple(shapes),
        scratch_shapes=[pltpu.SemaphoreType.DMA((n,)) for n in (size - 1, size - 1, 1)]
        + rider_scratch(riders)
        + scratch,
        compiler_params=pltpu.CompilerParams(
            collective_id=number, has_side_effects=True, vmem_limit_bytes=mib * MIB
        ),
        cost_estimate=cost(0, 170e6),
    )(values, *inputs, *work)
    return out if riders or work else out[0]


def first_kernel(a_ref, rank_ref, turned_ref, out_ref, slot_ref, send_sem, recv_sem, local_sem, *, far):
    greet(trade_peers(a_ref.shape[0]))
    trade = trade_start(a_ref, out_ref, send_sem, recv_sem, local_sem.at[0])
    for e in range(rank_ref.shape[0]):
        own = rank_ref[e : e + 1, :]
        smaller = (turned_ref[:, e : e + 1] < own).astype(F32)
        before = jnp.sum(smaller, axis=0, keepdims=True)
        slot_ref[e : e + 1, :] = jnp.where(own < far, jnp.minimum(before, SLOTS), -1.0)
    trade_end(*trade)


def run_first(values, rank_map, turned, far):
    size = values.shape[0]
    vmem = pl.BlockSpec(memory_space=pltpu.VMEM)
    return pl.pallas_call(
        functools.partial(first_kernel, far=far),
        in_specs=[hbm, vmem, vmem],
        out_specs=(hbm, vmem),
        out_shape=(
            jax.ShapeDtypeStruct(values.shape, values.dtype),
            jax.ShapeDtypeStruct(rank_map.shape, F32),
        ),
        scratch_shapes=[pltpu.SemaphoreType.DMA((n,)) for n in (size - 1, size - 1, 1)],
        compiler_params=pltpu.CompilerParams(
            collective_id=2, has_side_effects=True, vmem_limit_bytes=60 * MIB
        ),
        cost_estimate=cost(0, 170e6),
    )(values, rank_map, turned)


def reduce_chain(slot, part, keep_ref, send_ref, outs, acc, got, staged, send_sem, recv_sem):
    first, bits, row, rows, column, columns, order = part
    blocks = keep_ref.shape[0]
    stages = len(bits) + 1
    low = send_ref.dtype
    at = (pl.ds(row, rows), pl.ds(column, columns))
    copies = []

    def exchange(source, target, bit):
        n = slot + len(copies)
        copy = pltpu.make_async_remote_copy(
            src_ref=source,
            dst_ref=target,
            send_sem=send_sem.at[n],
            recv_sem=recv_sem.at[n],
            device_id=peer_of(bit),
            device_id_type=MESH,
        )
        copy.start()
        copies.append(copy)

    live = list(range(blocks))
    base_got, base_sent = 0, 0
    exchange(send_ref.at[(slice(None),) + at], got.at[(pl.ds(0, blocks),) + at], first)
    yield
    for stage in range(stages):
        copies[-1].wait_recv()

        def total(position):
            index = live[position]
            kept = keep_ref[(index,) + at].astype(F32) if stage == 0 else acc[(index,) + at]
            return kept + got[(base_got + position,) + at].astype(F32)

        if stage == stages - 1:
            low_column = 0
            for out_ref in outs:
                if low_column <= column < low_column + out_ref.shape[1]:
                    out_ref[at[0], pl.ds(column - low_column, columns)] = total(0)
                low_column += out_ref.shape[1]
            break
        mask = 1 << order[stage]
        rest = [i for i in live if not i & mask]
        for m, i in enumerate(rest):
            staged[(base_sent + m,) + at] = total(live.index(i ^ mask)).astype(low)
        exchange(
            staged.at[(pl.ds(base_sent, len(rest)),) + at],
            got.at[(pl.ds(base_got + len(live), len(rest)),) + at],
            bits[order[stage]],
        )
        for i in rest:
            acc[(i,) + at] = total(live.index(i))
        base_got += len(live)
        base_sent += len(rest)
        live = rest
        yield
    for copy in copies:
        copy.wait_send()


def reduce_kernel(*refs, jobs, plans, work):
    size = len(jobs)
    given = size - 1 if work else size
    inputs = sum(len(plan[3]) for plan in plans)
    keeps, sends, refs = list(refs[:given]), list(refs[given : 2 * given]), refs[2 * given :]
    sources, refs = refs[:inputs], refs[inputs:]
    compute = None
    if work:
        counts, body = work
        work_in, refs = refs[: counts[0]], refs[counts[0] :]
        work_out, refs = refs[: counts[1]], refs[counts[1] :]
        work_scratch, refs = refs[-counts[2] :], refs[: -counts[2]]
        compute = body(work_in, work_out, work_scratch)
        keeps.append(work_scratch[0])
        sends.append(work_scratch[1])
    outs = []
    for _, _, _, widths in jobs:
        outs.append(refs[: len(widths)])
        refs = refs[len(widths) :]
    targets, scratch = refs[: len(plans)], refs[len(plans) :]
    send_sem, recv_sem = scratch[3 * size : 3 * size + 2]
    used = {bit for first, bits, *_ in jobs for bit in (first,) + bits}
    used |= {plan[0] for plan in plans}
    starts, finishes, loads = ride_pieces(sources, targets, plans, scratch[3 * size + 2 :])
    for load in loads:
        load.start()
    greet([peer_of(bit) for bit in sorted(used)])
    chains, late, slot = [], [], 0
    for n, (first, bits, parts, _) in enumerate(jobs):
        for part in parts:
            (late if n >= given else chains).append(
                reduce_chain(
                    slot,
                    (first, bits) + part,
                    keeps[n],
                    sends[n],
                    outs[n],
                    *scratch[3 * n : 3 * n + 3],
                    send_sem,
                    recv_sem,
                )
            )
            slot += len(bits) + 1
    index = lax.axis_index("dp")
    outer = (index // BIT_ZH) % 2 == (index // BIT_ZL) % 2
    turn, last = 0, max([0] + [n for _, _, turns in starts for n in turns])
    while chains or turn <= last:
        rest = []
        for chain in chains:
            try:
                next(chain)
                rest.append(chain)
            except StopIteration:
                pass
        chains = rest
        for prepare, start, turns in starts:
            if prepare is not None and min(turns) == turn:
                prepare()
            if len(set(turns)) == 1:
                if turns[0] == turn:
                    start()
            else:
                for n, side in enumerate((outer, jnp.logical_not(outer))):
                    if turns[n] == turn:
                        pl.when(side)(start)
        if turn == 0 and work:
            compute()
            chains += late
        turn += 1
    for finish in finishes:
        finish()


def run_reduce(pairs, jobs, number, riders=(), work=None):
    slots = sum(len(parts) * (len(bits) + 1) for _, bits, parts, _ in jobs)
    vmem = pl.BlockSpec(memory_space=pltpu.VMEM)
    scratch, shapes = [], []
    arrays, work_specs, work_shapes, work_scratch, body = work or ((), (), (), (), None)
    late = [(shape, shape) for shape in work_scratch[:1]]
    for (keep, send), (_, _, _, widths) in zip(list(pairs) + late, jobs):
        blocks, rows, cols = keep.shape
        scratch += [
            pltpu.VMEM((blocks, rows, cols), F32),
            pltpu.VMEM((2 * blocks - 1, rows, cols), send.dtype),
            pltpu.VMEM((max(blocks - 1, 1), rows, cols), send.dtype),
        ]
        shapes += [jax.ShapeDtypeStruct((rows, width), F32) for width in widths]
    inputs = rider_inputs(riders)
    return pl.pallas_call(
        functools.partial(
            reduce_kernel,
            jobs=jobs,
            plans=tuple(rider.plan() for rider in riders),
            work=((len(arrays), len(work_shapes), len(work_scratch)), body) if work else None,
        ),
        in_specs=[vmem] * len(pairs) + [hbm] * (len(pairs) + len(inputs)) + list(work_specs),
        out_specs=(vmem,) * (len(work_shapes) + len(shapes)) + (hbm,) * len(riders),
        out_shape=tuple(work_shapes) + tuple(shapes) + rider_shapes(riders),
        scratch_shapes=scratch
        + [pltpu.SemaphoreType.DMA((n,)) for n in (slots, slots)]
        + rider_scratch(riders)
        + list(work_scratch),
        compiler_params=pltpu.CompilerParams(
            collective_id=number, has_side_effects=True, vmem_limit_bytes=60 * MIB
        ),
        cost_estimate=cost(0, 170e6),
    )(*(keep for keep, _ in pairs), *(send for _, send in pairs), *inputs, *arrays)


def sum_pair(kept, received):
    return kept.astype(F32) + received.astype(F32)


def add_low(*terms):
    return sum(term.astype(F32) for term in terms).astype(BF)


def join_kernel(place_ref, *refs):
    outs = refs[-3:]
    zl_at = place_ref[0]

    def total(*terms):
        return sum(term.astype(F32) for term in terms)

    def flat(ref):
        return ref[(0,) * (ref.ndim - 2)]

    def work(parts, part):
        for n in range(2):
            keep, got, more, other = parts[4 * n : 4 * n + 4]
            mine = total(*(flat(term) for term in (keep, got, more)))
            across = flat(other).astype(F32)
            for m in range(2):
                cols = slice(m * LANES, (m + 1) * LANES)
                at = pl.multiple_of((2 * m + zl_at) * LANES, LANES)
                outs[n][part, 0, :, pl.ds(at, LANES)] = mine[:, cols]
                at = pl.multiple_of((2 * m + 1 - zl_at) * LANES, LANES)
                outs[n][part, 0, :, pl.ds(at, LANES)] = across[:, cols]
        keep, got, more = parts[8:]
        outs[2][part, 0] = total(*(flat(term) for term in (keep, got, more)))

    work(refs[0:11], 0)
    work(refs[11:22], 1)


def run_join(place, halves):
    _, _, experts, rows, cols = halves[0][0].shape
    wide_rows, width = halves[0][8].shape[2:]
    arrays, specs = [], []
    for half in halves:
        for operand in half:
            array, lead = operand if isinstance(operand, tuple) else (operand, 0)
            extra = array.ndim - 3
            at = (lead,) + (0,) * (extra - 1) if extra else ()
            arrays.append(array)
            specs.append(
                pl.BlockSpec(
                    (1,) * (extra + 1) + array.shape[-2:],
                    lambda i, p, at=at: at + (i, 0, 0),
                )
            )
    shapes = [(rows, 2 * cols), (rows, 2 * cols), (wide_rows, width)]
    return pl.pallas_call(
        join_kernel,
        grid_spec=pltpu.PrefetchScalarGridSpec(
            num_scalar_prefetch=1,
            grid=(experts,),
            in_specs=specs,
            out_specs=tuple(
                pl.BlockSpec((2, 1) + shape, lambda i, p: (0, i, 0, 0)) for shape in shapes
            ),
        ),
        out_shape=tuple(jax.ShapeDtypeStruct((2, experts) + shape, F32) for shape in shapes),
        compiler_params=params(60, ("arbitrary",)),
        cost_estimate=cost(1e6, 26e6),
    )(place, *arrays)


def fast_body(
    hidden_in,
    gain_attn,
    w_query,
    w_key,
    w_value,
    w_output,
    gain_mlp,
    w_router,
    w_gate,
    w_up,
    w_down,
    expert_ids,
    slot_order,
    grad_out,
):
    inputs = hidden_in[0]
    cotangent = grad_out[0]
    chosen = expert_ids[0]
    tokens = inputs.shape[0]
    top = chosen.shape[1]
    local_experts = w_gate.shape[0]
    peers = lax.axis_size("expert")
    all_experts = local_experts * peers
    shards = lax.axis_size("dp")
    length = shards * tokens
    devices = shards * peers
    index = lax.axis_index("dp")
    column = lax.axis_index("expert")
    y_at = index % 2
    zl_at = (index // 2) % 2
    zh_at = index // 4
    place = jnp.stack(
        [zl_at, y_at, zl_at, zh_at, column * local_experts, index * peers + column]
    ).astype(jnp.int32)

    ranks = slot_order[0, 0].reshape(tokens, top)
    far = tokens * top
    names = jnp.arange(all_experts, dtype=jnp.int32)
    match = chosen.T[None] == names[:, None, None]
    rank_map = jnp.min(jnp.where(match, ranks.T[None], far), axis=1).astype(F32)
    turned = rank_map.T
    map_rows = jnp.pad(
        jnp.where(turned < far, 0.0, -1.0),
        ((0, 0), (0, LANES - all_experts)),
        constant_values=-1.0,
    )
    wr_pad = jnp.pad(w_router, ((0, 0), (0, LANES - all_experts)))
    wr_t = jnp.pad(w_router.T, ((0, LANES - all_experts), (0, 0)))

    half = HEAD_DIM // 2
    frequency = jnp.exp(-math.log(10000.0) * jnp.arange(half, dtype=F32) * 2.0 / HEAD_DIM)
    own_angles = (index * tokens + jnp.arange(tokens, dtype=jnp.int32)).astype(F32)[:, None] * frequency
    cos_own, sin_own = jnp.cos(own_angles), jnp.sin(own_angles)
    cos_tab = jnp.concatenate([cos_own] * 4, axis=1)
    sin_tab = jnp.concatenate([-sin_own, sin_own] * 2, axis=1)
    angles = frequency[:, None] * jnp.arange(length, dtype=jnp.int32).astype(F32)[None]
    cos_t, sin_t = jnp.cos(angles), jnp.sin(angles)

    normed, pack, g_own = run_pre(
        inputs, gain_attn, w_query, w_key, w_value, cos_tab, sin_tab, cotangent
    )
    pack, slot_map = run_first(pack, rank_map, turned, float(far))
    pack, slot_map, g_late = fence(pack, slot_map, g_own)
    g_x = swap_bit(g_own, X_BIT)
    g_z = swap_bit(g_late, ZL_BIT)
    maps = stack_swap(slot_map[None], X_BIT)
    out, out_t, lse = run_forward(pack)
    out, g_x, g_z, maps = fence(out, g_x, g_z, maps)
    g_zx = swap_bit(g_z, X_BIT)
    maps = stack_swap(maps, ZL_BIT)
    att = run_trade(out, 3, mib=16)
    att, g_zx, maps = fence(att, g_zx, maps)
    middle, normed_two, att_full = run_mid(att, w_output, inputs, gain_mlp)
    x_slots, g_slots, gates, maps = run_gather(
        normed_two, (g_own, g_x, g_z, g_zx), maps, wr_t, local_experts
    )
    expert_args = (place, x_slots, g_slots, gates, maps, w_gate, w_up, w_down)
    first = run_experts(*expert_args)
    gate_ka, gate_s0, gate_s1, early, up_ka, up_s0, up_s1, down_ka, down_s0, down_s1 = first[4:]
    down_ya = swap_bit(down_s1, Y_BIT)
    gate_ya = swap_bit(gate_s1, Y_BIT)
    early = swap_bit(early, ZH_BIT)
    mix_keep, mix_send, dx_keep, dx_send, *second = run_experts(*expert_args, prior=first[:4])
    gate_kb, gate_t0, gate_t1, _, up_kb, up_t0, up_t1, down_kb, down_t0, down_t1 = second
    down_ga = swap_bit(down_s0, Y_BIT)
    dx_send, down_ya, gate_ya, early = fence(dx_send, down_ya, gate_ya, early)
    gate_s0 = jnp.stack([gate_s0[0], add_low(gate_s0[1], early[1])])
    quarter = tokens // 4
    extra = dx_keep.shape[2]
    token_parts = tuple(
        (n * quarter, quarter, 0, extra, (1, 0) if n < 2 else (0, 1)) for n in (0, 2, 1, 3)
    )
    dx_sum, up_ya, gate_ga, mix_got, down_ma = run_reduce(
        ((dx_keep, dx_send),),
        ((C_BIT, (X_BIT, ZL_BIT), token_parts, (extra,)),),
        6,
        riders=(
            Rider(Y_BIT, up_s1),
            Rider(Y_BIT, gate_s0),
            Rider(C_BIT, mix_send, turns=(1,)),
            Rider(ZH_BIT, (down_ka, (1,)), down_ya, turns=(1, 0)),
        ),
    )
    dx_sum, gate_ya, down_ga, gate_t1 = fence(dx_sum, gate_ya, down_ga, gate_t1)
    gate_ma = swap_bit(add_low(gate_ka[1, 0], gate_ya[0]), ZH_BIT)
    gate_yb = swap_bit(gate_t1, Y_BIT)
    d_att, d_middle, d_low, d_log, ggain_mlp = run_post(
        dx_sum, middle, cotangent, normed_two, wr_pad, map_rows, gain_mlp, w_output
    )
    mix_keep = mix_keep.reshape(2, 2, tokens, WIDTH)
    mix_got = mix_got.reshape(2, 2, tokens, WIDTH)
    every = slice(None)
    d_out, up_yb, up_za, gate_oa, mix_x, out_keep, out_got = run_trade(
        d_att,
        4,
        work=(att_full, d_low),
        blocks=devices,
        riders=(
            Rider(Y_BIT, up_t1),
            Rider(ZH_BIT, (up_ka, (1, 1)), (up_ya, (1,))),
            Rider(ZL_BIT, (gate_ka, (0, 1)), (early, (0,)), (gate_ga, (1,))),
            Rider(X_BIT, (mix_keep, (every, 1)), (mix_got, (every, 1))),
        ),
    )
    split = (8, 2, WIDTH // devices, WIDTH)
    out_keep, out_got = out_keep.reshape(split), out_got.reshape(split)
    up_ga, down_yb, up_late, gate_late, gate_ma, d_out = fence(
        up_s0, down_t1, up_ya, gate_yb, gate_ma, d_out
    )
    both = jnp.stack([add_low(up_ka[1, 0], up_late[0]), add_low(gate_kb[1, 1], gate_late[1])])
    both = swap_bit(both, ZH_BIT)
    up_ga = swap_bit(up_ga, Y_BIT)
    down_yb = swap_bit(down_yb, Y_BIT)
    d_pack = run_backward(pack, d_out, out_t, lse, cos_t, sin_t)
    d_pack, both, up_ga, down_yb = fence(d_pack, both, up_ga, down_yb)
    d_pack, gate_gb, up_gb, gate_mb, up_zb, mix_z, out_x, up_oa = run_trade(
        d_pack,
        5,
        riders=(
            Rider(Y_BIT, gate_t0),
            Rider(Y_BIT, up_t0),
            Rider(ZH_BIT, (gate_kb, (1, 0)), (gate_yb, (0,))),
            Rider(ZH_BIT, (up_kb, (1, 1)), (up_yb, (1,))),
            Rider(
                ZL_BIT,
                (mix_keep, (slice(1, 2), 0)),
                (mix_got, (slice(1, 2), 0)),
                (mix_x, (slice(1, 2),)),
            ),
            Rider(X_BIT, (out_keep, (every, 1)), (out_got, (every, 1))),
            Rider(ZL_BIT, (up_ka, (0, 1)), (up_ga, (1,)), (up_za, (every,))),
        ),
    )
    d_pack, up_yb, down_yb, gate_gb, down_t0, mix_z, out_x = fence(
        d_pack, up_yb, down_yb, gate_gb, down_t0, mix_z, out_x
    )
    other = jnp.stack(
        [add_low(gate_kb[0, 1], gate_gb[1], both[1]), add_low(up_kb[0, 1], up_gb[1], up_zb)]
    )
    other = swap_bit(other, ZL_BIT)
    down_mb = swap_bit(add_low(down_kb[1], down_yb), ZH_BIT)
    down_gb = swap_bit(down_t0, Y_BIT)
    d_full, qkv_keep, qkv_send = run_qkvgrad(place, normed, d_pack, devices)
    mixed = sum_pair(mix_keep[0, 0], mix_got[0, 0]) + sum_pair(mix_x[0], mix_z[0])
    hidden_out = middle + mixed
    rows = WIDTH // devices
    out_held = add_low(out_keep[:, 0], out_got[:, 0], out_x).reshape(4, 2, rows, WIDTH)
    out_first, out_second = out_held[:, 0], out_held[:, 1]
    qkv_send, out_second, hidden_out = fence(qkv_send, out_second, hidden_out)
    qkv_parts = (
        (0, rows, 0, 768, (0, 1, 2, 3)),
        (0, rows, 768, 768, (1, 0, 2, 3)),
        (0, rows, 1536, 512, (0, 1, 2, 3)),
        (0, rows, 2048, 512, (1, 0, 2, 3)),
    )
    dense_bits = (X_BIT, Y_BIT, ZL_BIT, ZH_BIT)
    last = (d_full, w_query, w_key, w_value, d_middle, inputs, normed_two, d_log)
    grad_in, query_total, key_total, value_total, output_total, small, up_mb = run_reduce(
        ((qkv_keep, qkv_send), (out_first, out_second)),
        (
            (C_BIT, dense_bits, qkv_parts, (WIDTH, KV_HEADS * HEAD_DIM, KV_HEADS * HEAD_DIM)),
            (Y_BIT, (ZL_BIT, ZH_BIT), ((0, rows, 0, WIDTH, (0, 1)),), (WIDTH,)),
            (C_BIT, dense_bits, ((0, rows, 0, LANES, (0, 1, 2, 3)),), (LANES,)),
        ),
        7,
        riders=(Rider(ZH_BIT, (up_kb, (1, 0)), (up_yb, (0,))),),
        work=plan_last(last, gain_attn, ggain_mlp, devices),
    )
    query_total, small, down_mb, down_gb, other = fence(
        query_total, small, down_mb, down_gb, other
    )
    joined = run_join(
        place,
        (
            (gate_ka, gate_ga, gate_ma, gate_oa, up_ka, up_ga, (both, 0), up_oa)
            + (down_ka, down_ga, down_ma),
            (gate_kb, gate_gb, gate_mb, (other, 0), up_kb, up_gb, up_mb, (other, 1))
            + (down_kb, down_gb, down_mb),
        ),
    )
    gate_total, up_total, down_total = [
        total.reshape((local_experts,) + total.shape[2:]) for total in joined
    ]
    return (
        hidden_out[None],
        grad_in[None],
        small[:, LANES - 1],
        query_total,
        key_total,
        value_total,
        output_total,
        small[:, LANES - 2],
        small[:, :all_experts],
        gate_total,
        up_total,
        down_total,
    )


def fits(mesh):
    return mesh.shape["dp"] == KV_HEADS and mesh.shape["expert"] == 4


def solution(mesh):
    in_specs = (
        P("expert", "dp", None),
        P(),
        P(),
        P(),
        P(),
        P(),
        P(),
        P(),
        P("expert", None, None),
        P("expert", None, None),
        P("expert", None, None),
        P("expert", "dp", None),
        P("expert", "dp", None),
        P("expert", "dp", None),
    )
    out_specs = (
        P("expert", "dp", None),
        P("expert", "dp", None),
        P(("dp", "expert")),
        P(("dp", "expert"), None),
        P(("dp", "expert"), None),
        P(("dp", "expert"), None),
        P(("dp", "expert"), None),
        P(("dp", "expert")),
        P(("dp", "expert"), None),
        P("expert", "dp", None),
        P("expert", "dp", None),
        P("expert", "dp", None),
    )
    chosen = fast_body if fits(mesh) else body
    return jax.shard_map(chosen, mesh=mesh, in_specs=in_specs, out_specs=out_specs, check_vma=False)
```
